32 devices in a mesh: seq: 8 (over z, x), wt: 4 (over y, core).
Axes of the slice: x: 2, y: 2, z: 4, core: 2. Of those that a mesh axis runs over, the one named last changes fastest.
Arguments:
- inputs: bfloat16 [4, 2048, 1024], P('wt', 'seq'), may hold values from -6 to 6
- cotangent: bfloat16 [4, 2048, 1024], P('wt', 'seq'), may hold values from -6 to 6
- doc_lengths: int32 [4, 16], P('wt'), may hold values from 1 to 1024, 2048 in all within a row
- norm_gain: bfloat16 [1024], P(('seq', 'wt')), may hold values from 0.099609375 to 1.8984375
- norm_bias: bfloat16 [1024], P(('seq', 'wt')), may hold values from -3 to 3
- gate_weight: bfloat16 [1024, 3072], P(('seq', 'wt')), may hold values from -0.1875 to 0.1875
- value_weight: bfloat16 [1024, 512], P(('seq', 'wt')), may hold values from -0.1875 to 0.1875
- mix_weight: bfloat16 [512, 3072], P(('seq', 'wt')), may hold values from -0.25 to 0.25
- down_weight: bfloat16 [3072, 1024], P(('seq', 'wt')), may hold values from -0.15625 to 0.15625
- decay_rate: float32 [512, 512], P('seq'), may hold values from 0.0001 to 0.05
- frequency: float32 [512, 512], P('seq'), may hold values from 0.1 to 1
- kernel_re: float32 [512, 512], P('seq'), may hold values from -0.015625 to 0.015625
- kernel_im: float32 [512, 512], P('seq'), may hold values from -0.015625 to 0.015625
- log_step: float32 [512], P('seq'), may hold values from -0.7 to 0.7
- skip_gain: float32 [512], P('seq'), may hold values from 0.5 to 1.5
Outputs:
- outputs: bfloat16 [4, 2048, 1024], P('wt', 'seq')
- input_grad: float32 [4, 2048, 1024], P('wt', 'seq')
- norm_gain_grad: float32 [1024], P(('seq', 'wt'))
- norm_bias_grad: float32 [1024], P(('seq', 'wt'))
- gate_grad: float32 [1024, 3072], P(('seq', 'wt'))
- value_grad: float32 [1024, 512], P(('seq', 'wt'))
- mix_grad: float32 [512, 3072], P(('seq', 'wt'))
- down_grad: float32 [3072, 1024], P(('seq', 'wt'))
- decay_grad: float32 [512, 512], P('seq')
- frequency_grad: float32 [512, 512], P('seq')
- kernel_re_grad: float32 [512, 512], P('seq')
- kernel_im_grad: float32 [512, 512], P('seq')
- log_step_grad: float32 [512], P('seq')
- skip_grad: float32 [512], P('seq')
The draws below stay inside these ranges and needn't reach their ends.
Inputs may be any that keep to these rules, and one draw needn't show every extreme that they name: `doc_lengths`: the 16 document lengths of each sequence sum to 2048, and the longest is exactly 1024.
All inputs are finite; a program needn't handle non-finite values.
Results may differ from the reference program's by a relative error of at most 0.017.
Values may be sent and summed in bfloat16 or wider, within the bound.
A program may use at most 192 MiB of HBM per device.

```python
import math
import jax
import jax.numpy as jnp
import numpy as np
from jax import lax

D = 1024
F = 3072
H = 512
N = 512
BLOCK = 128
DOCS = 16
SEQS = 1
LEN = 2048
MOST = 1024
N_SEQ = 8
N_WT = 4


def block_scale(key, shape, pieces, low, largest):
    def one(axis_at, blocks):
        steps = jax.random.uniform(jax.random.fold_in(jax.random.fold_in(key, 6), axis_at), (blocks,), jnp.float32, low / len(pieces), largest / len(pieces))
        return jnp.repeat(jnp.exp(steps), shape[axis_at] // blocks).reshape((-1,) + (1,) * (len(shape) - axis_at - 1))

    level = one(*pieces[0])
    for cut in pieces[1:]:
        level = level * one(*cut)
    return level


def length_profile(number_of, total, reach, lean):
    portions = [(1 << 20) // math.isqrt(rank ** lean) + 1 for rank in range(2, number_of + 1)]
    rest, given = total - reach - (number_of - 1), [1] * (number_of - 1)
    while rest > 0:
        candidates = [i for i in range(number_of - 1) if given[i] < reach]
        whole, left = sum([portions[i] for i in candidates]), rest
        for i in candidates:
            extra = min(reach - given[i], max(1, left * portions[i] // whole), rest)
            given[i] = given[i] + extra
            rest = rest - extra
    return np.array([reach] + given)


def ragged_sizes(key, amount, total, most, lean):
    if amount == 2:
        one = jax.random.randint(key, (), max(1, total - most), min(most, total - 1) + 1)
        return jnp.stack([one, total - one])
    tallies = jnp.asarray(length_profile(amount, total, most, lean), jnp.int32)
    pairs = (amount - 1) // 2
    donor, sink = tallies[1:1 + 2 * pairs:2], tallies[2:2 + 2 * pairs:2]
    room = jnp.minimum(donor - 1, most - sink)
    shifted = jax.random.randint(jax.random.fold_in(key, 1), (pairs,), 0, 1 << 20) % (room + 1)
    tallies = tallies.at[1:1 + 2 * pairs:2].set(donor - shifted).at[2:2 + 2 * pairs:2].set(sink + shifted)
    return tallies[jax.random.permutation(jax.random.fold_in(key, 2), amount)]


def noise(key, extent, deviation, reach, cuts=(), held_as=jnp.bfloat16):
    drawn = deviation * jax.random.normal(key, extent, jnp.float32)
    if cuts:
        drawn = drawn * block_scale(key, extent, cuts, -0.22, 0.18)
    return jnp.clip(drawn, -reach, reach).astype(held_as)


def setup_inputs(seed: int = 0) -> dict:
    key_list = jax.random.split(jax.random.key(seed), 16)
    return {
        "inputs": noise(key_list[0], (SEQS * N_WT, LEN, D), 1.0, 6.0, ((0, 4), (1, 8))),
        "cotangent": noise(key_list[1], (SEQS * N_WT, LEN, D), 1.0, 6.0, ((0, 4), (1, 8))),
        "doc_lengths": jax.vmap(lambda own: ragged_sizes(own, DOCS, LEN, MOST, 2))(jax.random.split(key_list[2], (SEQS * N_WT))).reshape((SEQS * N_WT, DOCS)).astype(jnp.int32),
        "norm_gain": jnp.clip(1.0 + 0.18 * jax.random.normal(key_list[3], (D,), jnp.float32), 0.099609375, 1.8984375).astype(jnp.bfloat16),
        "norm_bias": noise(key_list[4], (D,), 0.5, 3.0, ((0, 32),)),
        "gate_weight": noise(key_list[5], (D, F), D ** -0.5, 0.1875, ((0, 32),)),
        "value_weight": noise(key_list[6], (D, H), D ** -0.5, 0.1875, ((0, 32),)),
        "mix_weight": noise(key_list[7], (H, F), H ** -0.5, 0.25, ((0, 32),)),
        "down_weight": noise(key_list[8], (F, D), (F // 2) ** -0.5, 0.15625, ((0, 32),)),
        "decay_rate": jnp.clip(jnp.exp(math.log(0.05) - 6.214608 * jax.random.uniform(key_list[9], (H, N), jnp.float32) ** block_scale(key_list[9], (H, N), ((0, 8),), -0.2, 0.2)), 0.0001, 0.05),
        "frequency": jnp.clip(0.1 + 0.9 * jax.random.uniform(key_list[10], (H, N), jnp.float32) ** block_scale(key_list[10], (H, N), ((0, 8),), -0.2, 0.2), 0.1, 1.0),
        "kernel_re": noise(key_list[11], (H, N), (256 * N) ** -0.5, 0.015625, ((0, 8),), jnp.float32),
        "kernel_im": noise(key_list[12], (H, N), (256 * N) ** -0.5, 0.015625, ((0, 8),), jnp.float32),
        "log_step": jnp.clip(jax.random.uniform(key_list[13], (H,), jnp.float32, -0.7, 0.7) * block_scale(key_list[13], (H,), ((0, 8),), -0.4, 0.0), -0.7, 0.7),
        "skip_gain": jnp.clip(0.5 + 1.0 * jax.random.uniform(key_list[14], (H,), jnp.float32) ** block_scale(key_list[14], (H,), ((0, 8),), -0.2, 0.2), 0.5, 1.5),
    }


norm_epsilon = 1e-05
group_width = 16
highest = lax.Precision.HIGHEST

@jax.custom_vjp
def low(v):
    return lax.optimization_barrier(v.astype(jnp.bfloat16)).astype(jnp.float32)

@jax.custom_vjp
def low_back(v):
    return v

def low_keep(v):
    return (low(v), None)

def low_pass(kept, grad):
    return (grad,)

def back_keep(v):
    return (v, None)

def back_low(kept, grad):
    return (low(grad),)
low.defvjp(low_keep, low_pass)
low_back.defvjp(back_keep, back_low)

def gelu_tanh(pre_act):
    return jax.nn.gelu(pre_act, approximate=True)

def layer_norm(token_rows, gain_vec, bias_vec):
    row_mean = lax.optimization_barrier(jnp.mean(token_rows, axis=-1, keepdims=True))
    centered = token_rows - row_mean
    spread = lax.optimization_barrier(jnp.mean(centered * centered, axis=-1, keepdims=True))
    return centered * lax.rsqrt(spread + norm_epsilon) * gain_vec + bias_vec

def doc_segments(doc_lengths, seq_length):
    ends = jnp.cumsum(doc_lengths, axis=-1).astype(jnp.int32)
    places = jnp.arange(seq_length, dtype=jnp.int32)
    passed = (places[None, :, None] >= ends[:, None, :]).astype(jnp.int32)
    return lax.optimization_barrier(jnp.sum(passed, axis=-1, dtype=jnp.int32))

def dss_mix(values, decay_rate, frequency, kernel_re, kernel_im, log_step, skip_gain, segment, block_len):
    seq_count, seq_length, channels = values.shape
    block_count = seq_length // block_len
    quad_count = block_count // 4
    step_size = jnp.exp(log_step)[:, None]
    damping = (decay_rate * step_size)[:, None, :]
    turning = (frequency * step_size)[:, None, :]
    offsets = jnp.arange(block_len, dtype=jnp.float32)
    after = (offsets + 1.0)[None, :, None]
    before = (block_len - 1.0 - offsets)[None, :, None]
    out_mag = jnp.exp(-damping * after)
    out_re = out_mag * jnp.cos(turning * after)
    out_im = out_mag * jnp.sin(turning * after)
    in_mag = jnp.exp(-damping * before)
    in_re = in_mag * jnp.cos(turning * before)
    in_im = in_mag * jnp.sin(turning * before)
    kernel_rev = lax.optimization_barrier(jnp.sum(in_re * kernel_re[:, None, :] - in_im * kernel_im[:, None, :], axis=-1))
    places = jnp.arange(block_len, dtype=jnp.int32)
    lag_table = places[:, None] - places[None, :]
    lookup = jnp.clip(block_len - 1 - lag_table, 0, block_len - 1).astype(jnp.int32)
    lower = (lag_table >= 0).astype(jnp.float32)
    toeplitz = jnp.take(kernel_rev, lookup.reshape(-1), axis=1).reshape(channels, block_len, block_len) * lower
    blocked = values.reshape(seq_count, block_count, block_len, channels)
    seg_blocks = segment.reshape(seq_count, block_count, block_len)

    def within(quad_pair):
        val_quad, seg_quad = quad_pair
        same = (seg_quad[:, :, :, None] == seg_quad[:, :, None, :]).astype(jnp.float32)
        weights = toeplitz[None, None] * same[:, :, None]
        return jnp.einsum('sgcpq,sgqc->sgpc', weights, val_quad, precision=highest)
    quad_items = (jnp.moveaxis(blocked.reshape(seq_count, quad_count, 4, block_len, channels), 1, 0), jnp.moveaxis(seg_blocks.reshape(seq_count, quad_count, 4, block_len), 1, 0))
    local_part = lax.map(jax.checkpoint(within), quad_items)
    local_part = jnp.moveaxis(local_part, 0, 1).reshape(seq_count, block_count, block_len, channels)
    seg_end = seg_blocks[:, :, -1]
    seg_prev = jnp.concatenate([jnp.full((seq_count, 1), -1, dtype=jnp.int32), seg_end[:, :-1]], axis=1)
    keep_in = (seg_blocks == seg_end[:, :, None]).astype(jnp.float32)
    keep_out = (seg_blocks == seg_prev[:, :, None]).astype(jnp.float32)
    masked = blocked * keep_in[:, :, :, None]
    gather_re = jnp.einsum('cpn,sbpc->bscn', in_re, masked, precision=highest)
    gather_im = jnp.einsum('cpn,sbpc->bscn', in_im, masked, precision=highest)
    flags = jnp.moveaxis((seg_end == seg_prev).astype(jnp.float32), 1, 0)
    jump_mag = jnp.exp(-damping[:, 0, :] * block_len)
    jump_re = jump_mag * jnp.cos(turning[:, 0, :] * block_len)
    jump_im = jump_mag * jnp.sin(turning[:, 0, :] * block_len)

    def advance(state_pair, block_item):
        state_re, state_im = state_pair
        part_re, part_im, live = block_item
        live = live[:, None, None]
        next_re = live * (jump_re * state_re - jump_im * state_im) + part_re
        next_im = live * (jump_re * state_im + jump_im * state_re) + part_im
        return ((next_re, next_im), (state_re, state_im))
    start = jnp.zeros((seq_count, channels, decay_rate.shape[1]), jnp.float32)
    unused, starts = lax.scan(advance, (start, start), (gather_re, gather_im, flags))
    start_re, start_im = starts
    mixed_re = kernel_re * start_re - kernel_im * start_im
    mixed_im = kernel_re * start_im + kernel_im * start_re
    carried = jnp.einsum('cpn,bscn->sbpc', out_re, mixed_re, precision=highest) - jnp.einsum('cpn,bscn->sbpc', out_im, mixed_im, precision=highest)
    total = local_part + carried * keep_out[:, :, :, None] + skip_gain * blocked
    return total.reshape(seq_count, seq_length, channels)

def group_dot(left, right):
    return jnp.einsum('wsrd,wsdf->wsrf', left, right, precision=highest)

def copies(array):
    return low_back(jnp.broadcast_to(array, (N_WT, N_SEQ) + array.shape))

def reference(inputs, cotangent, doc_lengths, norm_gain, norm_bias, gate_weight, value_weight, mix_weight, down_weight, decay_rate, frequency, kernel_re, kernel_im, log_step, skip_gain):
    seq_count, seq_length, model_width = inputs.shape
    segment = doc_segments(doc_lengths, seq_length)
    group_count = H // group_width
    per_group = seq_count // N_WT
    local_len = seq_length // N_SEQ

    def to_groups(array):
        width = array.shape[-1]
        moved = array.reshape(N_WT, per_group, N_SEQ, local_len, width).transpose(0, 2, 1, 3, 4)
        return moved.reshape(N_WT, N_SEQ, per_group * local_len, width)

    def from_groups(array):
        width = array.shape[-1]
        moved = array.reshape(N_WT, N_SEQ, per_group, local_len, width).transpose(0, 2, 1, 3, 4)
        return moved.reshape(seq_count, seq_length, width)

    def grouped(array):
        return array.reshape((group_count, group_width) + array.shape[1:])

    def mix_all(values, decay_in, freq_in, real_in, imag_in, step_in, skip_in):
        moved = values.reshape(seq_count, seq_length, group_count, group_width).transpose(2, 0, 1, 3)

        def one_group(group_item):
            return dss_mix(group_item[0], group_item[1], group_item[2], group_item[3], group_item[4], group_item[5], group_item[6], segment, BLOCK)
        parts = lax.map(jax.checkpoint(one_group), (moved, grouped(decay_in), grouped(freq_in), grouped(real_in), grouped(imag_in), grouped(step_in), grouped(skip_in)))
        return parts.transpose(1, 2, 0, 3).reshape(seq_count, seq_length, H)

    def forward(block_in, gain_in, bias_in, gate_in, value_in, mix_in, down_in, decay_in, freq_in, real_in, imag_in, step_in, skip_in):
        token_rows = to_groups(block_in)
        gain_copy = copies(gain_in)[:, :, None, :]
        bias_copy = copies(bias_in)[:, :, None, :]
        normed = low(layer_norm(token_rows, gain_copy, bias_copy))
        gate_pre = low_back(group_dot(normed, copies(gate_in)))
        gate_act = gelu_tanh(gate_pre)
        value_pre = low_back(group_dot(normed, copies(value_in)))
        value_act = low_back(low(gelu_tanh(value_pre)))
        mixed = mix_all(from_groups(value_act), decay_in, freq_in, real_in, imag_in, step_in, skip_in)
        mixed = to_groups(low_back(low(mixed)))
        expand = low_back(group_dot(mixed, copies(mix_in)))
        product = low(expand * gate_act)
        return from_groups(token_rows + group_dot(product, copies(down_in)))
    result, pullback = jax.vjp(forward, inputs.astype(jnp.float32), norm_gain.astype(jnp.float32), norm_bias.astype(jnp.float32), gate_weight.astype(jnp.float32), value_weight.astype(jnp.float32), mix_weight.astype(jnp.float32), down_weight.astype(jnp.float32), decay_rate, frequency, kernel_re, kernel_im, log_step, skip_gain)
    grads = pullback(cotangent.astype(jnp.float32))
    return (result.astype(jnp.bfloat16), grads[0], grads[1], grads[2], grads[3], grads[4], grads[5], grads[6], grads[7], grads[8], grads[9], grads[10], grads[11], grads[12])
```

```python
import functools

import jax
import jax.numpy as jnp
from jax import lax
from jax.experimental import pallas as pl
from jax.experimental.pallas import tpu as pltpu
from jax.sharding import PartitionSpec as P

LANES = 128
PAD = 16


def cmul(ar, ai, br, bi):
    return ar * br - ai * bi, ar * bi + ai * br


def power_rows(pw_re, pw_im, c, first, count, rows):
    width = pw_re.shape[2]
    place = lax.broadcasted_iota(jnp.int32, (rows, width), 0)
    re = jnp.ones((rows, width), jnp.float32)
    im = jnp.zeros((rows, width), jnp.float32)
    for bit in range(count):
        on = (place & (1 << bit)) != 0
        fr = jnp.where(on, pw_re[c, pl.ds(first + bit, 1), :], 1.0)
        fi = jnp.where(on, pw_im[c, pl.ds(first + bit, 1), :], 0.0)
        re, im = cmul(re, im, fr, fi)
    return re, im


def fill_lane_powers(pw_re, pw_im, c, tab_re, tab_im, extra):
    re, im = power_rows(pw_re, pw_im, c, 0, 3, 8)
    if extra:
        re, im = cmul(re, im, pw_re[c, pl.ds(0, 1), :], pw_im[c, pl.ds(0, 1), :])
    tab_re[0:8, :] = re
    tab_im[0:8, :] = im
    have, bit = 8, 3
    while have < LANES:
        re, im = cmul(
            tab_re[0:have, :],
            tab_im[0:have, :],
            pw_re[c, pl.ds(bit, 1), :],
            pw_im[c, pl.ds(bit, 1), :],
        )
        tab_re[have : 2 * have, :] = re
        tab_im[have : 2 * have, :] = im
        have, bit = 2 * have, bit + 1


def to_pieces(seg, val, rows, docs):
    total = jnp.zeros((rows, LANES), jnp.float32)
    for j in range(docs):
        at = pl.ds(PAD - j, rows)
        total = total + jnp.where(seg[at, :] == j, val[at, :], 0.0)
    return total


def from_pieces(seg, piece, rows, docs):
    own = seg[pl.ds(PAD, rows), :]
    total = jnp.zeros((rows, LANES), jnp.float32)
    for j in range(docs):
        total = total + jnp.where(own == j, piece[pl.ds(j, rows), :], 0.0)
    return total


def toeplitz(lags, d, last, lower, before):
    if d < last:
        row = jnp.broadcast_to(lags[d : d + 1, :], (LANES, LANES))
        here = pltpu.roll(row, 0, 1, stride=1, stride_axis=0)
    else:
        here = jnp.zeros((LANES, LANES), jnp.float32)
    return jnp.where(lower, here, before).astype(jnp.bfloat16), here


def dot(a, b, ca=1, cb=0):
    return lax.dot_general(a, b, (((ca,), (cb,)), ((), ())), preferred_element_type=jnp.float32)


def mix_forward_kernel(
    n_lag, docs, bits, v_ref, seg_ref, sid_ref, pw_re, pw_im, kr_ref, ki_ref, skip_ref,
    y_ref, lag_ref, vf, vp, yp, tab_re, tab_im,
):
    channels, rows, _ = v_ref.shape
    zero_pad = jnp.zeros((PAD, LANES), jnp.float32)
    vf[0:PAD, :] = zero_pad
    vp[0:PAD, :] = zero_pad
    yp[pl.ds(rows, PAD), :] = zero_pad
    lower = lax.broadcasted_iota(jnp.int32, (LANES, LANES), 1) >= lax.broadcasted_iota(
        jnp.int32, (LANES, LANES), 0
    )

    def channel(c, unused):
        fill_lane_powers(pw_re, pw_im, c, tab_re, tab_im, 0)
        dr, di = power_rows(pw_re, pw_im, c, 7, bits, n_lag)
        ar, ai = cmul(dr, di, kr_ref[pl.ds(c, 1), :], ki_ref[pl.ds(c, 1), :])
        lags = dot(ar.astype(jnp.bfloat16), tab_re[...].astype(jnp.bfloat16), 1, 1) - dot(
            ai.astype(jnp.bfloat16), tab_im[...].astype(jnp.bfloat16), 1, 1
        )
        lag_ref[c] = lags
        val = v_ref[c].astype(jnp.float32)
        vf[pl.ds(PAD, rows), :] = val
        vp[pl.ds(PAD, rows), :] = to_pieces(seg_ref, vf, rows, docs)
        sid = sid_ref[pl.ds(PAD, rows), :]
        before = jnp.zeros((LANES, LANES), jnp.float32)
        total = jnp.zeros((rows, LANES), jnp.float32)
        for d in range(n_lag + 1):
            at = pl.ds(PAD - d, rows)
            x = jnp.where(sid_ref[at, :] == sid, vp[at, :], 0.0).astype(jnp.bfloat16)
            t, before = toeplitz(lags, d, n_lag, lower, before)
            total = total + dot(x, t)
        yp[0:rows, :] = total
        out = from_pieces(seg_ref, yp, rows, docs) + skip_ref[pl.ds(c, 1), :] * val
        y_ref[c] = out.astype(jnp.bfloat16)
        return unused

    lax.fori_loop(0, channels, channel, 0)


def mix_backward_kernel(
    n_lag, docs, bits, v_ref, g_ref, seg_ref, sid_ref, pw_re, pw_im, kr_ref, ki_ref, rate_ref,
    freq_ref, dt_ref, skip_ref, lag_ref,
    dv_ref, kr_out, ki_out, rate_out, freq_out, step_out, skip_out,
    vf, gf, vp, gp, yp, tab_re, tab_im,
):
    channels, rows, _ = v_ref.shape
    zero_pad = jnp.zeros((PAD, LANES), jnp.float32)
    vf[0:PAD, :] = zero_pad
    gf[0:PAD, :] = zero_pad
    vp[0:PAD, :] = zero_pad
    gp[pl.ds(rows, PAD), :] = zero_pad
    yp[pl.ds(rows, PAD), :] = zero_pad
    lane = lax.broadcasted_iota(jnp.int32, (LANES, LANES), 1)
    row = lax.broadcasted_iota(jnp.int32, (LANES, LANES), 0)
    lower = lane >= row
    wraps = lane + row >= LANES
    flip = (lane + row == LANES - 1).astype(jnp.bfloat16)
    lag_place = (
        lax.broadcasted_iota(jnp.int32, (n_lag, LANES), 0) * LANES
        + lax.broadcasted_iota(jnp.int32, (n_lag, LANES), 1)
        + 1
    ).astype(jnp.float32)

    def channel(c, unused):
        own = pl.ds(c, 1)
        val = v_ref[c].astype(jnp.float32)
        grad = g_ref[c].astype(jnp.float32)
        vf[pl.ds(PAD, rows), :] = val
        gf[pl.ds(PAD, rows), :] = grad
        skip_grad = jnp.sum(jnp.sum(val * grad, axis=0, keepdims=True), axis=1, keepdims=True)
        g_piece = to_pieces(seg_ref, gf, rows, docs)
        gp[0:rows, :] = g_piece
        v_piece = to_pieces(seg_ref, vf, rows, docs).astype(jnp.bfloat16)
        vp[pl.ds(PAD, rows), :] = dot(v_piece, flip)
        g_turned = jnp.transpose(g_piece).astype(jnp.bfloat16)
        sid = sid_ref[pl.ds(PAD, rows), :]
        lags = lag_ref[c]
        before = jnp.zeros((LANES, LANES), jnp.float32)
        total = jnp.zeros((rows, LANES), jnp.float32)
        earlier = None
        sums = []
        for d in range(n_lag + 1):
            ahead = pl.ds(PAD + d, rows)
            x = jnp.where(sid_ref[ahead, :] == sid, gp[pl.ds(d, rows), :], 0.0)
            t, before = toeplitz(lags, d, n_lag, lower, before)
            total = total + dot(x.astype(jnp.bfloat16), t, 1, 1)
            at = pl.ds(PAD - d, rows)
            back = jnp.where(sid_ref[at, :] == sid, vp[at, :], 0.0).astype(jnp.bfloat16)
            pairs = dot(g_turned, back)
            if d:
                skew = jnp.where(wraps, earlier, pairs)
                skew = pltpu.roll(skew, 0, 1, stride=1, stride_axis=0)
                sums.append(jnp.sum(skew, axis=0, keepdims=True))
            earlier = pairs
        yp[0:rows, :] = total
        out = from_pieces(seg_ref, yp, rows, docs) + skip_ref[own, :] * grad
        dv_ref[c] = out.astype(jnp.bfloat16)
        lag_grad = jnp.concatenate(sums, axis=0)
        fill_lane_powers(pw_re, pw_im, c, tab_re, tab_im, 1)
        both = jnp.concatenate([lag_grad, lag_grad * lag_place], axis=0).astype(jnp.bfloat16)
        part_re = dot(both, tab_re[...].astype(jnp.bfloat16))
        part_im = dot(both, tab_im[...].astype(jnp.bfloat16))
        dr, di = power_rows(pw_re, pw_im, c, 7, bits, n_lag)
        gr, gi = cmul(dr, di, part_re[0:n_lag], part_im[0:n_lag])
        hr, hi = cmul(dr, di, part_re[n_lag:], part_im[n_lag:])
        gr, gi, hr, hi = (jnp.sum(a, axis=0, keepdims=True) for a in (gr, gi, hr, hi))
        kr, ki, dt = kr_ref[own, :], ki_ref[own, :], dt_ref[own, :]
        rate_grad = -dt * (kr * hr - ki * hi)
        freq_grad = -dt * (kr * hi + ki * hr)
        kr_out[own, :] = gr + skip_grad
        ki_out[own, :] = -gi
        rate_out[own, :] = rate_grad
        freq_out[own, :] = freq_grad
        step = jnp.sum(
            rate_grad * rate_ref[own, :] + freq_grad * freq_ref[own, :], axis=1, keepdims=True
        )
        step_out[own, :] = jnp.broadcast_to(step, (1, LANES))
        skip_out[own, :] = jnp.broadcast_to(skip_grad, (1, LANES))
        return unused

    lax.fori_loop(0, channels, channel, 0)


def vmem(*shape):
    return pltpu.VMEM(shape, jnp.float32)


def table_inputs(decay_rate, frequency, log_step, n_lag):
    bits = (n_lag - 1).bit_length()
    dt = jnp.exp(log_step)[:, None]
    powers = jnp.array([float(1 << b) for b in range(7 + bits)] + [0.0] * (9 - bits), jnp.float32)
    powers = powers[None, :, None]
    mag = jnp.exp(-(decay_rate * dt)[:, None, :] * powers)
    phase = (frequency * dt)[:, None, :] * powers
    return dt, bits, mag * jnp.cos(phase), mag * jnp.sin(phase)


def segment_tables(segment, docs):
    seqs, length = segment.shape
    blocks = length // LANES
    per = -(-(blocks + docs) // 8) * 8
    seg = segment.reshape(seqs, blocks, LANES)
    piece = seg + jnp.arange(blocks, dtype=jnp.int32)[None, :, None]
    hit = piece.reshape(seqs, 1, length) == jnp.arange(per, dtype=jnp.int32)[None, :, None]
    sid = jnp.max(jnp.where(hit, segment[:, None, :], -1), axis=-1)
    sid = jnp.where(sid >= 0, sid + docs * jnp.arange(seqs, dtype=jnp.int32)[:, None], -1)
    seg = jnp.pad(seg, ((0, 0), (0, per - blocks), (0, 0)), constant_values=-1)
    seg = jnp.pad(seg.reshape(seqs * per, LANES), ((PAD, PAD), (0, 0)), constant_values=-1)
    sid = jnp.pad(sid.reshape(seqs * per), ((PAD, PAD),), constant_values=-2)
    return seg, jnp.broadcast_to(sid[:, None], (seqs * per + 2 * PAD, LANES)), per


def mix_forward(v, seg, sid, docs, n_lag, bits, pw_re, pw_im, kr, ki, skip):
    channels, rows, _ = v.shape
    states = kr.shape[1]
    wide = jnp.broadcast_to(skip[:, None], (channels, LANES))
    return pl.pallas_call(
        functools.partial(mix_forward_kernel, n_lag, docs, bits),
        out_shape=(
            jax.ShapeDtypeStruct(v.shape, jnp.bfloat16),
            jax.ShapeDtypeStruct((channels, n_lag, LANES), jnp.float32),
        ),
        scratch_shapes=[
            vmem(PAD + rows, LANES), vmem(PAD + rows, LANES), vmem(rows + PAD, LANES),
            vmem(LANES, states), vmem(LANES, states),
        ],
        compiler_params=pltpu.CompilerParams(vmem_limit_bytes=32 << 20),
        name="mix_forward",
    )(v, seg, sid, pw_re, pw_im, kr, ki, wide)


def mix_backward(v, g, seg, sid, docs, n_lag, bits, pw_re, pw_im, kr, ki, rate, freq, dt, skip, lags):
    channels, rows, _ = v.shape
    states = kr.shape[1]
    wide = jnp.broadcast_to(skip[:, None], (channels, LANES))
    dt = jnp.broadcast_to(dt, (channels, states))
    full = jax.ShapeDtypeStruct((channels, states), jnp.float32)
    thin = jax.ShapeDtypeStruct((channels, LANES), jnp.float32)
    return pl.pallas_call(
        functools.partial(mix_backward_kernel, n_lag, docs, bits),
        out_shape=(jax.ShapeDtypeStruct(v.shape, jnp.bfloat16), full, full, full, full, thin, thin),
        scratch_shapes=[
            vmem(PAD + rows, LANES), vmem(PAD + rows, LANES), vmem(PAD + rows, LANES),
            vmem(rows + PAD, LANES), vmem(rows + PAD, LANES),
            vmem(LANES, states), vmem(LANES, states),
        ],
        compiler_params=pltpu.CompilerParams(vmem_limit_bytes=32 << 20),
        name="mix_backward",
    )(v, g, seg, sid, pw_re, pw_im, kr, ki, rate, freq, dt, wide, lags)


BOTH = ("seq", "wt")
norm_epsilon = 1e-05


def gelu_tanh(pre_act):
    return jax.nn.gelu(pre_act, approximate=True)


def layer_norm(token_rows, gain_vec, bias_vec):
    row_mean = jnp.mean(token_rows, axis=-1, keepdims=True)
    centered = token_rows - row_mean
    spread = jnp.mean(centered * centered, axis=-1, keepdims=True)
    return centered * lax.rsqrt(spread + norm_epsilon) * gain_vec + bias_vec


def doc_segments(doc_lengths, seq_length):
    docs = doc_lengths.shape[1]
    upto = jnp.arange(docs)[:, None] >= jnp.arange(docs)[None, :]
    ends = jnp.sum(jnp.where(upto[None], doc_lengths[:, None, :], 0), axis=-1)
    places = jnp.arange(seq_length, dtype=jnp.int32)
    passed = (places[None, None, :] >= ends[:, :, None]).astype(jnp.int32)
    return jnp.sum(passed, axis=1, dtype=jnp.int32)


def on_device(
    inputs, cotangent, doc_lengths, norm_gain, norm_bias, gate_weight, value_weight, mix_weight,
    down_weight, decay_rate, frequency, kernel_re, kernel_im, log_step, skip_gain,
):
    seq_count, local_len, model_width = inputs.shape
    row_count = seq_count * local_len
    n_seq, n_wt = lax.axis_size("seq"), lax.axis_size("wt")
    length = local_len * n_seq
    docs = doc_lengths.shape[1]
    n_lag = length // 2 // LANES
    blocks = length // LANES
    width = value_weight.shape[1]
    own_channels = width // (n_seq * n_wt)
    wt_index = lax.axis_index("wt")

    def gather(x, axes=BOTH):
        return lax.all_gather(x, axes, axis=0, tiled=True)

    value_full = gather(value_weight)
    gain_full, bias_full = gather(jnp.stack([norm_gain, norm_bias], axis=1)).T
    lengths_all = gather(doc_lengths, "wt")
    gate_full = gather(gate_weight)
    mix_full = gather(mix_weight)
    down_full = gather(down_weight)

    def own(x):
        return lax.dynamic_slice_in_dim(x, wt_index * own_channels, own_channels, 0)

    rate, freq, kr, ki = own(decay_rate), own(frequency), own(kernel_re), own(kernel_im)
    step, skip = own(log_step), own(skip_gain)
    dt, bits, pw_re, pw_im = table_inputs(rate, freq, step, n_lag)
    seg, sid, per = segment_tables(doc_segments(lengths_all, length), docs)

    def to_channels(turned):
        got = lax.all_to_all(turned, BOTH, split_axis=0, concat_axis=0, tiled=True)
        got = got.reshape(n_seq, n_wt, own_channels, seq_count, local_len // LANES, LANES)
        got = got.transpose(2, 1, 3, 0, 4, 5).reshape(own_channels, -1, blocks, LANES)
        got = jnp.pad(got, ((0, 0), (0, 0), (0, per - blocks), (0, 0)))
        return got.reshape(own_channels, -1, LANES)

    def to_tokens(held):
        held = held.reshape(own_channels, -1, per, LANES)[:, :, :blocks]
        held = held.reshape(own_channels, n_wt, seq_count, n_seq, local_len // LANES, LANES)
        held = held.transpose(3, 1, 0, 2, 4, 5).reshape(width, row_count)
        return lax.all_to_all(held, BOTH, split_axis=0, concat_axis=0, tiled=True)

    token_rows = inputs.reshape(row_count, model_width).astype(jnp.float32)
    normed, norm_back = jax.vjp(
        layer_norm, token_rows, gain_full.astype(jnp.float32), bias_full.astype(jnp.float32)
    )
    normed_low = normed.astype(jnp.bfloat16)
    value_pre = dot(value_full, normed_low, 0, 1)
    value_act, value_back = jax.vjp(gelu_tanh, value_pre)
    value_ch = to_channels(value_act.astype(jnp.bfloat16))
    mixed_ch, lags = mix_forward(value_ch, seg, sid, docs, n_lag, bits, pw_re, pw_im, kr, ki, skip)
    mixed = to_tokens(mixed_ch)
    gate_pre = dot(normed_low, gate_full)
    gate_act, gate_back = jax.vjp(gelu_tanh, gate_pre)
    expand = dot(mixed, mix_full, 0, 0)
    product_low = (expand * gate_act).astype(jnp.bfloat16)
    result = token_rows + dot(product_low, down_full)
    outputs = result.astype(jnp.bfloat16).reshape(inputs.shape)
    cot_rows = cotangent.reshape(row_count, model_width)
    down_grad = dot(product_low, cot_rows, 0, 0)
    product_grad = dot(cot_rows, down_full, 1, 1)
    expand_low = (product_grad * gate_act).astype(jnp.bfloat16)
    gate_pre_low = gate_back(product_grad * expand)[0].astype(jnp.bfloat16)
    mix_grad = dot(mixed, expand_low)
    mixed_grad = dot(mix_full, expand_low, 1, 1).astype(jnp.bfloat16)
    grad_ch = to_channels(mixed_grad)
    back = mix_backward(
        value_ch, grad_ch, seg, sid, docs, n_lag, bits, pw_re, pw_im, kr, ki, rate, freq, dt, skip,
        lags,
    )
    value_grad_tok = to_tokens(back[0])
    value_pre_low = value_back(value_grad_tok.astype(jnp.float32))[0].astype(jnp.bfloat16)
    states = rate.shape[1]
    packed = jnp.concatenate([back[3], back[4], back[1], back[2], back[5], back[6]], axis=1)
    packed = gather(packed, "wt")
    mixer_grads = [packed[:, i * states : (i + 1) * states] for i in range(4)]
    mixer_grads += [packed[:, 4 * states], packed[:, 4 * states + LANES]]
    gate_grad = dot(normed_low, gate_pre_low, 0, 0)
    value_grad = dot(normed_low, value_pre_low, 0, 1)
    normed_grad = dot(gate_pre_low, gate_full, 1, 1) + dot(value_pre_low, value_full, 0, 1)
    input_rows, gain_grad, bias_grad = norm_back(normed_grad)
    input_grad = (cot_rows.astype(jnp.float32) + input_rows).reshape(inputs.shape)

    def scatter(x):
        x = x.astype(jnp.bfloat16)
        return lax.psum_scatter(x, BOTH, scatter_dimension=0, tiled=True).astype(jnp.float32)

    down_piece, mix_piece, gate_piece = scatter(down_grad), scatter(mix_grad), scatter(gate_grad)
    value_piece = scatter(value_grad)
    norm_piece = scatter(jnp.stack([gain_grad, bias_grad], axis=1))
    return (
        outputs, input_grad, norm_piece[:, 0], norm_piece[:, 1], gate_piece, value_piece, mix_piece,
        down_piece, *mixer_grads,
    )


def solution(mesh):
    in_specs = (
        P("wt", "seq", None),
        P("wt", "seq", None),
        P("wt", None),
        P(("seq", "wt")),
        P(("seq", "wt")),
        P(("seq", "wt"), None),
        P(("seq", "wt"), None),
        P(("seq", "wt"), None),
        P(("seq", "wt"), None),
        P("seq", None),
        P("seq", None),
        P("seq", None),
        P("seq", None),
        P("seq"),
        P("seq"),
    )
    out_specs = (
        P("wt", "seq", None),
        P("wt", "seq", None),
        P(("seq", "wt")),
        P(("seq", "wt")),
        P(("seq", "wt"), None),
        P(("seq", "wt"), None),
        P(("seq", "wt"), None),
        P(("seq", "wt"), None),
        P("seq", None),
        P("seq", None),
        P("seq", None),
        P("seq", None),
        P("seq"),
        P("seq"),
    )
    return jax.shard_map(
        on_device, mesh=mesh, in_specs=in_specs, out_specs=out_specs, check_vma=False
    )
```

```python
import functools

import jax
import jax.numpy as jnp
from jax import lax
from jax.experimental import pallas as pl
from jax.experimental.pallas import tpu as pltpu
from jax.sharding import PartitionSpec as P

LANES = 128
PAD = 16


def cmul(ar, ai, br, bi):
    return ar * br - ai * bi, ar * bi + ai * br


def power_rows(pw_re, pw_im, c, first, count, rows):
    width = pw_re.shape[2]
    place = lax.broadcasted_iota(jnp.int32, (rows, width), 0)
    re = jnp.ones((rows, width), jnp.float32)
    im = jnp.zeros((rows, width), jnp.float32)
    for bit in range(count):
        on = (place & (1 << bit)) != 0
        fr = jnp.where(on, pw_re[c, pl.ds(first + bit, 1), :], 1.0)
        fi = jnp.where(on, pw_im[c, pl.ds(first + bit, 1), :], 0.0)
        re, im = cmul(re, im, fr, fi)
    return re, im


def fill_lane_powers(pw_re, pw_im, c, tab_re, tab_im, extra):
    re, im = power_rows(pw_re, pw_im, c, 0, 3, 8)
    if extra:
        re, im = cmul(re, im, pw_re[c, pl.ds(0, 1), :], pw_im[c, pl.ds(0, 1), :])
    tab_re[0:8, :] = re
    tab_im[0:8, :] = im
    have, bit = 8, 3
    while have < LANES:
        re, im = cmul(
            tab_re[0:have, :],
            tab_im[0:have, :],
            pw_re[c, pl.ds(bit, 1), :],
            pw_im[c, pl.ds(bit, 1), :],
        )
        tab_re[have : 2 * have, :] = re
        tab_im[have : 2 * have, :] = im
        have, bit = 2 * have, bit + 1


def to_pieces(seg, val, rows, docs):
    total = jnp.zeros((rows, LANES), jnp.float32)
    for j in range(docs):
        at = pl.ds(PAD - j, rows)
        total = total + jnp.where(seg[at, :] == j, val[at, :], 0.0)
    return total


def from_pieces(seg, piece, rows, docs):
    own = seg[pl.ds(PAD, rows), :]
    total = jnp.zeros((rows, LANES), jnp.float32)
    for j in range(docs):
        total = total + jnp.where(own == j, piece[pl.ds(j, rows), :], 0.0)
    return total


def toeplitz(lags, d, last, lower, before):
    if d < last:
        row = jnp.broadcast_to(lags[d : d + 1, :], (LANES, LANES))
        here = pltpu.roll(row, 0, 1, stride=1, stride_axis=0)
    else:
        here = jnp.zeros((LANES, LANES), jnp.float32)
    return jnp.where(lower, here, before).astype(jnp.bfloat16), here


def dot(a, b, ca=1, cb=0):
    return lax.dot_general(a, b, (((ca,), (cb,)), ((), ())), preferred_element_type=jnp.float32)


def mix_forward_kernel(
    n_lag, docs, bits, v_ref, seg_ref, sid_ref, pw_re, pw_im, kr_ref, ki_ref, skip_ref,
    y_ref, lag_ref, vf, vp, yp, tab_re, tab_im,
):
    channels, rows, _ = v_ref.shape
    zero_pad = jnp.zeros((PAD, LANES), jnp.float32)
    vf[0:PAD, :] = zero_pad
    vp[0:PAD, :] = zero_pad
    yp[pl.ds(rows, PAD), :] = zero_pad
    lower = lax.broadcasted_iota(jnp.int32, (LANES, LANES), 1) >= lax.broadcasted_iota(
        jnp.int32, (LANES, LANES), 0
    )

    def channel(c, unused):
        fill_lane_powers(pw_re, pw_im, c, tab_re, tab_im, 0)
        dr, di = power_rows(pw_re, pw_im, c, 7, bits, n_lag)
        ar, ai = cmul(dr, di, kr_ref[pl.ds(c, 1), :], ki_ref[pl.ds(c, 1), :])
        lags = dot(ar.astype(jnp.bfloat16), tab_re[...].astype(jnp.bfloat16), 1, 1) - dot(
            ai.astype(jnp.bfloat16), tab_im[...].astype(jnp.bfloat16), 1, 1
        )
        lag_ref[c] = lags
        val = v_ref[c].astype(jnp.float32)
        vf[pl.ds(PAD, rows), :] = val
        vp[pl.ds(PAD, rows), :] = to_pieces(seg_ref, vf, rows, docs)
        sid = sid_ref[pl.ds(PAD, rows), :]
        before = jnp.zeros((LANES, LANES), jnp.float32)
        total = jnp.zeros((rows, LANES), jnp.float32)
        for d in range(n_lag + 1):
            at = pl.ds(PAD - d, rows)
            x = jnp.where(sid_ref[at, :] == sid, vp[at, :], 0.0).astype(jnp.bfloat16)
            t, before = toeplitz(lags, d, n_lag, lower, before)
            total = total + dot(x, t)
        yp[0:rows, :] = total
        out = from_pieces(seg_ref, yp, rows, docs) + skip_ref[pl.ds(c, 1), :] * val
        y_ref[c] = out.astype(jnp.bfloat16)
        return unused

    lax.fori_loop(0, channels, channel, 0)


def mix_backward_kernel(
    n_lag, docs, bits, v_ref, g_ref, seg_ref, sid_ref, pw_re, pw_im, kr_ref, ki_ref, rate_ref,
    freq_ref, dt_ref, skip_ref, lag_ref,
    dv_ref, kr_out, ki_out, rate_out, freq_out, step_out, skip_out,
    vf, gf, vp, gp, yp, tab_re, tab_im,
):
    channels, rows, _ = v_ref.shape
    zero_pad = jnp.zeros((PAD, LANES), jnp.float32)
    vf[0:PAD, :] = zero_pad
    gf[0:PAD, :] = zero_pad
    vp[0:PAD, :] = zero_pad
    gp[pl.ds(rows, PAD), :] = zero_pad
    yp[pl.ds(rows, PAD), :] = zero_pad
    lane = lax.broadcasted_iota(jnp.int32, (LANES, LANES), 1)
    row = lax.broadcasted_iota(jnp.int32, (LANES, LANES), 0)
    lower = lane >= row
    wraps = lane + row >= LANES
    flip = (lane + row == LANES - 1).astype(jnp.bfloat16)
    lag_place = (
        lax.broadcasted_iota(jnp.int32, (n_lag, LANES), 0) * LANES
        + lax.broadcasted_iota(jnp.int32, (n_lag, LANES), 1)
        + 1
    ).astype(jnp.float32)

    def channel(c, unused):
        own = pl.ds(c, 1)
        val = v_ref[c].astype(jnp.float32)
        grad = g_ref[c].astype(jnp.float32)
        vf[pl.ds(PAD, rows), :] = val
        gf[pl.ds(PAD, rows), :] = grad
        skip_grad = jnp.sum(jnp.sum(val * grad, axis=0, keepdims=True), axis=1, keepdims=True)
        g_piece = to_pieces(seg_ref, gf, rows, docs)
        gp[0:rows, :] = g_piece
        v_piece = to_pieces(seg_ref, vf, rows, docs).astype(jnp.bfloat16)
        vp[pl.ds(PAD, rows), :] = dot(v_piece, flip)
        g_turned = jnp.transpose(g_piece).astype(jnp.bfloat16)
        sid = sid_ref[pl.ds(PAD, rows), :]
        lags = lag_ref[c]
        before = jnp.zeros((LANES, LANES), jnp.float32)
        total = jnp.zeros((rows, LANES), jnp.float32)
        earlier = None
        sums = []
        for d in range(n_lag + 1):
            ahead = pl.ds(PAD + d, rows)
            x = jnp.where(sid_ref[ahead, :] == sid, gp[pl.ds(d, rows), :], 0.0)
            t, before = toeplitz(lags, d, n_lag, lower, before)
            total = total + dot(x.astype(jnp.bfloat16), t, 1, 1)
            at = pl.ds(PAD - d, rows)
            back = jnp.where(sid_ref[at, :] == sid, vp[at, :], 0.0).astype(jnp.bfloat16)
            pairs = dot(g_turned, back)
            if d:
                skew = jnp.where(wraps, earlier, pairs)
                skew = pltpu.roll(skew, 0, 1, stride=1, stride_axis=0)
                sums.append(jnp.sum(skew, axis=0, keepdims=True))
            earlier = pairs
        yp[0:rows, :] = total
        out = from_pieces(seg_ref, yp, rows, docs) + skip_ref[own, :] * grad
        dv_ref[c] = out.astype(jnp.bfloat16)
        lag_grad = jnp.concatenate(sums, axis=0)
        fill_lane_powers(pw_re, pw_im, c, tab_re, tab_im, 1)
        both = jnp.concatenate([lag_grad, lag_grad * lag_place], axis=0).astype(jnp.bfloat16)
        part_re = dot(both, tab_re[...].astype(jnp.bfloat16))
        part_im = dot(both, tab_im[...].astype(jnp.bfloat16))
        dr, di = power_rows(pw_re, pw_im, c, 7, bits, n_lag)
        gr, gi = cmul(dr, di, part_re[0:n_lag], part_im[0:n_lag])
        hr, hi = cmul(dr, di, part_re[n_lag:], part_im[n_lag:])
        gr, gi, hr, hi = (jnp.sum(a, axis=0, keepdims=True) for a in (gr, gi, hr, hi))
        kr, ki, dt = kr_ref[own, :], ki_ref[own, :], dt_ref[own, :]
        rate_grad = -dt * (kr * hr - ki * hi)
        freq_grad = -dt * (kr * hi + ki * hr)
        kr_out[own, :] = gr + skip_grad
        ki_out[own, :] = -gi
        rate_out[own, :] = rate_grad
        freq_out[own, :] = freq_grad
        step = jnp.sum(
            rate_grad * rate_ref[own, :] + freq_grad * freq_ref[own, :], axis=1, keepdims=True
        )
        step_out[own, :] = jnp.broadcast_to(step, (1, LANES))
        skip_out[own, :] = jnp.broadcast_to(skip_grad, (1, LANES))
        return unused

    lax.fori_loop(0, channels, channel, 0)


def vmem(*shape):
    return pltpu.VMEM(shape, jnp.float32)


def table_inputs(decay_rate, frequency, log_step, n_lag):
    bits = (n_lag - 1).bit_length()
    dt = jnp.exp(log_step)[:, None]
    powers = jnp.array([float(1 << b) for b in range(7 + bits)] + [0.0] * (9 - bits), jnp.float32)
    powers = powers[None, :, None]
    mag = jnp.exp(-(decay_rate * dt)[:, None, :] * powers)
    phase = (frequency * dt)[:, None, :] * powers
    return dt, bits, mag * jnp.cos(phase), mag * jnp.sin(phase)


def segment_tables(segment, docs):
    seqs, length = segment.shape
    blocks = length // LANES
    per = -(-(blocks + docs) // 8) * 8
    seg = segment.reshape(seqs, blocks, LANES)
    piece = seg + jnp.arange(blocks, dtype=jnp.int32)[None, :, None]
    hit = piece.reshape(seqs, 1, length) == jnp.arange(per, dtype=jnp.int32)[None, :, None]
    sid = jnp.max(jnp.where(hit, segment[:, None, :], -1), axis=-1)
    sid = jnp.where(sid >= 0, sid + docs * jnp.arange(seqs, dtype=jnp.int32)[:, None], -1)
    seg = jnp.pad(seg, ((0, 0), (0, per - blocks), (0, 0)), constant_values=-1)
    seg = jnp.pad(seg.reshape(seqs * per, LANES), ((PAD, PAD), (0, 0)), constant_values=-1)
    sid = jnp.pad(sid.reshape(seqs * per), ((PAD, PAD),), constant_values=-2)
    return seg, jnp.broadcast_to(sid[:, None], (seqs * per + 2 * PAD, LANES)), per


def mix_forward(v, seg, sid, docs, n_lag, bits, pw_re, pw_im, kr, ki, skip):
    channels, rows, _ = v.shape
    states = kr.shape[1]
    wide = jnp.broadcast_to(skip[:, None], (channels, LANES))
    return pl.pallas_call(
        functools.partial(mix_forward_kernel, n_lag, docs, bits),
        out_shape=(
            jax.ShapeDtypeStruct(v.shape, jnp.bfloat16),
            jax.ShapeDtypeStruct((channels, n_lag, LANES), jnp.float32),
        ),
        scratch_shapes=[
            vmem(PAD + rows, LANES), vmem(PAD + rows, LANES), vmem(rows + PAD, LANES),
            vmem(LANES, states), vmem(LANES, states),
        ],
        compiler_params=pltpu.CompilerParams(vmem_limit_bytes=32 << 20),
        name="mix_forward",
    )(v, seg, sid, pw_re, pw_im, kr, ki, wide)


def mix_backward(v, g, seg, sid, docs, n_lag, bits, pw_re, pw_im, kr, ki, rate, freq, dt, skip, lags):
    channels, rows, _ = v.shape
    states = kr.shape[1]
    wide = jnp.broadcast_to(skip[:, None], (channels, LANES))
    dt = jnp.broadcast_to(dt, (channels, states))
    full = jax.ShapeDtypeStruct((channels, states), jnp.float32)
    thin = jax.ShapeDtypeStruct((channels, LANES), jnp.float32)
    return pl.pallas_call(
        functools.partial(mix_backward_kernel, n_lag, docs, bits),
        out_shape=(jax.ShapeDtypeStruct(v.shape, jnp.bfloat16), full, full, full, full, thin, thin),
        scratch_shapes=[
            vmem(PAD + rows, LANES), vmem(PAD + rows, LANES), vmem(PAD + rows, LANES),
            vmem(rows + PAD, LANES), vmem(rows + PAD, LANES),
            vmem(LANES, states), vmem(LANES, states),
        ],
        compiler_params=pltpu.CompilerParams(vmem_limit_bytes=32 << 20),
        name="mix_backward",
    )(v, g, seg, sid, pw_re, pw_im, kr, ki, rate, freq, dt, wide, lags)


BOTH = ("seq", "wt")
norm_epsilon = 1e-05


def gelu_tanh(pre_act):
    return jax.nn.gelu(pre_act, approximate=True)


def layer_norm(token_rows, gain_vec, bias_vec):
    row_mean = jnp.mean(token_rows, axis=-1, keepdims=True)
    centered = token_rows - row_mean
    spread = jnp.mean(centered * centered, axis=-1, keepdims=True)
    return centered * lax.rsqrt(spread + norm_epsilon) * gain_vec + bias_vec


def doc_segments(doc_lengths, seq_length):
    docs = doc_lengths.shape[1]
    upto = jnp.arange(docs)[:, None] >= jnp.arange(docs)[None, :]
    ends = jnp.sum(jnp.where(upto[None], doc_lengths[:, None, :], 0), axis=-1)
    places = jnp.arange(seq_length, dtype=jnp.int32)
    passed = (places[None, None, :] >= ends[:, :, None]).astype(jnp.int32)
    return jnp.sum(passed, axis=1, dtype=jnp.int32)


def after(x, first):
    return lax.optimization_barrier((x, first))[0]


class Ring:
    def __init__(self, axis, inner):
        self.axis, self.size = axis, lax.axis_size(axis)
        self.inner = min(inner, self.size)
        self.outer = self.size // self.inner
        self.me = lax.axis_index(axis)
        self.o, self.i = self.me // self.inner, self.me % self.inner

    def shift(self, x, k, j):
        to = [
            ((p // self.inner + k) % self.outer) * self.inner + (p % self.inner + j) % self.inner
            for p in range(self.size)
        ]
        return lax.ppermute(x, self.axis, list(enumerate(to)))

    def parts(self, x, joined):
        far = [(0, x)] + [(k, self.shift(x, k, 0)) for k in range(1, self.outer)]
        back = lambda k, j: ((self.o - k) % self.outer) * self.inner + (self.i - j) % self.inner
        out = [(back(k, 0), part) for k, part in far]
        for j in range(1, self.inner):
            if joined:
                near = self.shift(jnp.stack([part for _, part in far]), 0, j)
                out += [(back(k, j), near[k]) for k in range(self.outer)]
            else:
                out += [(back(k, j), self.shift(part, 0, j)) for k, part in far]
        return out

    def gather(self, x, joined=True):
        return self.place(self.parts(x, joined))

    def place(self, parts, axis=0):
        first = parts[0][1]
        out = jnp.zeros(first.shape[:axis] + (self.size,) + first.shape[axis:], first.dtype)
        for at, part in parts:
            out = lax.dynamic_update_index_in_dim(out, part, at, axis)
        return out

    def exchange(self, x):
        parts = []
        for k in range(self.outer):
            for j in range(self.inner):
                to = ((self.o + k) % self.outer) * self.inner + (self.i + j) % self.inner
                back = ((self.o - k) % self.outer) * self.inner + (self.i - j) % self.inner
                block = lax.dynamic_index_in_dim(x, to, 0, keepdims=False)
                parts.append((back, block if k == j == 0 else self.shift(block, k, j)))
        return self.place(parts)

    def scatter_sum(self, x):
        wide, narrow = jnp.float32, jnp.bfloat16
        x = x.astype(narrow).reshape((self.outer, self.inner) + x.shape[1:])
        pick = lambda j: lax.dynamic_index_in_dim(x, (self.i + j) % self.inner, 1, keepdims=False)
        held = pick(0).astype(wide)
        for j in range(1, self.inner):
            held = held + self.shift(pick(j), 0, j).astype(wide)
        low = held.astype(narrow)
        take = lambda a, k: lax.dynamic_index_in_dim(a, (self.o + k) % self.outer, 0, keepdims=False)
        total = take(held, 0)
        for k in range(1, self.outer):
            total = total + self.shift(take(low, k), k, 0).astype(wide)
        return total


def on_device(
    inputs, cotangent, doc_lengths, norm_gain, norm_bias, gate_weight, value_weight, mix_weight,
    down_weight, decay_rate, frequency, kernel_re, kernel_im, log_step, skip_gain,
):
    seq_count, local_len, model_width = inputs.shape
    row_count = seq_count * local_len
    n_seq, n_wt = lax.axis_size("seq"), lax.axis_size("wt")
    seq, wt = Ring("seq", 2 if n_seq <= 8 else 8), Ring("wt", 2)
    length = local_len * n_seq
    docs = doc_lengths.shape[1]
    n_lag = length // 2 // LANES
    blocks = length // LANES
    width = value_weight.shape[1]
    d_rows = value_weight.shape[0]
    h_rows = mix_weight.shape[0]
    f_rows = down_weight.shape[0]
    gate_width = gate_weight.shape[1]
    f_part = gate_width // n_wt
    low = jnp.bfloat16

    norm_row = jnp.concatenate([norm_gain, norm_bias])[None]
    norm_row = jnp.pad(norm_row, ((0, 15), (0, width - norm_row.shape[1])))
    front = seq.gather(wt.gather(jnp.concatenate([value_weight, norm_row], axis=0)))
    front = front.reshape(n_seq * n_wt, d_rows + 16, width)
    value_full = front[:, :d_rows].reshape(model_width, width)
    gain_full = front[:, d_rows, :d_rows].reshape(model_width)
    bias_full = front[:, d_rows, d_rows : 2 * d_rows].reshape(model_width)
    lengths_all = wt.gather(doc_lengths).reshape(n_wt * seq_count, docs)

    def columns(x):
        x = x.reshape(x.shape[0], n_seq, n_wt, f_rows).transpose(2, 0, 1, 3)
        return x.reshape(n_wt, -1, f_part)

    both_rows = d_rows + h_rows
    packed = columns(jnp.concatenate([gate_weight, mix_weight], axis=0))
    packed = wt.exchange(after(packed, front))
    parts = seq.parts(packed, False)
    gate_own = seq.place([(s, p[:, :d_rows]) for s, p in parts]).reshape(model_width, f_part)
    mix_own = seq.place([(s, p[:, d_rows:]) for s, p in parts]).reshape(width, f_part)
    down_own = seq.gather(after(down_weight, packed), False).reshape(f_part, model_width)

    own_channels = width // (n_seq * n_wt)

    def own(x):
        return lax.dynamic_slice_in_dim(x, wt.me * own_channels, own_channels, 0)

    rate, freq, kr, ki = own(decay_rate), own(frequency), own(kernel_re), own(kernel_im)
    step, skip = own(log_step), own(skip_gain)
    dt, bits, pw_re, pw_im = table_inputs(rate, freq, step, n_lag)
    seg, sid, per = segment_tables(doc_segments(lengths_all, length), docs)

    def to_channels(turned):
        got = lax.all_to_all(turned, BOTH, split_axis=0, concat_axis=0, tiled=True)
        got = got.reshape(n_seq, n_wt, own_channels, seq_count, local_len // LANES, LANES)
        got = got.transpose(2, 1, 3, 0, 4, 5).reshape(own_channels, -1, blocks, LANES)
        got = jnp.pad(got, ((0, 0), (0, 0), (0, per - blocks), (0, 0)))
        return got.reshape(own_channels, -1, LANES)

    def to_tokens(held):
        held = held.reshape(own_channels, -1, per, LANES)[:, :, :blocks]
        held = held.reshape(own_channels, n_wt, seq_count, n_seq, local_len // LANES, LANES)
        held = held.transpose(3, 1, 0, 2, 4, 5).reshape(width, row_count)
        return lax.all_to_all(held, BOTH, split_axis=0, concat_axis=0, tiled=True)

    token_rows = inputs.reshape(row_count, model_width).astype(jnp.float32)
    normed, norm_back = jax.vjp(
        layer_norm, token_rows, gain_full.astype(jnp.float32), bias_full.astype(jnp.float32)
    )
    normed_low = normed.astype(low)
    cot_rows = cotangent.reshape(row_count, model_width)
    pair = wt.gather(jnp.stack([normed_low, cot_rows]), True)
    normed_all = pair[:, 0].reshape(n_wt * row_count, model_width)
    cot_all = pair[:, 1].reshape(n_wt * row_count, model_width)

    value_pre = dot(value_full, normed_low, 0, 1)
    value_act, value_back = jax.vjp(gelu_tanh, value_pre)
    value_ch = to_channels(value_act.astype(low))
    mixed_ch, lags = mix_forward(value_ch, seg, sid, docs, n_lag, bits, pw_re, pw_im, kr, ki, skip)
    mixed = wt.gather(to_tokens(mixed_ch))
    mixed = mixed.transpose(1, 0, 2).reshape(width, n_wt * row_count)

    gate_pre = dot(normed_all, gate_own)
    gate_act, gate_back = jax.vjp(gelu_tanh, gate_pre)
    product_grad = dot(cot_all, down_own, 1, 1)
    expand = dot(mixed, mix_own, 0, 0)
    expand_low = (product_grad * gate_act).astype(low)
    mixed_grad = dot(mix_own, expand_low, 1, 1).astype(low)
    mixed_grad = mixed_grad.reshape(width, n_wt, row_count).transpose(1, 0, 2)
    mixed_grad = wt.scatter_sum(mixed_grad).astype(low)
    grad_ch = to_channels(mixed_grad)
    product_low = (expand * gate_act).astype(low)
    gate_pre_low = gate_back(product_grad * expand)[0].astype(low)

    down_grad = dot(product_low, cot_all, 0, 0).astype(low).reshape(n_seq, f_rows, model_width)
    mix_grad = dot(mixed, expand_low).astype(low).reshape(n_seq, n_wt * h_rows, f_part)
    gate_grad = dot(normed_all, gate_pre_low, 0, 0).astype(low).reshape(n_seq, n_wt * d_rows, f_part)
    down_piece = seq.scatter_sum(down_grad)
    mix_band = seq.scatter_sum(mix_grad)
    gate_band = seq.scatter_sum(gate_grad)

    result = dot(product_low, down_own).astype(low)
    gate_side = dot(gate_pre_low, gate_own, 1, 1).astype(low)
    tok = lambda x: x.reshape(n_wt, row_count, model_width)
    token_sums = wt.scatter_sum(jnp.stack([tok(result), tok(gate_side)], axis=1))
    outputs = (token_rows + token_sums[0]).astype(low).reshape(inputs.shape)

    back = mix_backward(
        value_ch, grad_ch, seg, sid, docs, n_lag, bits, pw_re, pw_im, kr, ki, rate, freq, dt, skip,
        lags,
    )
    value_grad_tok = to_tokens(back[0])
    value_pre_low = value_back(value_grad_tok.astype(jnp.float32))[0].astype(low)
    states = rate.shape[1]
    packed = jnp.concatenate([back[3], back[4], back[1], back[2], back[5], back[6]], axis=1)
    packed = wt.gather(packed).reshape(n_wt * own_channels, -1)
    mixer_grads = [packed[:, i * states : (i + 1) * states] for i in range(4)]
    mixer_grads += [packed[:, 4 * states], packed[:, 4 * states + LANES]]

    value_turn = wt.exchange(value_pre_low.reshape(n_wt, width // n_wt, row_count))
    value_turn = value_turn.transpose(1, 0, 2).reshape(width // n_wt, n_wt * row_count)
    value_grad = dot(normed_all, value_turn, 0, 1).reshape(n_seq, n_wt * d_rows, width // n_wt)
    value_band = seq.scatter_sum(value_grad)

    normed_grad = token_sums[1] + dot(value_pre_low, value_full, 0, 1)
    input_rows, gain_grad, bias_grad = norm_back(normed_grad)
    input_grad = (cot_rows.astype(jnp.float32) + input_rows).reshape(inputs.shape)
    vectors = jnp.stack([gain_grad, bias_grad]).astype(low).reshape(2, n_seq * n_wt, d_rows)
    vectors = lax.all_to_all(
        vectors.transpose(1, 0, 2), BOTH, split_axis=0, concat_axis=0, tiled=True
    )
    vectors = jnp.sum(vectors.astype(jnp.float32), axis=0)

    last = [
        gate_band.reshape(n_wt, d_rows, f_part),
        mix_band.reshape(n_wt, h_rows, f_part),
        value_band.reshape(n_wt, d_rows, width // n_wt),
    ]
    heads = wt.exchange(jnp.concatenate(last[:2], axis=1).astype(low)).astype(jnp.float32)
    tails = wt.exchange(last[2].astype(low)).astype(jnp.float32)

    def spread(x):
        rows = x.shape[1]
        x = x.reshape(n_wt, rows, n_seq, f_rows).transpose(1, 2, 0, 3)
        return x.reshape(rows, gate_width)

    value_piece = tails.transpose(1, 0, 2).reshape(d_rows, width)
    return (
        outputs, input_grad, vectors[0], vectors[1], spread(heads[:, :d_rows]), value_piece,
        spread(heads[:, d_rows:]), down_piece, *mixer_grads,
    )


def solution(mesh):
    in_specs = (
        P("wt", "seq", None),
        P("wt", "seq", None),
        P("wt", None),
        P(("seq", "wt")),
        P(("seq", "wt")),
        P(("seq", "wt"), None),
        P(("seq", "wt"), None),
        P(("seq", "wt"), None),
        P(("seq", "wt"), None),
        P("seq", None),
        P("seq", None),
        P("seq", None),
        P("seq", None),
        P("seq"),
        P("seq"),
    )
    out_specs = (
        P("wt", "seq", None),
        P("wt", "seq", None),
        P(("seq", "wt")),
        P(("seq", "wt")),
        P(("seq", "wt"), None),
        P(("seq", "wt"), None),
        P(("seq", "wt"), None),
        P(("seq", "wt"), None),
        P("seq", None),
        P("seq", None),
        P("seq", None),
        P("seq", None),
        P("seq"),
        P("seq"),
    )
    return jax.shard_map(
        on_device, mesh=mesh, in_specs=in_specs, out_specs=out_specs, check_vma=False
    )
```

```python
import functools

import jax
import jax.numpy as jnp
from jax import lax
from jax.experimental import pallas as pl
from jax.experimental.pallas import tpu as pltpu
from jax.sharding import PartitionSpec as P

LANES = 128
PAD = 16


MESH = pl.DeviceIdType.MESH


def place_of(flat, n_wt):
    return (flat // n_wt, flat % n_wt)


def meet(flat, n, n_wt):
    barrier = pltpu.get_barrier_semaphore()

    def tell(r, unused):
        pl.semaphore_signal(
            barrier, inc=1, device_id=place_of((flat + r) % n, n_wt), device_id_type=MESH
        )
        return unused

    lax.fori_loop(1, n, tell, 0)
    pl.semaphore_wait(barrier, n - 1)


def swap_copy(source, target, send_sem, recv_sem, slot, peer, n_wt):
    return pltpu.make_async_remote_copy(
        src_ref=source, dst_ref=target, send_sem=send_sem.at[slot], recv_sem=recv_sem.at[slot],
        device_id=place_of(peer, n_wt), device_id_type=MESH,
    )


def swap_start(send, target_of, send_sem, recv_sem, flat, n, n_wt):
    def one(r, unused):
        peer = (flat + r) % n
        swap_copy(send.at[peer], target_of(peer, flat), send_sem, recv_sem, r, peer, n_wt).start()
        return unused

    lax.fori_loop(1, n, one, 0)


def swap_wait(send, target_of, send_sem, recv_sem, flat, n, n_wt):
    def one(r, unused):
        source = (flat + n - r) % n
        swap_copy(
            send.at[source], target_of(flat, source), send_sem, recv_sem, r, source, n_wt
        ).wait()
        return unused

    lax.fori_loop(1, n, one, 0)


def rows_to_table(got, table, n_seq, n_wt, seq_count, local_blocks, per, channels):
    for s in range(n_seq):
        for w in range(n_wt):
            for k in range(seq_count):
                for b in range(local_blocks):
                    row = (w * seq_count + k) * per + s * local_blocks + b
                    lanes = pl.ds((k * local_blocks + b) * LANES, LANES)
                    table[pl.ds(row * channels, channels), :] = got[
                        s * n_wt + w, :, lanes
                    ].astype(jnp.float32)


def table_to_rows(table, send, n_seq, n_wt, seq_count, local_blocks, per, channels):
    for s in range(n_seq):
        for w in range(n_wt):
            for k in range(seq_count):
                for b in range(local_blocks):
                    row = (w * seq_count + k) * per + s * local_blocks + b
                    lanes = pl.ds((k * local_blocks + b) * LANES, LANES)
                    send[s * n_wt + w, :, lanes] = table[
                        pl.ds(row * channels, channels), :
                    ].astype(jnp.bfloat16)


def clear_unused(table, seqs, blocks, per, channels):
    for s in range(seqs):
        table[pl.ds((s * per + blocks) * channels, (per - blocks) * channels), :] = jnp.zeros(
            ((per - blocks) * channels, LANES), jnp.float32
        )


def share_over_wt(ref, s_me, w_me, n_wt, send_sem, recv_sem):
    inner = 2
    outer = n_wt // inner
    o, i = w_me // inner, w_me % inner
    other = (s_me, o * inner + 1 - i)

    def copy(block, slot, to):
        return pltpu.make_async_remote_copy(
            src_ref=ref.at[block], dst_ref=ref.at[block], send_sem=send_sem.at[slot],
            recv_sem=recv_sem.at[slot], device_id=to, device_id_type=MESH,
        )

    far = [copy(w_me, k, (s_me, ((o + k) % outer) * inner + i)) for k in range(1, outer)]
    near = [copy(w_me, outer, other)]
    for c in far + near:
        c.start()
    for k in range(1, outer):
        block = ((o + outer - k) % outer) * inner + i
        far[k - 1].wait_recv()
        c = copy(block, outer + k, other)
        c.start()
        near.append(c)
    for c in far:
        c.wait_send()
    for c in near:
        c.wait()


def cmul(ar, ai, br, bi):
    return ar * br - ai * bi, ar * bi + ai * br


def power_rows(pw_re, pw_im, c, first, count, rows):
    width = pw_re.shape[2]
    place = lax.broadcasted_iota(jnp.int32, (rows, width), 0)
    re = jnp.ones((rows, width), jnp.float32)
    im = jnp.zeros((rows, width), jnp.float32)
    for bit in range(count):
        on = (place & (1 << bit)) != 0
        fr = jnp.where(on, pw_re[c, pl.ds(first + bit, 1), :], 1.0)
        fi = jnp.where(on, pw_im[c, pl.ds(first + bit, 1), :], 0.0)
        re, im = cmul(re, im, fr, fi)
    return re, im


def fill_lane_powers(pw_re, pw_im, c, tab_re, tab_im, extra):
    re, im = power_rows(pw_re, pw_im, c, 0, 3, 8)
    if extra:
        re, im = cmul(re, im, pw_re[c, pl.ds(0, 1), :], pw_im[c, pl.ds(0, 1), :])
    tab_re[0:8, :] = re
    tab_im[0:8, :] = im
    have, bit = 8, 3
    while have < LANES:
        re, im = cmul(
            tab_re[0:have, :],
            tab_im[0:have, :],
            pw_re[c, pl.ds(bit, 1), :],
            pw_im[c, pl.ds(bit, 1), :],
        )
        tab_re[have : 2 * have, :] = re
        tab_im[have : 2 * have, :] = im
        have, bit = 2 * have, bit + 1


def to_pieces(seg, val, rows, docs):
    total = jnp.zeros((rows, LANES), jnp.float32)
    for j in range(docs):
        at = pl.ds(PAD - j, rows)
        total = total + jnp.where(seg[at, :] == j, val[at, :], 0.0)
    return total


def from_pieces(seg, piece, rows, docs):
    own = seg[pl.ds(PAD, rows), :]
    total = jnp.zeros((rows, LANES), jnp.float32)
    for j in range(docs):
        total = total + jnp.where(own == j, piece[pl.ds(j, rows), :], 0.0)
    return total


def toeplitz(lags, d, last, lower, before):
    if d < last:
        row = jnp.broadcast_to(lags[d : d + 1, :], (LANES, LANES))
        here = pltpu.roll(row, 0, 1, stride=1, stride_axis=0)
    else:
        here = jnp.zeros((LANES, LANES), jnp.float32)
    return jnp.where(lower, here, before).astype(jnp.bfloat16), here


def dot(a, b, ca=1, cb=0):
    return lax.dot_general(a, b, (((ca,), (cb,)), ((), ())), preferred_element_type=jnp.float32)


def mix_forward_kernel(
    n_lag, docs, bits, seq_count, per, value_ref, seg_ref, sid_ref, pw_re, pw_im, kr_ref, ki_ref,
    skip_ref, mixed_ref, v_ref, lag_ref, vf, vp, yp, tab_re, tab_im, table, got, back,
    in_send, in_recv, out_send, out_recv, wt_send, wt_recv, local_sem,
):
    channels, rows, _ = v_ref.shape
    n_seq, n_wt = lax.axis_size("seq"), lax.axis_size("wt")
    n = n_seq * n_wt
    s_me, w_me = lax.axis_index("seq"), lax.axis_index("wt")
    flat = s_me * n_wt + w_me
    local_blocks = value_ref.shape[2] // LANES // seq_count
    shape = (n_seq, n_wt, seq_count, local_blocks, per, channels)
    meet(flat, n, n_wt)
    into = lambda peer, slot: got.at[slot]
    swap_start(value_ref, into, in_send, in_recv, flat, n, n_wt)
    got[flat] = value_ref[flat]
    clear_unused(table, n_wt * seq_count, n_seq * local_blocks, per, channels)
    zero_pad = jnp.zeros((PAD, LANES), jnp.float32)
    vf[0:PAD, :] = zero_pad
    vp[0:PAD, :] = zero_pad
    yp[pl.ds(rows, PAD), :] = zero_pad
    lower = lax.broadcasted_iota(jnp.int32, (LANES, LANES), 1) >= lax.broadcasted_iota(
        jnp.int32, (LANES, LANES), 0
    )
    swap_wait(value_ref, into, in_send, in_recv, flat, n, n_wt)
    rows_to_table(got, table, *shape)

    def channel(c, unused):
        fill_lane_powers(pw_re, pw_im, c, tab_re, tab_im, 0)
        dr, di = power_rows(pw_re, pw_im, c, 7, bits, n_lag)
        ar, ai = cmul(dr, di, kr_ref[pl.ds(c, 1), :], ki_ref[pl.ds(c, 1), :])
        lags = dot(ar.astype(jnp.bfloat16), tab_re[...].astype(jnp.bfloat16), 1, 1) - dot(
            ai.astype(jnp.bfloat16), tab_im[...].astype(jnp.bfloat16), 1, 1
        )
        lag_ref[c] = lags
        val = table[pl.ds(c, rows, stride=channels), :]
        v_ref[c] = val.astype(jnp.bfloat16)
        vf[pl.ds(PAD, rows), :] = val
        vp[pl.ds(PAD, rows), :] = to_pieces(seg_ref, vf, rows, docs)
        sid = sid_ref[pl.ds(PAD, rows), :]
        before = jnp.zeros((LANES, LANES), jnp.float32)
        total = jnp.zeros((rows, LANES), jnp.float32)
        for d in range(n_lag + 1):
            at = pl.ds(PAD - d, rows)
            x = jnp.where(sid_ref[at, :] == sid, vp[at, :], 0.0).astype(jnp.bfloat16)
            t, before = toeplitz(lags, d, n_lag, lower, before)
            total = total + dot(x, t)
        yp[0:rows, :] = total
        out = from_pieces(seg_ref, yp, rows, docs) + skip_ref[pl.ds(c, 1), :] * val
        table[pl.ds(c, rows, stride=channels), :] = out
        return unused

    lax.fori_loop(0, channels, channel, 0)
    table_to_rows(table, back, *shape)
    home = lambda peer, slot: mixed_ref.at[peer % n_wt, slot]
    swap_start(back, home, out_send, out_recv, flat, n, n_wt)
    own = pltpu.make_async_copy(back.at[flat], mixed_ref.at[w_me, flat], local_sem)
    own.start()
    own.wait()
    swap_wait(back, home, out_send, out_recv, flat, n, n_wt)
    share_over_wt(mixed_ref, s_me, w_me, n_wt, wt_send, wt_recv)


def mix_backward_kernel(
    n_lag, docs, bits, seq_count, per, grad_ref, v_ref, seg_ref, sid_ref, pw_re, pw_im, kr_ref,
    ki_ref, rate_ref, freq_ref, dt_ref, skip_ref, lag_ref,
    dv_ref, all_out, vf, gf, vp, gp, yp, tab_re, tab_im, table, got, back,
    in_send, in_recv, out_send, out_recv, wt_send, wt_recv, local_sem, *held,
):
    grads, thin = held[:4], held[4:]
    channels, rows, _ = v_ref.shape
    states = kr_ref.shape[1]
    n_seq, n_wt = lax.axis_size("seq"), lax.axis_size("wt")
    n = n_seq * n_wt
    s_me, w_me = lax.axis_index("seq"), lax.axis_index("wt")
    flat = s_me * n_wt + w_me
    local_blocks = grad_ref.shape[2] // LANES // seq_count
    shape = (n_seq, n_wt, seq_count, local_blocks, per, channels)
    meet(flat, n, n_wt)
    into = lambda peer, slot: got.at[slot]
    swap_start(grad_ref, into, in_send, in_recv, flat, n, n_wt)
    got[flat] = grad_ref[flat]
    clear_unused(table, n_wt * seq_count, n_seq * local_blocks, per, channels)
    zero_pad = jnp.zeros((PAD, LANES), jnp.float32)
    vf[0:PAD, :] = zero_pad
    gf[0:PAD, :] = zero_pad
    vp[0:PAD, :] = zero_pad
    gp[pl.ds(rows, PAD), :] = zero_pad
    yp[pl.ds(rows, PAD), :] = zero_pad
    lane = lax.broadcasted_iota(jnp.int32, (LANES, LANES), 1)
    row = lax.broadcasted_iota(jnp.int32, (LANES, LANES), 0)
    lower = lane >= row
    wraps = lane + row >= LANES
    flip = (lane + row == LANES - 1).astype(jnp.bfloat16)
    lag_place = (
        lax.broadcasted_iota(jnp.int32, (n_lag, LANES), 0) * LANES
        + lax.broadcasted_iota(jnp.int32, (n_lag, LANES), 1)
        + 1
    ).astype(jnp.float32)
    swap_wait(grad_ref, into, in_send, in_recv, flat, n, n_wt)
    rows_to_table(got, table, *shape)

    def channel(c, unused):
        own = pl.ds(c, 1)
        val = v_ref[c].astype(jnp.float32)
        grad = table[pl.ds(c, rows, stride=channels), :]
        vf[pl.ds(PAD, rows), :] = val
        gf[pl.ds(PAD, rows), :] = grad
        skip_grad = jnp.sum(jnp.sum(val * grad, axis=0, keepdims=True), axis=1, keepdims=True)
        g_piece = to_pieces(seg_ref, gf, rows, docs)
        gp[0:rows, :] = g_piece
        v_piece = to_pieces(seg_ref, vf, rows, docs).astype(jnp.bfloat16)
        vp[pl.ds(PAD, rows), :] = dot(v_piece, flip)
        g_turned = jnp.transpose(g_piece).astype(jnp.bfloat16)
        sid = sid_ref[pl.ds(PAD, rows), :]
        lags = lag_ref[c]
        before = jnp.zeros((LANES, LANES), jnp.float32)
        total = jnp.zeros((rows, LANES), jnp.float32)
        earlier = None
        sums = []
        for d in range(n_lag + 1):
            ahead = pl.ds(PAD + d, rows)
            x = jnp.where(sid_ref[ahead, :] == sid, gp[pl.ds(d, rows), :], 0.0)
            t, before = toeplitz(lags, d, n_lag, lower, before)
            total = total + dot(x.astype(jnp.bfloat16), t, 1, 1)
            at = pl.ds(PAD - d, rows)
            back = jnp.where(sid_ref[at, :] == sid, vp[at, :], 0.0).astype(jnp.bfloat16)
            pairs = dot(g_turned, back)
            if d:
                skew = jnp.where(wraps, earlier, pairs)
                skew = pltpu.roll(skew, 0, 1, stride=1, stride_axis=0)
                sums.append(jnp.sum(skew, axis=0, keepdims=True))
            earlier = pairs
        yp[0:rows, :] = total
        out = from_pieces(seg_ref, yp, rows, docs) + skip_ref[own, :] * grad
        table[pl.ds(c, rows, stride=channels), :] = out
        lag_grad = jnp.concatenate(sums, axis=0)
        fill_lane_powers(pw_re, pw_im, c, tab_re, tab_im, 1)
        both = jnp.concatenate([lag_grad, lag_grad * lag_place], axis=0).astype(jnp.bfloat16)
        part_re = dot(both, tab_re[...].astype(jnp.bfloat16))
        part_im = dot(both, tab_im[...].astype(jnp.bfloat16))
        dr, di = power_rows(pw_re, pw_im, c, 7, bits, n_lag)
        gr, gi = cmul(dr, di, part_re[0:n_lag], part_im[0:n_lag])
        hr, hi = cmul(dr, di, part_re[n_lag:], part_im[n_lag:])
        gr, gi, hr, hi = (jnp.sum(a, axis=0, keepdims=True) for a in (gr, gi, hr, hi))
        kr, ki, dt = kr_ref[own, :], ki_ref[own, :], dt_ref[own, :]
        rate_grad = -dt * (kr * hr - ki * hi)
        freq_grad = -dt * (kr * hi + ki * hr)
        for at, row_out in enumerate((rate_grad, freq_grad, gr + skip_grad, -gi)):
            grads[at][own, :] = row_out
        step = jnp.sum(
            rate_grad * rate_ref[own, :] + freq_grad * freq_ref[own, :], axis=1, keepdims=True
        )
        for at, one in enumerate((step, skip_grad)):
            thin[at][own, :] = jnp.broadcast_to(one, (1, LANES))
        return unused

    lax.fori_loop(0, channels, channel, 0)
    table_to_rows(table, back, *shape)
    home = lambda peer, slot: dv_ref.at[slot]
    swap_start(back, home, out_send, out_recv, flat, n, n_wt)
    own = pltpu.make_async_copy(back.at[flat], dv_ref.at[flat], local_sem)
    own.start()
    for at in range(4):
        all_out[w_me, :, pl.ds(at * states, states)] = grads[at][...]
    for at in range(2):
        all_out[w_me, :, pl.ds(4 * states + at * LANES, LANES)] = thin[at][...]
    share_over_wt(all_out, s_me, w_me, n_wt, wt_send, wt_recv)
    own.wait()
    swap_wait(back, home, out_send, out_recv, flat, n, n_wt)


def vmem(*shape):
    return pltpu.VMEM(shape, jnp.float32)


def table_inputs(decay_rate, frequency, log_step, n_lag):
    bits = (n_lag - 1).bit_length()
    dt = jnp.exp(log_step)[:, None]
    powers = jnp.array([float(1 << b) for b in range(7 + bits)] + [0.0] * (9 - bits), jnp.float32)
    powers = powers[None, :, None]
    mag = jnp.exp(-(decay_rate * dt)[:, None, :] * powers)
    phase = (frequency * dt)[:, None, :] * powers
    return dt, bits, mag * jnp.cos(phase), mag * jnp.sin(phase)


def segment_tables(segment, docs):
    seqs, length = segment.shape
    blocks = length // LANES
    per = -(-(blocks + docs) // 8) * 8
    seg = segment.reshape(seqs, blocks, LANES)
    piece = seg + jnp.arange(blocks, dtype=jnp.int32)[None, :, None]
    hit = piece.reshape(seqs, 1, length) == jnp.arange(per, dtype=jnp.int32)[None, :, None]
    sid = jnp.max(jnp.where(hit, segment[:, None, :], -1), axis=-1)
    sid = jnp.where(sid >= 0, sid + docs * jnp.arange(seqs, dtype=jnp.int32)[:, None], -1)
    seg = jnp.pad(seg, ((0, 0), (0, per - blocks), (0, 0)), constant_values=-1)
    seg = jnp.pad(seg.reshape(seqs * per, LANES), ((PAD, PAD), (0, 0)), constant_values=-1)
    sid = jnp.pad(sid.reshape(seqs * per), ((PAD, PAD),), constant_values=-2)
    return seg, jnp.broadcast_to(sid[:, None], (seqs * per + 2 * PAD, LANES)), per


def scratch_for(rows, states, n, channels, local, n_wt, pads):
    return (
        [vmem(PAD + rows, LANES)] * pads
        + [vmem(LANES, states), vmem(LANES, states), vmem(rows * channels, LANES)]
        + [pltpu.VMEM((n, channels, local), jnp.bfloat16)] * 2
        + [pltpu.SemaphoreType.DMA((n,))] * 4
        + [pltpu.SemaphoreType.DMA((n_wt + 1,))] * 2
        + [pltpu.SemaphoreType.DMA]
    )


def mix_forward(value, seg, sid, per, seq_count, docs, n_lag, bits, pw_re, pw_im, kr, ki, skip):
    n, channels, local = value.shape
    rows = seg.shape[0] - 2 * PAD
    states = kr.shape[1]
    n_wt = lax.axis_size("wt")
    wide = jnp.broadcast_to(skip[:, None], (channels, LANES))
    return pl.pallas_call(
        functools.partial(mix_forward_kernel, n_lag, docs, bits, seq_count, per),
        out_shape=(
            jax.ShapeDtypeStruct((n_wt, n, channels, local), jnp.bfloat16),
            jax.ShapeDtypeStruct((channels, rows, LANES), jnp.bfloat16),
            jax.ShapeDtypeStruct((channels, n_lag, LANES), jnp.float32),
        ),
        in_specs=[pl.BlockSpec(memory_space=pltpu.VMEM)] * 8,
        out_specs=(pl.BlockSpec(memory_space=pltpu.VMEM),) * 3,
        scratch_shapes=scratch_for(rows, states, n, channels, local, n_wt, 3),
        compiler_params=pltpu.CompilerParams(
            vmem_limit_bytes=48 << 20, collective_id=1, has_side_effects=True
        ),
        cost_estimate=pl.CostEstimate(flops=20_000_000_000, bytes_accessed=4_000_000, transcendentals=0),
        name="mix_forward",
    )(value, seg, sid, pw_re, pw_im, kr, ki, wide)


def mix_backward(
    grad, v, seg, sid, per, seq_count, docs, n_lag, bits, pw_re, pw_im, kr, ki, rate, freq, dt,
    skip, lags,
):
    n, channels, local = grad.shape
    rows = seg.shape[0] - 2 * PAD
    states = kr.shape[1]
    n_wt = lax.axis_size("wt")
    wide = jnp.broadcast_to(skip[:, None], (channels, LANES))
    dt = jnp.broadcast_to(dt, (channels, states))
    return pl.pallas_call(
        functools.partial(mix_backward_kernel, n_lag, docs, bits, seq_count, per),
        out_shape=(
            jax.ShapeDtypeStruct(grad.shape, jnp.bfloat16),
            jax.ShapeDtypeStruct((n_wt, channels, 4 * states + 2 * LANES), jnp.float32),
        ),
        in_specs=[pl.BlockSpec(memory_space=pltpu.VMEM)] * 13,
        out_specs=(pl.BlockSpec(memory_space=pltpu.VMEM),) * 2,
        scratch_shapes=scratch_for(rows, states, n, channels, local, n_wt, 5)
        + [vmem(channels, states)] * 4
        + [vmem(channels, LANES)] * 2,
        compiler_params=pltpu.CompilerParams(
            vmem_limit_bytes=48 << 20, collective_id=2, has_side_effects=True
        ),
        cost_estimate=pl.CostEstimate(flops=25_000_000_000, bytes_accessed=4_000_000, transcendentals=0),
        name="mix_backward",
    )(grad, v, seg, sid, pw_re, pw_im, kr, ki, rate, freq, dt, wide, lags)


BOTH = ("seq", "wt")
norm_epsilon = 1e-05


def gelu_tanh(pre_act):
    return jax.nn.gelu(pre_act, approximate=True)


def layer_norm(token_rows, gain_vec, bias_vec):
    row_mean = jnp.mean(token_rows, axis=-1, keepdims=True)
    centered = token_rows - row_mean
    spread = jnp.mean(centered * centered, axis=-1, keepdims=True)
    return centered * lax.rsqrt(spread + norm_epsilon) * gain_vec + bias_vec


def doc_segments(doc_lengths, seq_length):
    docs = doc_lengths.shape[1]
    upto = jnp.arange(docs)[:, None] >= jnp.arange(docs)[None, :]
    ends = jnp.sum(jnp.where(upto[None], doc_lengths[:, None, :], 0), axis=-1)
    places = jnp.arange(seq_length, dtype=jnp.int32)
    passed = (places[None, None, :] >= ends[:, :, None]).astype(jnp.int32)
    return jnp.sum(passed, axis=1, dtype=jnp.int32)


def after(x, first):
    return lax.optimization_barrier((x, first))[0]


class Ring:
    def __init__(self, axis, inner):
        self.axis, self.size = axis, lax.axis_size(axis)
        self.inner = min(inner, self.size)
        self.outer = self.size // self.inner
        self.me = lax.axis_index(axis)
        self.o, self.i = self.me // self.inner, self.me % self.inner

    def shift(self, x, k, j):
        to = [
            ((p // self.inner + k) % self.outer) * self.inner + (p % self.inner + j) % self.inner
            for p in range(self.size)
        ]
        return lax.ppermute(x, self.axis, list(enumerate(to)))

    def parts(self, x, joined):
        far = [(0, x)] + [(k, self.shift(x, k, 0)) for k in range(1, self.outer)]
        back = lambda k, j: ((self.o - k) % self.outer) * self.inner + (self.i - j) % self.inner
        out = [(back(k, 0), part) for k, part in far]
        for j in range(1, self.inner):
            if joined:
                near = self.shift(jnp.stack([part for _, part in far]), 0, j)
                out += [(back(k, j), near[k]) for k in range(self.outer)]
            else:
                out += [(back(k, j), self.shift(part, 0, j)) for k, part in far]
        return out

    def gather(self, x, joined=True):
        return self.place(self.parts(x, joined))

    def place(self, parts, axis=0):
        first = parts[0][1]
        out = jnp.zeros(first.shape[:axis] + (self.size,) + first.shape[axis:], first.dtype)
        for at, part in parts:
            out = lax.dynamic_update_index_in_dim(out, part, at, axis)
        return out

    def exchange(self, x):
        parts = []
        for k in range(self.outer):
            for j in range(self.inner):
                to = ((self.o + k) % self.outer) * self.inner + (self.i + j) % self.inner
                back = ((self.o - k) % self.outer) * self.inner + (self.i - j) % self.inner
                block = lax.dynamic_index_in_dim(x, to, 0, keepdims=False)
                parts.append((back, block if k == j == 0 else self.shift(block, k, j)))
        return self.place(parts)

    def scatter_sum(self, x):
        wide, narrow = jnp.float32, jnp.bfloat16
        x = x.astype(narrow).reshape((self.outer, self.inner) + x.shape[1:])
        pick = lambda j: lax.dynamic_index_in_dim(x, (self.i + j) % self.inner, 1, keepdims=False)
        held = pick(0).astype(wide)
        for j in range(1, self.inner):
            held = held + self.shift(pick(j), 0, j).astype(wide)
        low = held.astype(narrow)
        take = lambda a, k: lax.dynamic_index_in_dim(a, (self.o + k) % self.outer, 0, keepdims=False)
        total = take(held, 0)
        for k in range(1, self.outer):
            total = total + self.shift(take(low, k), k, 0).astype(wide)
        return total


def on_device(
    inputs, cotangent, doc_lengths, norm_gain, norm_bias, gate_weight, value_weight, mix_weight,
    down_weight, decay_rate, frequency, kernel_re, kernel_im, log_step, skip_gain,
):
    seq_count, local_len, model_width = inputs.shape
    row_count = seq_count * local_len
    n_seq, n_wt = lax.axis_size("seq"), lax.axis_size("wt")
    seq, wt = Ring("seq", 2 if n_seq <= 8 else 8), Ring("wt", 2)
    length = local_len * n_seq
    docs = doc_lengths.shape[1]
    n_lag = length // 2 // LANES
    blocks = length // LANES
    width = value_weight.shape[1]
    d_rows = value_weight.shape[0]
    h_rows = mix_weight.shape[0]
    f_rows = down_weight.shape[0]
    gate_width = gate_weight.shape[1]
    f_part = gate_width // n_wt
    low = jnp.bfloat16

    norm_row = jnp.concatenate([norm_gain, norm_bias])[None]
    norm_row = jnp.pad(norm_row, ((0, 15), (0, width - norm_row.shape[1])))
    front = seq.gather(wt.gather(jnp.concatenate([value_weight, norm_row], axis=0)))
    front = front.reshape(n_seq * n_wt, d_rows + 16, width)
    value_full = front[:, :d_rows].reshape(model_width, width)
    gain_full = front[:, d_rows, :d_rows].reshape(model_width)
    bias_full = front[:, d_rows, d_rows : 2 * d_rows].reshape(model_width)
    lengths_all = wt.gather(doc_lengths).reshape(n_wt * seq_count, docs)

    def columns(x):
        x = x.reshape(x.shape[0], n_seq, n_wt, f_rows).transpose(2, 0, 1, 3)
        return x.reshape(n_wt, -1, f_part)

    both_rows = d_rows + h_rows
    packed = columns(jnp.concatenate([gate_weight, mix_weight], axis=0))
    packed = wt.exchange(after(packed, front))
    parts = seq.parts(packed, False)
    gate_own = seq.place([(s, p[:, :d_rows]) for s, p in parts]).reshape(model_width, f_part)
    mix_own = seq.place([(s, p[:, d_rows:]) for s, p in parts]).reshape(width, f_part)
    down_own = seq.gather(after(down_weight, packed), False).reshape(f_part, model_width)

    own_channels = width // (n_seq * n_wt)

    def own(x):
        return lax.dynamic_slice_in_dim(x, wt.me * own_channels, own_channels, 0)

    rate, freq, kr, ki = own(decay_rate), own(frequency), own(kernel_re), own(kernel_im)
    step, skip = own(log_step), own(skip_gain)
    dt, bits, pw_re, pw_im = table_inputs(rate, freq, step, n_lag)
    seg, sid, per = segment_tables(doc_segments(lengths_all, length), docs)

    token_rows = inputs.reshape(row_count, model_width).astype(jnp.float32)
    normed, norm_back = jax.vjp(
        layer_norm, token_rows, gain_full.astype(jnp.float32), bias_full.astype(jnp.float32)
    )
    normed_low = normed.astype(low)
    cot_rows = cotangent.reshape(row_count, model_width)
    pair = wt.gather(jnp.stack([normed_low, cot_rows]), True)
    normed_all = pair[:, 0].reshape(n_wt * row_count, model_width)
    cot_all = pair[:, 1].reshape(n_wt * row_count, model_width)

    value_pre = dot(value_full, normed_low, 0, 1)
    value_act, value_back = jax.vjp(gelu_tanh, value_pre)
    by_device = (n_seq * n_wt, own_channels, row_count)
    mixed, value_ch, lags = mix_forward(
        value_act.astype(low).reshape(by_device), seg, sid, per, seq_count, docs, n_lag, bits, pw_re,
        pw_im, kr, ki, skip,
    )
    mixed = mixed.reshape(n_wt, width, row_count)
    mixed = mixed.transpose(1, 0, 2).reshape(width, n_wt * row_count)

    gate_pre = dot(normed_all, gate_own)
    gate_act, gate_back = jax.vjp(gelu_tanh, gate_pre)
    product_grad = dot(cot_all, down_own, 1, 1)
    expand = dot(mixed, mix_own, 0, 0)
    expand_low = (product_grad * gate_act).astype(low)
    mixed_grad = dot(mix_own, expand_low, 1, 1).astype(low)
    mixed_grad = mixed_grad.reshape(width, n_wt, row_count).transpose(1, 0, 2)
    mixed_grad = wt.scatter_sum(mixed_grad).astype(low)
    product_low = (expand * gate_act).astype(low)
    gate_pre_low = gate_back(product_grad * expand)[0].astype(low)

    down_grad = dot(product_low, cot_all, 0, 0).astype(low).reshape(n_seq, f_rows, model_width)
    mix_grad = dot(mixed, expand_low).astype(low).reshape(n_seq, n_wt * h_rows, f_part)
    gate_grad = dot(normed_all, gate_pre_low, 0, 0).astype(low).reshape(n_seq, n_wt * d_rows, f_part)
    down_piece = seq.scatter_sum(down_grad)
    mix_band = seq.scatter_sum(mix_grad)
    gate_band = seq.scatter_sum(gate_grad)

    result = dot(product_low, down_own).astype(low)
    gate_side = dot(gate_pre_low, gate_own, 1, 1).astype(low)
    tok = lambda x: x.reshape(n_wt, row_count, model_width)
    token_sums = wt.scatter_sum(jnp.stack([tok(result), tok(gate_side)], axis=1))
    outputs = (token_rows + token_sums[0]).astype(low).reshape(inputs.shape)

    value_grad_tok, packed = mix_backward(
        mixed_grad.reshape(by_device), value_ch, seg, sid, per, seq_count, docs, n_lag, bits, pw_re,
        pw_im, kr, ki, rate, freq, dt, skip, lags,
    )
    value_grad_tok = value_grad_tok.reshape(width, row_count).astype(jnp.float32)
    value_pre_low = value_back(value_grad_tok)[0].astype(low)
    states = rate.shape[1]
    packed = packed.reshape(n_wt * own_channels, -1)
    mixer_grads = [packed[:, i * states : (i + 1) * states] for i in range(4)]
    mixer_grads += [packed[:, 4 * states], packed[:, 4 * states + LANES]]

    value_turn = wt.exchange(value_pre_low.reshape(n_wt, width // n_wt, row_count))
    value_turn = value_turn.transpose(1, 0, 2).reshape(width // n_wt, n_wt * row_count)
    value_grad = dot(normed_all, value_turn, 0, 1).reshape(n_seq, n_wt * d_rows, width // n_wt)
    value_band = seq.scatter_sum(value_grad)

    normed_grad = token_sums[1] + dot(value_pre_low, value_full, 0, 1)
    input_rows, gain_grad, bias_grad = norm_back(normed_grad)
    input_grad = (cot_rows.astype(jnp.float32) + input_rows).reshape(inputs.shape)
    vectors = jnp.stack([gain_grad, bias_grad]).astype(low).reshape(2, n_seq * n_wt, d_rows)
    vectors = lax.all_to_all(
        vectors.transpose(1, 0, 2), BOTH, split_axis=0, concat_axis=0, tiled=True
    )
    vectors = jnp.sum(vectors.astype(jnp.float32), axis=0)

    last = [
        gate_band.reshape(n_wt, d_rows, f_part),
        mix_band.reshape(n_wt, h_rows, f_part),
        value_band.reshape(n_wt, d_rows, width // n_wt),
    ]
    heads = wt.exchange(jnp.concatenate(last[:2], axis=1).astype(low)).astype(jnp.float32)
    tails = wt.exchange(last[2].astype(low)).astype(jnp.float32)

    def spread(x):
        rows = x.shape[1]
        x = x.reshape(n_wt, rows, n_seq, f_rows).transpose(1, 2, 0, 3)
        return x.reshape(rows, gate_width)

    value_piece = tails.transpose(1, 0, 2).reshape(d_rows, width)
    return (
        outputs, input_grad, vectors[0], vectors[1], spread(heads[:, :d_rows]), value_piece,
        spread(heads[:, d_rows:]), down_piece, *mixer_grads,
    )


def solution(mesh):
    in_specs = (
        P("wt", "seq", None),
        P("wt", "seq", None),
        P("wt", None),
        P(("seq", "wt")),
        P(("seq", "wt")),
        P(("seq", "wt"), None),
        P(("seq", "wt"), None),
        P(("seq", "wt"), None),
        P(("seq", "wt"), None),
        P("seq", None),
        P("seq", None),
        P("seq", None),
        P("seq", None),
        P("seq"),
        P("seq"),
    )
    out_specs = (
        P("wt", "seq", None),
        P("wt", "seq", None),
        P(("seq", "wt")),
        P(("seq", "wt")),
        P(("seq", "wt"), None),
        P(("seq", "wt"), None),
        P(("seq", "wt"), None),
        P(("seq", "wt"), None),
        P("seq", None),
        P("seq", None),
        P("seq", None),
        P("seq", None),
        P("seq"),
        P("seq"),
    )
    return jax.shard_map(
        on_device, mesh=mesh, in_specs=in_specs, out_specs=out_specs, check_vma=False
    )
```

```python
import functools

import jax
import jax.numpy as jnp
from jax import lax
from jax.experimental import pallas as pl
from jax.experimental.pallas import tpu as pltpu
from jax.sharding import PartitionSpec as P

LANES = 128
PAD = 16


MESH = pl.DeviceIdType.MESH


def place_of(flat, n_wt):
    return (flat // n_wt, flat % n_wt)


def meet(flat, n, n_wt):
    barrier = pltpu.get_barrier_semaphore()

    def tell(r, unused):
        pl.semaphore_signal(
            barrier, inc=1, device_id=place_of((flat + r) % n, n_wt), device_id_type=MESH
        )
        return unused

    lax.fori_loop(1, n, tell, 0)
    pl.semaphore_wait(barrier, n - 1)


def swap_copy(source, target, send_sem, recv_sem, slot, peer, n_wt):
    return pltpu.make_async_remote_copy(
        src_ref=source, dst_ref=target, send_sem=send_sem.at[slot], recv_sem=recv_sem.at[slot],
        device_id=place_of(peer, n_wt), device_id_type=MESH,
    )


def swap_start(send, target_of, send_sem, recv_sem, flat, n, n_wt):
    def one(r, unused):
        peer = (flat + r) % n
        swap_copy(send.at[peer], target_of(peer, flat), send_sem, recv_sem, r, peer, n_wt).start()
        return unused

    lax.fori_loop(1, n, one, 0)


def swap_wait(send, target_of, send_sem, recv_sem, flat, n, n_wt):
    def one(r, unused):
        source = (flat + n - r) % n
        swap_copy(
            send.at[source], target_of(flat, source), send_sem, recv_sem, r, source, n_wt
        ).wait()
        return unused

    lax.fori_loop(1, n, one, 0)


def rows_to_table(got, table, n_seq, n_wt, seq_count, local_blocks, per, channels):
    for s in range(n_seq):
        for w in range(n_wt):
            for k in range(seq_count):
                for b in range(local_blocks):
                    row = (w * seq_count + k) * per + s * local_blocks + b
                    lanes = pl.ds((k * local_blocks + b) * LANES, LANES)
                    table[pl.ds(row * channels, channels), :] = got[
                        s * n_wt + w, :, lanes
                    ].astype(jnp.float32)


def table_to_rows(table, send, n_seq, n_wt, seq_count, local_blocks, per, channels):
    for s in range(n_seq):
        for w in range(n_wt):
            for k in range(seq_count):
                for b in range(local_blocks):
                    row = (w * seq_count + k) * per + s * local_blocks + b
                    lanes = pl.ds((k * local_blocks + b) * LANES, LANES)
                    send[s * n_wt + w, :, lanes] = table[
                        pl.ds(row * channels, channels), :
                    ].astype(jnp.bfloat16)


def clear_unused(table, seqs, blocks, per, channels):
    for s in range(seqs):
        table[pl.ds((s * per + blocks) * channels, (per - blocks) * channels), :] = jnp.zeros(
            ((per - blocks) * channels, LANES), jnp.float32
        )


def share_over_wt(ref, s_me, w_me, n_wt, send_sem, recv_sem):
    inner = 2
    outer = n_wt // inner
    o, i = w_me // inner, w_me % inner
    other = (s_me, o * inner + 1 - i)

    def copy(block, slot, to):
        return pltpu.make_async_remote_copy(
            src_ref=ref.at[block], dst_ref=ref.at[block], send_sem=send_sem.at[slot],
            recv_sem=recv_sem.at[slot], device_id=to, device_id_type=MESH,
        )

    far = [copy(w_me, k, (s_me, ((o + k) % outer) * inner + i)) for k in range(1, outer)]
    near = [copy(w_me, outer, other)]
    for c in far + near:
        c.start()
    for k in range(1, outer):
        block = ((o + outer - k) % outer) * inner + i
        far[k - 1].wait_recv()
        c = copy(block, outer + k, other)
        c.start()
        near.append(c)
    for c in far:
        c.wait_send()
    for c in near:
        c.wait()


def cmul(ar, ai, br, bi):
    return ar * br - ai * bi, ar * bi + ai * br


def power_rows(pw_re, pw_im, c, first, count, rows):
    width = pw_re.shape[2]
    place = lax.broadcasted_iota(jnp.int32, (rows, width), 0)
    re = jnp.ones((rows, width), jnp.float32)
    im = jnp.zeros((rows, width), jnp.float32)
    for bit in range(count):
        on = (place & (1 << bit)) != 0
        fr = jnp.where(on, pw_re[c, pl.ds(first + bit, 1), :], 1.0)
        fi = jnp.where(on, pw_im[c, pl.ds(first + bit, 1), :], 0.0)
        re, im = cmul(re, im, fr, fi)
    return re, im


def fill_lane_powers(pw_re, pw_im, c, tab_re, tab_im, extra):
    re, im = power_rows(pw_re, pw_im, c, 0, 3, 8)
    if extra:
        re, im = cmul(re, im, pw_re[c, pl.ds(0, 1), :], pw_im[c, pl.ds(0, 1), :])
    tab_re[0:8, :] = re
    tab_im[0:8, :] = im
    have, bit = 8, 3
    while have < LANES:
        re, im = cmul(
            tab_re[0:have, :],
            tab_im[0:have, :],
            pw_re[c, pl.ds(bit, 1), :],
            pw_im[c, pl.ds(bit, 1), :],
        )
        tab_re[have : 2 * have, :] = re
        tab_im[have : 2 * have, :] = im
        have, bit = 2 * have, bit + 1


def to_pieces(seg, val, rows, docs):
    total = jnp.zeros((rows, LANES), jnp.float32)
    for j in range(docs):
        at = pl.ds(PAD - j, rows)
        total = total + jnp.where(seg[at, :] == j, val[at, :], 0.0)
    return total


def from_pieces(seg, piece, rows, docs):
    own = seg[pl.ds(PAD, rows), :]
    total = jnp.zeros((rows, LANES), jnp.float32)
    for j in range(docs):
        total = total + jnp.where(own == j, piece[pl.ds(j, rows), :], 0.0)
    return total


def toeplitz(lags, d, last, lower, before):
    if d < last:
        row = jnp.broadcast_to(lags[d : d + 1, :], (LANES, LANES))
        here = pltpu.roll(row, 0, 1, stride=1, stride_axis=0)
    else:
        here = jnp.zeros((LANES, LANES), jnp.float32)
    return jnp.where(lower, here, before).astype(jnp.bfloat16), here


def dot(a, b, ca=1, cb=0):
    return lax.dot_general(a, b, (((ca,), (cb,)), ((), ())), preferred_element_type=jnp.float32)


def mix_backward_kernel(
    n_lag, docs, bits, seq_count, per, grad_ref, v_ref, seg_ref, sid_ref, pw_re, pw_im, kr_ref,
    ki_ref, rate_ref, freq_ref, dt_ref, skip_ref, lag_ref,
    dv_ref, all_out, vf, gf, vp, gp, yp, tab_re, tab_im, table, got, back,
    in_send, in_recv, out_send, out_recv, wt_send, wt_recv, local_sem, *held,
):
    grads, thin = held[:4], held[4:]
    channels, rows, _ = v_ref.shape
    states = kr_ref.shape[1]
    n_seq, n_wt = lax.axis_size("seq"), lax.axis_size("wt")
    n = n_seq * n_wt
    s_me, w_me = lax.axis_index("seq"), lax.axis_index("wt")
    flat = s_me * n_wt + w_me
    local_blocks = grad_ref.shape[2] // LANES // seq_count
    shape = (n_seq, n_wt, seq_count, local_blocks, per, channels)
    meet(flat, n, n_wt)
    into = lambda peer, slot: got.at[slot]
    swap_start(grad_ref, into, in_send, in_recv, flat, n, n_wt)
    got[flat] = grad_ref[flat]
    clear_unused(table, n_wt * seq_count, n_seq * local_blocks, per, channels)
    zero_pad = jnp.zeros((PAD, LANES), jnp.float32)
    vf[0:PAD, :] = zero_pad
    gf[0:PAD, :] = zero_pad
    vp[0:PAD, :] = zero_pad
    gp[pl.ds(rows, PAD), :] = zero_pad
    yp[pl.ds(rows, PAD), :] = zero_pad
    lane = lax.broadcasted_iota(jnp.int32, (LANES, LANES), 1)
    row = lax.broadcasted_iota(jnp.int32, (LANES, LANES), 0)
    lower = lane >= row
    wraps = lane + row >= LANES
    flip = (lane + row == LANES - 1).astype(jnp.bfloat16)
    lag_place = (
        lax.broadcasted_iota(jnp.int32, (n_lag, LANES), 0) * LANES
        + lax.broadcasted_iota(jnp.int32, (n_lag, LANES), 1)
        + 1
    ).astype(jnp.float32)
    swap_wait(grad_ref, into, in_send, in_recv, flat, n, n_wt)
    rows_to_table(got, table, *shape)

    def channel(c, unused):
        own = pl.ds(c, 1)
        val = v_ref[c].astype(jnp.float32)
        grad = table[pl.ds(c, rows, stride=channels), :]
        vf[pl.ds(PAD, rows), :] = val
        gf[pl.ds(PAD, rows), :] = grad
        skip_grad = jnp.sum(jnp.sum(val * grad, axis=0, keepdims=True), axis=1, keepdims=True)
        g_piece = to_pieces(seg_ref, gf, rows, docs)
        gp[0:rows, :] = g_piece
        v_piece = to_pieces(seg_ref, vf, rows, docs).astype(jnp.bfloat16)
        vp[pl.ds(PAD, rows), :] = dot(v_piece, flip)
        g_turned = jnp.transpose(g_piece).astype(jnp.bfloat16)
        sid = sid_ref[pl.ds(PAD, rows), :]
        lags = lag_ref[c]
        before = jnp.zeros((LANES, LANES), jnp.float32)
        total = jnp.zeros((rows, LANES), jnp.float32)
        earlier = None
        sums = []
        for d in range(n_lag + 1):
            ahead = pl.ds(PAD + d, rows)
            x = jnp.where(sid_ref[ahead, :] == sid, gp[pl.ds(d, rows), :], 0.0)
            t, before = toeplitz(lags, d, n_lag, lower, before)
            total = total + dot(x.astype(jnp.bfloat16), t, 1, 1)
            at = pl.ds(PAD - d, rows)
            back = jnp.where(sid_ref[at, :] == sid, vp[at, :], 0.0).astype(jnp.bfloat16)
            pairs = dot(g_turned, back)
            if d:
                skew = jnp.where(wraps, earlier, pairs)
                skew = pltpu.roll(skew, 0, 1, stride=1, stride_axis=0)
                sums.append(jnp.sum(skew, axis=0, keepdims=True))
            earlier = pairs
        yp[0:rows, :] = total
        out = from_pieces(seg_ref, yp, rows, docs) + skip_ref[own, :] * grad
        table[pl.ds(c, rows, stride=channels), :] = out
        lag_grad = jnp.concatenate(sums, axis=0)
        fill_lane_powers(pw_re, pw_im, c, tab_re, tab_im, 1)
        both = jnp.concatenate([lag_grad, lag_grad * lag_place], axis=0).astype(jnp.bfloat16)
        part_re = dot(both, tab_re[...].astype(jnp.bfloat16))
        part_im = dot(both, tab_im[...].astype(jnp.bfloat16))
        dr, di = power_rows(pw_re, pw_im, c, 7, bits, n_lag)
        gr, gi = cmul(dr, di, part_re[0:n_lag], part_im[0:n_lag])
        hr, hi = cmul(dr, di, part_re[n_lag:], part_im[n_lag:])
        gr, gi, hr, hi = (jnp.sum(a, axis=0, keepdims=True) for a in (gr, gi, hr, hi))
        kr, ki, dt = kr_ref[own, :], ki_ref[own, :], dt_ref[own, :]
        rate_grad = -dt * (kr * hr - ki * hi)
        freq_grad = -dt * (kr * hi + ki * hr)
        for at, row_out in enumerate((rate_grad, freq_grad, gr + skip_grad, -gi)):
            grads[at][own, :] = row_out
        step = jnp.sum(
            rate_grad * rate_ref[own, :] + freq_grad * freq_ref[own, :], axis=1, keepdims=True
        )
        for at, one in enumerate((step, skip_grad)):
            thin[at][own, :] = jnp.broadcast_to(one, (1, LANES))
        return unused

    lax.fori_loop(0, channels, channel, 0)
    table_to_rows(table, back, *shape)
    home = lambda peer, slot: dv_ref.at[slot]
    swap_start(back, home, out_send, out_recv, flat, n, n_wt)
    own = pltpu.make_async_copy(back.at[flat], dv_ref.at[flat], local_sem)
    own.start()
    for at in range(4):
        all_out[w_me, :, pl.ds(at * states, states)] = grads[at][...]
    for at in range(2):
        all_out[w_me, :, pl.ds(4 * states + at * LANES, LANES)] = thin[at][...]
    share_over_wt(all_out, s_me, w_me, n_wt, wt_send, wt_recv)
    own.wait()
    swap_wait(back, home, out_send, out_recv, flat, n, n_wt)


def vmem(*shape):
    return pltpu.VMEM(shape, jnp.float32)


def table_inputs(decay_rate, frequency, log_step, n_lag):
    bits = (n_lag - 1).bit_length()
    dt = jnp.exp(log_step)[:, None]
    powers = jnp.array([float(1 << b) for b in range(7 + bits)] + [0.0] * (9 - bits), jnp.float32)
    powers = powers[None, :, None]
    mag = jnp.exp(-(decay_rate * dt)[:, None, :] * powers)
    phase = (frequency * dt)[:, None, :] * powers
    return dt, bits, mag * jnp.cos(phase), mag * jnp.sin(phase)


def segment_tables(segment, docs):
    seqs, length = segment.shape
    blocks = length // LANES
    per = -(-(blocks + docs) // 8) * 8
    seg = segment.reshape(seqs, blocks, LANES)
    piece = seg + jnp.arange(blocks, dtype=jnp.int32)[None, :, None]
    hit = piece.reshape(seqs, 1, length) == jnp.arange(per, dtype=jnp.int32)[None, :, None]
    sid = jnp.max(jnp.where(hit, segment[:, None, :], -1), axis=-1)
    sid = jnp.where(sid >= 0, sid + docs * jnp.arange(seqs, dtype=jnp.int32)[:, None], -1)
    seg = jnp.pad(seg, ((0, 0), (0, per - blocks), (0, 0)), constant_values=-1)
    seg = jnp.pad(seg.reshape(seqs * per, LANES), ((PAD, PAD), (0, 0)), constant_values=-1)
    sid = jnp.pad(sid.reshape(seqs * per), ((PAD, PAD),), constant_values=-2)
    return seg, jnp.broadcast_to(sid[:, None], (seqs * per + 2 * PAD, LANES)), per


def scratch_for(rows, states, n, channels, local, n_wt, pads):
    return (
        [vmem(PAD + rows, LANES)] * pads
        + [vmem(LANES, states), vmem(LANES, states), vmem(rows * channels, LANES)]
        + [pltpu.VMEM((n, channels, local), jnp.bfloat16)] * 2
        + [pltpu.SemaphoreType.DMA((n,))] * 4
        + [pltpu.SemaphoreType.DMA((n_wt + 1,))] * 2
        + [pltpu.SemaphoreType.DMA]
    )


def mix_backward(
    grad, v, seg, sid, per, seq_count, docs, n_lag, bits, pw_re, pw_im, kr, ki, rate, freq, dt,
    skip, lags,
):
    n, channels, local = grad.shape
    rows = seg.shape[0] - 2 * PAD
    states = kr.shape[1]
    n_wt = lax.axis_size("wt")
    wide = jnp.broadcast_to(skip[:, None], (channels, LANES))
    dt = jnp.broadcast_to(dt, (channels, states))
    return pl.pallas_call(
        functools.partial(mix_backward_kernel, n_lag, docs, bits, seq_count, per),
        out_shape=(
            jax.ShapeDtypeStruct(grad.shape, jnp.bfloat16),
            jax.ShapeDtypeStruct((n_wt, channels, 4 * states + 2 * LANES), jnp.float32),
        ),
        in_specs=[pl.BlockSpec(memory_space=pltpu.VMEM)] * 13,
        out_specs=(pl.BlockSpec(memory_space=pltpu.VMEM),) * 2,
        scratch_shapes=scratch_for(rows, states, n, channels, local, n_wt, 5)
        + [vmem(channels, states)] * 4
        + [vmem(channels, LANES)] * 2,
        compiler_params=pltpu.CompilerParams(
            vmem_limit_bytes=48 << 20, collective_id=2, has_side_effects=True
        ),
        cost_estimate=pl.CostEstimate(flops=25_000_000_000, bytes_accessed=4_000_000, transcendentals=0),
        name="mix_backward",
    )(grad, v, seg, sid, pw_re, pw_im, kr, ki, rate, freq, dt, wide, lags)


class Wires:
    def __init__(self, send_sem, recv_sem):
        self.send_sem, self.recv_sem, self.used, self.open = send_sem, recv_sem, 0, []

    def send(self, source, target, to):
        c = pltpu.make_async_remote_copy(
            src_ref=source, dst_ref=target, send_sem=self.send_sem.at[self.used],
            recv_sem=self.recv_sem.at[self.used], device_id=to, device_id_type=MESH,
        )
        self.used += 1
        self.open.append(c)
        c.start()
        return c

    def sent(self):
        for c in self.open:
            c.wait_send()
        self.open = []


def rms(x32):
    mean = jnp.mean(x32, axis=-1, keepdims=True)
    centered = x32 - mean
    spread = jnp.mean(centered * centered, axis=-1, keepdims=True)
    return centered * lax.rsqrt(spread + norm_epsilon)


def regroup(x, n_seq, n_wt, width):
    cut = lambda s, w: x[:, (s * n_wt + w) * width : (s * n_wt + w + 1) * width]
    return [jnp.concatenate([cut(s, w) for s in range(n_seq)], axis=1) for w in range(n_wt)]


def front_wires(n_seq, n_wt, inner):
    outer = n_seq // inner
    value = (n_seq - 1) + n_seq * (n_wt // 2 - 1) + n_seq * (n_wt // 2)
    weights = 2 * (n_wt - 1) + 3 * (outer - 1) + 3 * (inner - 1) * outer
    tokens = 2 * (n_wt // 2 - 1) + 2 * (n_wt // 2)
    mixed = (n_wt // 2 - 1) + n_wt // 2
    return value + weights + tokens + mixed


def front_kernel(
    n_lag, docs, bits, seq_count, per, inner_seq,
    x_ref, cot_ref, vpack_ref, gate_in, mix_in, down_in, seg_ref, sid_ref, pw_re, pw_im, kr_ref,
    ki_ref, skip_ref,
    pair, gate_out, mix_out, down_out, mixed_ref, v_ref, lag_ref, pre_ref, value_full, norm_out,
    vf, vp, yp, tab_re, tab_im, table, got, back, front, xhat, act_send, gate_cut, mix_cut,
    in_send, in_recv, out_send, out_recv, wire_send, wire_recv, local_sem,
):
    channels, rows, _ = v_ref.shape
    n_seq, n_wt = lax.axis_size("seq"), lax.axis_size("wt")
    n = n_seq * n_wt
    s_me, w_me = lax.axis_index("seq"), lax.axis_index("wt")
    flat = s_me * n_wt + w_me
    row_count, model_width = x_ref.shape
    width = pre_ref.shape[1]
    d_rows, h_rows, f_rows = gate_in.shape[0], mix_in.shape[0], down_in.shape[0]
    local_blocks = row_count // LANES // seq_count
    shape = (n_seq, n_wt, seq_count, local_blocks, per, channels)
    outer_wt = n_wt // 2
    o, i = w_me // 2, w_me % 2
    sibling = o * 2 + 1 - i
    far_to = lambda k: ((o + k) % outer_wt) * 2 + i
    far_from = lambda k: ((o + outer_wt - k) % outer_wt) * 2 + i
    outer_seq = n_seq // inner_seq
    so, si = s_me // inner_seq, s_me % inner_seq
    step_to = lambda k, j: ((so + k) % outer_seq) * inner_seq + (si + j) % inner_seq
    step_from = lambda k: ((so + outer_seq - k) % outer_seq) * inner_seq + si
    wires = Wires(wire_send, wire_recv)

    meet(flat, n, n_wt)

    front[s_me, w_me] = vpack_ref[...]
    first = []
    for k in range(1, n_seq):
        to = ((s_me + k) % n_seq, w_me)
        first.append(wires.send(front.at[s_me, w_me], front.at[s_me, w_me], to))

    second, third = [], []

    def spread_value(s):
        block = front.at[s, w_me]
        for k in range(1, outer_wt):
            second.append((s, k, wires.send(block, block, (s_me, far_to(k)))))
        third.append(wires.send(block, block, (s_me, sibling)))

    spread_value(s_me)

    for ref, cut in ((gate_in, gate_cut), (mix_in, mix_cut)):
        whole = ref[...].astype(jnp.float32)
        for w, part in enumerate(regroup(whole, n_seq, n_wt, f_rows)):
            cut[w] = part.astype(jnp.bfloat16)
    down_out[s_me] = down_in[...]
    gate_out[s_me, w_me] = gate_cut[w_me]
    mix_out[s_me, w_me] = mix_cut[w_me]

    chunk = min(32, row_count)

    def normalise(r, unused):
        at = pl.ds(r * chunk, chunk)
        xhat[at, :] = rms(x_ref[at, :].astype(jnp.float32))
        return unused

    lax.fori_loop(0, row_count // chunk, normalise, 0)
    pair[w_me, 1] = cot_ref[...]

    for k in range(1, n_seq):
        first[k - 1].wait_recv()
        spread_value((s_me + n_seq - k) % n_seq)

    turn = []
    for k in range(outer_wt):
        for j in range(2):
            if k or j:
                w = ((o + k) % outer_wt) * 2 + (i + j) % 2
                turn.append(wires.send(gate_cut.at[w], gate_out.at[s_me, w_me], (s_me, w)))
                turn.append(wires.send(mix_cut.at[w], mix_out.at[s_me, w_me], (s_me, w)))
    late = [wires.send(down_out.at[s_me], down_out.at[s_me], (step_to(k, 0), w_me)) for k in range(1, outer_seq)]
    near = [wires.send(down_out.at[s_me], down_out.at[s_me], (step_to(0, j), w_me)) for j in range(1, inner_seq)]

    for s, k, c in second:
        c.wait_recv()
        block = front.at[s, far_from(k)]
        third.append(wires.send(block, block, (s_me, sibling)))
    for c in third:
        c.wait_recv()

    for f in range(n):
        value_full[pl.ds(f * d_rows, d_rows), :] = front[f // n_wt, f % n_wt, 0:d_rows, :]
    share = LANES // d_rows
    for b in range(model_width // LANES):
        total = jnp.zeros((2, LANES), jnp.float32)
        for f in range(b * share, (b + 1) * share):
            total = total + front[f // n_wt, f % n_wt, d_rows : d_rows + 2, 0:LANES].astype(jnp.float32)
        norm_out[:, pl.ds(b * LANES, LANES)] = total

    def project(r, unused):
        at = pl.ds(pl.multiple_of(r * LANES, LANES), LANES)
        normed = (xhat[at, :] * norm_out[0:1, :] + norm_out[1:2, :]).astype(jnp.bfloat16)
        pair[w_me, 0, at, :] = normed
        pre = dot(normed, value_full[...])
        pre_ref[at, :] = pre
        turned = jnp.transpose(gelu_tanh(pre))
        for p in range(n):
            act_send[p, :, at] = turned[p * channels : (p + 1) * channels, :].astype(jnp.bfloat16)
        return unused

    lax.fori_loop(0, row_count // LANES, project, 0)
    into = lambda peer, slot: got.at[slot]
    swap_start(act_send, into, in_send, in_recv, flat, n, n_wt)
    got[flat] = act_send[flat]

    for c in turn:
        c.wait_recv()
    for k in range(1, outer_seq):
        to = (step_to(k, 0), w_me)
        late.append(wires.send(gate_out.at[s_me], gate_out.at[s_me], to))
        late.append(wires.send(mix_out.at[s_me], mix_out.at[s_me], to))
    for j in range(1, inner_seq):
        to = (step_to(0, j), w_me)
        near.append(wires.send(gate_out.at[s_me], gate_out.at[s_me], to))
        near.append(wires.send(mix_out.at[s_me], mix_out.at[s_me], to))

    clear_unused(table, n_wt * seq_count, n_seq * local_blocks, per, channels)
    zero_pad = jnp.zeros((PAD, LANES), jnp.float32)
    vf[0:PAD, :] = zero_pad
    vp[0:PAD, :] = zero_pad
    yp[pl.ds(rows, PAD), :] = zero_pad
    lower = lax.broadcasted_iota(jnp.int32, (LANES, LANES), 1) >= lax.broadcasted_iota(
        jnp.int32, (LANES, LANES), 0
    )
    swap_wait(act_send, into, in_send, in_recv, flat, n, n_wt)

    far_pair = []
    for at in range(2):
        block = pair.at[w_me, at]
        for k in range(1, outer_wt):
            far_pair.append((k, at, wires.send(block, block, (s_me, far_to(k)))))
    near_pair = [wires.send(pair.at[w_me, at], pair.at[w_me, at], (s_me, sibling)) for at in range(2)]

    rows_to_table(got, table, *shape)

    def channel(c, unused):
        fill_lane_powers(pw_re, pw_im, c, tab_re, tab_im, 0)
        dr, di = power_rows(pw_re, pw_im, c, 7, bits, n_lag)
        ar, ai = cmul(dr, di, kr_ref[pl.ds(c, 1), :], ki_ref[pl.ds(c, 1), :])
        lags = dot(ar.astype(jnp.bfloat16), tab_re[...].astype(jnp.bfloat16), 1, 1) - dot(
            ai.astype(jnp.bfloat16), tab_im[...].astype(jnp.bfloat16), 1, 1
        )
        lag_ref[c] = lags
        val = table[pl.ds(c, rows, stride=channels), :]
        v_ref[c] = val.astype(jnp.bfloat16)
        vf[pl.ds(PAD, rows), :] = val
        vp[pl.ds(PAD, rows), :] = to_pieces(seg_ref, vf, rows, docs)
        sid = sid_ref[pl.ds(PAD, rows), :]
        before = jnp.zeros((LANES, LANES), jnp.float32)
        total = jnp.zeros((rows, LANES), jnp.float32)
        for d in range(n_lag + 1):
            at = pl.ds(PAD - d, rows)
            x = jnp.where(sid_ref[at, :] == sid, vp[at, :], 0.0).astype(jnp.bfloat16)
            t, before = toeplitz(lags, d, n_lag, lower, before)
            total = total + dot(x, t)
        yp[0:rows, :] = total
        out = from_pieces(seg_ref, yp, rows, docs) + skip_ref[pl.ds(c, 1), :] * val
        table[pl.ds(c, rows, stride=channels), :] = out
        return unused

    def pass_on(at, k):
        late[at].wait_recv()
        ref = (down_out, gate_out, mix_out)[0 if at < outer_seq - 1 else 1 + (at - outer_seq + 1) % 2]
        block = ref.at[step_from(k)]
        for j in range(1, inner_seq):
            near.append(wires.send(block, block, (step_to(0, j), w_me)))

    half = channels // 2
    lax.fori_loop(0, half, channel, 0)
    for k in range(1, outer_seq):
        pass_on(k - 1, k)
    lax.fori_loop(half, channels, channel, 0)
    table_to_rows(table, back, *shape)
    home = lambda peer, slot: mixed_ref.at[peer % n_wt, slot]
    swap_start(back, home, out_send, out_recv, flat, n, n_wt)
    own = pltpu.make_async_copy(back.at[flat], mixed_ref.at[w_me, flat], local_sem)
    own.start()
    first_two = outer_seq - 1
    for at in range(2 * (outer_seq - 1)):
        pass_on(first_two + at, at // 2 + 1)
    own.wait()
    swap_wait(back, home, out_send, out_recv, flat, n, n_wt)

    block = mixed_ref.at[w_me]
    far_mixed = [wires.send(block, block, (s_me, far_to(k))) for k in range(1, outer_wt)]
    ends = [wires.send(block, block, (s_me, sibling))]
    for k, at, c in far_pair:
        c.wait_recv()
        block = pair.at[far_from(k), at]
        near_pair.append(wires.send(block, block, (s_me, sibling)))
    for k in range(1, outer_wt):
        far_mixed[k - 1].wait_recv()
        block = mixed_ref.at[far_from(k)]
        ends.append(wires.send(block, block, (s_me, sibling)))
    for c in near + near_pair + ends:
        c.wait_recv()
    wires.sent()


def front_call(
    x, cot, vpack, gate, mix, down, seg, sid, per, seq_count, docs, n_lag, bits, inner_seq, pw_re,
    pw_im, kr, ki, skip,
):
    n_seq, n_wt = lax.axis_size("seq"), lax.axis_size("wt")
    n = n_seq * n_wt
    channels, states = kr.shape
    rows = seg.shape[0] - 2 * PAD
    local, model_width = x.shape
    width = vpack.shape[1]
    f_part = gate.shape[1] // n_wt
    wide = jnp.broadcast_to(skip[:, None], (channels, LANES))
    low = jnp.bfloat16
    wires = front_wires(n_seq, n_wt, inner_seq)
    out = jax.ShapeDtypeStruct
    return pl.pallas_call(
        functools.partial(front_kernel, n_lag, docs, bits, seq_count, per, inner_seq),
        out_shape=(
            out((n_wt, 2, local, model_width), low),
            out((n_seq, n_wt) + (gate.shape[0], f_part), low),
            out((n_seq, n_wt) + (mix.shape[0], f_part), low),
            out((n_seq,) + down.shape, low),
            out((n_wt, n, channels, local), low),
            out((channels, rows, LANES), low),
            out((channels, n_lag, LANES), jnp.float32),
            out((local, width), jnp.float32),
            out((model_width, width), low),
            out((2, model_width), jnp.float32),
        ),
        in_specs=[pl.BlockSpec(memory_space=pltpu.VMEM)] * 13,
        out_specs=(pl.BlockSpec(memory_space=pltpu.VMEM),) * 10,
        scratch_shapes=[vmem(PAD + rows, LANES)] * 3
        + [vmem(LANES, states), vmem(LANES, states), vmem(rows * channels, LANES)]
        + [pltpu.VMEM((n, channels, local), low)] * 2
        + [pltpu.VMEM((n_seq, n_wt) + vpack.shape, low), vmem(local, model_width)]
        + [pltpu.VMEM((n, channels, local), low)]
        + [pltpu.VMEM((n_wt, gate.shape[0], f_part), low), pltpu.VMEM((n_wt, mix.shape[0], f_part), low)]
        + [pltpu.SemaphoreType.DMA((n,))] * 4
        + [pltpu.SemaphoreType.DMA((wires,))] * 2
        + [pltpu.SemaphoreType.DMA],
        compiler_params=pltpu.CompilerParams(
            vmem_limit_bytes=56 << 20, collective_id=1, has_side_effects=True
        ),
        cost_estimate=pl.CostEstimate(
            flops=60_000_000_000, bytes_accessed=4_000_000, transcendentals=0
        ),
        name="front",
    )(x, cot, vpack, gate, mix, down, seg, sid, pw_re, pw_im, kr, ki, wide)


BOTH = ("seq", "wt")
norm_epsilon = 1e-05


def gelu_tanh(pre_act):
    return jax.nn.gelu(pre_act, approximate=True)


def layer_norm(token_rows, gain_vec, bias_vec):
    row_mean = jnp.mean(token_rows, axis=-1, keepdims=True)
    centered = token_rows - row_mean
    spread = jnp.mean(centered * centered, axis=-1, keepdims=True)
    return centered * lax.rsqrt(spread + norm_epsilon) * gain_vec + bias_vec


def doc_segments(doc_lengths, seq_length):
    docs = doc_lengths.shape[1]
    upto = jnp.arange(docs)[:, None] >= jnp.arange(docs)[None, :]
    ends = jnp.sum(jnp.where(upto[None], doc_lengths[:, None, :], 0), axis=-1)
    places = jnp.arange(seq_length, dtype=jnp.int32)
    passed = (places[None, None, :] >= ends[:, :, None]).astype(jnp.int32)
    return jnp.sum(passed, axis=1, dtype=jnp.int32)


def after(x, first):
    return lax.optimization_barrier((x, first))[0]


class Ring:
    def __init__(self, axis, inner):
        self.axis, self.size = axis, lax.axis_size(axis)
        self.inner = min(inner, self.size)
        self.outer = self.size // self.inner
        self.me = lax.axis_index(axis)
        self.o, self.i = self.me // self.inner, self.me % self.inner

    def shift(self, x, k, j):
        to = [
            ((p // self.inner + k) % self.outer) * self.inner + (p % self.inner + j) % self.inner
            for p in range(self.size)
        ]
        return lax.ppermute(x, self.axis, list(enumerate(to)))

    def parts(self, x, joined):
        far = [(0, x)] + [(k, self.shift(x, k, 0)) for k in range(1, self.outer)]
        back = lambda k, j: ((self.o - k) % self.outer) * self.inner + (self.i - j) % self.inner
        out = [(back(k, 0), part) for k, part in far]
        for j in range(1, self.inner):
            if joined:
                near = self.shift(jnp.stack([part for _, part in far]), 0, j)
                out += [(back(k, j), near[k]) for k in range(self.outer)]
            else:
                out += [(back(k, j), self.shift(part, 0, j)) for k, part in far]
        return out

    def gather(self, x, joined=True):
        return self.place(self.parts(x, joined))

    def place(self, parts, axis=0):
        first = parts[0][1]
        out = jnp.zeros(first.shape[:axis] + (self.size,) + first.shape[axis:], first.dtype)
        for at, part in parts:
            out = lax.dynamic_update_index_in_dim(out, part, at, axis)
        return out

    def exchange(self, x):
        parts = []
        for k in range(self.outer):
            for j in range(self.inner):
                to = ((self.o + k) % self.outer) * self.inner + (self.i + j) % self.inner
                back = ((self.o - k) % self.outer) * self.inner + (self.i - j) % self.inner
                block = lax.dynamic_index_in_dim(x, to, 0, keepdims=False)
                parts.append((back, block if k == j == 0 else self.shift(block, k, j)))
        return self.place(parts)

    def scatter_sum(self, x):
        wide, narrow = jnp.float32, jnp.bfloat16
        x = x.astype(narrow).reshape((self.outer, self.inner) + x.shape[1:])
        pick = lambda j: lax.dynamic_index_in_dim(x, (self.i + j) % self.inner, 1, keepdims=False)
        held = pick(0).astype(wide)
        for j in range(1, self.inner):
            held = held + self.shift(pick(j), 0, j).astype(wide)
        low = held.astype(narrow)
        take = lambda a, k: lax.dynamic_index_in_dim(a, (self.o + k) % self.outer, 0, keepdims=False)
        total = take(held, 0)
        for k in range(1, self.outer):
            total = total + self.shift(take(low, k), k, 0).astype(wide)
        return total


def on_device(
    inputs, cotangent, doc_lengths, norm_gain, norm_bias, gate_weight, value_weight, mix_weight,
    down_weight, decay_rate, frequency, kernel_re, kernel_im, log_step, skip_gain,
):
    seq_count, local_len, model_width = inputs.shape
    row_count = seq_count * local_len
    n_seq, n_wt = lax.axis_size("seq"), lax.axis_size("wt")
    seq, wt = Ring("seq", 2 if n_seq <= 8 else 8), Ring("wt", 2)
    length = local_len * n_seq
    docs = doc_lengths.shape[1]
    n_lag = length // 2 // LANES
    blocks = length // LANES
    width = value_weight.shape[1]
    d_rows = value_weight.shape[0]
    h_rows = mix_weight.shape[0]
    f_rows = down_weight.shape[0]
    gate_width = gate_weight.shape[1]
    f_part = gate_width // n_wt
    low = jnp.bfloat16

    lengths_all = wt.gather(doc_lengths).reshape(n_wt * seq_count, docs)
    flat = seq.me * n_wt + wt.me
    norm_rows = jnp.zeros((16, width), low)
    norm_rows = lax.dynamic_update_slice(
        norm_rows, jnp.stack([norm_gain, norm_bias]), (0, flat * d_rows % LANES)
    )
    vpack = jnp.concatenate([value_weight, norm_rows], axis=0)

    own_channels = width // (n_seq * n_wt)

    def own(x):
        return lax.dynamic_slice_in_dim(x, wt.me * own_channels, own_channels, 0)

    rate, freq, kr, ki = own(decay_rate), own(frequency), own(kernel_re), own(kernel_im)
    step, skip = own(log_step), own(skip_gain)
    dt, bits, pw_re, pw_im = table_inputs(rate, freq, step, n_lag)
    seg, sid, per = segment_tables(doc_segments(lengths_all, length), docs)

    token_rows = inputs.reshape(row_count, model_width)
    cot_rows = cotangent.reshape(row_count, model_width)
    by_device = (n_seq * n_wt, own_channels, row_count)
    pair, gate_own, mix_own, down_own, mixed, value_ch, lags, value_pre, value_full, norm_vec = front_call(
        token_rows, cot_rows, vpack, gate_weight, mix_weight, down_weight, seg, sid, per, seq_count,
        docs, n_lag, bits, seq.inner, pw_re, pw_im, kr, ki, skip,
    )
    token_rows = token_rows.astype(jnp.float32)
    normed_all = pair[:, 0].reshape(n_wt * row_count, model_width)
    cot_all = pair[:, 1].reshape(n_wt * row_count, model_width)
    gate_own = gate_own.reshape(model_width, f_part)
    mix_own = mix_own.reshape(width, f_part)
    down_own = down_own.reshape(f_part, model_width)
    mixed = mixed.reshape(n_wt, width, row_count)
    mixed = mixed.transpose(1, 0, 2).reshape(width, n_wt * row_count)

    gate_pre = dot(normed_all, gate_own)
    gate_act, gate_back = jax.vjp(gelu_tanh, gate_pre)
    product_grad = dot(cot_all, down_own, 1, 1)
    expand = dot(mixed, mix_own, 0, 0)
    expand_low = (product_grad * gate_act).astype(low)
    mixed_grad = dot(mix_own, expand_low, 1, 1).astype(low)
    mixed_grad = mixed_grad.reshape(width, n_wt, row_count).transpose(1, 0, 2)
    mixed_grad = wt.scatter_sum(mixed_grad).astype(low)
    product_low = (expand * gate_act).astype(low)
    gate_pre_low = gate_back(product_grad * expand)[0].astype(low)

    down_grad = dot(product_low, cot_all, 0, 0).astype(low).reshape(n_seq, f_rows, model_width)
    mix_grad = dot(mixed, expand_low).astype(low).reshape(n_seq, n_wt * h_rows, f_part)
    gate_grad = dot(normed_all, gate_pre_low, 0, 0).astype(low).reshape(n_seq, n_wt * d_rows, f_part)
    down_piece = seq.scatter_sum(down_grad)
    mix_band = seq.scatter_sum(mix_grad)
    gate_band = seq.scatter_sum(gate_grad)

    result = dot(product_low, down_own).astype(low)
    gate_side = dot(gate_pre_low, gate_own, 1, 1).astype(low)
    tok = lambda x: x.reshape(n_wt, row_count, model_width)
    token_sums = wt.scatter_sum(jnp.stack([tok(result), tok(gate_side)], axis=1))
    outputs = (token_rows + token_sums[0]).astype(low).reshape(inputs.shape)

    value_grad_tok, packed = mix_backward(
        mixed_grad.reshape(by_device), value_ch, seg, sid, per, seq_count, docs, n_lag, bits, pw_re,
        pw_im, kr, ki, rate, freq, dt, skip, lags,
    )
    value_grad_tok = value_grad_tok.reshape(width, row_count).astype(jnp.float32)
    value_back = jax.vjp(gelu_tanh, value_pre.T)[1]
    value_pre_low = value_back(value_grad_tok)[0].astype(low)
    norm_back = jax.vjp(layer_norm, token_rows, norm_vec[0], norm_vec[1])[1]
    states = rate.shape[1]
    packed = packed.reshape(n_wt * own_channels, -1)
    mixer_grads = [packed[:, i * states : (i + 1) * states] for i in range(4)]
    mixer_grads += [packed[:, 4 * states], packed[:, 4 * states + LANES]]

    value_turn = wt.exchange(value_pre_low.reshape(n_wt, width // n_wt, row_count))
    value_turn = value_turn.transpose(1, 0, 2).reshape(width // n_wt, n_wt * row_count)
    value_grad = dot(normed_all, value_turn, 0, 1).reshape(n_seq, n_wt * d_rows, width // n_wt)
    value_band = seq.scatter_sum(value_grad)

    normed_grad = token_sums[1] + dot(value_pre_low, value_full, 0, 1)
    input_rows, gain_grad, bias_grad = norm_back(normed_grad)
    input_grad = (cot_rows.astype(jnp.float32) + input_rows).reshape(inputs.shape)
    vectors = jnp.stack([gain_grad, bias_grad]).astype(low).reshape(2, n_seq * n_wt, d_rows)
    vectors = lax.all_to_all(
        vectors.transpose(1, 0, 2), BOTH, split_axis=0, concat_axis=0, tiled=True
    )
    vectors = jnp.sum(vectors.astype(jnp.float32), axis=0)

    last = [
        gate_band.reshape(n_wt, d_rows, f_part),
        mix_band.reshape(n_wt, h_rows, f_part),
        value_band.reshape(n_wt, d_rows, width // n_wt),
    ]
    heads = wt.exchange(jnp.concatenate(last[:2], axis=1).astype(low)).astype(jnp.float32)
    tails = wt.exchange(last[2].astype(low)).astype(jnp.float32)

    def spread(x):
        rows = x.shape[1]
        x = x.reshape(n_wt, rows, n_seq, f_rows).transpose(1, 2, 0, 3)
        return x.reshape(rows, gate_width)

    value_piece = tails.transpose(1, 0, 2).reshape(d_rows, width)
    return (
        outputs, input_grad, vectors[0], vectors[1], spread(heads[:, :d_rows]), value_piece,
        spread(heads[:, d_rows:]), down_piece, *mixer_grads,
    )


def solution(mesh):
    in_specs = (
        P("wt", "seq", None),
        P("wt", "seq", None),
        P("wt", None),
        P(("seq", "wt")),
        P(("seq", "wt")),
        P(("seq", "wt"), None),
        P(("seq", "wt"), None),
        P(("seq", "wt"), None),
        P(("seq", "wt"), None),
        P("seq", None),
        P("seq", None),
        P("seq", None),
        P("seq", None),
        P("seq"),
        P("seq"),
    )
    out_specs = (
        P("wt", "seq", None),
        P("wt", "seq", None),
        P(("seq", "wt")),
        P(("seq", "wt")),
        P(("seq", "wt"), None),
        P(("seq", "wt"), None),
        P(("seq", "wt"), None),
        P(("seq", "wt"), None),
        P("seq", None),
        P("seq", None),
        P("seq", None),
        P("seq", None),
        P("seq"),
        P("seq"),
    )
    return jax.shard_map(
        on_device, mesh=mesh, in_specs=in_specs, out_specs=out_specs, check_vma=False
    )
```

```python
import functools

import jax
import jax.numpy as jnp
from jax import lax
from jax.experimental import pallas as pl
from jax.experimental.pallas import tpu as pltpu
from jax.sharding import PartitionSpec as P

LANES = 128
PAD = 16


MESH = pl.DeviceIdType.MESH


def place_of(flat, n_wt):
    return (flat // n_wt, flat % n_wt)


def meet(flat, n, n_wt):
    barrier = pltpu.get_barrier_semaphore()

    def tell(r, unused):
        pl.semaphore_signal(
            barrier, inc=1, device_id=place_of((flat + r) % n, n_wt), device_id_type=MESH
        )
        return unused

    lax.fori_loop(1, n, tell, 0)
    pl.semaphore_wait(barrier, n - 1)


def swap_copy(source, target, send_sem, recv_sem, slot, peer, n_wt):
    return pltpu.make_async_remote_copy(
        src_ref=source, dst_ref=target, send_sem=send_sem.at[slot], recv_sem=recv_sem.at[slot],
        device_id=place_of(peer, n_wt), device_id_type=MESH,
    )


def swap_start(send, target_of, send_sem, recv_sem, flat, n, n_wt):
    def one(r, unused):
        peer = (flat + r) % n
        swap_copy(send.at[peer], target_of(peer, flat), send_sem, recv_sem, r, peer, n_wt).start()
        return unused

    lax.fori_loop(1, n, one, 0)


def swap_wait(send, target_of, send_sem, recv_sem, flat, n, n_wt):
    def one(r, unused):
        source = (flat + n - r) % n
        swap_copy(
            send.at[source], target_of(flat, source), send_sem, recv_sem, r, source, n_wt
        ).wait()
        return unused

    lax.fori_loop(1, n, one, 0)


def rows_to_table(got, table, n_seq, n_wt, seq_count, local_blocks, per, channels):
    for s in range(n_seq):
        for w in range(n_wt):
            for k in range(seq_count):
                for b in range(local_blocks):
                    row = (w * seq_count + k) * per + s * local_blocks + b
                    lanes = pl.ds((k * local_blocks + b) * LANES, LANES)
                    table[pl.ds(row * channels, channels), :] = got[
                        s * n_wt + w, :, lanes
                    ].astype(jnp.float32)


def table_to_rows(table, send, n_seq, n_wt, seq_count, local_blocks, per, channels):
    for s in range(n_seq):
        for w in range(n_wt):
            for k in range(seq_count):
                for b in range(local_blocks):
                    row = (w * seq_count + k) * per + s * local_blocks + b
                    lanes = pl.ds((k * local_blocks + b) * LANES, LANES)
                    send[s * n_wt + w, :, lanes] = table[
                        pl.ds(row * channels, channels), :
                    ].astype(jnp.bfloat16)


def clear_unused(table, seqs, blocks, per, channels):
    for s in range(seqs):
        table[pl.ds((s * per + blocks) * channels, (per - blocks) * channels), :] = jnp.zeros(
            ((per - blocks) * channels, LANES), jnp.float32
        )


def share_over_wt(ref, s_me, w_me, n_wt, send_sem, recv_sem):
    inner = 2
    outer = n_wt // inner
    o, i = w_me // inner, w_me % inner
    other = (s_me, o * inner + 1 - i)

    def copy(block, slot, to):
        return pltpu.make_async_remote_copy(
            src_ref=ref.at[block], dst_ref=ref.at[block], send_sem=send_sem.at[slot],
            recv_sem=recv_sem.at[slot], device_id=to, device_id_type=MESH,
        )

    far = [copy(w_me, k, (s_me, ((o + k) % outer) * inner + i)) for k in range(1, outer)]
    near = [copy(w_me, outer, other)]
    for c in far + near:
        c.start()
    for k in range(1, outer):
        block = ((o + outer - k) % outer) * inner + i
        far[k - 1].wait_recv()
        c = copy(block, outer + k, other)
        c.start()
        near.append(c)
    for c in far:
        c.wait_send()
    for c in near:
        c.wait()


def cmul(ar, ai, br, bi):
    return ar * br - ai * bi, ar * bi + ai * br


def power_rows(pw_re, pw_im, c, first, count, rows):
    width = pw_re.shape[2]
    place = lax.broadcasted_iota(jnp.int32, (rows, width), 0)
    re = jnp.ones((rows, width), jnp.float32)
    im = jnp.zeros((rows, width), jnp.float32)
    for bit in range(count):
        on = (place & (1 << bit)) != 0
        fr = jnp.where(on, pw_re[c, pl.ds(first + bit, 1), :], 1.0)
        fi = jnp.where(on, pw_im[c, pl.ds(first + bit, 1), :], 0.0)
        re, im = cmul(re, im, fr, fi)
    return re, im


def fill_lane_powers(pw_re, pw_im, c, tab_re, tab_im, extra):
    re, im = power_rows(pw_re, pw_im, c, 0, 3, 8)
    if extra:
        re, im = cmul(re, im, pw_re[c, pl.ds(0, 1), :], pw_im[c, pl.ds(0, 1), :])
    tab_re[0:8, :] = re
    tab_im[0:8, :] = im
    have, bit = 8, 3
    while have < LANES:
        re, im = cmul(
            tab_re[0:have, :],
            tab_im[0:have, :],
            pw_re[c, pl.ds(bit, 1), :],
            pw_im[c, pl.ds(bit, 1), :],
        )
        tab_re[have : 2 * have, :] = re
        tab_im[have : 2 * have, :] = im
        have, bit = 2 * have, bit + 1


def to_pieces(seg, val, rows, docs):
    total = jnp.zeros((rows, LANES), jnp.float32)
    for j in range(docs):
        at = pl.ds(PAD - j, rows)
        total = total + jnp.where(seg[at, :] == j, val[at, :], 0.0)
    return total


def from_pieces(seg, piece, rows, docs):
    own = seg[pl.ds(PAD, rows), :]
    total = jnp.zeros((rows, LANES), jnp.float32)
    for j in range(docs):
        total = total + jnp.where(own == j, piece[pl.ds(j, rows), :], 0.0)
    return total


def toeplitz(lags, d, last, lower, before):
    if d < last:
        row = jnp.broadcast_to(lags[d : d + 1, :], (LANES, LANES))
        here = pltpu.roll(row, 0, 1, stride=1, stride_axis=0)
    else:
        here = jnp.zeros((LANES, LANES), jnp.float32)
    return jnp.where(lower, here, before).astype(jnp.bfloat16), here


def dot(a, b, ca=1, cb=0):
    return lax.dot_general(a, b, (((ca,), (cb,)), ((), ())), preferred_element_type=jnp.float32)


def vmem(*shape):
    return pltpu.VMEM(shape, jnp.float32)


def table_inputs(decay_rate, frequency, log_step, n_lag):
    bits = (n_lag - 1).bit_length()
    dt = jnp.exp(log_step)[:, None]
    powers = jnp.array([float(1 << b) for b in range(7 + bits)] + [0.0] * (9 - bits), jnp.float32)
    powers = powers[None, :, None]
    mag = jnp.exp(-(decay_rate * dt)[:, None, :] * powers)
    phase = (frequency * dt)[:, None, :] * powers
    return dt, bits, mag * jnp.cos(phase), mag * jnp.sin(phase)


def segment_tables(segment, docs):
    seqs, length = segment.shape
    blocks = length // LANES
    per = -(-(blocks + docs) // 8) * 8
    seg = segment.reshape(seqs, blocks, LANES)
    piece = seg + jnp.arange(blocks, dtype=jnp.int32)[None, :, None]
    hit = piece.reshape(seqs, 1, length) == jnp.arange(per, dtype=jnp.int32)[None, :, None]
    sid = jnp.max(jnp.where(hit, segment[:, None, :], -1), axis=-1)
    sid = jnp.where(sid >= 0, sid + docs * jnp.arange(seqs, dtype=jnp.int32)[:, None], -1)
    seg = jnp.pad(seg, ((0, 0), (0, per - blocks), (0, 0)), constant_values=-1)
    seg = jnp.pad(seg.reshape(seqs * per, LANES), ((PAD, PAD), (0, 0)), constant_values=-1)
    sid = jnp.pad(sid.reshape(seqs * per), ((PAD, PAD),), constant_values=-2)
    return seg, jnp.broadcast_to(sid[:, None], (seqs * per + 2 * PAD, LANES)), per


class Wires:
    def __init__(self, send_sem, recv_sem):
        self.send_sem, self.recv_sem, self.used, self.open = send_sem, recv_sem, 0, []

    def send(self, source, target, to):
        c = pltpu.make_async_remote_copy(
            src_ref=source, dst_ref=target, send_sem=self.send_sem.at[self.used],
            recv_sem=self.recv_sem.at[self.used], device_id=to, device_id_type=MESH,
        )
        self.used += 1
        self.open.append(c)
        c.start()
        return c

    def sent(self):
        for c in self.open:
            c.wait_send()
        self.open = []


def rms(x32):
    mean = jnp.mean(x32, axis=-1, keepdims=True)
    centered = x32 - mean
    spread = jnp.mean(centered * centered, axis=-1, keepdims=True)
    return centered * lax.rsqrt(spread + norm_epsilon)


def regroup(x, n_seq, n_wt, width):
    cut = lambda s, w: x[:, (s * n_wt + w) * width : (s * n_wt + w + 1) * width]
    return [jnp.concatenate([cut(s, w) for s in range(n_seq)], axis=1) for w in range(n_wt)]


def front_wires(n_seq, n_wt, inner):
    outer = n_seq // inner
    value = (n_seq - 1) + n_seq * (n_wt // 2 - 1) + n_seq * (n_wt // 2)
    weights = 2 * (n_wt - 1) + 3 * (outer - 1) + 3 * (inner - 1) * outer
    tokens = 2 * (n_wt // 2 - 1) + 2 * (n_wt // 2)
    mixed = (n_wt // 2 - 1) + n_wt // 2
    return value + weights + tokens + mixed


def front_kernel(
    n_lag, docs, bits, seq_count, per, inner_seq,
    x_ref, cot_ref, vpack_ref, gate_in, mix_in, down_in, seg_ref, sid_ref, pw_re, pw_im, kr_ref,
    ki_ref, skip_ref,
    pair, gate_out, mix_out, down_out, mixed_ref, v_ref, lag_ref, pre_ref, value_full, norm_out,
    vf, vp, yp, tab_re, tab_im, table, got, back, front, xhat, act_send, gate_cut, mix_cut,
    in_send, in_recv, out_send, out_recv, wire_send, wire_recv, local_sem,
):
    channels, rows, _ = v_ref.shape
    n_seq, n_wt = lax.axis_size("seq"), lax.axis_size("wt")
    n = n_seq * n_wt
    s_me, w_me = lax.axis_index("seq"), lax.axis_index("wt")
    flat = s_me * n_wt + w_me
    row_count, model_width = x_ref.shape
    width = pre_ref.shape[1]
    d_rows, h_rows, f_rows = gate_in.shape[0], mix_in.shape[0], down_in.shape[0]
    local_blocks = row_count // LANES // seq_count
    shape = (n_seq, n_wt, seq_count, local_blocks, per, channels)
    outer_wt = n_wt // 2
    o, i = w_me // 2, w_me % 2
    sibling = o * 2 + 1 - i
    far_to = lambda k: ((o + k) % outer_wt) * 2 + i
    far_from = lambda k: ((o + outer_wt - k) % outer_wt) * 2 + i
    outer_seq = n_seq // inner_seq
    so, si = s_me // inner_seq, s_me % inner_seq
    step_to = lambda k, j: ((so + k) % outer_seq) * inner_seq + (si + j) % inner_seq
    step_from = lambda k: ((so + outer_seq - k) % outer_seq) * inner_seq + si
    wires = Wires(wire_send, wire_recv)

    meet(flat, n, n_wt)

    front[s_me, w_me] = vpack_ref[...]
    first = []
    for k in range(1, n_seq):
        to = ((s_me + k) % n_seq, w_me)
        first.append(wires.send(front.at[s_me, w_me], front.at[s_me, w_me], to))

    second, third = [], []

    def spread_value(s):
        block = front.at[s, w_me]
        for k in range(1, outer_wt):
            second.append((s, k, wires.send(block, block, (s_me, far_to(k)))))
        third.append(wires.send(block, block, (s_me, sibling)))

    spread_value(s_me)

    for ref, cut in ((gate_in, gate_cut), (mix_in, mix_cut)):
        whole = ref[...].astype(jnp.float32)
        for w, part in enumerate(regroup(whole, n_seq, n_wt, f_rows)):
            cut[w] = part.astype(jnp.bfloat16)
    down_out[s_me] = down_in[...]
    gate_out[s_me, w_me] = gate_cut[w_me]
    mix_out[s_me, w_me] = mix_cut[w_me]

    chunk = min(32, row_count)

    def normalise(r, unused):
        at = pl.ds(r * chunk, chunk)
        xhat[at, :] = rms(x_ref[at, :].astype(jnp.float32))
        return unused

    lax.fori_loop(0, row_count // chunk, normalise, 0)
    pair[w_me, 1] = cot_ref[...]

    for k in range(1, n_seq):
        first[k - 1].wait_recv()
        spread_value((s_me + n_seq - k) % n_seq)

    turn = []
    for k in range(outer_wt):
        for j in range(2):
            if k or j:
                w = ((o + k) % outer_wt) * 2 + (i + j) % 2
                turn.append(wires.send(gate_cut.at[w], gate_out.at[s_me, w_me], (s_me, w)))
                turn.append(wires.send(mix_cut.at[w], mix_out.at[s_me, w_me], (s_me, w)))
    late = [wires.send(down_out.at[s_me], down_out.at[s_me], (step_to(k, 0), w_me)) for k in range(1, outer_seq)]
    near = [wires.send(down_out.at[s_me], down_out.at[s_me], (step_to(0, j), w_me)) for j in range(1, inner_seq)]

    for s, k, c in second:
        c.wait_recv()
        block = front.at[s, far_from(k)]
        third.append(wires.send(block, block, (s_me, sibling)))
    for c in third:
        c.wait_recv()

    for f in range(n):
        value_full[pl.ds(f * d_rows, d_rows), :] = front[f // n_wt, f % n_wt, 0:d_rows, :]
    share = LANES // d_rows
    for b in range(model_width // LANES):
        total = jnp.zeros((2, LANES), jnp.float32)
        for f in range(b * share, (b + 1) * share):
            total = total + front[f // n_wt, f % n_wt, d_rows : d_rows + 2, 0:LANES].astype(jnp.float32)
        norm_out[:, pl.ds(b * LANES, LANES)] = total

    def project(r, unused):
        at = pl.ds(pl.multiple_of(r * LANES, LANES), LANES)
        normed = (xhat[at, :] * norm_out[0:1, :] + norm_out[1:2, :]).astype(jnp.bfloat16)
        pair[w_me, 0, at, :] = normed
        pre = dot(normed, value_full[...])
        pre_ref[at, :] = pre
        turned = jnp.transpose(gelu_tanh(pre))
        for p in range(n):
            act_send[p, :, at] = turned[p * channels : (p + 1) * channels, :].astype(jnp.bfloat16)
        return unused

    lax.fori_loop(0, row_count // LANES, project, 0)
    into = lambda peer, slot: got.at[slot]
    swap_start(act_send, into, in_send, in_recv, flat, n, n_wt)
    got[flat] = act_send[flat]

    for c in turn:
        c.wait_recv()
    for k in range(1, outer_seq):
        to = (step_to(k, 0), w_me)
        late.append(wires.send(gate_out.at[s_me], gate_out.at[s_me], to))
        late.append(wires.send(mix_out.at[s_me], mix_out.at[s_me], to))
    for j in range(1, inner_seq):
        to = (step_to(0, j), w_me)
        near.append(wires.send(gate_out.at[s_me], gate_out.at[s_me], to))
        near.append(wires.send(mix_out.at[s_me], mix_out.at[s_me], to))

    clear_unused(table, n_wt * seq_count, n_seq * local_blocks, per, channels)
    zero_pad = jnp.zeros((PAD, LANES), jnp.float32)
    vf[0:PAD, :] = zero_pad
    vp[0:PAD, :] = zero_pad
    yp[pl.ds(rows, PAD), :] = zero_pad
    lower = lax.broadcasted_iota(jnp.int32, (LANES, LANES), 1) >= lax.broadcasted_iota(
        jnp.int32, (LANES, LANES), 0
    )
    swap_wait(act_send, into, in_send, in_recv, flat, n, n_wt)

    far_pair = []
    for at in range(2):
        block = pair.at[w_me, at]
        for k in range(1, outer_wt):
            far_pair.append((k, at, wires.send(block, block, (s_me, far_to(k)))))
    near_pair = [wires.send(pair.at[w_me, at], pair.at[w_me, at], (s_me, sibling)) for at in range(2)]

    rows_to_table(got, table, *shape)

    def channel(c, unused):
        fill_lane_powers(pw_re, pw_im, c, tab_re, tab_im, 0)
        dr, di = power_rows(pw_re, pw_im, c, 7, bits, n_lag)
        ar, ai = cmul(dr, di, kr_ref[pl.ds(c, 1), :], ki_ref[pl.ds(c, 1), :])
        lags = dot(ar.astype(jnp.bfloat16), tab_re[...].astype(jnp.bfloat16), 1, 1) - dot(
            ai.astype(jnp.bfloat16), tab_im[...].astype(jnp.bfloat16), 1, 1
        )
        lag_ref[c] = lags
        val = table[pl.ds(c, rows, stride=channels), :]
        v_ref[c] = val.astype(jnp.bfloat16)
        vf[pl.ds(PAD, rows), :] = val
        vp[pl.ds(PAD, rows), :] = to_pieces(seg_ref, vf, rows, docs)
        sid = sid_ref[pl.ds(PAD, rows), :]
        before = jnp.zeros((LANES, LANES), jnp.float32)
        total = jnp.zeros((rows, LANES), jnp.float32)
        for d in range(n_lag + 1):
            at = pl.ds(PAD - d, rows)
            x = jnp.where(sid_ref[at, :] == sid, vp[at, :], 0.0).astype(jnp.bfloat16)
            t, before = toeplitz(lags, d, n_lag, lower, before)
            total = total + dot(x, t)
        yp[0:rows, :] = total
        out = from_pieces(seg_ref, yp, rows, docs) + skip_ref[pl.ds(c, 1), :] * val
        table[pl.ds(c, rows, stride=channels), :] = out
        return unused

    def pass_on(at, k):
        late[at].wait_recv()
        ref = (down_out, gate_out, mix_out)[0 if at < outer_seq - 1 else 1 + (at - outer_seq + 1) % 2]
        block = ref.at[step_from(k)]
        for j in range(1, inner_seq):
            near.append(wires.send(block, block, (step_to(0, j), w_me)))

    half = channels // 2
    lax.fori_loop(0, half, channel, 0)
    for k in range(1, outer_seq):
        pass_on(k - 1, k)
    lax.fori_loop(half, channels, channel, 0)
    table_to_rows(table, back, *shape)
    home = lambda peer, slot: mixed_ref.at[peer % n_wt, slot]
    swap_start(back, home, out_send, out_recv, flat, n, n_wt)
    own = pltpu.make_async_copy(back.at[flat], mixed_ref.at[w_me, flat], local_sem)
    own.start()
    first_two = outer_seq - 1
    for at in range(2 * (outer_seq - 1)):
        pass_on(first_two + at, at // 2 + 1)
    own.wait()
    swap_wait(back, home, out_send, out_recv, flat, n, n_wt)

    block = mixed_ref.at[w_me]
    far_mixed = [wires.send(block, block, (s_me, far_to(k))) for k in range(1, outer_wt)]
    ends = [wires.send(block, block, (s_me, sibling))]
    for k, at, c in far_pair:
        c.wait_recv()
        block = pair.at[far_from(k), at]
        near_pair.append(wires.send(block, block, (s_me, sibling)))
    for k in range(1, outer_wt):
        far_mixed[k - 1].wait_recv()
        block = mixed_ref.at[far_from(k)]
        ends.append(wires.send(block, block, (s_me, sibling)))
    for c in near + near_pair + ends:
        c.wait_recv()
    wires.sent()


def front_call(
    x, cot, vpack, gate, mix, down, seg, sid, per, seq_count, docs, n_lag, bits, inner_seq, pw_re,
    pw_im, kr, ki, skip,
):
    n_seq, n_wt = lax.axis_size("seq"), lax.axis_size("wt")
    n = n_seq * n_wt
    channels, states = kr.shape
    rows = seg.shape[0] - 2 * PAD
    local, model_width = x.shape
    width = vpack.shape[1]
    f_part = gate.shape[1] // n_wt
    wide = jnp.broadcast_to(skip[:, None], (channels, LANES))
    low = jnp.bfloat16
    wires = front_wires(n_seq, n_wt, inner_seq)
    out = jax.ShapeDtypeStruct
    return pl.pallas_call(
        functools.partial(front_kernel, n_lag, docs, bits, seq_count, per, inner_seq),
        out_shape=(
            out((n_wt, 2, local, model_width), low),
            out((n_seq, n_wt) + (gate.shape[0], f_part), low),
            out((n_seq, n_wt) + (mix.shape[0], f_part), low),
            out((n_seq,) + down.shape, low),
            out((n_wt, n, channels, local), low),
            out((channels, rows, LANES), low),
            out((channels, n_lag, LANES), jnp.float32),
            out((local, width), jnp.float32),
            out((model_width, width), low),
            out((2, model_width), jnp.float32),
        ),
        in_specs=[pl.BlockSpec(memory_space=pltpu.VMEM)] * 13,
        out_specs=(pl.BlockSpec(memory_space=pltpu.VMEM),) * 10,
        scratch_shapes=[vmem(PAD + rows, LANES)] * 3
        + [vmem(LANES, states), vmem(LANES, states), vmem(rows * channels, LANES)]
        + [pltpu.VMEM((n, channels, local), low)] * 2
        + [pltpu.VMEM((n_seq, n_wt) + vpack.shape, low), vmem(local, model_width)]
        + [pltpu.VMEM((n, channels, local), low)]
        + [pltpu.VMEM((n_wt, gate.shape[0], f_part), low), pltpu.VMEM((n_wt, mix.shape[0], f_part), low)]
        + [pltpu.SemaphoreType.DMA((n,))] * 4
        + [pltpu.SemaphoreType.DMA((wires,))] * 2
        + [pltpu.SemaphoreType.DMA],
        compiler_params=pltpu.CompilerParams(
            vmem_limit_bytes=56 << 20, collective_id=1, has_side_effects=True
        ),
        cost_estimate=pl.CostEstimate(
            flops=60_000_000_000, bytes_accessed=4_000_000, transcendentals=0
        ),
        name="front",
    )(x, cot, vpack, gate, mix, down, seg, sid, pw_re, pw_im, kr, ki, wide)


GELU_A = 0.7978845608028654
GELU_B = 0.044715


def gelu_pair(v):
    square = v * v
    t = jnp.tanh(GELU_A * (v + GELU_B * v * square))
    half = 0.5 * (1.0 + t)
    slope = half + 0.5 * v * (1.0 - t * t) * (GELU_A * (1.0 + 3.0 * GELU_B * square))
    return v * half, slope


def back_wires(n_seq, n_wt, inner):
    outer = n_seq // inner
    over_seq = 4 * ((inner - 1) + (outer - 1))
    over_wt = 2 * (1 + n_wt // 2 - 1)
    return over_seq + over_wt + 3 * (n_wt - 1) + (n_wt // 2 - 1) + n_wt // 2 + n_wt - 1


class SeqSum:
    def __init__(self, wires, send, near_in, far_in, so, si, outer, inner, s_to):
        self.wires, self.send, self.near_in, self.far_in = wires, send, near_in, far_in
        self.so, self.outer, self.inner, self.s_to = so, outer, inner, s_to

    def begin(self):
        self.near = [
            self.wires.send(self.send.at[j], self.near_in.at[j - 1], self.s_to(0, j))
            for j in range(1, self.inner)
        ]

    def turn(self):
        for c in self.near:
            c.wait_recv()
        for z in range(self.outer):
            total = self.send[0, z].astype(jnp.float32)
            for j in range(1, self.inner):
                total = total + self.near_in[j - 1, z].astype(jnp.float32)
            self.send[0, z] = total.astype(jnp.bfloat16)
        self.far = []
        for k in range(1, self.outer):
            z = (self.so + k) % self.outer
            self.far.append(
                self.wires.send(self.send.at[0, z], self.far_in.at[k - 1], self.s_to(k, 0))
            )

    def end(self):
        for c in self.far:
            c.wait_recv()
        total = self.send[0, self.so].astype(jnp.float32)
        for k in range(1, self.outer):
            total = total + self.far_in[k - 1].astype(jnp.float32)
        return total


def back_kernel(
    n_lag, docs, bits, seq_count, per, inner_seq,
    pair, gate_w, mix_w, down_w, mixed, v_ref, lag_ref, pre_ref, value_full, norm_vec, x_ref,
    seg_ref, sid_ref, pw_re, pw_im, kr_ref, ki_ref, rate_ref, freq_ref, dt_ref, skip_ref,
    out_ref, in_grad, gate_last, value_last, mix_last, down_out, norm_out, all_out,
    vf, gf, vp, gp, yp, tab_re, tab_im, table, got, back, dv_ref,
    product, expand_grad, gate_grad, mg, mg_in, mg_far, tok, tok_in, tok_far,
    down_flat, down_s, down_n, down_f, mix_s, mix_n, mix_f, gate_s, gate_n, gate_f,
    value_s, value_n, value_f, turned, value_cut, value_all, last_send, norm_last,
    in_send, in_recv, out_send, out_recv, wire_send, wire_recv, local_sem, *held,
):
    grads, thin = held[:4], held[4:]
    low, wide = jnp.bfloat16, jnp.float32
    channels, rows, _ = v_ref.shape
    states = kr_ref.shape[1]
    n_seq, n_wt = lax.axis_size("seq"), lax.axis_size("wt")
    n = n_seq * n_wt
    s_me, w_me = lax.axis_index("seq"), lax.axis_index("wt")
    flat = s_me * n_wt + w_me
    row_count, model_width = x_ref.shape
    width = mix_w.shape[0]
    f_part = gate_w.shape[1]
    f_rows = f_part // n_seq
    d_band, h_band, v_band = model_width // n_seq, width // n_seq, width // n_wt
    d_rows, h_rows = d_band // n_wt, h_band // n_wt
    local_blocks = row_count // LANES // seq_count
    shape = (n_seq, n_wt, seq_count, local_blocks, per, channels)
    outer_wt = n_wt // 2
    o, i = w_me // 2, w_me % 2
    sibling = (s_me, o * 2 + 1 - i)
    far_to = lambda k: (s_me, ((o + k) % outer_wt) * 2 + i)
    outer_seq = n_seq // inner_seq
    so, si = s_me // inner_seq, s_me % inner_seq
    s_to = lambda k, j: (((so + k) % outer_seq) * inner_seq + (si + j) % inner_seq, w_me)
    wires = Wires(wire_send, wire_recv)
    sums = lambda send, near_in, far_in: SeqSum(
        wires, send, near_in, far_in, so, si, outer_seq, inner_seq, s_to
    )
    down_sum, mix_sum = sums(down_s, down_n, down_f), sums(mix_s, mix_n, mix_f)
    gate_sum, value_sum = sums(gate_s, gate_n, gate_f), sums(value_s, value_n, value_f)

    meet(flat, n, n_wt)

    def tokens(t, unused):
        j, k = 1 - t // outer_wt, outer_wt - 1 - t % outer_wt
        w = ((o + k) % outer_wt) * 2 + (i + j) % 2
        at = pl.ds(pl.multiple_of(w * row_count, row_count), row_count)
        act, slope = gelu_pair(dot(pair[w, 0], gate_w[...]))
        from_out = dot(pair[w, 1], down_w[...], 1, 1)
        expand = dot(mixed[w], mix_w[...], 0, 0)
        product[at, :] = (expand * act).astype(low)
        gate_grad[at, :] = (from_out * expand * slope).astype(low)
        grad = (from_out * act).astype(low)
        expand_grad[at, :] = grad
        mg[j, k] = dot(mix_w[...], grad, 1, 1).astype(low)
        return unused

    lax.fori_loop(0, outer_wt, tokens, 0)
    near = wires.send(mg.at[1], mg_in, sibling)
    lax.fori_loop(outer_wt, n_wt, tokens, 0)
    near.wait_recv()
    far = []
    for k in range(1, outer_wt):
        mg[0, k] = (mg[0, k].astype(wide) + mg_in[k].astype(wide)).astype(low)
        far.append(wires.send(mg.at[0, k], mg_far.at[k - 1], far_to(k)))

    piece = min(256, f_part)
    every = n_wt * row_count

    def down_part(r, unused):
        at = pl.ds(pl.multiple_of(r * piece, piece), piece)
        cot = pair[:, 1].reshape(every, model_width)
        down_flat[at, :] = dot(product[:, at], cot, 0, 0)
        return unused

    lax.fori_loop(0, f_part // piece, down_part, 0)
    def bands(size):
        for s in range(n_seq):
            j = (s % inner_seq + inner_seq - si) % inner_seq
            yield j, s // inner_seq, slice(s * size, (s + 1) * size)

    for j, z, at in bands(f_rows):
        down_s[j, z] = down_flat[at, :].astype(low)
    down_sum.begin()
    for j, z, at in bands(h_band):
        total = dot(mixed[0, at, :], expand_grad[0:row_count, :])
        for w in range(1, n_wt):
            total = total + dot(
                mixed[w, at, :], expand_grad[w * row_count : (w + 1) * row_count, :]
            )
        mix_s[j, z] = total.astype(low)
    mix_sum.begin()

    total = mg[0, 0].astype(wide) + mg_in[0].astype(wide)
    for k in range(1, outer_wt):
        far[k - 1].wait_recv()
        total = total + mg_far[k - 1].astype(wide)
    turned[...] = total
    for p in range(n):
        back[p] = turned[p * channels : (p + 1) * channels, :].astype(low)
    into = lambda peer, slot: got.at[slot]
    swap_start(back, into, in_send, in_recv, flat, n, n_wt)
    got[flat] = back[flat]

    for j, z, at in bands(d_band):
        normed = pair[:, 0, :, at].reshape(every, d_band)
        gate_s[j, z] = dot(normed, gate_grad[...], 0, 0).astype(low)
    gate_sum.begin()

    def token_part(t, unused):
        j, k = 1 - t // outer_wt, outer_wt - 1 - t % outer_wt
        w = ((o + k) % outer_wt) * 2 + (i + j) % 2
        at = pl.ds(pl.multiple_of(w * row_count, row_count), row_count)
        tok[j, k, 0] = dot(product[at, :], down_w[...]).astype(low)
        tok[j, k, 1] = dot(gate_grad[at, :], gate_w[...], 1, 1).astype(low)
        return unused

    lax.fori_loop(0, outer_wt, token_part, 0)
    tok_near = wires.send(tok.at[1], tok_in, sibling)
    lax.fori_loop(outer_wt, n_wt, token_part, 0)

    zero_pad = jnp.zeros((PAD, LANES), wide)
    clear_unused(table, n_wt * seq_count, n_seq * local_blocks, per, channels)
    vf[0:PAD, :] = zero_pad
    gf[0:PAD, :] = zero_pad
    vp[0:PAD, :] = zero_pad
    gp[pl.ds(rows, PAD), :] = zero_pad
    yp[pl.ds(rows, PAD), :] = zero_pad
    tok_near.wait_recv()
    tok_sent = []
    for k in range(1, outer_wt):
        for a in range(2):
            tok[0, k, a] = (tok[0, k, a].astype(wide) + tok_in[k, a].astype(wide)).astype(low)
        tok_sent.append(wires.send(tok.at[0, k], tok_far.at[k - 1], far_to(k)))
    swap_wait(back, into, in_send, in_recv, flat, n, n_wt)
    down_sum.turn()
    rows_to_table(got, table, *shape)

    lane = lax.broadcasted_iota(jnp.int32, (LANES, LANES), 1)
    row = lax.broadcasted_iota(jnp.int32, (LANES, LANES), 0)
    lower = lane >= row
    wraps = lane + row >= LANES
    flip = (lane + row == LANES - 1).astype(jnp.bfloat16)
    lag_place = (
        lax.broadcasted_iota(jnp.int32, (n_lag, LANES), 0) * LANES
        + lax.broadcasted_iota(jnp.int32, (n_lag, LANES), 1)
        + 1
    ).astype(jnp.float32)

    def channel(c, unused):
        own = pl.ds(c, 1)
        val = v_ref[c].astype(jnp.float32)
        grad = table[pl.ds(c, rows, stride=channels), :]
        vf[pl.ds(PAD, rows), :] = val
        gf[pl.ds(PAD, rows), :] = grad
        skip_grad = jnp.sum(jnp.sum(val * grad, axis=0, keepdims=True), axis=1, keepdims=True)
        g_piece = to_pieces(seg_ref, gf, rows, docs)
        gp[0:rows, :] = g_piece
        v_piece = to_pieces(seg_ref, vf, rows, docs).astype(jnp.bfloat16)
        vp[pl.ds(PAD, rows), :] = dot(v_piece, flip)
        g_turned = jnp.transpose(g_piece).astype(jnp.bfloat16)
        sid = sid_ref[pl.ds(PAD, rows), :]
        lags = lag_ref[c]
        before = jnp.zeros((LANES, LANES), jnp.float32)
        total = jnp.zeros((rows, LANES), jnp.float32)
        earlier = None
        sums = []
        for d in range(n_lag + 1):
            ahead = pl.ds(PAD + d, rows)
            x = jnp.where(sid_ref[ahead, :] == sid, gp[pl.ds(d, rows), :], 0.0)
            t, before = toeplitz(lags, d, n_lag, lower, before)
            total = total + dot(x.astype(jnp.bfloat16), t, 1, 1)
            at = pl.ds(PAD - d, rows)
            back = jnp.where(sid_ref[at, :] == sid, vp[at, :], 0.0).astype(jnp.bfloat16)
            pairs = dot(g_turned, back)
            if d:
                skew = jnp.where(wraps, earlier, pairs)
                skew = pltpu.roll(skew, 0, 1, stride=1, stride_axis=0)
                sums.append(jnp.sum(skew, axis=0, keepdims=True))
            earlier = pairs
        yp[0:rows, :] = total
        out = from_pieces(seg_ref, yp, rows, docs) + skip_ref[own, :] * grad
        table[pl.ds(c, rows, stride=channels), :] = out
        lag_grad = jnp.concatenate(sums, axis=0)
        fill_lane_powers(pw_re, pw_im, c, tab_re, tab_im, 1)
        both = jnp.concatenate([lag_grad, lag_grad * lag_place], axis=0).astype(jnp.bfloat16)
        part_re = dot(both, tab_re[...].astype(jnp.bfloat16))
        part_im = dot(both, tab_im[...].astype(jnp.bfloat16))
        dr, di = power_rows(pw_re, pw_im, c, 7, bits, n_lag)
        gr, gi = cmul(dr, di, part_re[0:n_lag], part_im[0:n_lag])
        hr, hi = cmul(dr, di, part_re[n_lag:], part_im[n_lag:])
        gr, gi, hr, hi = (jnp.sum(a, axis=0, keepdims=True) for a in (gr, gi, hr, hi))
        kr, ki, dt = kr_ref[own, :], ki_ref[own, :], dt_ref[own, :]
        rate_grad = -dt * (kr * hr - ki * hi)
        freq_grad = -dt * (kr * hi + ki * hr)
        for at, row_out in enumerate((rate_grad, freq_grad, gr + skip_grad, -gi)):
            grads[at][own, :] = row_out
        step = jnp.sum(
            rate_grad * rate_ref[own, :] + freq_grad * freq_ref[own, :], axis=1, keepdims=True
        )
        for at, one in enumerate((step, skip_grad)):
            thin[at][own, :] = jnp.broadcast_to(one, (1, LANES))
        return unused

    half = channels // 2
    lax.fori_loop(0, half, channel, 0)
    mix_sum.turn()
    lax.fori_loop(half, channels, channel, 0)
    table_to_rows(table, back, *shape)
    home = lambda peer, slot: dv_ref.at[slot]
    swap_start(back, home, out_send, out_recv, flat, n, n_wt)
    own = pltpu.make_async_copy(back.at[flat], dv_ref.at[flat], local_sem)
    own.start()
    gate_sum.turn()
    for at in range(4):
        all_out[w_me, :, pl.ds(at * states, states)] = grads[at][...]
    for at in range(2):
        all_out[w_me, :, pl.ds(4 * states + at * LANES, LANES)] = thin[at][...]
    block = all_out.at[w_me]
    far_all = [wires.send(block, block, far_to(k)) for k in range(1, outer_wt)]
    near_all = [wires.send(block, block, sibling)]

    for c in tok_sent:
        c.wait_recv()
    result = x_ref[...].astype(wide) + tok[0, 0, 0].astype(wide) + tok_in[0, 0].astype(wide)
    for k in range(1, outer_wt):
        result = result + tok_far[k - 1, 0].astype(wide)
    out_ref[...] = result.astype(low)
    own.wait()
    swap_wait(back, home, out_send, out_recv, flat, n, n_wt)

    for p in range(n):
        turned[pl.ds(p * channels, channels), :] = dv_ref[p].astype(wide)
    value_grad = jnp.transpose(turned[...]) * gelu_pair(pre_ref[...])[1]
    value_low = value_grad.astype(low)
    for w in range(n_wt):
        value_cut[w] = value_low[:, w * v_band : (w + 1) * v_band]
    value_all[w_me] = value_cut[w_me]
    moves = []
    for k in range(outer_wt):
        for j in range(2):
            if k or j:
                w = ((o + k) % outer_wt) * 2 + (i + j) % 2
                moves.append(wires.send(value_cut.at[w], value_all.at[w_me], (s_me, w)))

    normed_grad = dot(value_low, value_full[...], 1, 1)
    normed_grad = normed_grad + tok[0, 0, 1].astype(wide) + tok_in[0, 1].astype(wide)
    for k in range(1, outer_wt):
        normed_grad = normed_grad + tok_far[k - 1, 1].astype(wide)
    x32 = x_ref[...].astype(wide)
    centered = x32 - jnp.mean(x32, axis=-1, keepdims=True)
    scale = lax.rsqrt(jnp.mean(centered * centered, axis=-1, keepdims=True) + norm_epsilon)
    xhat = centered * scale
    g = normed_grad * norm_vec[0:1, :]
    inner_grad = g - jnp.mean(g, axis=-1, keepdims=True)
    inner_grad = inner_grad - xhat * jnp.mean(g * xhat, axis=-1, keepdims=True)
    in_grad[...] = pair[w_me, 1].astype(wide) + inner_grad * scale
    vectors = jnp.concatenate(
        [
            jnp.sum(normed_grad * xhat, axis=0, keepdims=True),
            jnp.sum(normed_grad, axis=0, keepdims=True),
            jnp.zeros((14, model_width), wide),
        ],
        axis=0,
    )
    norm_last[...] = vectors

    for c in moves:
        c.wait_recv()
    vector_lanes = min(d_band, LANES)
    for j, z, at in bands(d_band):
        normed = pair[:, 0, :, at].reshape(every, d_band)
        value_s[j, z, 0:d_band, :] = dot(
            normed, value_all[...].reshape(every, v_band), 0, 0
        ).astype(low)
        value_s[j, z, pl.ds(d_band, 16), 0:vector_lanes] = norm_last[:, at].astype(low)
    value_sum.begin()
    down_out[...] = down_sum.end()
    mix_band = mix_sum.end().astype(low)
    gate_band = gate_sum.end().astype(low)
    value_sum.turn()
    for w in range(n_wt):
        gate_cut = gate_band[w * d_rows : (w + 1) * d_rows, :]
        mix_cut = mix_band[w * h_rows : (w + 1) * h_rows, :]
        last_send[w] = jnp.concatenate([gate_cut, mix_cut], axis=0)
    heads = gate_last
    heads[w_me] = last_send[w_me]
    ends = []

    def spread(source, target):
        for k in range(outer_wt):
            for j in range(2):
                if k or j:
                    w = ((o + k) % outer_wt) * 2 + (i + j) % 2
                    ends.append(wires.send(source.at[w], target.at[w_me], (s_me, w)))

    spread(last_send, heads)
    for k in range(1, outer_wt):
        far_all[k - 1].wait_recv()
        block = all_out.at[((o + outer_wt - k) % outer_wt) * 2 + i]
        near_all.append(wires.send(block, block, sibling))
    value_band = value_sum.end()
    tail_send = mix_last
    for w in range(n_wt):
        tail_send[w, 0:d_rows, :] = value_band[w * d_rows : (w + 1) * d_rows, :].astype(low)
        tail_send[w, pl.ds(d_rows, 16), :] = value_band[d_band : d_band + 16, :].astype(low)
    value_last[w_me] = tail_send[w_me]
    spread(tail_send, value_last)
    for c in ends + near_all:
        c.wait_recv()
    wires.sent()
    norm = jnp.zeros((16, v_band), wide)
    for w in range(n_wt):
        norm = norm + value_last[w, pl.ds(d_rows, 16), :].astype(wide)
    norm_out[...] = norm


def back_call(
    pair, gate_w, mix_w, down_w, mixed, v, lags, pre, value_full, norm_vec, x, seg, sid, per,
    seq_count, docs, n_lag, bits, inner_seq, pw_re, pw_im, kr, ki, rate, freq, dt, skip,
):
    n_seq, n_wt = lax.axis_size("seq"), lax.axis_size("wt")
    n = n_seq * n_wt
    channels, states = kr.shape
    rows = seg.shape[0] - 2 * PAD
    local, model_width = x.shape
    width, f_part = mix_w.shape
    d_band, h_band, v_band = model_width // n_seq, width // n_seq, width // n_wt
    d_rows, h_rows = d_band // n_wt, h_band // n_wt
    f_rows = f_part // n_seq
    inner, outer, outer_wt = inner_seq, n_seq // inner_seq, n_wt // 2
    wide = jnp.broadcast_to(skip[:, None], (channels, LANES))
    dt = jnp.broadcast_to(dt, (channels, states))
    low = jnp.bfloat16
    half = lambda *s: pltpu.VMEM(s, low)
    out = jax.ShapeDtypeStruct
    wires = back_wires(n_seq, n_wt, inner)

    def seq_scratch(*block):
        return [
            half(inner, outer, *block), half(max(inner - 1, 1), outer, *block),
            half(max(outer - 1, 1), *block),
        ]

    every = n_wt * local
    return pl.pallas_call(
        functools.partial(back_kernel, n_lag, docs, bits, seq_count, per, inner_seq),
        out_shape=(
            out((local, model_width), low),
            out((local, model_width), jnp.float32),
            out((n_wt, d_rows + h_rows, f_part), low),
            out((n_wt, d_rows + 16, v_band), low),
            out((n_wt, d_rows + 16, v_band), low),
            out((f_rows, model_width), jnp.float32),
            out((16, v_band), jnp.float32),
            out((n_wt, channels, 4 * states + 2 * LANES), jnp.float32),
        ),
        in_specs=[pl.BlockSpec(memory_space=pltpu.VMEM)] * 21,
        out_specs=(pl.BlockSpec(memory_space=pltpu.VMEM),) * 8,
        scratch_shapes=[vmem(PAD + rows, LANES)] * 5
        + [vmem(LANES, states), vmem(LANES, states), vmem(rows * channels, LANES)]
        + [half(n, channels, local)] * 3
        + [half(every, f_part)] * 3
        + [half(2, outer_wt, width, local), half(outer_wt, width, local)]
        + [half(max(outer_wt - 1, 1), width, local)]
        + [half(2, outer_wt, 2, local, model_width), half(outer_wt, 2, local, model_width)]
        + [half(max(outer_wt - 1, 1), 2, local, model_width)]
        + [vmem(f_part, model_width)]
        + seq_scratch(f_rows, model_width)
        + seq_scratch(h_band, f_part)
        + seq_scratch(d_band, f_part)
        + seq_scratch(d_band + 16, v_band)
        + [vmem(width, local), half(n_wt, local, v_band), half(n_wt, local, v_band)]
        + [half(n_wt, d_rows + h_rows, f_part), vmem(16, model_width)]
        + [pltpu.SemaphoreType.DMA((n,))] * 4
        + [pltpu.SemaphoreType.DMA((wires,))] * 2
        + [pltpu.SemaphoreType.DMA]
        + [vmem(channels, states)] * 4
        + [vmem(channels, LANES)] * 2,
        compiler_params=pltpu.CompilerParams(
            vmem_limit_bytes=62 << 20, collective_id=2, has_side_effects=True
        ),
        cost_estimate=pl.CostEstimate(
            flops=60_000_000_000, bytes_accessed=4_000_000, transcendentals=0
        ),
        name="back",
    )(
        pair, gate_w, mix_w, down_w, mixed, v, lags, pre, value_full, norm_vec, x, seg, sid, pw_re,
        pw_im, kr, ki, rate, freq, dt, wide,
    )


BOTH = ("seq", "wt")
norm_epsilon = 1e-05


def gelu_tanh(pre_act):
    return jax.nn.gelu(pre_act, approximate=True)


def layer_norm(token_rows, gain_vec, bias_vec):
    row_mean = jnp.mean(token_rows, axis=-1, keepdims=True)
    centered = token_rows - row_mean
    spread = jnp.mean(centered * centered, axis=-1, keepdims=True)
    return centered * lax.rsqrt(spread + norm_epsilon) * gain_vec + bias_vec


def doc_segments(doc_lengths, seq_length):
    docs = doc_lengths.shape[1]
    upto = jnp.arange(docs)[:, None] >= jnp.arange(docs)[None, :]
    ends = jnp.sum(jnp.where(upto[None], doc_lengths[:, None, :], 0), axis=-1)
    places = jnp.arange(seq_length, dtype=jnp.int32)
    passed = (places[None, None, :] >= ends[:, :, None]).astype(jnp.int32)
    return jnp.sum(passed, axis=1, dtype=jnp.int32)


def after(x, first):
    return lax.optimization_barrier((x, first))[0]


class Ring:
    def __init__(self, axis, inner):
        self.axis, self.size = axis, lax.axis_size(axis)
        self.inner = min(inner, self.size)
        self.outer = self.size // self.inner
        self.me = lax.axis_index(axis)
        self.o, self.i = self.me // self.inner, self.me % self.inner

    def shift(self, x, k, j):
        to = [
            ((p // self.inner + k) % self.outer) * self.inner + (p % self.inner + j) % self.inner
            for p in range(self.size)
        ]
        return lax.ppermute(x, self.axis, list(enumerate(to)))

    def parts(self, x, joined):
        far = [(0, x)] + [(k, self.shift(x, k, 0)) for k in range(1, self.outer)]
        back = lambda k, j: ((self.o - k) % self.outer) * self.inner + (self.i - j) % self.inner
        out = [(back(k, 0), part) for k, part in far]
        for j in range(1, self.inner):
            if joined:
                near = self.shift(jnp.stack([part for _, part in far]), 0, j)
                out += [(back(k, j), near[k]) for k in range(self.outer)]
            else:
                out += [(back(k, j), self.shift(part, 0, j)) for k, part in far]
        return out

    def gather(self, x, joined=True):
        return self.place(self.parts(x, joined))

    def place(self, parts, axis=0):
        first = parts[0][1]
        out = jnp.zeros(first.shape[:axis] + (self.size,) + first.shape[axis:], first.dtype)
        for at, part in parts:
            out = lax.dynamic_update_index_in_dim(out, part, at, axis)
        return out

    def exchange(self, x):
        parts = []
        for k in range(self.outer):
            for j in range(self.inner):
                to = ((self.o + k) % self.outer) * self.inner + (self.i + j) % self.inner
                back = ((self.o - k) % self.outer) * self.inner + (self.i - j) % self.inner
                block = lax.dynamic_index_in_dim(x, to, 0, keepdims=False)
                parts.append((back, block if k == j == 0 else self.shift(block, k, j)))
        return self.place(parts)

    def scatter_sum(self, x):
        wide, narrow = jnp.float32, jnp.bfloat16
        x = x.astype(narrow).reshape((self.outer, self.inner) + x.shape[1:])
        pick = lambda j: lax.dynamic_index_in_dim(x, (self.i + j) % self.inner, 1, keepdims=False)
        held = pick(0).astype(wide)
        for j in range(1, self.inner):
            held = held + self.shift(pick(j), 0, j).astype(wide)
        low = held.astype(narrow)
        take = lambda a, k: lax.dynamic_index_in_dim(a, (self.o + k) % self.outer, 0, keepdims=False)
        total = take(held, 0)
        for k in range(1, self.outer):
            total = total + self.shift(take(low, k), k, 0).astype(wide)
        return total


def on_device(
    inputs, cotangent, doc_lengths, norm_gain, norm_bias, gate_weight, value_weight, mix_weight,
    down_weight, decay_rate, frequency, kernel_re, kernel_im, log_step, skip_gain,
):
    seq_count, local_len, model_width = inputs.shape
    row_count = seq_count * local_len
    n_seq, n_wt = lax.axis_size("seq"), lax.axis_size("wt")
    seq, wt = Ring("seq", 2 if n_seq <= 8 else 8), Ring("wt", 2)
    length = local_len * n_seq
    docs = doc_lengths.shape[1]
    n_lag = length // 2 // LANES
    blocks = length // LANES
    width = value_weight.shape[1]
    d_rows = value_weight.shape[0]
    h_rows = mix_weight.shape[0]
    f_rows = down_weight.shape[0]
    gate_width = gate_weight.shape[1]
    f_part = gate_width // n_wt
    low = jnp.bfloat16

    lengths_all = wt.gather(doc_lengths).reshape(n_wt * seq_count, docs)
    flat = seq.me * n_wt + wt.me
    norm_rows = jnp.zeros((16, width), low)
    norm_rows = lax.dynamic_update_slice(
        norm_rows, jnp.stack([norm_gain, norm_bias]), (0, flat * d_rows % LANES)
    )
    vpack = jnp.concatenate([value_weight, norm_rows], axis=0)

    own_channels = width // (n_seq * n_wt)

    def own(x):
        return lax.dynamic_slice_in_dim(x, wt.me * own_channels, own_channels, 0)

    rate, freq, kr, ki = own(decay_rate), own(frequency), own(kernel_re), own(kernel_im)
    step, skip = own(log_step), own(skip_gain)
    dt, bits, pw_re, pw_im = table_inputs(rate, freq, step, n_lag)
    seg, sid, per = segment_tables(doc_segments(lengths_all, length), docs)

    token_rows = inputs.reshape(row_count, model_width)
    cot_rows = cotangent.reshape(row_count, model_width)
    by_device = (n_seq * n_wt, own_channels, row_count)
    pair, gate_own, mix_own, down_own, mixed, value_ch, lags, value_pre, value_full, norm_vec = front_call(
        token_rows, cot_rows, vpack, gate_weight, mix_weight, down_weight, seg, sid, per, seq_count,
        docs, n_lag, bits, seq.inner, pw_re, pw_im, kr, ki, skip,
    )
    gate_own = gate_own.reshape(model_width, f_part)
    mix_own = mix_own.reshape(width, f_part)
    down_own = down_own.reshape(f_part, model_width)
    mixed = mixed.reshape(n_wt, width, row_count)

    outputs, input_grad, heads, tails, unused, down_piece, norm, packed = back_call(
        pair, gate_own, mix_own, down_own, mixed, value_ch, lags, value_pre, value_full, norm_vec,
        token_rows, seg, sid, per, seq_count, docs, n_lag, bits, seq.inner, pw_re, pw_im, kr, ki, rate,
        freq, dt, skip,
    )
    states = rate.shape[1]
    packed = packed.reshape(n_wt * own_channels, -1)
    mixer_grads = [packed[:, i * states : (i + 1) * states] for i in range(4)]
    mixer_grads += [packed[:, 4 * states], packed[:, 4 * states + LANES]]

    def spread(x):
        rows = x.shape[1]
        x = x.astype(jnp.float32).reshape(n_wt, rows, n_seq, f_rows).transpose(1, 2, 0, 3)
        return x.reshape(rows, gate_width)

    value_piece = tails[:, :d_rows].astype(jnp.float32).transpose(1, 0, 2).reshape(d_rows, width)
    own_lanes = lax.dynamic_slice(norm, (0, wt.me * d_rows), (2, d_rows))
    return (
        outputs.reshape(inputs.shape), input_grad.reshape(inputs.shape), own_lanes[0], own_lanes[1],
        spread(heads[:, :d_rows]), value_piece, spread(heads[:, d_rows:]), down_piece, *mixer_grads,
    )


def solution(mesh):
    in_specs = (
        P("wt", "seq", None),
        P("wt", "seq", None),
        P("wt", None),
        P(("seq", "wt")),
        P(("seq", "wt")),
        P(("seq", "wt"), None),
        P(("seq", "wt"), None),
        P(("seq", "wt"), None),
        P(("seq", "wt"), None),
        P("seq", None),
        P("seq", None),
        P("seq", None),
        P("seq", None),
        P("seq"),
        P("seq"),
    )
    out_specs = (
        P("wt", "seq", None),
        P("wt", "seq", None),
        P(("seq", "wt")),
        P(("seq", "wt")),
        P(("seq", "wt"), None),
        P(("seq", "wt"), None),
        P(("seq", "wt"), None),
        P(("seq", "wt"), None),
        P("seq", None),
        P("seq", None),
        P("seq", None),
        P("seq", None),
        P("seq"),
        P("seq"),
    )
    return jax.shard_map(
        on_device, mesh=mesh, in_specs=in_specs, out_specs=out_specs, check_vma=False
    )
```

```python
import functools

import jax
import jax.numpy as jnp
from jax import lax
from jax.experimental import pallas as pl
from jax.experimental.pallas import tpu as pltpu
from jax.sharding import PartitionSpec as P

LANES = 128
PAD = 16


MESH = pl.DeviceIdType.MESH


def place_of(flat, n_wt):
    return (flat // n_wt, flat % n_wt)


def meet(flat, n, n_wt):
    barrier = pltpu.get_barrier_semaphore()

    def tell(r, unused):
        pl.semaphore_signal(
            barrier, inc=1, device_id=place_of((flat + r) % n, n_wt), device_id_type=MESH
        )
        return unused

    lax.fori_loop(1, n, tell, 0)
    pl.semaphore_wait(barrier, n - 1)


def swap_copy(source, target, send_sem, recv_sem, slot, peer, n_wt):
    return pltpu.make_async_remote_copy(
        src_ref=source, dst_ref=target, send_sem=send_sem.at[slot], recv_sem=recv_sem.at[slot],
        device_id=place_of(peer, n_wt), device_id_type=MESH,
    )


def swap_start(send, target_of, send_sem, recv_sem, flat, n, n_wt):
    def one(r, unused):
        peer = (flat + r) % n
        swap_copy(send.at[peer], target_of(peer, flat), send_sem, recv_sem, r, peer, n_wt).start()
        return unused

    lax.fori_loop(1, n, one, 0)


def swap_wait(send, target_of, send_sem, recv_sem, flat, n, n_wt):
    def one(r, unused):
        source = (flat + n - r) % n
        swap_copy(
            send.at[source], target_of(flat, source), send_sem, recv_sem, r, source, n_wt
        ).wait()
        return unused

    lax.fori_loop(1, n, one, 0)


def rows_to_table(got, table, n_seq, n_wt, seq_count, local_blocks, per, channels):
    for s in range(n_seq):
        for w in range(n_wt):
            for k in range(seq_count):
                for b in range(local_blocks):
                    row = (w * seq_count + k) * per + s * local_blocks + b
                    lanes = pl.ds((k * local_blocks + b) * LANES, LANES)
                    table[pl.ds(row * channels, channels), :] = got[
                        s * n_wt + w, :, lanes
                    ].astype(jnp.float32)


def table_to_rows(table, send, n_seq, n_wt, seq_count, local_blocks, per, channels):
    for s in range(n_seq):
        for w in range(n_wt):
            for k in range(seq_count):
                for b in range(local_blocks):
                    row = (w * seq_count + k) * per + s * local_blocks + b
                    lanes = pl.ds((k * local_blocks + b) * LANES, LANES)
                    send[s * n_wt + w, :, lanes] = table[
                        pl.ds(row * channels, channels), :
                    ].astype(jnp.bfloat16)


def clear_unused(table, seqs, blocks, per, channels):
    for s in range(seqs):
        table[pl.ds((s * per + blocks) * channels, (per - blocks) * channels), :] = jnp.zeros(
            ((per - blocks) * channels, LANES), jnp.float32
        )


def share_over_wt(ref, s_me, w_me, n_wt, send_sem, recv_sem):
    inner = 2
    outer = n_wt // inner
    o, i = w_me // inner, w_me % inner
    other = (s_me, o * inner + 1 - i)

    def copy(block, slot, to):
        return pltpu.make_async_remote_copy(
            src_ref=ref.at[block], dst_ref=ref.at[block], send_sem=send_sem.at[slot],
            recv_sem=recv_sem.at[slot], device_id=to, device_id_type=MESH,
        )

    far = [copy(w_me, k, (s_me, ((o + k) % outer) * inner + i)) for k in range(1, outer)]
    near = [copy(w_me, outer, other)]
    for c in far + near:
        c.start()
    for k in range(1, outer):
        block = ((o + outer - k) % outer) * inner + i
        far[k - 1].wait_recv()
        c = copy(block, outer + k, other)
        c.start()
        near.append(c)
    for c in far:
        c.wait_send()
    for c in near:
        c.wait()


def cmul(ar, ai, br, bi):
    return ar * br - ai * bi, ar * bi + ai * br


def power_rows(pw_re, pw_im, c, first, count, rows):
    width = pw_re.shape[2]
    place = lax.broadcasted_iota(jnp.int32, (rows, width), 0)
    re = jnp.ones((rows, width), jnp.float32)
    im = jnp.zeros((rows, width), jnp.float32)
    for bit in range(count):
        on = (place & (1 << bit)) != 0
        fr = jnp.where(on, pw_re[c, pl.ds(first + bit, 1), :], 1.0)
        fi = jnp.where(on, pw_im[c, pl.ds(first + bit, 1), :], 0.0)
        re, im = cmul(re, im, fr, fi)
    return re, im


def fill_lane_powers(pw_re, pw_im, c, tab_re, tab_im, extra):
    re, im = power_rows(pw_re, pw_im, c, 0, 3, 8)
    if extra:
        re, im = cmul(re, im, pw_re[c, pl.ds(0, 1), :], pw_im[c, pl.ds(0, 1), :])
    tab_re[0:8, :] = re
    tab_im[0:8, :] = im
    have, bit = 8, 3
    while have < LANES:
        re, im = cmul(
            tab_re[0:have, :],
            tab_im[0:have, :],
            pw_re[c, pl.ds(bit, 1), :],
            pw_im[c, pl.ds(bit, 1), :],
        )
        tab_re[have : 2 * have, :] = re
        tab_im[have : 2 * have, :] = im
        have, bit = 2 * have, bit + 1


def to_pieces(seg, val, rows, docs):
    total = jnp.zeros((rows, LANES), jnp.float32)
    for j in range(docs):
        at = pl.ds(PAD - j, rows)
        total = total + jnp.where(seg[at, :] == j, val[at, :], 0.0)
    return total


def from_pieces(seg, piece, rows, docs):
    own = seg[pl.ds(PAD, rows), :]
    total = jnp.zeros((rows, LANES), jnp.float32)
    for j in range(docs):
        total = total + jnp.where(own == j, piece[pl.ds(j, rows), :], 0.0)
    return total


def toeplitz(lags, d, last, lower, before):
    if d < last:
        row = jnp.broadcast_to(lags[d : d + 1, :], (LANES, LANES))
        here = pltpu.roll(row, 0, 1, stride=1, stride_axis=0)
    else:
        here = jnp.zeros((LANES, LANES), jnp.float32)
    return jnp.where(lower, here, before).astype(jnp.bfloat16), here


def dot(a, b, ca=1, cb=0):
    return lax.dot_general(a, b, (((ca,), (cb,)), ((), ())), preferred_element_type=jnp.float32)


def vmem(*shape):
    return pltpu.VMEM(shape, jnp.float32)


def table_inputs(decay_rate, frequency, log_step, n_lag):
    bits = (n_lag - 1).bit_length()
    dt = jnp.exp(log_step)[:, None]
    powers = jnp.array([float(1 << b) for b in range(7 + bits)] + [0.0] * (9 - bits), jnp.float32)
    powers = powers[None, :, None]
    mag = jnp.exp(-(decay_rate * dt)[:, None, :] * powers)
    phase = (frequency * dt)[:, None, :] * powers
    return dt, bits, mag * jnp.cos(phase), mag * jnp.sin(phase)


def segment_tables(segment, docs):
    seqs, length = segment.shape
    blocks = length // LANES
    per = -(-(blocks + docs) // 8) * 8
    seg = segment.reshape(seqs, blocks, LANES)
    piece = seg + jnp.arange(blocks, dtype=jnp.int32)[None, :, None]
    hit = piece.reshape(seqs, 1, length) == jnp.arange(per, dtype=jnp.int32)[None, :, None]
    sid = jnp.max(jnp.where(hit, segment[:, None, :], -1), axis=-1)
    sid = jnp.where(sid >= 0, sid + docs * jnp.arange(seqs, dtype=jnp.int32)[:, None], -1)
    seg = jnp.pad(seg, ((0, 0), (0, per - blocks), (0, 0)), constant_values=-1)
    seg = jnp.pad(seg.reshape(seqs * per, LANES), ((PAD, PAD), (0, 0)), constant_values=-1)
    sid = jnp.pad(sid.reshape(seqs * per), ((PAD, PAD),), constant_values=-2)
    return seg, jnp.broadcast_to(sid[:, None], (seqs * per + 2 * PAD, LANES)), per


class Wires:
    def __init__(self, send_sem, recv_sem):
        self.send_sem, self.recv_sem, self.used, self.open = send_sem, recv_sem, 0, []

    def send(self, source, target, to):
        c = pltpu.make_async_remote_copy(
            src_ref=source, dst_ref=target, send_sem=self.send_sem.at[self.used],
            recv_sem=self.recv_sem.at[self.used], device_id=to, device_id_type=MESH,
        )
        self.used += 1
        self.open.append(c)
        c.start()
        return c

    def sent(self):
        for c in self.open:
            c.wait_send()
        self.open = []


class SeqGather:
    def __init__(self, ref, send_sem, recv_sem, so, si, outer, inner, w_me):
        self.ref, self.send_sem, self.recv_sem = ref, send_sem, recv_sem
        self.so, self.si, self.outer, self.inner, self.w_me = so, si, outer, inner, w_me

    def copy(self, z, slot, to_z, j):
        block = self.ref.at[z * self.inner + self.si]
        to = (to_z * self.inner + (self.si + j) % self.inner, self.w_me)
        return pltpu.make_async_remote_copy(
            src_ref=block, dst_ref=block, send_sem=self.send_sem.at[slot],
            recv_sem=self.recv_sem.at[slot], device_id=to, device_id_type=MESH,
        )

    def along(self, up, k, z):
        slot = (0 if up else self.outer) + k
        return self.copy(z, slot, self.so + 1 if up else self.so - 1, 0)

    def across(self, z, j):
        return self.copy(z, 2 * self.outer + z * self.inner + j, self.so, j)

    def ends(self, up):
        return self.so < self.outer - 1 if up else self.so > 0

    def launch(self, z, k, ups):
        for up in ups:
            if k < self.outer:
                pl.when(self.ends(up))(lambda up=up: self.along(up, k, z).start())
        for j in range(1, self.inner):
            self.across(z, j).start()

    def begin(self):
        self.launch(self.so, 1, (True, False))

    def hop(self, k):
        for up in (True, False):
            z = self.so - k if up else self.so + k
            there = z >= 0 if up else z < self.outer

            @pl.when(there)
            def _():
                self.along(up, k, z).wait_recv()
                self.launch(z, k + 1, (up,))

    def end(self):
        for z in range(self.outer):
            for j in range(1, self.inner):
                block = self.copy(z, 2 * self.outer + z * self.inner + j, self.so, j)
                block.wait_recv()
                block.wait_send()
        for k in range(1, self.outer):
            for up in (True, False):
                z = self.so - k + 1 if up else self.so + k - 1
                from_here = (z >= 0 if up else z < self.outer) & self.ends(up)
                pl.when(from_here)(lambda up=up, k=k, z=z: self.along(up, k, z).wait_send())


def rms(x32):
    mean = jnp.mean(x32, axis=-1, keepdims=True)
    centered = x32 - mean
    spread = jnp.mean(centered * centered, axis=-1, keepdims=True)
    return centered * lax.rsqrt(spread + norm_epsilon)


def regroup(x, n_seq, n_wt, width):
    cut = lambda s, w: x[:, (s * n_wt + w) * width : (s * n_wt + w + 1) * width]
    return [jnp.concatenate([cut(s, w) for s in range(n_seq)], axis=1) for w in range(n_wt)]


def front_wires(n_seq, n_wt):
    value = (n_seq - 1) + n_seq * (n_wt // 2 - 1) + n_seq * (n_wt // 2)
    weights = 2 * (n_wt - 1)
    tokens = 2 * (n_wt // 2 - 1) + 2 * (n_wt // 2)
    mixed = (n_wt // 2 - 1) + n_wt // 2
    return value + weights + tokens + mixed


def front_kernel(
    n_lag, docs, bits, seq_count, per, inner_seq,
    x_ref, cot_ref, vpack_ref, gate_in, mix_in, down_in, seg_ref, sid_ref, pw_re, pw_im, kr_ref,
    ki_ref, skip_ref,
    pair, gate_out, mix_out, down_out, mixed_ref, v_ref, lag_ref, pre_ref, value_full, norm_out,
    vf, vp, yp, tab_re, tab_im, table, got, back, front, xhat, act_send, gate_cut, mix_cut,
    in_send, in_recv, out_send, out_recv, wire_send, wire_recv, local_sem, *hop_sems,
):
    channels, rows, _ = v_ref.shape
    n_seq, n_wt = lax.axis_size("seq"), lax.axis_size("wt")
    n = n_seq * n_wt
    s_me, w_me = lax.axis_index("seq"), lax.axis_index("wt")
    flat = s_me * n_wt + w_me
    row_count, model_width = x_ref.shape
    width = pre_ref.shape[1]
    d_rows, h_rows, f_rows = gate_in.shape[0], mix_in.shape[0], down_in.shape[0]
    local_blocks = row_count // LANES // seq_count
    shape = (n_seq, n_wt, seq_count, local_blocks, per, channels)
    outer_wt = n_wt // 2
    o, i = w_me // 2, w_me % 2
    sibling = o * 2 + 1 - i
    far_to = lambda k: ((o + k) % outer_wt) * 2 + i
    far_from = lambda k: ((o + outer_wt - k) % outer_wt) * 2 + i
    outer_seq = n_seq // inner_seq
    so, si = s_me // inner_seq, s_me % inner_seq
    rings = [
        SeqGather(ref, hop_sems[2 * at], hop_sems[2 * at + 1], so, si, outer_seq, inner_seq, w_me)
        for at, ref in enumerate((down_out, gate_out, mix_out))
    ]
    down_ring, gate_ring, mix_ring = rings
    wires = Wires(wire_send, wire_recv)

    meet(flat, n, n_wt)

    front[s_me, w_me] = vpack_ref[...]
    first = []
    for k in range(1, n_seq):
        to = ((s_me + k) % n_seq, w_me)
        first.append(wires.send(front.at[s_me, w_me], front.at[s_me, w_me], to))

    second, third = [], []

    def spread_value(s):
        block = front.at[s, w_me]
        for k in range(1, outer_wt):
            second.append((s, k, wires.send(block, block, (s_me, far_to(k)))))
        third.append(wires.send(block, block, (s_me, sibling)))

    spread_value(s_me)
    down_out[s_me] = down_in[...]
    down_ring.begin()

    for ref, cut in ((gate_in, gate_cut), (mix_in, mix_cut)):
        whole = ref[...].astype(jnp.float32)
        for w, part in enumerate(regroup(whole, n_seq, n_wt, f_rows)):
            cut[w] = part.astype(jnp.bfloat16)
    gate_out[s_me, w_me] = gate_cut[w_me]
    mix_out[s_me, w_me] = mix_cut[w_me]
    turn = []
    for source, target in ((gate_cut, gate_out), (mix_cut, mix_out)):
        for k in range(outer_wt):
            for j in range(2):
                if k or j:
                    w = ((o + k) % outer_wt) * 2 + (i + j) % 2
                    turn.append(wires.send(source.at[w], target.at[s_me, w_me], (s_me, w)))

    chunk = min(32, row_count)

    def normalise(r, unused):
        at = pl.ds(r * chunk, chunk)
        xhat[at, :] = rms(x_ref[at, :].astype(jnp.float32))
        return unused

    lax.fori_loop(0, row_count // chunk, normalise, 0)
    pair[w_me, 1] = cot_ref[...]

    for k in range(1, n_seq):
        first[k - 1].wait_recv()
        spread_value((s_me + n_seq - k) % n_seq)

    for c in turn[: n_wt - 1]:
        c.wait_recv()
    gate_ring.begin()
    for c in turn[n_wt - 1 :]:
        c.wait_recv()
    mix_ring.begin()
    if outer_seq > 1:
        down_ring.hop(1)
    for s, k, c in second:
        c.wait_recv()
        block = front.at[s, far_from(k)]
        third.append(wires.send(block, block, (s_me, sibling)))
    for c in third:
        c.wait_recv()

    for f in range(n):
        value_full[pl.ds(f * d_rows, d_rows), :] = front[f // n_wt, f % n_wt, 0:d_rows, :]
    share = LANES // d_rows
    for b in range(model_width // LANES):
        total = jnp.zeros((2, LANES), jnp.float32)
        for f in range(b * share, (b + 1) * share):
            total = total + front[f // n_wt, f % n_wt, d_rows : d_rows + 2, 0:LANES].astype(jnp.float32)
        norm_out[:, pl.ds(b * LANES, LANES)] = total

    def project(r, unused):
        at = pl.ds(pl.multiple_of(r * LANES, LANES), LANES)
        normed = (xhat[at, :] * norm_out[0:1, :] + norm_out[1:2, :]).astype(jnp.bfloat16)
        pair[w_me, 0, at, :] = normed
        pre = dot(normed, value_full[...])
        pre_ref[at, :] = pre
        turned = jnp.transpose(gelu_tanh(pre))
        for p in range(n):
            act_send[p, :, at] = turned[p * channels : (p + 1) * channels, :].astype(jnp.bfloat16)
        return unused

    lax.fori_loop(0, row_count // LANES, project, 0)
    into = lambda peer, slot: got.at[slot]
    swap_start(act_send, into, in_send, in_recv, flat, n, n_wt)
    got[flat] = act_send[flat]

    if outer_seq > 1:
        gate_ring.hop(1)
        mix_ring.hop(1)
    clear_unused(table, n_wt * seq_count, n_seq * local_blocks, per, channels)
    zero_pad = jnp.zeros((PAD, LANES), jnp.float32)
    vf[0:PAD, :] = zero_pad
    vp[0:PAD, :] = zero_pad
    yp[pl.ds(rows, PAD), :] = zero_pad
    lower = lax.broadcasted_iota(jnp.int32, (LANES, LANES), 1) >= lax.broadcasted_iota(
        jnp.int32, (LANES, LANES), 0
    )
    swap_wait(act_send, into, in_send, in_recv, flat, n, n_wt)

    far_pair = []
    for at in range(2):
        block = pair.at[w_me, at]
        for k in range(1, outer_wt):
            far_pair.append((k, at, wires.send(block, block, (s_me, far_to(k)))))
    near_pair = [wires.send(pair.at[w_me, at], pair.at[w_me, at], (s_me, sibling)) for at in range(2)]

    rows_to_table(got, table, *shape)

    def channel(c, unused):
        fill_lane_powers(pw_re, pw_im, c, tab_re, tab_im, 0)
        dr, di = power_rows(pw_re, pw_im, c, 7, bits, n_lag)
        ar, ai = cmul(dr, di, kr_ref[pl.ds(c, 1), :], ki_ref[pl.ds(c, 1), :])
        lags = dot(ar.astype(jnp.bfloat16), tab_re[...].astype(jnp.bfloat16), 1, 1) - dot(
            ai.astype(jnp.bfloat16), tab_im[...].astype(jnp.bfloat16), 1, 1
        )
        lag_ref[c] = lags
        val = table[pl.ds(c, rows, stride=channels), :]
        v_ref[c] = val.astype(jnp.bfloat16)
        vf[pl.ds(PAD, rows), :] = val
        vp[pl.ds(PAD, rows), :] = to_pieces(seg_ref, vf, rows, docs)
        sid = sid_ref[pl.ds(PAD, rows), :]
        before = jnp.zeros((LANES, LANES), jnp.float32)
        total = jnp.zeros((rows, LANES), jnp.float32)
        for d in range(n_lag + 1):
            at = pl.ds(PAD - d, rows)
            x = jnp.where(sid_ref[at, :] == sid, vp[at, :], 0.0).astype(jnp.bfloat16)
            t, before = toeplitz(lags, d, n_lag, lower, before)
            total = total + dot(x, t)
        yp[0:rows, :] = total
        out = from_pieces(seg_ref, yp, rows, docs) + skip_ref[pl.ds(c, 1), :] * val
        table[pl.ds(c, rows, stride=channels), :] = out
        return unused

    hops = [(ring, k) for k in range(2, outer_seq) for ring in rings]
    runs = min(4, channels)
    for run in range(runs):
        lax.fori_loop(run * channels // runs, (run + 1) * channels // runs, channel, 0)
        for ring, k in hops[run * len(hops) // (runs + 1) : (run + 1) * len(hops) // (runs + 1)]:
            ring.hop(k)
    table_to_rows(table, back, *shape)
    home = lambda peer, slot: mixed_ref.at[peer % n_wt, slot]
    swap_start(back, home, out_send, out_recv, flat, n, n_wt)
    own = pltpu.make_async_copy(back.at[flat], mixed_ref.at[w_me, flat], local_sem)
    own.start()
    for ring, k in hops[runs * len(hops) // (runs + 1) :]:
        ring.hop(k)
    own.wait()
    swap_wait(back, home, out_send, out_recv, flat, n, n_wt)

    block = mixed_ref.at[w_me]
    far_mixed = [wires.send(block, block, (s_me, far_to(k))) for k in range(1, outer_wt)]
    ends = [wires.send(block, block, (s_me, sibling))]
    for k, at, c in far_pair:
        c.wait_recv()
        block = pair.at[far_from(k), at]
        near_pair.append(wires.send(block, block, (s_me, sibling)))
    for k in range(1, outer_wt):
        far_mixed[k - 1].wait_recv()
        block = mixed_ref.at[far_from(k)]
        ends.append(wires.send(block, block, (s_me, sibling)))
    for c in near_pair + ends:
        c.wait_recv()
    for ring in rings:
        ring.end()
    wires.sent()


def front_call(
    x, cot, vpack, gate, mix, down, seg, sid, per, seq_count, docs, n_lag, bits, inner_seq, pw_re,
    pw_im, kr, ki, skip,
):
    n_seq, n_wt = lax.axis_size("seq"), lax.axis_size("wt")
    n = n_seq * n_wt
    channels, states = kr.shape
    rows = seg.shape[0] - 2 * PAD
    local, model_width = x.shape
    width = vpack.shape[1]
    f_part = gate.shape[1] // n_wt
    wide = jnp.broadcast_to(skip[:, None], (channels, LANES))
    low = jnp.bfloat16
    wires = front_wires(n_seq, n_wt)
    hops = (2 + inner_seq) * (n_seq // inner_seq)
    out = jax.ShapeDtypeStruct
    return pl.pallas_call(
        functools.partial(front_kernel, n_lag, docs, bits, seq_count, per, inner_seq),
        out_shape=(
            out((n_wt, 2, local, model_width), low),
            out((n_seq, n_wt) + (gate.shape[0], f_part), low),
            out((n_seq, n_wt) + (mix.shape[0], f_part), low),
            out((n_seq,) + down.shape, low),
            out((n_wt, n, channels, local), low),
            out((channels, rows, LANES), low),
            out((channels, n_lag, LANES), jnp.float32),
            out((local, width), jnp.float32),
            out((model_width, width), low),
            out((2, model_width), jnp.float32),
        ),
        in_specs=[pl.BlockSpec(memory_space=pltpu.VMEM)] * 13,
        out_specs=(pl.BlockSpec(memory_space=pltpu.VMEM),) * 10,
        scratch_shapes=[vmem(PAD + rows, LANES)] * 3
        + [vmem(LANES, states), vmem(LANES, states), vmem(rows * channels, LANES)]
        + [pltpu.VMEM((n, channels, local), low)] * 2
        + [pltpu.VMEM((n_seq, n_wt) + vpack.shape, low), vmem(local, model_width)]
        + [pltpu.VMEM((n, channels, local), low)]
        + [pltpu.VMEM((n_wt, gate.shape[0], f_part), low), pltpu.VMEM((n_wt, mix.shape[0], f_part), low)]
        + [pltpu.SemaphoreType.DMA((n,))] * 4
        + [pltpu.SemaphoreType.DMA((wires,))] * 2
        + [pltpu.SemaphoreType.DMA]
        + [pltpu.SemaphoreType.DMA((hops,))] * 6,
        compiler_params=pltpu.CompilerParams(
            vmem_limit_bytes=56 << 20, collective_id=1, has_side_effects=True
        ),
        cost_estimate=pl.CostEstimate(
            flops=60_000_000_000, bytes_accessed=4_000_000, transcendentals=0
        ),
        name="front",
    )(x, cot, vpack, gate, mix, down, seg, sid, pw_re, pw_im, kr, ki, wide)


GELU_A = 0.7978845608028654
GELU_B = 0.044715


def gelu_pair(v):
    square = v * v
    t = jnp.tanh(GELU_A * (v + GELU_B * v * square))
    half = 0.5 * (1.0 + t)
    slope = half + 0.5 * v * (1.0 - t * t) * (GELU_A * (1.0 + 3.0 * GELU_B * square))
    return v * half, slope


def back_wires(n_seq, n_wt, inner):
    outer = n_seq // inner
    over_seq = 4 * ((inner - 1) + (outer - 1))
    over_wt = 2 * (1 + n_wt // 2 - 1)
    return over_seq + over_wt + 3 * (n_wt - 1) + (n_wt // 2 - 1) + n_wt // 2 + n_wt - 1


class SeqSum:
    def __init__(self, wires, send, near_in, far_in, so, si, outer, inner, s_to):
        self.wires, self.send, self.near_in, self.far_in = wires, send, near_in, far_in
        self.so, self.outer, self.inner, self.s_to = so, outer, inner, s_to

    def begin(self):
        self.near = [
            self.wires.send(self.send.at[j], self.near_in.at[j - 1], self.s_to(0, j))
            for j in range(1, self.inner)
        ]

    def turn(self):
        for c in self.near:
            c.wait_recv()
        for z in range(self.outer):
            total = self.send[0, z].astype(jnp.float32)
            for j in range(1, self.inner):
                total = total + self.near_in[j - 1, z].astype(jnp.float32)
            self.send[0, z] = total.astype(jnp.bfloat16)
        self.far = []
        for k in range(1, self.outer):
            z = (self.so + k) % self.outer
            self.far.append(
                self.wires.send(self.send.at[0, z], self.far_in.at[k - 1], self.s_to(k, 0))
            )

    def end(self):
        for c in self.far:
            c.wait_recv()
        total = self.send[0, self.so].astype(jnp.float32)
        for k in range(1, self.outer):
            total = total + self.far_in[k - 1].astype(jnp.float32)
        return total


def back_kernel(
    n_lag, docs, bits, seq_count, per, inner_seq,
    pair, gate_w, mix_w, down_w, mixed, v_ref, lag_ref, pre_ref, value_full, norm_vec, x_ref,
    seg_ref, sid_ref, pw_re, pw_im, kr_ref, ki_ref, rate_ref, freq_ref, dt_ref, skip_ref,
    out_ref, in_grad, gate_last, value_last, mix_last, down_out, norm_out, all_out,
    vf, gf, vp, gp, yp, tab_re, tab_im, table, got, back, dv_ref,
    product, expand_grad, gate_grad, mg, mg_in, mg_far, tok, tok_in, tok_far,
    down_flat, down_s, down_n, down_f, mix_s, mix_n, mix_f, gate_s, gate_n, gate_f,
    value_s, value_n, value_f, turned, value_cut, value_all, last_send, norm_last,
    in_send, in_recv, out_send, out_recv, wire_send, wire_recv, local_sem, *held,
):
    grads, thin = held[:4], held[4:]
    low, wide = jnp.bfloat16, jnp.float32
    channels, rows, _ = v_ref.shape
    states = kr_ref.shape[1]
    n_seq, n_wt = lax.axis_size("seq"), lax.axis_size("wt")
    n = n_seq * n_wt
    s_me, w_me = lax.axis_index("seq"), lax.axis_index("wt")
    flat = s_me * n_wt + w_me
    row_count, model_width = x_ref.shape
    width = mix_w.shape[0]
    f_part = gate_w.shape[1]
    f_rows = f_part // n_seq
    d_band, h_band, v_band = model_width // n_seq, width // n_seq, width // n_wt
    d_rows, h_rows = d_band // n_wt, h_band // n_wt
    local_blocks = row_count // LANES // seq_count
    shape = (n_seq, n_wt, seq_count, local_blocks, per, channels)
    outer_wt = n_wt // 2
    o, i = w_me // 2, w_me % 2
    sibling = (s_me, o * 2 + 1 - i)
    far_to = lambda k: (s_me, ((o + k) % outer_wt) * 2 + i)
    outer_seq = n_seq // inner_seq
    so, si = s_me // inner_seq, s_me % inner_seq
    s_to = lambda k, j: (((so + k) % outer_seq) * inner_seq + (si + j) % inner_seq, w_me)
    wires = Wires(wire_send, wire_recv)
    sums = lambda send, near_in, far_in: SeqSum(
        wires, send, near_in, far_in, so, si, outer_seq, inner_seq, s_to
    )
    down_sum, mix_sum = sums(down_s, down_n, down_f), sums(mix_s, mix_n, mix_f)
    gate_sum, value_sum = sums(gate_s, gate_n, gate_f), sums(value_s, value_n, value_f)

    meet(flat, n, n_wt)

    def tokens(t, unused):
        j, k = 1 - t // outer_wt, outer_wt - 1 - t % outer_wt
        w = ((o + k) % outer_wt) * 2 + (i + j) % 2
        at = pl.ds(pl.multiple_of(w * row_count, row_count), row_count)
        act, slope = gelu_pair(dot(pair[w, 0], gate_w[...]))
        from_out = dot(pair[w, 1], down_w[...], 1, 1)
        expand = dot(mixed[w], mix_w[...], 0, 0)
        product[at, :] = (expand * act).astype(low)
        gate_grad[at, :] = (from_out * expand * slope).astype(low)
        grad = (from_out * act).astype(low)
        expand_grad[at, :] = grad
        mg[j, k] = dot(mix_w[...], grad, 1, 1).astype(low)
        return unused

    lax.fori_loop(0, outer_wt, tokens, 0)
    near = wires.send(mg.at[1], mg_in, sibling)
    lax.fori_loop(outer_wt, n_wt, tokens, 0)
    piece = min(256, f_part)
    every = n_wt * row_count

    def down_part(r, unused):
        at = pl.ds(pl.multiple_of(r * piece, piece), piece)
        cot = pair[:, 1].reshape(every, model_width)
        down_flat[at, :] = dot(product[:, at], cot, 0, 0)
        return unused

    lax.fori_loop(0, f_part // piece, down_part, 0)
    def bands(size):
        for s in range(n_seq):
            j = (s % inner_seq + inner_seq - si) % inner_seq
            yield j, s // inner_seq, slice(s * size, (s + 1) * size)

    for j, z, at in bands(f_rows):
        down_s[j, z] = down_flat[at, :].astype(low)
    down_sum.begin()
    near.wait_recv()
    far = []
    for k in range(1, outer_wt):
        mg[0, k] = (mg[0, k].astype(wide) + mg_in[k].astype(wide)).astype(low)
        far.append(wires.send(mg.at[0, k], mg_far.at[k - 1], far_to(k)))

    for j, z, at in bands(d_band):
        normed = pair[:, 0, :, at].reshape(every, d_band)
        gate_s[j, z] = dot(normed, gate_grad[...], 0, 0).astype(low)

    total = mg[0, 0].astype(wide) + mg_in[0].astype(wide)
    for k in range(1, outer_wt):
        far[k - 1].wait_recv()
        total = total + mg_far[k - 1].astype(wide)
    turned[...] = total
    for p in range(n):
        back[p] = turned[p * channels : (p + 1) * channels, :].astype(low)
    into = lambda peer, slot: got.at[slot]
    swap_start(back, into, in_send, in_recv, flat, n, n_wt)
    got[flat] = back[flat]

    for j, z, at in bands(h_band):
        total = dot(mixed[0, at, :], expand_grad[0:row_count, :])
        for w in range(1, n_wt):
            total = total + dot(
                mixed[w, at, :], expand_grad[w * row_count : (w + 1) * row_count, :]
            )
        mix_s[j, z] = total.astype(low)

    def token_part(t, unused):
        j, k = 1 - t // outer_wt, outer_wt - 1 - t % outer_wt
        w = ((o + k) % outer_wt) * 2 + (i + j) % 2
        at = pl.ds(pl.multiple_of(w * row_count, row_count), row_count)
        tok[j, k, 0] = dot(product[at, :], down_w[...]).astype(low)
        tok[j, k, 1] = dot(gate_grad[at, :], gate_w[...], 1, 1).astype(low)
        return unused

    lax.fori_loop(0, outer_wt, token_part, 0)
    tok_near = wires.send(tok.at[1], tok_in, sibling)
    lax.fori_loop(outer_wt, n_wt, token_part, 0)

    zero_pad = jnp.zeros((PAD, LANES), wide)
    clear_unused(table, n_wt * seq_count, n_seq * local_blocks, per, channels)
    vf[0:PAD, :] = zero_pad
    gf[0:PAD, :] = zero_pad
    vp[0:PAD, :] = zero_pad
    gp[pl.ds(rows, PAD), :] = zero_pad
    yp[pl.ds(rows, PAD), :] = zero_pad
    tok_near.wait_recv()
    tok_sent = []
    for k in range(1, outer_wt):
        for a in range(2):
            tok[0, k, a] = (tok[0, k, a].astype(wide) + tok_in[k, a].astype(wide)).astype(low)
        tok_sent.append(wires.send(tok.at[0, k], tok_far.at[k - 1], far_to(k)))
    swap_wait(back, into, in_send, in_recv, flat, n, n_wt)
    gate_sum.begin()
    mix_sum.begin()
    rows_to_table(got, table, *shape)

    lane = lax.broadcasted_iota(jnp.int32, (LANES, LANES), 1)
    row = lax.broadcasted_iota(jnp.int32, (LANES, LANES), 0)
    lower = lane >= row
    wraps = lane + row >= LANES
    flip = (lane + row == LANES - 1).astype(jnp.bfloat16)
    lag_place = (
        lax.broadcasted_iota(jnp.int32, (n_lag, LANES), 0) * LANES
        + lax.broadcasted_iota(jnp.int32, (n_lag, LANES), 1)
        + 1
    ).astype(jnp.float32)

    def channel(c, unused):
        own = pl.ds(c, 1)
        val = v_ref[c].astype(jnp.float32)
        grad = table[pl.ds(c, rows, stride=channels), :]
        vf[pl.ds(PAD, rows), :] = val
        gf[pl.ds(PAD, rows), :] = grad
        skip_grad = jnp.sum(jnp.sum(val * grad, axis=0, keepdims=True), axis=1, keepdims=True)
        g_piece = to_pieces(seg_ref, gf, rows, docs)
        gp[0:rows, :] = g_piece
        v_piece = to_pieces(seg_ref, vf, rows, docs).astype(jnp.bfloat16)
        vp[pl.ds(PAD, rows), :] = dot(v_piece, flip)
        g_turned = jnp.transpose(g_piece).astype(jnp.bfloat16)
        sid = sid_ref[pl.ds(PAD, rows), :]
        lags = lag_ref[c]
        before = jnp.zeros((LANES, LANES), jnp.float32)
        total = jnp.zeros((rows, LANES), jnp.float32)
        earlier = None
        sums = []
        for d in range(n_lag + 1):
            ahead = pl.ds(PAD + d, rows)
            x = jnp.where(sid_ref[ahead, :] == sid, gp[pl.ds(d, rows), :], 0.0)
            t, before = toeplitz(lags, d, n_lag, lower, before)
            total = total + dot(x.astype(jnp.bfloat16), t, 1, 1)
            at = pl.ds(PAD - d, rows)
            back = jnp.where(sid_ref[at, :] == sid, vp[at, :], 0.0).astype(jnp.bfloat16)
            pairs = dot(g_turned, back)
            if d:
                skew = jnp.where(wraps, earlier, pairs)
                skew = pltpu.roll(skew, 0, 1, stride=1, stride_axis=0)
                sums.append(jnp.sum(skew, axis=0, keepdims=True))
            earlier = pairs
        yp[0:rows, :] = total
        out = from_pieces(seg_ref, yp, rows, docs) + skip_ref[own, :] * grad
        table[pl.ds(c, rows, stride=channels), :] = out
        lag_grad = jnp.concatenate(sums, axis=0)
        fill_lane_powers(pw_re, pw_im, c, tab_re, tab_im, 1)
        both = jnp.concatenate([lag_grad, lag_grad * lag_place], axis=0).astype(jnp.bfloat16)
        part_re = dot(both, tab_re[...].astype(jnp.bfloat16))
        part_im = dot(both, tab_im[...].astype(jnp.bfloat16))
        dr, di = power_rows(pw_re, pw_im, c, 7, bits, n_lag)
        gr, gi = cmul(dr, di, part_re[0:n_lag], part_im[0:n_lag])
        hr, hi = cmul(dr, di, part_re[n_lag:], part_im[n_lag:])
        gr, gi, hr, hi = (jnp.sum(a, axis=0, keepdims=True) for a in (gr, gi, hr, hi))
        kr, ki, dt = kr_ref[own, :], ki_ref[own, :], dt_ref[own, :]
        rate_grad = -dt * (kr * hr - ki * hi)
        freq_grad = -dt * (kr * hi + ki * hr)
        for at, row_out in enumerate((rate_grad, freq_grad, gr + skip_grad, -gi)):
            grads[at][own, :] = row_out
        step = jnp.sum(
            rate_grad * rate_ref[own, :] + freq_grad * freq_ref[own, :], axis=1, keepdims=True
        )
        for at, one in enumerate((step, skip_grad)):
            thin[at][own, :] = jnp.broadcast_to(one, (1, LANES))
        return unused

    lax.fori_loop(0 * channels // 4, 1 * channels // 4, channel, 0)
    down_sum.turn()
    lax.fori_loop(1 * channels // 4, 2 * channels // 4, channel, 0)
    lax.fori_loop(2 * channels // 4, 3 * channels // 4, channel, 0)
    lax.fori_loop(3 * channels // 4, 4 * channels // 4, channel, 0)
    table_to_rows(table, back, *shape)
    home = lambda peer, slot: dv_ref.at[slot]
    swap_start(back, home, out_send, out_recv, flat, n, n_wt)
    own = pltpu.make_async_copy(back.at[flat], dv_ref.at[flat], local_sem)
    own.start()
    gate_sum.turn()
    for at in range(4):
        all_out[w_me, :, pl.ds(at * states, states)] = grads[at][...]
    for at in range(2):
        all_out[w_me, :, pl.ds(4 * states + at * LANES, LANES)] = thin[at][...]
    block = all_out.at[w_me]
    far_all = [wires.send(block, block, far_to(k)) for k in range(1, outer_wt)]
    near_all = [wires.send(block, block, sibling)]

    for c in tok_sent:
        c.wait_recv()
    result = x_ref[...].astype(wide) + tok[0, 0, 0].astype(wide) + tok_in[0, 0].astype(wide)
    for k in range(1, outer_wt):
        result = result + tok_far[k - 1, 0].astype(wide)
    out_ref[...] = result.astype(low)
    own.wait()
    swap_wait(back, home, out_send, out_recv, flat, n, n_wt)

    for p in range(n):
        turned[pl.ds(p * channels, channels), :] = dv_ref[p].astype(wide)
    value_grad = jnp.transpose(turned[...]) * gelu_pair(pre_ref[...])[1]
    value_low = value_grad.astype(low)
    for w in range(n_wt):
        value_cut[w] = value_low[:, w * v_band : (w + 1) * v_band]
    value_all[w_me] = value_cut[w_me]
    moves = []
    for k in range(outer_wt):
        for j in range(2):
            if k or j:
                w = ((o + k) % outer_wt) * 2 + (i + j) % 2
                moves.append(wires.send(value_cut.at[w], value_all.at[w_me], (s_me, w)))

    mix_sum.turn()
    normed_grad = dot(value_low, value_full[...], 1, 1)
    normed_grad = normed_grad + tok[0, 0, 1].astype(wide) + tok_in[0, 1].astype(wide)
    for k in range(1, outer_wt):
        normed_grad = normed_grad + tok_far[k - 1, 1].astype(wide)
    x32 = x_ref[...].astype(wide)
    centered = x32 - jnp.mean(x32, axis=-1, keepdims=True)
    scale = lax.rsqrt(jnp.mean(centered * centered, axis=-1, keepdims=True) + norm_epsilon)
    xhat = centered * scale
    g = normed_grad * norm_vec[0:1, :]
    inner_grad = g - jnp.mean(g, axis=-1, keepdims=True)
    inner_grad = inner_grad - xhat * jnp.mean(g * xhat, axis=-1, keepdims=True)
    in_grad[...] = pair[w_me, 1].astype(wide) + inner_grad * scale
    vectors = jnp.concatenate(
        [
            jnp.sum(normed_grad * xhat, axis=0, keepdims=True),
            jnp.sum(normed_grad, axis=0, keepdims=True),
            jnp.zeros((14, model_width), wide),
        ],
        axis=0,
    )
    norm_last[...] = vectors

    for c in moves:
        c.wait_recv()
    vector_lanes = min(d_band, LANES)
    for j, z, at in bands(d_band):
        normed = pair[:, 0, :, at].reshape(every, d_band)
        value_s[j, z, 0:d_band, :] = dot(
            normed, value_all[...].reshape(every, v_band), 0, 0
        ).astype(low)
        value_s[j, z, pl.ds(d_band, 16), 0:vector_lanes] = norm_last[:, at].astype(low)
    value_sum.begin()
    down_out[...] = down_sum.end()
    mix_band = mix_sum.end().astype(low)
    gate_band = gate_sum.end().astype(low)
    value_sum.turn()
    for w in range(n_wt):
        gate_cut = gate_band[w * d_rows : (w + 1) * d_rows, :]
        mix_cut = mix_band[w * h_rows : (w + 1) * h_rows, :]
        last_send[w] = jnp.concatenate([gate_cut, mix_cut], axis=0)
    heads = gate_last
    heads[w_me] = last_send[w_me]
    ends = []

    def spread(source, target):
        for k in range(outer_wt):
            for j in range(2):
                if k or j:
                    w = ((o + k) % outer_wt) * 2 + (i + j) % 2
                    ends.append(wires.send(source.at[w], target.at[w_me], (s_me, w)))

    spread(last_send, heads)
    for k in range(1, outer_wt):
        far_all[k - 1].wait_recv()
        block = all_out.at[((o + outer_wt - k) % outer_wt) * 2 + i]
        near_all.append(wires.send(block, block, sibling))
    value_band = value_sum.end()
    tail_send = mix_last
    for w in range(n_wt):
        tail_send[w, 0:d_rows, :] = value_band[w * d_rows : (w + 1) * d_rows, :].astype(low)
        tail_send[w, pl.ds(d_rows, 16), :] = value_band[d_band : d_band + 16, :].astype(low)
    value_last[w_me] = tail_send[w_me]
    spread(tail_send, value_last)
    for c in ends + near_all:
        c.wait_recv()
    wires.sent()
    norm = jnp.zeros((16, v_band), wide)
    for w in range(n_wt):
        norm = norm + value_last[w, pl.ds(d_rows, 16), :].astype(wide)
    norm_out[...] = norm


def back_call(
    pair, gate_w, mix_w, down_w, mixed, v, lags, pre, value_full, norm_vec, x, seg, sid, per,
    seq_count, docs, n_lag, bits, inner_seq, pw_re, pw_im, kr, ki, rate, freq, dt, skip,
):
    n_seq, n_wt = lax.axis_size("seq"), lax.axis_size("wt")
    n = n_seq * n_wt
    channels, states = kr.shape
    rows = seg.shape[0] - 2 * PAD
    local, model_width = x.shape
    width, f_part = mix_w.shape
    d_band, h_band, v_band = model_width // n_seq, width // n_seq, width // n_wt
    d_rows, h_rows = d_band // n_wt, h_band // n_wt
    f_rows = f_part // n_seq
    inner, outer, outer_wt = inner_seq, n_seq // inner_seq, n_wt // 2
    wide = jnp.broadcast_to(skip[:, None], (channels, LANES))
    dt = jnp.broadcast_to(dt, (channels, states))
    low = jnp.bfloat16
    half = lambda *s: pltpu.VMEM(s, low)
    out = jax.ShapeDtypeStruct
    wires = back_wires(n_seq, n_wt, inner)

    def seq_scratch(*block):
        return [
            half(inner, outer, *block), half(max(inner - 1, 1), outer, *block),
            half(max(outer - 1, 1), *block),
        ]

    every = n_wt * local
    return pl.pallas_call(
        functools.partial(back_kernel, n_lag, docs, bits, seq_count, per, inner_seq),
        out_shape=(
            out((local, model_width), low),
            out((local, model_width), jnp.float32),
            out((n_wt, d_rows + h_rows, f_part), low),
            out((n_wt, d_rows + 16, v_band), low),
            out((n_wt, d_rows + 16, v_band), low),
            out((f_rows, model_width), jnp.float32),
            out((16, v_band), jnp.float32),
            out((n_wt, channels, 4 * states + 2 * LANES), jnp.float32),
        ),
        in_specs=[pl.BlockSpec(memory_space=pltpu.VMEM)] * 21,
        out_specs=(pl.BlockSpec(memory_space=pltpu.VMEM),) * 8,
        scratch_shapes=[vmem(PAD + rows, LANES)] * 5
        + [vmem(LANES, states), vmem(LANES, states), vmem(rows * channels, LANES)]
        + [half(n, channels, local)] * 3
        + [half(every, f_part)] * 3
        + [half(2, outer_wt, width, local), half(outer_wt, width, local)]
        + [half(max(outer_wt - 1, 1), width, local)]
        + [half(2, outer_wt, 2, local, model_width), half(outer_wt, 2, local, model_width)]
        + [half(max(outer_wt - 1, 1), 2, local, model_width)]
        + [vmem(f_part, model_width)]
        + seq_scratch(f_rows, model_width)
        + seq_scratch(h_band, f_part)
        + seq_scratch(d_band, f_part)
        + seq_scratch(d_band + 16, v_band)
        + [vmem(width, local), half(n_wt, local, v_band), half(n_wt, local, v_band)]
        + [half(n_wt, d_rows + h_rows, f_part), vmem(16, model_width)]
        + [pltpu.SemaphoreType.DMA((n,))] * 4
        + [pltpu.SemaphoreType.DMA((wires,))] * 2
        + [pltpu.SemaphoreType.DMA]
        + [vmem(channels, states)] * 4
        + [vmem(channels, LANES)] * 2,
        compiler_params=pltpu.CompilerParams(
            vmem_limit_bytes=62 << 20, collective_id=2, has_side_effects=True
        ),
        cost_estimate=pl.CostEstimate(
            flops=60_000_000_000, bytes_accessed=4_000_000, transcendentals=0
        ),
        name="back",
    )(
        pair, gate_w, mix_w, down_w, mixed, v, lags, pre, value_full, norm_vec, x, seg, sid, pw_re,
        pw_im, kr, ki, rate, freq, dt, wide,
    )


BOTH = ("seq", "wt")
norm_epsilon = 1e-05


def gelu_tanh(pre_act):
    return jax.nn.gelu(pre_act, approximate=True)


def layer_norm(token_rows, gain_vec, bias_vec):
    row_mean = jnp.mean(token_rows, axis=-1, keepdims=True)
    centered = token_rows - row_mean
    spread = jnp.mean(centered * centered, axis=-1, keepdims=True)
    return centered * lax.rsqrt(spread + norm_epsilon) * gain_vec + bias_vec


def doc_segments(doc_lengths, seq_length):
    docs = doc_lengths.shape[1]
    upto = jnp.arange(docs)[:, None] >= jnp.arange(docs)[None, :]
    ends = jnp.sum(jnp.where(upto[None], doc_lengths[:, None, :], 0), axis=-1)
    places = jnp.arange(seq_length, dtype=jnp.int32)
    passed = (places[None, None, :] >= ends[:, :, None]).astype(jnp.int32)
    return jnp.sum(passed, axis=1, dtype=jnp.int32)


def after(x, first):
    return lax.optimization_barrier((x, first))[0]


class Ring:
    def __init__(self, axis, inner):
        self.axis, self.size = axis, lax.axis_size(axis)
        self.inner = min(inner, self.size)
        self.outer = self.size // self.inner
        self.me = lax.axis_index(axis)
        self.o, self.i = self.me // self.inner, self.me % self.inner

    def shift(self, x, k, j):
        to = [
            ((p // self.inner + k) % self.outer) * self.inner + (p % self.inner + j) % self.inner
            for p in range(self.size)
        ]
        return lax.ppermute(x, self.axis, list(enumerate(to)))

    def parts(self, x, joined):
        far = [(0, x)] + [(k, self.shift(x, k, 0)) for k in range(1, self.outer)]
        back = lambda k, j: ((self.o - k) % self.outer) * self.inner + (self.i - j) % self.inner
        out = [(back(k, 0), part) for k, part in far]
        for j in range(1, self.inner):
            if joined:
                near = self.shift(jnp.stack([part for _, part in far]), 0, j)
                out += [(back(k, j), near[k]) for k in range(self.outer)]
            else:
                out += [(back(k, j), self.shift(part, 0, j)) for k, part in far]
        return out

    def gather(self, x, joined=True):
        return self.place(self.parts(x, joined))

    def place(self, parts, axis=0):
        first = parts[0][1]
        out = jnp.zeros(first.shape[:axis] + (self.size,) + first.shape[axis:], first.dtype)
        for at, part in parts:
            out = lax.dynamic_update_index_in_dim(out, part, at, axis)
        return out

    def exchange(self, x):
        parts = []
        for k in range(self.outer):
            for j in range(self.inner):
                to = ((self.o + k) % self.outer) * self.inner + (self.i + j) % self.inner
                back = ((self.o - k) % self.outer) * self.inner + (self.i - j) % self.inner
                block = lax.dynamic_index_in_dim(x, to, 0, keepdims=False)
                parts.append((back, block if k == j == 0 else self.shift(block, k, j)))
        return self.place(parts)

    def scatter_sum(self, x):
        wide, narrow = jnp.float32, jnp.bfloat16
        x = x.astype(narrow).reshape((self.outer, self.inner) + x.shape[1:])
        pick = lambda j: lax.dynamic_index_in_dim(x, (self.i + j) % self.inner, 1, keepdims=False)
        held = pick(0).astype(wide)
        for j in range(1, self.inner):
            held = held + self.shift(pick(j), 0, j).astype(wide)
        low = held.astype(narrow)
        take = lambda a, k: lax.dynamic_index_in_dim(a, (self.o + k) % self.outer, 0, keepdims=False)
        total = take(held, 0)
        for k in range(1, self.outer):
            total = total + self.shift(take(low, k), k, 0).astype(wide)
        return total


def on_device(
    inputs, cotangent, doc_lengths, norm_gain, norm_bias, gate_weight, value_weight, mix_weight,
    down_weight, decay_rate, frequency, kernel_re, kernel_im, log_step, skip_gain,
):
    seq_count, local_len, model_width = inputs.shape
    row_count = seq_count * local_len
    n_seq, n_wt = lax.axis_size("seq"), lax.axis_size("wt")
    seq, wt = Ring("seq", 2 if n_seq <= 8 else 8), Ring("wt", 2)
    length = local_len * n_seq
    docs = doc_lengths.shape[1]
    n_lag = length // 2 // LANES
    blocks = length // LANES
    width = value_weight.shape[1]
    d_rows = value_weight.shape[0]
    h_rows = mix_weight.shape[0]
    f_rows = down_weight.shape[0]
    gate_width = gate_weight.shape[1]
    f_part = gate_width // n_wt
    low = jnp.bfloat16

    lengths_all = wt.gather(doc_lengths).reshape(n_wt * seq_count, docs)
    flat = seq.me * n_wt + wt.me
    norm_rows = jnp.zeros((16, width), low)
    norm_rows = lax.dynamic_update_slice(
        norm_rows, jnp.stack([norm_gain, norm_bias]), (0, flat * d_rows % LANES)
    )
    vpack = jnp.concatenate([value_weight, norm_rows], axis=0)

    own_channels = width // (n_seq * n_wt)

    def own(x):
        return lax.dynamic_slice_in_dim(x, wt.me * own_channels, own_channels, 0)

    rate, freq, kr, ki = own(decay_rate), own(frequency), own(kernel_re), own(kernel_im)
    step, skip = own(log_step), own(skip_gain)
    dt, bits, pw_re, pw_im = table_inputs(rate, freq, step, n_lag)
    seg, sid, per = segment_tables(doc_segments(lengths_all, length), docs)

    token_rows = inputs.reshape(row_count, model_width)
    cot_rows = cotangent.reshape(row_count, model_width)
    by_device = (n_seq * n_wt, own_channels, row_count)
    pair, gate_own, mix_own, down_own, mixed, value_ch, lags, value_pre, value_full, norm_vec = front_call(
        token_rows, cot_rows, vpack, gate_weight, mix_weight, down_weight, seg, sid, per, seq_count,
        docs, n_lag, bits, seq.inner, pw_re, pw_im, kr, ki, skip,
    )
    gate_own = gate_own.reshape(model_width, f_part)
    mix_own = mix_own.reshape(width, f_part)
    down_own = down_own.reshape(f_part, model_width)
    mixed = mixed.reshape(n_wt, width, row_count)

    outputs, input_grad, heads, tails, unused, down_piece, norm, packed = back_call(
        pair, gate_own, mix_own, down_own, mixed, value_ch, lags, value_pre, value_full, norm_vec,
        token_rows, seg, sid, per, seq_count, docs, n_lag, bits, seq.inner, pw_re, pw_im, kr, ki, rate,
        freq, dt, skip,
    )
    states = rate.shape[1]
    packed = packed.reshape(n_wt * own_channels, -1)
    mixer_grads = [packed[:, i * states : (i + 1) * states] for i in range(4)]
    mixer_grads += [packed[:, 4 * states], packed[:, 4 * states + LANES]]

    def spread(x):
        rows = x.shape[1]
        x = x.astype(jnp.float32).reshape(n_wt, rows, n_seq, f_rows).transpose(1, 2, 0, 3)
        return x.reshape(rows, gate_width)

    value_piece = tails[:, :d_rows].astype(jnp.float32).transpose(1, 0, 2).reshape(d_rows, width)
    own_lanes = lax.dynamic_slice(norm, (0, wt.me * d_rows), (2, d_rows))
    return (
        outputs.reshape(inputs.shape), input_grad.reshape(inputs.shape), own_lanes[0], own_lanes[1],
        spread(heads[:, :d_rows]), value_piece, spread(heads[:, d_rows:]), down_piece, *mixer_grads,
    )


def solution(mesh):
    in_specs = (
        P("wt", "seq", None),
        P("wt", "seq", None),
        P("wt", None),
        P(("seq", "wt")),
        P(("seq", "wt")),
        P(("seq", "wt"), None),
        P(("seq", "wt"), None),
        P(("seq", "wt"), None),
        P(("seq", "wt"), None),
        P("seq", None),
        P("seq", None),
        P("seq", None),
        P("seq", None),
        P("seq"),
        P("seq"),
    )
    out_specs = (
        P("wt", "seq", None),
        P("wt", "seq", None),
        P(("seq", "wt")),
        P(("seq", "wt")),
        P(("seq", "wt"), None),
        P(("seq", "wt"), None),
        P(("seq", "wt"), None),
        P(("seq", "wt"), None),
        P("seq", None),
        P("seq", None),
        P("seq", None),
        P("seq", None),
        P("seq"),
        P("seq"),
    )
    return jax.shard_map(
        on_device, mesh=mesh, in_specs=in_specs, out_specs=out_specs, check_vma=False
    )
```

```python
import functools

import jax
import jax.numpy as jnp
from jax import lax
from jax.experimental import pallas as pl
from jax.experimental.pallas import tpu as pltpu
from jax.sharding import PartitionSpec as P

LANES = 128
PAD = 16


MESH = pl.DeviceIdType.MESH


def place_of(flat, n_wt):
    return (flat // n_wt, flat % n_wt)


def meet(flat, n, n_wt):
    barrier = pltpu.get_barrier_semaphore()

    def tell(r, unused):
        pl.semaphore_signal(
            barrier, inc=1, device_id=place_of((flat + r) % n, n_wt), device_id_type=MESH
        )
        return unused

    lax.fori_loop(1, n, tell, 0)
    pl.semaphore_wait(barrier, n - 1)


def swap_copy(source, target, send_sem, recv_sem, slot, peer, n_wt):
    return pltpu.make_async_remote_copy(
        src_ref=source, dst_ref=target, send_sem=send_sem.at[slot], recv_sem=recv_sem.at[slot],
        device_id=place_of(peer, n_wt), device_id_type=MESH,
    )


def swap_start(send, target_of, send_sem, recv_sem, flat, n, n_wt):
    def one(r, unused):
        peer = (flat + r) % n
        swap_copy(send.at[peer], target_of(peer, flat), send_sem, recv_sem, r, peer, n_wt).start()
        return unused

    lax.fori_loop(1, n, one, 0)


def swap_wait(send, target_of, send_sem, recv_sem, flat, n, n_wt):
    def one(r, unused):
        source = (flat + n - r) % n
        swap_copy(
            send.at[source], target_of(flat, source), send_sem, recv_sem, r, source, n_wt
        ).wait()
        return unused

    lax.fori_loop(1, n, one, 0)


def rows_to_table(got, table, n_seq, n_wt, seq_count, local_blocks, per, channels):
    for s in range(n_seq):
        for w in range(n_wt):
            for k in range(seq_count):
                for b in range(local_blocks):
                    row = (w * seq_count + k) * per + s * local_blocks + b
                    lanes = pl.ds((k * local_blocks + b) * LANES, LANES)
                    table[pl.ds(row * channels, channels), :] = got[
                        s * n_wt + w, :, lanes
                    ].astype(jnp.float32)


def table_to_rows(table, send, n_seq, n_wt, seq_count, local_blocks, per, channels):
    for s in range(n_seq):
        for w in range(n_wt):
            for k in range(seq_count):
                for b in range(local_blocks):
                    row = (w * seq_count + k) * per + s * local_blocks + b
                    lanes = pl.ds((k * local_blocks + b) * LANES, LANES)
                    send[s * n_wt + w, :, lanes] = table[
                        pl.ds(row * channels, channels), :
                    ].astype(jnp.bfloat16)


def clear_unused(table, seqs, blocks, per, channels):
    for s in range(seqs):
        table[pl.ds((s * per + blocks) * channels, (per - blocks) * channels), :] = jnp.zeros(
            ((per - blocks) * channels, LANES), jnp.float32
        )


def share_over_wt(ref, s_me, w_me, n_wt, send_sem, recv_sem):
    inner = 2
    outer = n_wt // inner
    o, i = w_me // inner, w_me % inner
    other = (s_me, o * inner + 1 - i)

    def copy(block, slot, to):
        return pltpu.make_async_remote_copy(
            src_ref=ref.at[block], dst_ref=ref.at[block], send_sem=send_sem.at[slot],
            recv_sem=recv_sem.at[slot], device_id=to, device_id_type=MESH,
        )

    far = [copy(w_me, k, (s_me, ((o + k) % outer) * inner + i)) for k in range(1, outer)]
    near = [copy(w_me, outer, other)]
    for c in far + near:
        c.start()
    for k in range(1, outer):
        block = ((o + outer - k) % outer) * inner + i
        far[k - 1].wait_recv()
        c = copy(block, outer + k, other)
        c.start()
        near.append(c)
    for c in far:
        c.wait_send()
    for c in near:
        c.wait()


def cmul(ar, ai, br, bi):
    return ar * br - ai * bi, ar * bi + ai * br


def power_rows(pw_re, pw_im, c, first, count, rows):
    width = pw_re.shape[2]
    place = lax.broadcasted_iota(jnp.int32, (rows, width), 0)
    re = jnp.ones((rows, width), jnp.float32)
    im = jnp.zeros((rows, width), jnp.float32)
    for bit in range(count):
        on = (place & (1 << bit)) != 0
        fr = jnp.where(on, pw_re[first + bit, pl.ds(c, 1), :], 1.0)
        fi = jnp.where(on, pw_im[first + bit, pl.ds(c, 1), :], 0.0)
        re, im = cmul(re, im, fr, fi)
    return re, im


def fill_lane_powers(pw_re, pw_im, c, tab_re, tab_im, extra):
    re, im = power_rows(pw_re, pw_im, c, 0, 3, 8)
    if extra:
        re, im = cmul(re, im, pw_re[0, pl.ds(c, 1), :], pw_im[0, pl.ds(c, 1), :])
    tab_re[0:8, :] = re
    tab_im[0:8, :] = im
    have, bit = 8, 3
    while have < LANES:
        re, im = cmul(
            tab_re[0:have, :],
            tab_im[0:have, :],
            pw_re[bit, pl.ds(c, 1), :],
            pw_im[bit, pl.ds(c, 1), :],
        )
        tab_re[have : 2 * have, :] = re
        tab_im[have : 2 * have, :] = im
        have, bit = 2 * have, bit + 1


def to_pieces(seg, val, rows, docs):
    total = jnp.zeros((rows, LANES), jnp.float32)
    for j in range(docs):
        at = pl.ds(PAD - j, rows)
        total = total + jnp.where(seg[at, :] == j, val[at, :], 0.0)
    return total


def from_pieces(seg, piece, rows, docs):
    own = seg[pl.ds(PAD, rows), :]
    total = jnp.zeros((rows, LANES), jnp.float32)
    for j in range(docs):
        total = total + jnp.where(own == j, piece[pl.ds(j, rows), :], 0.0)
    return total


def toeplitz(lags, d, last, lower, before):
    if d < last:
        row = jnp.broadcast_to(lags[d : d + 1, :], (LANES, LANES))
        here = pltpu.roll(row, 0, 1, stride=1, stride_axis=0)
    else:
        here = jnp.zeros((LANES, LANES), jnp.float32)
    return jnp.where(lower, here, before).astype(jnp.bfloat16), here


def dot(a, b, ca=1, cb=0):
    return lax.dot_general(a, b, (((ca,), (cb,)), ((), ())), preferred_element_type=jnp.float32)


def vmem(*shape):
    return pltpu.VMEM(shape, jnp.float32)


def own_column(row_ref, first, count):
    size = row_ref.shape[1]
    lane = lax.broadcasted_iota(jnp.int32, (count, size), 1)
    place = lax.broadcasted_iota(jnp.int32, (count, size), 0)
    return jnp.sum(jnp.where(lane == place + first, row_ref[...], 0.0), axis=1, keepdims=True)


def own_rows(ref, w_me, n_wt, count):
    out = ref[0:count, :]
    for w in range(1, n_wt):
        out = jnp.where(w_me == w, ref[w * count : (w + 1) * count, :], out)
    return out


def fill_powers(rate, freq, dt, pw_re, pw_im):
    for p in range(pw_re.shape[0]):
        if p % 4:
            re, im = cmul(re, im, re, im)
        else:
            mag, angle = jnp.exp(-rate * dt * float(1 << p)), freq * dt * float(1 << p)
            re, im = mag * jnp.cos(angle), mag * jnp.sin(angle)
        pw_re[p] = re
        pw_im[p] = im


def fill_segments(lens, seg_ref, sid_ref, docs, blocks, per, seqs):
    rows = seg_ref.shape[0]
    seg_ref[0:PAD, :] = jnp.full((PAD, LANES), -1, jnp.int32)
    sid_ref[0:PAD, :] = jnp.full((PAD, LANES), -2, jnp.int32)
    seg_ref[rows - PAD : rows, :] = jnp.full((PAD, LANES), -1, jnp.int32)
    sid_ref[rows - PAD : rows, :] = jnp.full((PAD, LANES), -2, jnp.int32)
    row = lax.broadcasted_iota(jnp.int32, (per, LANES), 0)
    position = row * LANES + lax.broadcasted_iota(jnp.int32, (per, LANES), 1)
    group = seqs // lens.shape[0]
    for q in range(seqs):
        ends = jnp.zeros((1, 1), jnp.int32)
        seg = jnp.zeros((per, LANES), jnp.int32)
        for j in range(docs):
            ends = ends + lens[q // group, q % group : q % group + 1, j : j + 1]
            seg = seg + (position >= ends).astype(jnp.int32)
        seg = jnp.where(row < blocks, seg, -1)
        at = pl.ds(PAD + q * per, per)
        seg_ref[at, :] = seg
        best = jnp.full((per, LANES), -1, jnp.int32)
        for i in range(blocks):
            one = seg[i : i + 1, :]
            best = jnp.maximum(best, jnp.where(one + i == row, one, -1))
        best = jnp.max(best.astype(jnp.float32), axis=1, keepdims=True).astype(jnp.int32)
        best = jnp.where(best >= 0, best + docs * q, -1)
        sid_ref[at, :] = jnp.broadcast_to(best, (per, LANES))


class Wires:
    def __init__(self, send_sem, recv_sem):
        self.send_sem, self.recv_sem, self.used, self.open = send_sem, recv_sem, 0, []

    def send(self, source, target, to):
        c = pltpu.make_async_remote_copy(
            src_ref=source, dst_ref=target, send_sem=self.send_sem.at[self.used],
            recv_sem=self.recv_sem.at[self.used], device_id=to, device_id_type=MESH,
        )
        self.used += 1
        self.open.append(c)
        c.start()
        return c

    def sent(self):
        for c in self.open:
            c.wait_send()
        self.open = []


class SeqGather:
    def __init__(self, ref, send_sem, recv_sem, so, si, outer, inner, w_me):
        self.ref, self.send_sem, self.recv_sem = ref, send_sem, recv_sem
        self.so, self.si, self.outer, self.inner, self.w_me = so, si, outer, inner, w_me

    def copy(self, z, slot, to_z, j):
        block = self.ref.at[z * self.inner + self.si]
        to = (to_z * self.inner + (self.si + j) % self.inner, self.w_me)
        return pltpu.make_async_remote_copy(
            src_ref=block, dst_ref=block, send_sem=self.send_sem.at[slot],
            recv_sem=self.recv_sem.at[slot], device_id=to, device_id_type=MESH,
        )

    def along(self, up, k, z):
        slot = (0 if up else self.outer) + k
        return self.copy(z, slot, self.so + 1 if up else self.so - 1, 0)

    def across(self, z, j):
        return self.copy(z, 2 * self.outer + z * self.inner + j, self.so, j)

    def ends(self, up):
        return self.so < self.outer - 1 if up else self.so > 0

    def launch(self, z, k, ups):
        for up in ups:
            if k < self.outer:
                pl.when(self.ends(up))(lambda up=up: self.along(up, k, z).start())
        for j in range(1, self.inner):
            self.across(z, j).start()

    def begin(self):
        self.launch(self.so, 1, (True, False))

    def hop(self, k):
        for up in (True, False):
            z = self.so - k if up else self.so + k
            there = z >= 0 if up else z < self.outer

            @pl.when(there)
            def _():
                self.along(up, k, z).wait_recv()
                self.launch(z, k + 1, (up,))

    def end(self):
        for z in range(self.outer):
            for j in range(1, self.inner):
                block = self.copy(z, 2 * self.outer + z * self.inner + j, self.so, j)
                block.wait_recv()
                block.wait_send()
        for k in range(1, self.outer):
            for up in (True, False):
                z = self.so - k + 1 if up else self.so + k - 1
                from_here = (z >= 0 if up else z < self.outer) & self.ends(up)
                pl.when(from_here)(lambda up=up, k=k, z=z: self.along(up, k, z).wait_send())


def rms(x32):
    mean = jnp.mean(x32, axis=-1, keepdims=True)
    centered = x32 - mean
    spread = jnp.mean(centered * centered, axis=-1, keepdims=True)
    return centered * lax.rsqrt(spread + norm_epsilon)


def regroup(x, n_seq, n_wt, width):
    cut = lambda s, w: x[:, (s * n_wt + w) * width : (s * n_wt + w + 1) * width]
    return [jnp.concatenate([cut(s, w) for s in range(n_seq)], axis=1) for w in range(n_wt)]


def front_wires(n_seq, n_wt):
    value = (n_seq - 1) + n_seq * (n_wt // 2 - 1) + n_seq * (n_wt // 2)
    weights = 2 * (n_wt - 1)
    tokens = 2 * (n_wt // 2 - 1) + 2 * (n_wt // 2)
    mixed = 2 * ((n_wt // 2 - 1) + n_wt // 2)
    return value + weights + tokens + mixed


def front_kernel(
    n_lag, docs, bits, seq_count, per, inner_seq,
    x_ref, cot_ref, value_in, gain_in, bias_in, gate_in, mix_in, down_in, lens_in, rate_ref, freq_ref,
    kr_all, ki_all, step_ref, skip_all,
    pair, gate_out, mix_out, down_out, mixed_ref, v_ref, lag_ref, pre_ref, value_full, norm_out,
    seg_ref, sid_ref,
    lens, pw_re, pw_im, kr_ref, ki_ref, skip_ref, vf, vp, yp, tab_re, tab_im, table, got, back, front, xhat, act_send, gate_cut, mix_cut,
    in_send, in_recv, out_send, out_recv, wire_send, wire_recv, local_sem, *hop_sems,
):
    channels, rows, _ = v_ref.shape
    n_seq, n_wt = lax.axis_size("seq"), lax.axis_size("wt")
    n = n_seq * n_wt
    s_me, w_me = lax.axis_index("seq"), lax.axis_index("wt")
    flat = s_me * n_wt + w_me
    row_count, model_width = x_ref.shape
    width = pre_ref.shape[1]
    d_rows, h_rows, f_rows = gate_in.shape[0], mix_in.shape[0], down_in.shape[0]
    local_blocks = row_count // LANES // seq_count
    shape = (n_seq, n_wt, seq_count, local_blocks, per, channels)
    outer_wt = n_wt // 2
    o, i = w_me // 2, w_me % 2
    sibling = o * 2 + 1 - i
    far_to = lambda k: ((o + k) % outer_wt) * 2 + i
    far_from = lambda k: ((o + outer_wt - k) % outer_wt) * 2 + i
    outer_seq = n_seq // inner_seq
    so, si = s_me // inner_seq, s_me % inner_seq
    rings = [
        SeqGather(ref, hop_sems[2 * at], hop_sems[2 * at + 1], so, si, outer_seq, inner_seq, w_me)
        for at, ref in enumerate((down_out, gate_out, mix_out))
    ]
    down_ring, gate_ring, mix_ring = rings
    wires = Wires(wire_send, wire_recv)

    meet(flat, n, n_wt)

    lens[w_me, 0:seq_count, 0:docs] = lens_in[...]
    block = lens.at[w_me]
    far_lens = [wires.send(block, block, (s_me, far_to(k))) for k in range(1, outer_wt)]
    near_lens = [wires.send(block, block, (s_me, sibling))]

    norm_rows = jnp.concatenate(
        [gain_in[...], bias_in[...], jnp.zeros((14, d_rows), jnp.bfloat16)], axis=0
    ).astype(jnp.float32)
    norm_rows = jnp.concatenate([norm_rows, jnp.zeros((16, LANES - d_rows), jnp.float32)], axis=1)
    norm_rows = pltpu.roll(norm_rows, (flat * d_rows) % LANES, 1)
    front[s_me, w_me, 0:16, :] = jnp.zeros((16, width), jnp.bfloat16)
    front[s_me, w_me, 0:16, 0:LANES] = norm_rows.astype(jnp.bfloat16)
    front[s_me, w_me, pl.ds(16, d_rows), :] = value_in[...]
    first = []
    for k in range(1, n_seq):
        to = ((s_me + k) % n_seq, w_me)
        first.append(wires.send(front.at[s_me, w_me], front.at[s_me, w_me], to))

    second, third = [], []

    def spread_value(s):
        block = front.at[s, w_me]
        for k in range(1, outer_wt):
            second.append((s, k, wires.send(block, block, (s_me, far_to(k)))))
        third.append(wires.send(block, block, (s_me, sibling)))

    spread_value(s_me)
    down_out[s_me] = down_in[...]
    down_ring.begin()

    for ref, cut in ((gate_in, gate_cut), (mix_in, mix_cut)):
        whole = ref[...].astype(jnp.float32)
        for w, part in enumerate(regroup(whole, n_seq, n_wt, f_rows)):
            cut[w] = part.astype(jnp.bfloat16)
    gate_out[s_me, w_me] = gate_cut[w_me]
    mix_out[s_me, w_me] = mix_cut[w_me]
    turn = []
    for source, target in ((gate_cut, gate_out), (mix_cut, mix_out)):
        for k in range(outer_wt):
            for j in range(2):
                if k or j:
                    w = ((o + k) % outer_wt) * 2 + (i + j) % 2
                    turn.append(wires.send(source.at[w], target.at[s_me, w_me], (s_me, w)))

    chunk = min(32, row_count)

    def normalise(r, unused):
        at = pl.ds(r * chunk, chunk)
        xhat[at, :] = rms(x_ref[at, :].astype(jnp.float32))
        return unused

    lax.fori_loop(0, row_count // chunk, normalise, 0)
    pair[w_me, 1] = cot_ref[...]
    mine = lambda ref: own_rows(ref, w_me, n_wt, channels)
    fill_powers(
        mine(rate_ref), mine(freq_ref),
        jnp.exp(own_column(step_ref, w_me * channels, channels)), pw_re, pw_im,
    )
    kr_ref[...] = mine(kr_all)
    ki_ref[...] = mine(ki_all)
    skip_ref[...] = jnp.broadcast_to(
        own_column(skip_all, w_me * channels, channels), (channels, LANES)
    )

    for k in range(1, n_seq):
        first[k - 1].wait_recv()
        spread_value((s_me + n_seq - k) % n_seq)

    for c in turn[: n_wt - 1]:
        c.wait_recv()
    gate_ring.begin()
    for c in turn[n_wt - 1 :]:
        c.wait_recv()
    mix_ring.begin()
    if outer_seq > 1:
        down_ring.hop(1)
    for k in range(1, outer_wt):
        far_lens[k - 1].wait_recv()
        block = lens.at[far_from(k)]
        near_lens.append(wires.send(block, block, (s_me, sibling)))
    for s, k, c in second:
        c.wait_recv()
        block = front.at[s, far_from(k)]
        third.append(wires.send(block, block, (s_me, sibling)))
    for c in third + near_lens:
        c.wait_recv()

    for f in range(n):
        value_full[pl.ds(f * d_rows, d_rows), :] = front[f // n_wt, f % n_wt, pl.ds(16, d_rows), :]
    share = LANES // d_rows
    for b in range(model_width // LANES):
        total = jnp.zeros((2, LANES), jnp.float32)
        for f in range(b * share, (b + 1) * share):
            total = total + front[f // n_wt, f % n_wt, 0:16, 0:LANES].astype(jnp.float32)[0:2]
        norm_out[:, pl.ds(b * LANES, LANES)] = total

    def project(r, unused):
        at = pl.ds(pl.multiple_of(r * LANES, LANES), LANES)
        normed = (xhat[at, :] * norm_out[0:1, :] + norm_out[1:2, :]).astype(jnp.bfloat16)
        pair[w_me, 0, at, :] = normed
        pre = dot(normed, value_full[...])
        pre_ref[at, :] = pre
        turned = jnp.transpose(gelu_tanh(pre))
        for p in range(n):
            act_send[p, :, at] = turned[p * channels : (p + 1) * channels, :].astype(jnp.bfloat16)
        return unused

    lax.fori_loop(0, row_count // LANES, project, 0)
    into = lambda peer, slot: got.at[slot]
    swap_start(act_send, into, in_send, in_recv, flat, n, n_wt)
    got[flat] = act_send[flat]
    fill_segments(lens, seg_ref, sid_ref, docs, n_seq * local_blocks, per, n_wt * seq_count)

    if outer_seq > 1:
        gate_ring.hop(1)
        mix_ring.hop(1)
    clear_unused(table, n_wt * seq_count, n_seq * local_blocks, per, channels)
    zero_pad = jnp.zeros((PAD, LANES), jnp.float32)
    vf[0:PAD, :] = zero_pad
    vp[0:PAD, :] = zero_pad
    yp[pl.ds(rows, PAD), :] = zero_pad
    lower = lax.broadcasted_iota(jnp.int32, (LANES, LANES), 1) >= lax.broadcasted_iota(
        jnp.int32, (LANES, LANES), 0
    )
    swap_wait(act_send, into, in_send, in_recv, flat, n, n_wt)

    far_pair = []
    for at in range(2):
        block = pair.at[w_me, at]
        for k in range(1, outer_wt):
            far_pair.append((k, at, wires.send(block, block, (s_me, far_to(k)))))
    near_pair = [wires.send(pair.at[w_me, at], pair.at[w_me, at], (s_me, sibling)) for at in range(2)]

    rows_to_table(got, table, *shape)

    def channel(c, unused):
        fill_lane_powers(pw_re, pw_im, c, tab_re, tab_im, 0)
        dr, di = power_rows(pw_re, pw_im, c, 7, bits, n_lag)
        ar, ai = cmul(dr, di, kr_ref[pl.ds(c, 1), :], ki_ref[pl.ds(c, 1), :])
        lags = dot(ar.astype(jnp.bfloat16), tab_re[...].astype(jnp.bfloat16), 1, 1) - dot(
            ai.astype(jnp.bfloat16), tab_im[...].astype(jnp.bfloat16), 1, 1
        )
        lag_ref[c] = lags
        val = table[pl.ds(c, rows, stride=channels), :]
        v_ref[c] = val.astype(jnp.bfloat16)
        vf[pl.ds(PAD, rows), :] = val
        vp[pl.ds(PAD, rows), :] = to_pieces(seg_ref, vf, rows, docs)
        sid = sid_ref[pl.ds(PAD, rows), :]
        before = jnp.zeros((LANES, LANES), jnp.float32)
        total = jnp.zeros((rows, LANES), jnp.float32)
        for d in range(n_lag + 1):
            at = pl.ds(PAD - d, rows)
            x = jnp.where(sid_ref[at, :] == sid, vp[at, :], 0.0).astype(jnp.bfloat16)
            t, before = toeplitz(lags, d, n_lag, lower, before)
            total = total + dot(x, t)
        yp[0:rows, :] = total
        out = from_pieces(seg_ref, yp, rows, docs) + skip_ref[pl.ds(c, 1), :] * val
        table[pl.ds(c, rows, stride=channels), :] = out
        return unused

    hops = [(ring, k) for k in range(2, outer_seq) for ring in rings]
    runs = min(4, channels)
    for run in range(runs):
        lax.fori_loop(run * channels // runs, (run + 1) * channels // runs, channel, 0)
        for ring, k in hops[run * len(hops) // (runs + 1) : (run + 1) * len(hops) // (runs + 1)]:
            ring.hop(k)
    table_to_rows(table, back, *shape)
    home = lambda peer, slot: mixed_ref.at[peer % n_wt, slot]
    swap_start(back, home, out_send, out_recv, flat, n, n_wt)
    own = pltpu.make_async_copy(back.at[flat], mixed_ref.at[w_me, flat], local_sem)
    own.start()
    for ring, k in hops[runs * len(hops) // (runs + 1) :]:
        ring.hop(k)
    own.wait()
    swap_wait(back, home, out_send, out_recv, flat, n, n_wt)

    block = mixed_ref.at[w_me]
    far_mixed = [wires.send(block, block, (s_me, far_to(k))) for k in range(1, outer_wt)]
    ends = [wires.send(block, block, (s_me, sibling))]
    for k, at, c in far_pair:
        c.wait_recv()
        block = pair.at[far_from(k), at]
        near_pair.append(wires.send(block, block, (s_me, sibling)))
    for k in range(1, outer_wt):
        far_mixed[k - 1].wait_recv()
        block = mixed_ref.at[far_from(k)]
        ends.append(wires.send(block, block, (s_me, sibling)))
    for c in near_pair + ends:
        c.wait_recv()
    for ring in rings:
        ring.end()
    wires.sent()


def front_call(
    x, cot, value, gain, bias, gate, mix, down, lens, rate, freq, kr, ki, step, skip, n_lag, inner_seq,
):
    n_seq, n_wt = lax.axis_size("seq"), lax.axis_size("wt")
    n = n_seq * n_wt
    seq_count, docs = lens.shape
    local, model_width = x.shape
    states = kr.shape[1]
    width = value.shape[1]
    channels = width // n
    blocks = n_seq * local // seq_count // LANES
    per = -(-(blocks + docs) // 8) * 8
    rows = n_wt * seq_count * per
    bits = (n_lag - 1).bit_length()
    f_part = gate.shape[1] // n_wt
    low = jnp.bfloat16
    wires = front_wires(n_seq, n_wt)
    hops = (2 + inner_seq) * (n_seq // inner_seq)
    out = jax.ShapeDtypeStruct
    table = out((rows + 2 * PAD, LANES), jnp.int32)
    return pl.pallas_call(
        functools.partial(front_kernel, n_lag, docs, bits, seq_count, per, inner_seq),
        out_shape=(
            out((n_wt, 2, local, model_width), low),
            out((n_seq, n_wt) + (gate.shape[0], f_part), low),
            out((n_seq, n_wt) + (mix.shape[0], f_part), low),
            out((n_seq,) + down.shape, low),
            out((n_wt, n, channels, local), low),
            out((channels, rows, LANES), low),
            out((channels, n_lag, LANES), jnp.float32),
            out((local, width), jnp.float32),
            out((model_width, width), low),
            out((2, model_width), jnp.float32),
            table, table,
        ),
        in_specs=[pl.BlockSpec(memory_space=pltpu.VMEM)] * 15,
        out_specs=(pl.BlockSpec(memory_space=pltpu.VMEM),) * 12,
        scratch_shapes=[pltpu.VMEM((n_wt, 8, LANES), jnp.int32)]
        + [vmem(7 + bits, channels, states)] * 2
        + [vmem(channels, states)] * 2
        + [vmem(channels, LANES)]
        + [vmem(PAD + rows, LANES)] * 3
        + [vmem(LANES, states), vmem(LANES, states), vmem(rows * channels, LANES)]
        + [pltpu.VMEM((n, channels, local), low)] * 2
        + [pltpu.VMEM((n_seq, n_wt, 16 + value.shape[0], width), low), vmem(local, model_width)]
        + [pltpu.VMEM((n, channels, local), low)]
        + [pltpu.VMEM((n_wt, gate.shape[0], f_part), low), pltpu.VMEM((n_wt, mix.shape[0], f_part), low)]
        + [pltpu.SemaphoreType.DMA((n,))] * 4
        + [pltpu.SemaphoreType.DMA((wires,))] * 2
        + [pltpu.SemaphoreType.DMA]
        + [pltpu.SemaphoreType.DMA((hops,))] * 6,
        compiler_params=pltpu.CompilerParams(
            vmem_limit_bytes=56 << 20, collective_id=1, has_side_effects=True
        ),
        cost_estimate=pl.CostEstimate(
            flops=60_000_000_000, bytes_accessed=4_000_000, transcendentals=0
        ),
        name="front",
    )(x, cot, value, gain, bias, gate, mix, down, lens, rate, freq, kr, ki, step, skip)


GELU_A = 0.7978845608028654
GELU_B = 0.044715


def gelu_pair(v):
    square = v * v
    t = jnp.tanh(GELU_A * (v + GELU_B * v * square))
    half = 0.5 * (1.0 + t)
    slope = half + 0.5 * v * (1.0 - t * t) * (GELU_A * (1.0 + 3.0 * GELU_B * square))
    return v * half, slope


def back_wires(n_seq, n_wt, inner):
    outer = n_seq // inner
    over_seq = 4 * ((inner - 1) + (outer - 1))
    over_wt = 2 * (1 + n_wt // 2 - 1)
    return over_seq + over_wt + 3 * (n_wt - 1) + (n_wt // 2 - 1) + n_wt // 2 + n_wt - 1


class SeqSum:
    def __init__(self, wires, send, near_in, far_in, so, si, outer, inner, s_to):
        self.wires, self.send, self.near_in, self.far_in = wires, send, near_in, far_in
        self.so, self.outer, self.inner, self.s_to = so, outer, inner, s_to

    def begin(self):
        self.near = [
            self.wires.send(self.send.at[j], self.near_in.at[j - 1], self.s_to(0, j))
            for j in range(1, self.inner)
        ]

    def turn(self):
        for c in self.near:
            c.wait_recv()
        for z in range(self.outer):
            total = self.send[0, z].astype(jnp.float32)
            for j in range(1, self.inner):
                total = total + self.near_in[j - 1, z].astype(jnp.float32)
            self.send[0, z] = total.astype(jnp.bfloat16)
        self.far = []
        for k in range(1, self.outer):
            z = (self.so + k) % self.outer
            self.far.append(
                self.wires.send(self.send.at[0, z], self.far_in.at[k - 1], self.s_to(k, 0))
            )

    def end(self):
        for c in self.far:
            c.wait_recv()
        total = self.send[0, self.so].astype(jnp.float32)
        for k in range(1, self.outer):
            total = total + self.far_in[k - 1].astype(jnp.float32)
        return total


def back_kernel(
    n_lag, docs, bits, seq_count, per, inner_seq,
    pair, gate_w, mix_w, down_w, mixed, v_ref, lag_ref, pre_ref, value_full, norm_vec, x_ref,
    seg_ref, sid_ref, rate_all, freq_all, kr_all, ki_all, step_ref, skip_all,
    out_ref, in_grad, gate_last, value_last, mix_last, down_out, norm_out, all_out,
    pw_re, pw_im, kr_ref, ki_ref, rate_ref, freq_ref, dt_ref, skip_ref, vf, gf, vp, gp, yp, tab_re, tab_im, table, got, back, dv_ref,
    product, expand_grad, gate_grad, mg, mg_in, mg_far, tok, tok_in, tok_far,
    down_flat, down_s, down_n, down_f, mix_s, mix_n, mix_f, gate_s, gate_n, gate_f,
    value_s, value_n, value_f, turned, value_cut, value_all, last_send, norm_last,
    in_send, in_recv, out_send, out_recv, wire_send, wire_recv, local_sem, *held,
):
    grads, thin = held[:4], held[4:]
    low, wide = jnp.bfloat16, jnp.float32
    channels, rows, _ = v_ref.shape
    states = kr_all.shape[1]
    n_seq, n_wt = lax.axis_size("seq"), lax.axis_size("wt")
    n = n_seq * n_wt
    s_me, w_me = lax.axis_index("seq"), lax.axis_index("wt")
    flat = s_me * n_wt + w_me
    row_count, model_width = x_ref.shape
    width = mix_w.shape[0]
    f_part = gate_w.shape[1]
    f_rows = f_part // n_seq
    d_band, h_band, v_band = model_width // n_seq, width // n_seq, width // n_wt
    d_rows, h_rows = d_band // n_wt, h_band // n_wt
    local_blocks = row_count // LANES // seq_count
    shape = (n_seq, n_wt, seq_count, local_blocks, per, channels)
    outer_wt = n_wt // 2
    o, i = w_me // 2, w_me % 2
    sibling = (s_me, o * 2 + 1 - i)
    far_to = lambda k: (s_me, ((o + k) % outer_wt) * 2 + i)
    outer_seq = n_seq // inner_seq
    so, si = s_me // inner_seq, s_me % inner_seq
    s_to = lambda k, j: (((so + k) % outer_seq) * inner_seq + (si + j) % inner_seq, w_me)
    wires = Wires(wire_send, wire_recv)
    sums = lambda send, near_in, far_in: SeqSum(
        wires, send, near_in, far_in, so, si, outer_seq, inner_seq, s_to
    )
    down_sum, mix_sum = sums(down_s, down_n, down_f), sums(mix_s, mix_n, mix_f)
    gate_sum, value_sum = sums(gate_s, gate_n, gate_f), sums(value_s, value_n, value_f)

    meet(flat, n, n_wt)

    def tokens(t, unused):
        j, k = 1 - t // outer_wt, outer_wt - 1 - t % outer_wt
        w = ((o + k) % outer_wt) * 2 + (i + j) % 2
        at = pl.ds(pl.multiple_of(w * row_count, row_count), row_count)
        act, slope = gelu_pair(dot(pair[w, 0], gate_w[...]))
        from_out = dot(pair[w, 1], down_w[...], 1, 1)
        expand = dot(mixed[w], mix_w[...], 0, 0)
        product[at, :] = (expand * act).astype(low)
        gate_grad[at, :] = (from_out * expand * slope).astype(low)
        grad = (from_out * act).astype(low)
        expand_grad[at, :] = grad
        mg[j, k] = dot(mix_w[...], grad, 1, 1).astype(low)
        return unused

    lax.fori_loop(0, outer_wt, tokens, 0)
    near = wires.send(mg.at[1], mg_in, sibling)
    lax.fori_loop(outer_wt, n_wt, tokens, 0)
    piece = min(256, f_part)
    every = n_wt * row_count

    def down_part(r, unused):
        at = pl.ds(pl.multiple_of(r * piece, piece), piece)
        cot = pair[:, 1].reshape(every, model_width)
        down_flat[at, :] = dot(product[:, at], cot, 0, 0)
        return unused

    lax.fori_loop(0, f_part // piece, down_part, 0)
    def bands(size):
        for s in range(n_seq):
            j = (s % inner_seq + inner_seq - si) % inner_seq
            yield j, s // inner_seq, slice(s * size, (s + 1) * size)

    for j, z, at in bands(f_rows):
        down_s[j, z] = down_flat[at, :].astype(low)
    down_sum.begin()
    near.wait_recv()
    far = []
    for k in range(1, outer_wt):
        mg[0, k] = (mg[0, k].astype(wide) + mg_in[k].astype(wide)).astype(low)
        far.append(wires.send(mg.at[0, k], mg_far.at[k - 1], far_to(k)))

    for j, z, at in bands(d_band):
        normed = pair[:, 0, :, at].reshape(every, d_band)
        gate_s[j, z] = dot(normed, gate_grad[...], 0, 0).astype(low)

    total = mg[0, 0].astype(wide) + mg_in[0].astype(wide)
    for k in range(1, outer_wt):
        far[k - 1].wait_recv()
        total = total + mg_far[k - 1].astype(wide)
    turned[...] = total
    for p in range(n):
        back[p] = turned[p * channels : (p + 1) * channels, :].astype(low)
    into = lambda peer, slot: got.at[slot]
    swap_start(back, into, in_send, in_recv, flat, n, n_wt)
    got[flat] = back[flat]

    for j, z, at in bands(h_band):
        total = dot(mixed[0, at, :], expand_grad[0:row_count, :])
        for w in range(1, n_wt):
            total = total + dot(
                mixed[w, at, :], expand_grad[w * row_count : (w + 1) * row_count, :]
            )
        mix_s[j, z] = total.astype(low)

    def token_part(t, unused):
        j, k = 1 - t // outer_wt, outer_wt - 1 - t % outer_wt
        w = ((o + k) % outer_wt) * 2 + (i + j) % 2
        at = pl.ds(pl.multiple_of(w * row_count, row_count), row_count)
        tok[j, k, 0] = dot(product[at, :], down_w[...]).astype(low)
        tok[j, k, 1] = dot(gate_grad[at, :], gate_w[...], 1, 1).astype(low)
        return unused

    lax.fori_loop(0, outer_wt, token_part, 0)
    tok_near = wires.send(tok.at[1], tok_in, sibling)
    lax.fori_loop(outer_wt, n_wt, token_part, 0)

    mine = lambda ref: own_rows(ref, w_me, n_wt, channels)
    for one, every_one in ((kr_ref, kr_all), (ki_ref, ki_all), (rate_ref, rate_all), (freq_ref, freq_all)):
        one[...] = mine(every_one)
    dt = jnp.exp(own_column(step_ref, w_me * channels, channels))
    dt_ref[...] = jnp.broadcast_to(dt, (channels, states))
    fill_powers(rate_ref[...], freq_ref[...], dt, pw_re, pw_im)
    skip_ref[...] = jnp.broadcast_to(
        own_column(skip_all, w_me * channels, channels), (channels, LANES)
    )
    zero_pad = jnp.zeros((PAD, LANES), wide)
    clear_unused(table, n_wt * seq_count, n_seq * local_blocks, per, channels)
    vf[0:PAD, :] = zero_pad
    gf[0:PAD, :] = zero_pad
    vp[0:PAD, :] = zero_pad
    gp[pl.ds(rows, PAD), :] = zero_pad
    yp[pl.ds(rows, PAD), :] = zero_pad
    tok_near.wait_recv()
    tok_sent = []
    for k in range(1, outer_wt):
        for a in range(2):
            tok[0, k, a] = (tok[0, k, a].astype(wide) + tok_in[k, a].astype(wide)).astype(low)
        tok_sent.append(wires.send(tok.at[0, k], tok_far.at[k - 1], far_to(k)))
    swap_wait(back, into, in_send, in_recv, flat, n, n_wt)
    gate_sum.begin()
    mix_sum.begin()
    rows_to_table(got, table, *shape)

    lane = lax.broadcasted_iota(jnp.int32, (LANES, LANES), 1)
    row = lax.broadcasted_iota(jnp.int32, (LANES, LANES), 0)
    lower = lane >= row
    wraps = lane + row >= LANES
    flip = (lane + row == LANES - 1).astype(jnp.bfloat16)
    lag_place = (
        lax.broadcasted_iota(jnp.int32, (n_lag, LANES), 0) * LANES
        + lax.broadcasted_iota(jnp.int32, (n_lag, LANES), 1)
        + 1
    ).astype(jnp.float32)

    def channel(c, unused):
        own = pl.ds(c, 1)
        val = v_ref[c].astype(jnp.float32)
        grad = table[pl.ds(c, rows, stride=channels), :]
        vf[pl.ds(PAD, rows), :] = val
        gf[pl.ds(PAD, rows), :] = grad
        skip_grad = jnp.sum(jnp.sum(val * grad, axis=0, keepdims=True), axis=1, keepdims=True)
        g_piece = to_pieces(seg_ref, gf, rows, docs)
        gp[0:rows, :] = g_piece
        v_piece = to_pieces(seg_ref, vf, rows, docs).astype(jnp.bfloat16)
        vp[pl.ds(PAD, rows), :] = dot(v_piece, flip)
        g_turned = jnp.transpose(g_piece).astype(jnp.bfloat16)
        sid = sid_ref[pl.ds(PAD, rows), :]
        lags = lag_ref[c]
        before = jnp.zeros((LANES, LANES), jnp.float32)
        total = jnp.zeros((rows, LANES), jnp.float32)
        earlier = None
        sums = []
        for d in range(n_lag + 1):
            ahead = pl.ds(PAD + d, rows)
            x = jnp.where(sid_ref[ahead, :] == sid, gp[pl.ds(d, rows), :], 0.0)
            t, before = toeplitz(lags, d, n_lag, lower, before)
            total = total + dot(x.astype(jnp.bfloat16), t, 1, 1)
            at = pl.ds(PAD - d, rows)
            back = jnp.where(sid_ref[at, :] == sid, vp[at, :], 0.0).astype(jnp.bfloat16)
            pairs = dot(g_turned, back)
            if d:
                skew = jnp.where(wraps, earlier, pairs)
                skew = pltpu.roll(skew, 0, 1, stride=1, stride_axis=0)
                sums.append(jnp.sum(skew, axis=0, keepdims=True))
            earlier = pairs
        yp[0:rows, :] = total
        out = from_pieces(seg_ref, yp, rows, docs) + skip_ref[own, :] * grad
        table[pl.ds(c, rows, stride=channels), :] = out
        lag_grad = jnp.concatenate(sums, axis=0)
        fill_lane_powers(pw_re, pw_im, c, tab_re, tab_im, 1)
        both = jnp.concatenate([lag_grad, lag_grad * lag_place], axis=0).astype(jnp.bfloat16)
        part_re = dot(both, tab_re[...].astype(jnp.bfloat16))
        part_im = dot(both, tab_im[...].astype(jnp.bfloat16))
        dr, di = power_rows(pw_re, pw_im, c, 7, bits, n_lag)
        gr, gi = cmul(dr, di, part_re[0:n_lag], part_im[0:n_lag])
        hr, hi = cmul(dr, di, part_re[n_lag:], part_im[n_lag:])
        gr, gi, hr, hi = (jnp.sum(a, axis=0, keepdims=True) for a in (gr, gi, hr, hi))
        kr, ki, dt = kr_ref[own, :], ki_ref[own, :], dt_ref[own, :]
        rate_grad = -dt * (kr * hr - ki * hi)
        freq_grad = -dt * (kr * hi + ki * hr)
        for at, row_out in enumerate((rate_grad, freq_grad, gr + skip_grad, -gi)):
            grads[at][own, :] = row_out
        step = jnp.sum(
            rate_grad * rate_ref[own, :] + freq_grad * freq_ref[own, :], axis=1, keepdims=True
        )
        for at, one in enumerate((step, skip_grad)):
            thin[at][own, :] = jnp.broadcast_to(one, (1, LANES))
        return unused

    lax.fori_loop(0 * channels // 4, 1 * channels // 4, channel, 0)
    down_sum.turn()
    lax.fori_loop(1 * channels // 4, 2 * channels // 4, channel, 0)
    lax.fori_loop(2 * channels // 4, 3 * channels // 4, channel, 0)
    lax.fori_loop(3 * channels // 4, 4 * channels // 4, channel, 0)
    table_to_rows(table, back, *shape)
    home = lambda peer, slot: dv_ref.at[slot]
    swap_start(back, home, out_send, out_recv, flat, n, n_wt)
    own = pltpu.make_async_copy(back.at[flat], dv_ref.at[flat], local_sem)
    own.start()
    gate_sum.turn()
    for at in range(4):
        all_out[w_me, :, pl.ds(at * states, states)] = grads[at][...]
    for at in range(2):
        all_out[w_me, :, pl.ds(4 * states + at * LANES, LANES)] = thin[at][...]
    block = all_out.at[w_me]
    far_all = [wires.send(block, block, far_to(k)) for k in range(1, outer_wt)]
    near_all = [wires.send(block, block, sibling)]

    for c in tok_sent:
        c.wait_recv()
    result = x_ref[...].astype(wide) + tok[0, 0, 0].astype(wide) + tok_in[0, 0].astype(wide)
    for k in range(1, outer_wt):
        result = result + tok_far[k - 1, 0].astype(wide)
    out_ref[...] = result.astype(low)
    own.wait()
    swap_wait(back, home, out_send, out_recv, flat, n, n_wt)

    for p in range(n):
        turned[pl.ds(p * channels, channels), :] = dv_ref[p].astype(wide)
    value_grad = jnp.transpose(turned[...]) * gelu_pair(pre_ref[...])[1]
    value_low = value_grad.astype(low)
    for w in range(n_wt):
        value_cut[w] = value_low[:, w * v_band : (w + 1) * v_band]
    value_all[w_me] = value_cut[w_me]
    moves = []
    for k in range(outer_wt):
        for j in range(2):
            if k or j:
                w = ((o + k) % outer_wt) * 2 + (i + j) % 2
                moves.append(wires.send(value_cut.at[w], value_all.at[w_me], (s_me, w)))

    mix_sum.turn()
    normed_grad = dot(value_low, value_full[...], 1, 1)
    normed_grad = normed_grad + tok[0, 0, 1].astype(wide) + tok_in[0, 1].astype(wide)
    for k in range(1, outer_wt):
        normed_grad = normed_grad + tok_far[k - 1, 1].astype(wide)
    x32 = x_ref[...].astype(wide)
    centered = x32 - jnp.mean(x32, axis=-1, keepdims=True)
    scale = lax.rsqrt(jnp.mean(centered * centered, axis=-1, keepdims=True) + norm_epsilon)
    xhat = centered * scale
    g = normed_grad * norm_vec[0:1, :]
    inner_grad = g - jnp.mean(g, axis=-1, keepdims=True)
    inner_grad = inner_grad - xhat * jnp.mean(g * xhat, axis=-1, keepdims=True)
    in_grad[...] = pair[w_me, 1].astype(wide) + inner_grad * scale
    vectors = jnp.concatenate(
        [
            jnp.sum(normed_grad * xhat, axis=0, keepdims=True),
            jnp.sum(normed_grad, axis=0, keepdims=True),
            jnp.zeros((14, model_width), wide),
        ],
        axis=0,
    )
    norm_last[...] = vectors

    for c in moves:
        c.wait_recv()
    vector_lanes = min(d_band, LANES)
    for j, z, at in bands(d_band):
        normed = pair[:, 0, :, at].reshape(every, d_band)
        value_s[j, z, 0:d_band, :] = dot(
            normed, value_all[...].reshape(every, v_band), 0, 0
        ).astype(low)
        value_s[j, z, pl.ds(d_band, 16), 0:vector_lanes] = norm_last[:, at].astype(low)
    value_sum.begin()
    down_out[...] = down_sum.end()
    mix_band = mix_sum.end().astype(low)
    gate_band = gate_sum.end().astype(low)
    value_sum.turn()
    for w in range(n_wt):
        gate_cut = gate_band[w * d_rows : (w + 1) * d_rows, :]
        mix_cut = mix_band[w * h_rows : (w + 1) * h_rows, :]
        last_send[w] = jnp.concatenate([gate_cut, mix_cut], axis=0)
    heads = gate_last
    heads[w_me] = last_send[w_me]
    ends = []

    def spread(source, target):
        for k in range(outer_wt):
            for j in range(2):
                if k or j:
                    w = ((o + k) % outer_wt) * 2 + (i + j) % 2
                    ends.append(wires.send(source.at[w], target.at[w_me], (s_me, w)))

    spread(last_send, heads)
    for k in range(1, outer_wt):
        far_all[k - 1].wait_recv()
        block = all_out.at[((o + outer_wt - k) % outer_wt) * 2 + i]
        near_all.append(wires.send(block, block, sibling))
    value_band = value_sum.end()
    tail_send = mix_last
    for w in range(n_wt):
        tail_send[w, 0:d_rows, :] = value_band[w * d_rows : (w + 1) * d_rows, :].astype(low)
        tail_send[w, pl.ds(d_rows, 16), :] = value_band[d_band : d_band + 16, :].astype(low)
    value_last[w_me] = tail_send[w_me]
    spread(tail_send, value_last)
    for c in ends + near_all:
        c.wait_recv()
    wires.sent()
    norm = jnp.zeros((16, v_band), wide)
    for w in range(n_wt):
        norm = norm + value_last[w, pl.ds(d_rows, 16), :].astype(wide)
    norm_out[...] = norm


def back_call(
    pair, gate_w, mix_w, down_w, mixed, v, lags, pre, value_full, norm_vec, x, seg, sid, rate, freq, kr,
    ki, step, skip, seq_count, docs, n_lag, inner_seq,
):
    n_seq, n_wt = lax.axis_size("seq"), lax.axis_size("wt")
    n = n_seq * n_wt
    channels, rows, _ = v.shape
    states = kr.shape[1]
    per = rows // (n_wt * seq_count)
    bits = (n_lag - 1).bit_length()
    local, model_width = x.shape
    width, f_part = mix_w.shape
    d_band, h_band, v_band = model_width // n_seq, width // n_seq, width // n_wt
    d_rows, h_rows = d_band // n_wt, h_band // n_wt
    f_rows = f_part // n_seq
    inner, outer, outer_wt = inner_seq, n_seq // inner_seq, n_wt // 2
    low = jnp.bfloat16
    half = lambda *s: pltpu.VMEM(s, low)
    out = jax.ShapeDtypeStruct
    wires = back_wires(n_seq, n_wt, inner)

    def seq_scratch(*block):
        return [
            half(inner, outer, *block), half(max(inner - 1, 1), outer, *block),
            half(max(outer - 1, 1), *block),
        ]

    every = n_wt * local
    return pl.pallas_call(
        functools.partial(back_kernel, n_lag, docs, bits, seq_count, per, inner_seq),
        out_shape=(
            out((local, model_width), low),
            out((local, model_width), jnp.float32),
            out((n_wt, d_rows + h_rows, f_part), low),
            out((n_wt, d_rows + 16, v_band), low),
            out((n_wt, d_rows + 16, v_band), low),
            out((f_rows, model_width), jnp.float32),
            out((16, v_band), jnp.float32),
            out((n_wt, channels, 4 * states + 2 * LANES), jnp.float32),
        ),
        in_specs=[pl.BlockSpec(memory_space=pltpu.VMEM)] * 19,
        out_specs=(pl.BlockSpec(memory_space=pltpu.VMEM),) * 8,
        scratch_shapes=[vmem(7 + bits, channels, states)] * 2
        + [vmem(channels, states)] * 5
        + [vmem(channels, LANES)]
        + [vmem(PAD + rows, LANES)] * 5
        + [vmem(LANES, states), vmem(LANES, states), vmem(rows * channels, LANES)]
        + [half(n, channels, local)] * 3
        + [half(every, f_part)] * 3
        + [half(2, outer_wt, width, local), half(outer_wt, width, local)]
        + [half(max(outer_wt - 1, 1), width, local)]
        + [half(2, outer_wt, 2, local, model_width), half(outer_wt, 2, local, model_width)]
        + [half(max(outer_wt - 1, 1), 2, local, model_width)]
        + [vmem(f_part, model_width)]
        + seq_scratch(f_rows, model_width)
        + seq_scratch(h_band, f_part)
        + seq_scratch(d_band, f_part)
        + seq_scratch(d_band + 16, v_band)
        + [vmem(width, local), half(n_wt, local, v_band), half(n_wt, local, v_band)]
        + [half(n_wt, d_rows + h_rows, f_part), vmem(16, model_width)]
        + [pltpu.SemaphoreType.DMA((n,))] * 4
        + [pltpu.SemaphoreType.DMA((wires,))] * 2
        + [pltpu.SemaphoreType.DMA]
        + [vmem(channels, states)] * 4
        + [vmem(channels, LANES)] * 2,
        compiler_params=pltpu.CompilerParams(
            vmem_limit_bytes=62 << 20, collective_id=2, has_side_effects=True
        ),
        cost_estimate=pl.CostEstimate(
            flops=60_000_000_000, bytes_accessed=4_000_000, transcendentals=0
        ),
        name="back",
    )(
        pair, gate_w, mix_w, down_w, mixed, v, lags, pre, value_full, norm_vec, x, seg, sid, rate, freq,
        kr, ki, step, skip,
    )


def finish_kernel(
    out_ref, grad_ref, heads, tails, down_ref, norm_ref, all_ref,
    outputs, in_grad, gain, bias, gate, value, mix, down, rate, freq, kr, ki, step, skip,
):
    n_seq, n_wt = lax.axis_size("seq"), lax.axis_size("wt")
    w_me = lax.axis_index("wt")
    wide = jnp.float32
    d_rows, h_rows = gate.shape[0], mix.shape[0]
    f_rows = heads.shape[2] // n_seq
    channels, states = all_ref.shape[1], rate.shape[1]
    outputs[...] = out_ref[...]
    in_grad[...] = grad_ref[...]
    down[...] = down_ref[...]
    for ref, first, rows in ((gate, 0, d_rows), (mix, d_rows, h_rows)):
        parts = [heads[w].astype(wide)[first : first + rows, :] for w in range(n_wt)]
        cut = [
            parts[w][:, s * f_rows : (s + 1) * f_rows] for s in range(n_seq) for w in range(n_wt)
        ]
        ref[...] = jnp.concatenate(cut, axis=1)
    value[...] = jnp.concatenate(
        [tails[w].astype(wide)[0:d_rows, :] for w in range(n_wt)], axis=1
    )
    share = norm_ref.shape[1]
    own = pltpu.roll(norm_ref[...], (share - w_me * d_rows) % share, 1)[:, 0:d_rows]
    gain[...] = own[0:1, :]
    bias[...] = own[1:2, :]
    for at, ref in enumerate((rate, freq, kr, ki)):
        for w in range(n_wt):
            ref[pl.ds(w * channels, channels), :] = all_ref[w, :, pl.ds(at * states, states)]
    total = n_wt * channels
    lane = lax.broadcasted_iota(jnp.int32, (channels, LANES), 1)
    place = lax.broadcasted_iota(jnp.int32, (channels, LANES), 0)
    for at, ref in enumerate((step, skip)):
        row = jnp.zeros((1, LANES), wide)
        for w in range(n_wt):
            thin = all_ref[w, :, pl.ds(4 * states + at * LANES, LANES)]
            hit = jnp.where(lane == place + w * channels, thin, 0.0)
            row = row + jnp.sum(hit, axis=0, keepdims=True)
        ref[...] = row[:, 0:total]


def finish_call(out, grad, heads, tails, down, norm, packed, gate_width, d_rows, h_rows, states):
    n_wt, channels, _ = packed.shape
    total = n_wt * channels
    wide = jnp.float32
    shape = jax.ShapeDtypeStruct
    full = shape((total, states), wide)
    return pl.pallas_call(
        finish_kernel,
        out_shape=(
            shape(out.shape, out.dtype), shape(grad.shape, wide), shape((1, d_rows), wide),
            shape((1, d_rows), wide), shape((d_rows, gate_width), wide),
            shape((d_rows, n_wt * tails.shape[2]), wide), shape((h_rows, gate_width), wide),
            shape(down.shape, wide), full, full, full, full, shape((1, total), wide),
            shape((1, total), wide),
        ),
        in_specs=[pl.BlockSpec(memory_space=pltpu.VMEM)] * 7,
        out_specs=(pl.BlockSpec(memory_space=pltpu.VMEM),) * 14,
        compiler_params=pltpu.CompilerParams(vmem_limit_bytes=60 << 20),
        name="finish",
    )(out, grad, heads, tails, down, norm, packed)


BOTH = ("seq", "wt")
norm_epsilon = 1e-05


def gelu_tanh(pre_act):
    return jax.nn.gelu(pre_act, approximate=True)


def on_device(
    inputs, cotangent, doc_lengths, norm_gain, norm_bias, gate_weight, value_weight, mix_weight,
    down_weight, decay_rate, frequency, kernel_re, kernel_im, log_step, skip_gain,
):
    seq_count, local_len, model_width = inputs.shape
    n_seq, n_wt = lax.axis_size("seq"), lax.axis_size("wt")
    inner_seq = 2 if n_seq <= 8 else 8
    rows = lambda x: x.reshape(seq_count * local_len, model_width)
    line = lambda x: x.reshape(1, -1)
    width, gate_width = mix_weight.shape[0] * n_seq * n_wt, gate_weight.shape[1]
    f_part = gate_width // n_wt
    n_lag = local_len * n_seq // 2 // LANES
    params = (decay_rate, frequency, kernel_re, kernel_im, line(log_step), line(skip_gain))
    pair, gate_own, mix_own, down_own, mixed, value_ch, lags, pre, value_full, norm, seg, sid = front_call(
        rows(inputs), rows(cotangent), value_weight, line(norm_gain), line(norm_bias), gate_weight,
        mix_weight, down_weight, doc_lengths, *params, n_lag, inner_seq,
    )
    raw = back_call(
        pair, gate_own.reshape(model_width, f_part), mix_own.reshape(width, f_part),
        down_own.reshape(f_part, model_width), mixed.reshape(n_wt, width, -1), value_ch, lags, pre,
        value_full, norm, rows(inputs), seg, sid, *params, seq_count, doc_lengths.shape[1], n_lag,
        inner_seq,
    )
    out, grad, heads, tails, unused, down, vectors, packed = raw
    done = finish_call(
        out, grad, heads, tails, down, vectors, packed, gate_width, value_weight.shape[0],
        mix_weight.shape[0], kernel_re.shape[1],
    )
    flat = [done[i].reshape(-1) for i in (2, 3, 12, 13)]
    return (
        done[0].reshape(inputs.shape), done[1].reshape(inputs.shape), flat[0], flat[1], *done[4:8],
        *done[8:12], flat[2], flat[3],
    )


def solution(mesh):
    in_specs = (
        P("wt", "seq", None),
        P("wt", "seq", None),
        P("wt", None),
        P(("seq", "wt")),
        P(("seq", "wt")),
        P(("seq", "wt"), None),
        P(("seq", "wt"), None),
        P(("seq", "wt"), None),
        P(("seq", "wt"), None),
        P("seq", None),
        P("seq", None),
        P("seq", None),
        P("seq", None),
        P("seq"),
        P("seq"),
    )
    out_specs = (
        P("wt", "seq", None),
        P("wt", "seq", None),
        P(("seq", "wt")),
        P(("seq", "wt")),
        P(("seq", "wt"), None),
        P(("seq", "wt"), None),
        P(("seq", "wt"), None),
        P(("seq", "wt"), None),
        P("seq", None),
        P("seq", None),
        P("seq", None),
        P("seq", None),
        P("seq"),
        P("seq"),
    )
    return jax.shard_map(
        on_device, mesh=mesh, in_specs=in_specs, out_specs=out_specs, check_vma=False
    )
```

```python
import functools

import jax
import jax.numpy as jnp
from jax import lax
from jax.experimental import pallas as pl
from jax.experimental.pallas import tpu as pltpu
from jax.sharding import PartitionSpec as P

LANES = 128
PAD = 16


MESH = pl.DeviceIdType.MESH


def place_of(flat, n_wt):
    return (flat // n_wt, flat % n_wt)


def meet(flat, n, n_wt):
    barrier = pltpu.get_barrier_semaphore()

    def tell(r, unused):
        pl.semaphore_signal(
            barrier, inc=1, device_id=place_of((flat + r) % n, n_wt), device_id_type=MESH
        )
        return unused

    lax.fori_loop(1, n, tell, 0)
    pl.semaphore_wait(barrier, n - 1)


def swap_copy(source, target, send_sem, recv_sem, slot, peer, n_wt):
    return pltpu.make_async_remote_copy(
        src_ref=source, dst_ref=target, send_sem=send_sem.at[slot], recv_sem=recv_sem.at[slot],
        device_id=place_of(peer, n_wt), device_id_type=MESH,
    )


def swap_start(send, target_of, send_sem, recv_sem, flat, n, n_wt):
    def one(r, unused):
        peer = (flat + r) % n
        swap_copy(send.at[peer], target_of(peer, flat), send_sem, recv_sem, r, peer, n_wt).start()
        return unused

    lax.fori_loop(1, n, one, 0)


def swap_wait(send, target_of, send_sem, recv_sem, flat, n, n_wt):
    def one(r, unused):
        source = (flat + n - r) % n
        swap_copy(
            send.at[source], target_of(flat, source), send_sem, recv_sem, r, source, n_wt
        ).wait()
        return unused

    lax.fori_loop(1, n, one, 0)


def rows_to_table(got, table, n_seq, n_wt, seq_count, local_blocks, per, channels):
    for s in range(n_seq):
        for w in range(n_wt):
            for k in range(seq_count):
                for b in range(local_blocks):
                    row = (w * seq_count + k) * per + s * local_blocks + b
                    lanes = pl.ds((k * local_blocks + b) * LANES, LANES)
                    table[pl.ds(row * channels, channels), :] = got[
                        s * n_wt + w, :, lanes
                    ].astype(jnp.float32)


def table_to_rows(table, send, n_seq, n_wt, seq_count, local_blocks, per, channels):
    for s in range(n_seq):
        for w in range(n_wt):
            for k in range(seq_count):
                for b in range(local_blocks):
                    row = (w * seq_count + k) * per + s * local_blocks + b
                    lanes = pl.ds((k * local_blocks + b) * LANES, LANES)
                    send[s * n_wt + w, :, lanes] = table[
                        pl.ds(row * channels, channels), :
                    ].astype(jnp.bfloat16)


def clear_unused(table, seqs, blocks, per, channels):
    for s in range(seqs):
        table[pl.ds((s * per + blocks) * channels, (per - blocks) * channels), :] = jnp.zeros(
            ((per - blocks) * channels, LANES), jnp.float32
        )


def share_over_wt(ref, s_me, w_me, n_wt, send_sem, recv_sem):
    inner = 2
    outer = n_wt // inner
    o, i = w_me // inner, w_me % inner
    other = (s_me, o * inner + 1 - i)

    def copy(block, slot, to):
        return pltpu.make_async_remote_copy(
            src_ref=ref.at[block], dst_ref=ref.at[block], send_sem=send_sem.at[slot],
            recv_sem=recv_sem.at[slot], device_id=to, device_id_type=MESH,
        )

    far = [copy(w_me, k, (s_me, ((o + k) % outer) * inner + i)) for k in range(1, outer)]
    near = [copy(w_me, outer, other)]
    for c in far + near:
        c.start()
    for k in range(1, outer):
        block = ((o + outer - k) % outer) * inner + i
        far[k - 1].wait_recv()
        c = copy(block, outer + k, other)
        c.start()
        near.append(c)
    for c in far:
        c.wait_send()
    for c in near:
        c.wait()


def cmul(ar, ai, br, bi):
    return ar * br - ai * bi, ar * bi + ai * br


def power_rows(pw_re, pw_im, c, first, count, rows):
    width = pw_re.shape[2]
    place = lax.broadcasted_iota(jnp.int32, (rows, width), 0)
    re = jnp.ones((rows, width), jnp.float32)
    im = jnp.zeros((rows, width), jnp.float32)
    for bit in range(count):
        on = (place & (1 << bit)) != 0
        fr = jnp.where(on, pw_re[first + bit, pl.ds(c, 1), :], 1.0)
        fi = jnp.where(on, pw_im[first + bit, pl.ds(c, 1), :], 0.0)
        re, im = cmul(re, im, fr, fi)
    return re, im


def fill_lane_powers(pw_re, pw_im, c, tab_re, tab_im, extra):
    re, im = power_rows(pw_re, pw_im, c, 0, 3, 8)
    if extra:
        re, im = cmul(re, im, pw_re[0, pl.ds(c, 1), :], pw_im[0, pl.ds(c, 1), :])
    tab_re[0:8, :] = re
    tab_im[0:8, :] = im
    have, bit = 8, 3
    while have < LANES:
        re, im = cmul(
            tab_re[0:have, :],
            tab_im[0:have, :],
            pw_re[bit, pl.ds(c, 1), :],
            pw_im[bit, pl.ds(c, 1), :],
        )
        tab_re[have : 2 * have, :] = re
        tab_im[have : 2 * have, :] = im
        have, bit = 2 * have, bit + 1


def to_pieces(seg, val, rows, docs):
    total = jnp.zeros((rows, LANES), jnp.float32)
    for j in range(docs):
        at = pl.ds(PAD - j, rows)
        total = total + jnp.where(seg[at, :] == j, val[at, :], 0.0)
    return total


def from_pieces(seg, piece, rows, docs):
    own = seg[pl.ds(PAD, rows), :]
    total = jnp.zeros((rows, LANES), jnp.float32)
    for j in range(docs):
        total = total + jnp.where(own == j, piece[pl.ds(j, rows), :], 0.0)
    return total


def toeplitz(lags, d, last, lower, before):
    if d < last:
        row = jnp.broadcast_to(lags[d : d + 1, :], (LANES, LANES))
        here = pltpu.roll(row, 0, 1, stride=1, stride_axis=0)
    else:
        here = jnp.zeros((LANES, LANES), jnp.float32)
    return jnp.where(lower, here, before).astype(jnp.bfloat16), here


def dot(a, b, ca=1, cb=0):
    return lax.dot_general(a, b, (((ca,), (cb,)), ((), ())), preferred_element_type=jnp.float32)


def vmem(*shape):
    return pltpu.VMEM(shape, jnp.float32)


def own_column(row_ref, first, count):
    size = row_ref.shape[1]
    lane = lax.broadcasted_iota(jnp.int32, (count, size), 1)
    place = lax.broadcasted_iota(jnp.int32, (count, size), 0)
    return jnp.sum(jnp.where(lane == place + first, row_ref[...], 0.0), axis=1, keepdims=True)


def own_rows(ref, w_me, n_wt, count):
    out = ref[0:count, :]
    for w in range(1, n_wt):
        out = jnp.where(w_me == w, ref[w * count : (w + 1) * count, :], out)
    return out


def fill_powers(rate, freq, dt, pw_re, pw_im):
    for p in range(pw_re.shape[0]):
        if p % 4:
            re, im = cmul(re, im, re, im)
        else:
            mag, angle = jnp.exp(-rate * dt * float(1 << p)), freq * dt * float(1 << p)
            re, im = mag * jnp.cos(angle), mag * jnp.sin(angle)
        pw_re[p] = re
        pw_im[p] = im


def fill_segments(lens, seg_ref, sid_ref, docs, blocks, per, seqs):
    rows = seg_ref.shape[0]
    seg_ref[0:PAD, :] = jnp.full((PAD, LANES), -1, jnp.int32)
    sid_ref[0:PAD, :] = jnp.full((PAD, LANES), -2, jnp.int32)
    seg_ref[rows - PAD : rows, :] = jnp.full((PAD, LANES), -1, jnp.int32)
    sid_ref[rows - PAD : rows, :] = jnp.full((PAD, LANES), -2, jnp.int32)
    row = lax.broadcasted_iota(jnp.int32, (per, LANES), 0)
    position = row * LANES + lax.broadcasted_iota(jnp.int32, (per, LANES), 1)
    group = seqs // lens.shape[0]
    for q in range(seqs):
        ends = jnp.zeros((1, 1), jnp.int32)
        seg = jnp.zeros((per, LANES), jnp.int32)
        for j in range(docs):
            ends = ends + lens[q // group, q % group : q % group + 1, j : j + 1]
            seg = seg + (position >= ends).astype(jnp.int32)
        seg = jnp.where(row < blocks, seg, -1)
        at = pl.ds(PAD + q * per, per)
        seg_ref[at, :] = seg
        best = jnp.full((per, LANES), -1, jnp.int32)
        for i in range(blocks):
            one = seg[i : i + 1, :]
            best = jnp.maximum(best, jnp.where(one + i == row, one, -1))
        best = jnp.max(best.astype(jnp.float32), axis=1, keepdims=True).astype(jnp.int32)
        best = jnp.where(best >= 0, best + docs * q, -1)
        sid_ref[at, :] = jnp.broadcast_to(best, (per, LANES))


class Wires:
    def __init__(self, send_sem, recv_sem):
        self.send_sem, self.recv_sem, self.used, self.open = send_sem, recv_sem, 0, []

    def send(self, source, target, to):
        c = pltpu.make_async_remote_copy(
            src_ref=source, dst_ref=target, send_sem=self.send_sem.at[self.used],
            recv_sem=self.recv_sem.at[self.used], device_id=to, device_id_type=MESH,
        )
        self.used += 1
        self.open.append(c)
        c.start()
        return c

    def sent(self):
        for c in self.open:
            c.wait_send()
        self.open = []


class SeqGather:
    def __init__(self, ref, send_sem, recv_sem, so, si, outer, inner, w_me):
        self.ref, self.send_sem, self.recv_sem = ref, send_sem, recv_sem
        self.so, self.si, self.outer, self.inner, self.w_me = so, si, outer, inner, w_me

    def copy(self, z, slot, to_z, j):
        block = self.ref.at[z * self.inner + self.si]
        to = (to_z * self.inner + (self.si + j) % self.inner, self.w_me)
        return pltpu.make_async_remote_copy(
            src_ref=block, dst_ref=block, send_sem=self.send_sem.at[slot],
            recv_sem=self.recv_sem.at[slot], device_id=to, device_id_type=MESH,
        )

    def along(self, up, k, z):
        slot = (0 if up else self.outer) + k
        return self.copy(z, slot, self.so + 1 if up else self.so - 1, 0)

    def across(self, z, j):
        return self.copy(z, 2 * self.outer + z * self.inner + j, self.so, j)

    def ends(self, up):
        return self.so < self.outer - 1 if up else self.so > 0

    def launch(self, z, k, ups):
        for up in ups:
            if k < self.outer:
                pl.when(self.ends(up))(lambda up=up: self.along(up, k, z).start())
        for j in range(1, self.inner):
            self.across(z, j).start()

    def begin(self):
        self.launch(self.so, 1, (True, False))

    def hop(self, k):
        for up in (True, False):
            z = self.so - k if up else self.so + k
            there = z >= 0 if up else z < self.outer

            @pl.when(there)
            def _():
                self.along(up, k, z).wait_recv()
                self.launch(z, k + 1, (up,))

    def end(self):
        for z in range(self.outer):
            for j in range(1, self.inner):
                block = self.copy(z, 2 * self.outer + z * self.inner + j, self.so, j)
                block.wait_recv()
                block.wait_send()
        for k in range(1, self.outer):
            for up in (True, False):
                z = self.so - k + 1 if up else self.so + k - 1
                from_here = (z >= 0 if up else z < self.outer) & self.ends(up)
                pl.when(from_here)(lambda up=up, k=k, z=z: self.along(up, k, z).wait_send())


def rms(x32):
    mean = jnp.mean(x32, axis=-1, keepdims=True)
    centered = x32 - mean
    spread = jnp.mean(centered * centered, axis=-1, keepdims=True)
    return centered * lax.rsqrt(spread + norm_epsilon)


def regroup(x, n_seq, n_wt, width):
    cut = lambda s, w: x[:, (s * n_wt + w) * width : (s * n_wt + w + 1) * width]
    return [jnp.concatenate([cut(s, w) for s in range(n_seq)], axis=1) for w in range(n_wt)]


def front_wires(n_seq, n_wt):
    value = (n_seq - 1) + n_seq * (n_wt // 2 - 1) + n_seq * (n_wt // 2)
    weights = 2 * (n_wt - 1)
    tokens = 2 * (n_wt // 2 - 1) + 2 * (n_wt // 2)
    mixed = 2 * ((n_wt // 2 - 1) + n_wt // 2)
    return value + weights + tokens + mixed


def front_kernel(
    n_lag, docs, bits, seq_count, per, inner_seq, loads,
    x_ref, cot_ref, value_in, gain_in, bias_in, gate_in, mix_in, down_in, lens_in, rate_ref, freq_ref,
    kr_all, ki_all, step_ref, skip_all,
    pair, gate_out, mix_out, down_out, mixed_ref, v_ref, lag_ref, pre_ref, value_full, norm_out,
    seg_ref, sid_ref,
    lens, pw_re, pw_im, kr_ref, ki_ref, skip_ref, vf, vp, yp, tab_re, tab_im, table, got, back, front, xhat, act_send, gate_cut, mix_cut,
    in_send, in_recv, out_send, out_recv, wire_send, wire_recv, local_sem, *hop_sems,
):
    channels, rows, _ = v_ref.shape
    n_seq, n_wt = lax.axis_size("seq"), lax.axis_size("wt")
    n = n_seq * n_wt
    s_me, w_me = lax.axis_index("seq"), lax.axis_index("wt")
    flat = s_me * n_wt + w_me
    row_count, model_width = x_ref.shape
    width = pre_ref.shape[1]
    d_rows, h_rows, f_rows = gate_in.shape[0], mix_in.shape[0], down_in.shape[0]
    local_blocks = row_count // LANES // seq_count
    shape = (n_seq, n_wt, seq_count, local_blocks, per, channels)
    outer_wt = n_wt // 2
    o, i = w_me // 2, w_me % 2
    sibling = o * 2 + 1 - i
    far_to = lambda k: ((o + k) % outer_wt) * 2 + i
    far_from = lambda k: ((o + outer_wt - k) % outer_wt) * 2 + i
    outer_seq = n_seq // inner_seq
    so, si = s_me // inner_seq, s_me % inner_seq
    rings = [
        SeqGather(ref, hop_sems[2 * at], hop_sems[2 * at + 1], so, si, outer_seq, inner_seq, w_me)
        for at, ref in enumerate((down_out, gate_out, mix_out))
    ]
    down_ring, gate_ring, mix_ring = rings
    wires = Wires(wire_send, wire_recv)

    meet(flat, n, n_wt)
    for c in loads:
        c.wait()

    lens[w_me, 0:seq_count, 0:docs] = lens_in[...]
    block = lens.at[w_me]
    far_lens = [wires.send(block, block, (s_me, far_to(k))) for k in range(1, outer_wt)]
    near_lens = [wires.send(block, block, (s_me, sibling))]

    norm_rows = jnp.concatenate(
        [gain_in[...], bias_in[...], jnp.zeros((14, d_rows), jnp.bfloat16)], axis=0
    ).astype(jnp.float32)
    norm_rows = jnp.concatenate([norm_rows, jnp.zeros((16, LANES - d_rows), jnp.float32)], axis=1)
    norm_rows = pltpu.roll(norm_rows, (flat * d_rows) % LANES, 1)
    front[s_me, w_me, 0:16, :] = jnp.zeros((16, width), jnp.bfloat16)
    front[s_me, w_me, 0:16, 0:LANES] = norm_rows.astype(jnp.bfloat16)
    front[s_me, w_me, pl.ds(16, d_rows), :] = value_in[...]
    first = []
    for k in range(1, n_seq):
        to = ((s_me + k) % n_seq, w_me)
        first.append(wires.send(front.at[s_me, w_me], front.at[s_me, w_me], to))

    second, third = [], []

    def spread_value(s):
        block = front.at[s, w_me]
        for k in range(1, outer_wt):
            second.append((s, k, wires.send(block, block, (s_me, far_to(k)))))
        third.append(wires.send(block, block, (s_me, sibling)))

    spread_value(s_me)
    down_out[s_me] = down_in[...]
    down_ring.begin()

    for ref, cut in ((gate_in, gate_cut), (mix_in, mix_cut)):
        whole = ref[...].astype(jnp.float32)
        for w, part in enumerate(regroup(whole, n_seq, n_wt, f_rows)):
            cut[w] = part.astype(jnp.bfloat16)
    gate_out[s_me, w_me] = gate_cut[w_me]
    mix_out[s_me, w_me] = mix_cut[w_me]
    turn = []
    for source, target in ((gate_cut, gate_out), (mix_cut, mix_out)):
        for k in range(outer_wt):
            for j in range(2):
                if k or j:
                    w = ((o + k) % outer_wt) * 2 + (i + j) % 2
                    turn.append(wires.send(source.at[w], target.at[s_me, w_me], (s_me, w)))

    chunk = min(32, row_count)

    def normalise(r, unused):
        at = pl.ds(r * chunk, chunk)
        xhat[at, :] = rms(x_ref[at, :].astype(jnp.float32))
        return unused

    lax.fori_loop(0, row_count // chunk, normalise, 0)
    pair[w_me, 1] = cot_ref[...]
    mine = lambda ref: own_rows(ref, w_me, n_wt, channels)
    fill_powers(
        mine(rate_ref), mine(freq_ref),
        jnp.exp(own_column(step_ref, w_me * channels, channels)), pw_re, pw_im,
    )
    kr_ref[...] = mine(kr_all)
    ki_ref[...] = mine(ki_all)
    skip_ref[...] = jnp.broadcast_to(
        own_column(skip_all, w_me * channels, channels), (channels, LANES)
    )

    for k in range(1, n_seq):
        first[k - 1].wait_recv()
        spread_value((s_me + n_seq - k) % n_seq)

    for c in turn[: n_wt - 1]:
        c.wait_recv()
    gate_ring.begin()
    for c in turn[n_wt - 1 :]:
        c.wait_recv()
    mix_ring.begin()
    if outer_seq > 1:
        down_ring.hop(1)
    for k in range(1, outer_wt):
        far_lens[k - 1].wait_recv()
        block = lens.at[far_from(k)]
        near_lens.append(wires.send(block, block, (s_me, sibling)))
    for s, k, c in second:
        c.wait_recv()
        block = front.at[s, far_from(k)]
        third.append(wires.send(block, block, (s_me, sibling)))
    for c in third + near_lens:
        c.wait_recv()

    for f in range(n):
        value_full[pl.ds(f * d_rows, d_rows), :] = front[f // n_wt, f % n_wt, pl.ds(16, d_rows), :]
    share = LANES // d_rows
    for b in range(model_width // LANES):
        total = jnp.zeros((2, LANES), jnp.float32)
        for f in range(b * share, (b + 1) * share):
            total = total + front[f // n_wt, f % n_wt, 0:16, 0:LANES].astype(jnp.float32)[0:2]
        norm_out[:, pl.ds(b * LANES, LANES)] = total

    def project(r, unused):
        at = pl.ds(pl.multiple_of(r * LANES, LANES), LANES)
        normed = (xhat[at, :] * norm_out[0:1, :] + norm_out[1:2, :]).astype(jnp.bfloat16)
        pair[w_me, 0, at, :] = normed
        pre = dot(normed, value_full[...])
        pre_ref[at, :] = pre
        turned = jnp.transpose(gelu_tanh(pre))
        for p in range(n):
            act_send[p, :, at] = turned[p * channels : (p + 1) * channels, :].astype(jnp.bfloat16)
        return unused

    lax.fori_loop(0, row_count // LANES, project, 0)
    into = lambda peer, slot: got.at[slot]
    swap_start(act_send, into, in_send, in_recv, flat, n, n_wt)
    got[flat] = act_send[flat]
    fill_segments(lens, seg_ref, sid_ref, docs, n_seq * local_blocks, per, n_wt * seq_count)

    if outer_seq > 1:
        gate_ring.hop(1)
        mix_ring.hop(1)
    clear_unused(table, n_wt * seq_count, n_seq * local_blocks, per, channels)
    zero_pad = jnp.zeros((PAD, LANES), jnp.float32)
    vf[0:PAD, :] = zero_pad
    vp[0:PAD, :] = zero_pad
    yp[pl.ds(rows, PAD), :] = zero_pad
    lower = lax.broadcasted_iota(jnp.int32, (LANES, LANES), 1) >= lax.broadcasted_iota(
        jnp.int32, (LANES, LANES), 0
    )
    swap_wait(act_send, into, in_send, in_recv, flat, n, n_wt)

    far_pair = []
    for at in range(2):
        block = pair.at[w_me, at]
        for k in range(1, outer_wt):
            far_pair.append((k, at, wires.send(block, block, (s_me, far_to(k)))))
    near_pair = [wires.send(pair.at[w_me, at], pair.at[w_me, at], (s_me, sibling)) for at in range(2)]

    rows_to_table(got, table, *shape)

    def channel(c, unused):
        fill_lane_powers(pw_re, pw_im, c, tab_re, tab_im, 0)
        dr, di = power_rows(pw_re, pw_im, c, 7, bits, n_lag)
        ar, ai = cmul(dr, di, kr_ref[pl.ds(c, 1), :], ki_ref[pl.ds(c, 1), :])
        lags = dot(ar.astype(jnp.bfloat16), tab_re[...].astype(jnp.bfloat16), 1, 1) - dot(
            ai.astype(jnp.bfloat16), tab_im[...].astype(jnp.bfloat16), 1, 1
        )
        lag_ref[c] = lags
        val = table[pl.ds(c, rows, stride=channels), :]
        v_ref[c] = val.astype(jnp.bfloat16)
        vf[pl.ds(PAD, rows), :] = val
        vp[pl.ds(PAD, rows), :] = to_pieces(seg_ref, vf, rows, docs)
        sid = sid_ref[pl.ds(PAD, rows), :]
        before = jnp.zeros((LANES, LANES), jnp.float32)
        total = jnp.zeros((rows, LANES), jnp.float32)
        for d in range(n_lag + 1):
            at = pl.ds(PAD - d, rows)
            x = jnp.where(sid_ref[at, :] == sid, vp[at, :], 0.0).astype(jnp.bfloat16)
            t, before = toeplitz(lags, d, n_lag, lower, before)
            total = total + dot(x, t)
        yp[0:rows, :] = total
        out = from_pieces(seg_ref, yp, rows, docs) + skip_ref[pl.ds(c, 1), :] * val
        table[pl.ds(c, rows, stride=channels), :] = out
        return unused

    hops = [(ring, k) for k in range(2, outer_seq) for ring in rings]
    runs = min(4, channels)
    for run in range(runs):
        lax.fori_loop(run * channels // runs, (run + 1) * channels // runs, channel, 0)
        for ring, k in hops[run * len(hops) // (runs + 1) : (run + 1) * len(hops) // (runs + 1)]:
            ring.hop(k)
    table_to_rows(table, back, *shape)
    home = lambda peer, slot: mixed_ref.at[peer % n_wt, slot]
    swap_start(back, home, out_send, out_recv, flat, n, n_wt)
    own = pltpu.make_async_copy(back.at[flat], mixed_ref.at[w_me, flat], local_sem)
    own.start()
    for ring, k in hops[runs * len(hops) // (runs + 1) :]:
        ring.hop(k)
    own.wait()
    swap_wait(back, home, out_send, out_recv, flat, n, n_wt)

    block = mixed_ref.at[w_me]
    far_mixed = [wires.send(block, block, (s_me, far_to(k))) for k in range(1, outer_wt)]
    ends = [wires.send(block, block, (s_me, sibling))]
    for k, at, c in far_pair:
        c.wait_recv()
        block = pair.at[far_from(k), at]
        near_pair.append(wires.send(block, block, (s_me, sibling)))
    for k in range(1, outer_wt):
        far_mixed[k - 1].wait_recv()
        block = mixed_ref.at[far_from(k)]
        ends.append(wires.send(block, block, (s_me, sibling)))
    for c in near_pair + ends:
        c.wait_recv()
    for ring in rings:
        ring.end()
    wires.sent()


def front_loading(n_lag, docs, bits, seq_count, per, inner_seq, n_in, *refs):
    sources, held, load_sem = refs[:n_in], refs[-n_in - 1 : -1], refs[-1]
    loads = [
        pltpu.make_async_copy(source, target, load_sem.at[at])
        for at, (source, target) in enumerate(zip(sources, held))
    ]
    for c in loads:
        c.start()
    front_kernel(
        n_lag, docs, bits, seq_count, per, inner_seq, loads, *held, *refs[n_in : -n_in - 1]
    )


def front_call(
    x, cot, value, gain, bias, gate, mix, down, lens, rate, freq, kr, ki, step, skip, n_lag, inner_seq,
):
    n_seq, n_wt = lax.axis_size("seq"), lax.axis_size("wt")
    n = n_seq * n_wt
    seq_count, docs = lens.shape
    local, model_width = x.shape
    states = kr.shape[1]
    width = value.shape[1]
    channels = width // n
    blocks = n_seq * local // seq_count // LANES
    per = -(-(blocks + docs) // 8) * 8
    rows = n_wt * seq_count * per
    bits = (n_lag - 1).bit_length()
    f_part = gate.shape[1] // n_wt
    low = jnp.bfloat16
    wires = front_wires(n_seq, n_wt)
    hops = (2 + inner_seq) * (n_seq // inner_seq)
    out = jax.ShapeDtypeStruct
    arrays = (x, cot, value, gain, bias, gate, mix, down, lens, rate, freq, kr, ki, step, skip)
    table = out((rows + 2 * PAD, LANES), jnp.int32)
    return pl.pallas_call(
        functools.partial(
            front_loading, n_lag, docs, bits, seq_count, per, inner_seq, len(arrays)
        ),
        out_shape=(
            out((n_wt, 2, local, model_width), low),
            out((n_seq, n_wt) + (gate.shape[0], f_part), low),
            out((n_seq, n_wt) + (mix.shape[0], f_part), low),
            out((n_seq,) + down.shape, low),
            out((n_wt, n, channels, local), low),
            out((channels, rows, LANES), low),
            out((channels, n_lag, LANES), jnp.float32),
            out((local, width), jnp.float32),
            out((model_width, width), low),
            out((2, model_width), jnp.float32),
            table, table,
        ),
        in_specs=[pl.BlockSpec(memory_space=pltpu.HBM)] * len(arrays),
        out_specs=(pl.BlockSpec(memory_space=pltpu.VMEM),) * 12,
        scratch_shapes=[pltpu.VMEM((n_wt, 8, LANES), jnp.int32)]
        + [vmem(7 + bits, channels, states)] * 2
        + [vmem(channels, states)] * 2
        + [vmem(channels, LANES)]
        + [vmem(PAD + rows, LANES)] * 3
        + [vmem(LANES, states), vmem(LANES, states), vmem(rows * channels, LANES)]
        + [pltpu.VMEM((n, channels, local), low)] * 2
        + [pltpu.VMEM((n_seq, n_wt, 16 + value.shape[0], width), low), vmem(local, model_width)]
        + [pltpu.VMEM((n, channels, local), low)]
        + [pltpu.VMEM((n_wt, gate.shape[0], f_part), low), pltpu.VMEM((n_wt, mix.shape[0], f_part), low)]
        + [pltpu.SemaphoreType.DMA((n,))] * 4
        + [pltpu.SemaphoreType.DMA((wires,))] * 2
        + [pltpu.SemaphoreType.DMA]
        + [pltpu.SemaphoreType.DMA((hops,))] * 6
        + [pltpu.VMEM(a.shape, a.dtype) for a in arrays]
        + [pltpu.SemaphoreType.DMA((len(arrays),))],
        compiler_params=pltpu.CompilerParams(
            vmem_limit_bytes=(38 if n <= 32 else 58) << 20, collective_id=1, has_side_effects=True
        ),
        cost_estimate=pl.CostEstimate(
            flops=60_000_000_000, bytes_accessed=4_000_000, transcendentals=0
        ),
        name="front",
    )(*[pltpu.with_memory_space_constraint(a, pltpu.HBM) for a in arrays])


GELU_A = 0.7978845608028654
GELU_B = 0.044715


def gelu_pair(v):
    square = v * v
    t = jnp.tanh(GELU_A * (v + GELU_B * v * square))
    half = 0.5 * (1.0 + t)
    slope = half + 0.5 * v * (1.0 - t * t) * (GELU_A * (1.0 + 3.0 * GELU_B * square))
    return v * half, slope


def back_wires(n_seq, n_wt, inner):
    outer = n_seq // inner
    over_seq = 4 * ((inner - 1) * outer + (outer - 1))
    over_wt = 2 * (1 + n_wt // 2 - 1)
    return over_seq + over_wt + 3 * (n_wt - 1) + (n_wt // 2 - 1) + n_wt // 2 + n_wt - 1


class SeqSum:
    def __init__(self, wires, send, near_in, far_in, so, si, outer, inner, s_to):
        self.wires, self.send, self.near_in, self.far_in = wires, send, near_in, far_in
        self.so, self.outer, self.inner, self.s_to = so, outer, inner, s_to
        self.near, self.far, self.held = {}, [], None

    def begin(self, *distances):
        for k in distances or range(1, self.outer + 1):
            k = k % self.outer
            if k in self.near:
                continue
            z = (self.so + k) % self.outer
            self.near[k] = [
                self.wires.send(self.send.at[j, z], self.near_in.at[j - 1, k], self.s_to(0, j))
                for j in range(1, self.inner)
            ]

    def turn(self, *distances):
        for k in distances or range(1, self.outer + 1):
            k = k % self.outer
            if k not in self.near or k in self.far:
                continue
            for c in self.near[k]:
                c.wait_recv()
            z = (self.so + k) % self.outer
            total = self.send[0, z].astype(jnp.float32)
            for j in range(1, self.inner):
                total = total + self.near_in[j - 1, k].astype(jnp.float32)
            self.send[0, z] = total.astype(jnp.bfloat16)
            if k:
                self.near[-k] = self.wires.send(
                    self.send.at[0, z], self.far_in.at[k - 1], self.s_to(k, 0)
                )
            self.far.append(k)

    def end(self):
        total = self.send[0, self.so].astype(jnp.float32)
        for k in range(1, self.outer):
            self.near[-k].wait_recv()
            total = total + self.far_in[k - 1].astype(jnp.float32)
        return total


def back_kernel(
    n_lag, docs, bits, seq_count, per, inner_seq,
    pair, gate_w, mix_w, down_w, mixed, v_ref, lag_ref, pre_ref, value_full, norm_vec, x_ref,
    seg_ref, sid_ref, rate_all, freq_all, kr_all, ki_all, step_ref, skip_all,
    out_ref, in_grad, gate_last, value_last, mix_last, down_out, norm_out, all_out,
    pw_re, pw_im, kr_ref, ki_ref, rate_ref, freq_ref, dt_ref, skip_ref, vf, gf, vp, gp, yp, tab_re, tab_im, table, got, back, dv_ref,
    product, expand_grad, gate_grad, mg, mg_in, mg_far, tok, tok_in, tok_far,
    down_flat, down_s, down_n, down_f, mix_s, mix_n, mix_f, gate_s, gate_n, gate_f,
    value_s, value_n, value_f, turned, value_cut, value_all, last_send, norm_last,
    in_send, in_recv, out_send, out_recv, wire_send, wire_recv, local_sem, *held,
):
    grads, thin = held[:4], held[4:]
    low, wide = jnp.bfloat16, jnp.float32
    channels, rows, _ = v_ref.shape
    states = kr_all.shape[1]
    n_seq, n_wt = lax.axis_size("seq"), lax.axis_size("wt")
    n = n_seq * n_wt
    s_me, w_me = lax.axis_index("seq"), lax.axis_index("wt")
    flat = s_me * n_wt + w_me
    row_count, model_width = x_ref.shape
    width = mix_w.shape[0]
    f_part = gate_w.shape[1]
    f_rows = f_part // n_seq
    d_band, h_band, v_band = model_width // n_seq, width // n_seq, width // n_wt
    d_rows, h_rows = d_band // n_wt, h_band // n_wt
    local_blocks = row_count // LANES // seq_count
    shape = (n_seq, n_wt, seq_count, local_blocks, per, channels)
    outer_wt = n_wt // 2
    o, i = w_me // 2, w_me % 2
    sibling = (s_me, o * 2 + 1 - i)
    far_to = lambda k: (s_me, ((o + k) % outer_wt) * 2 + i)
    outer_seq = n_seq // inner_seq
    so, si = s_me // inner_seq, s_me % inner_seq
    s_to = lambda k, j: (((so + k) % outer_seq) * inner_seq + (si + j) % inner_seq, w_me)
    wires = Wires(wire_send, wire_recv)
    sums = lambda send, near_in, far_in: SeqSum(
        wires, send, near_in, far_in, so, si, outer_seq, inner_seq, s_to
    )
    down_sum, mix_sum = sums(down_s, down_n, down_f), sums(mix_s, mix_n, mix_f)
    gate_sum, value_sum = sums(gate_s, gate_n, gate_f), sums(value_s, value_n, value_f)

    meet(flat, n, n_wt)

    def tokens(t, unused):
        j, k = 1 - t // outer_wt, outer_wt - 1 - t % outer_wt
        w = ((o + k) % outer_wt) * 2 + (i + j) % 2
        at = pl.ds(pl.multiple_of(w * row_count, row_count), row_count)
        act, slope = gelu_pair(dot(pair[w, 0], gate_w[...]))
        from_out = dot(pair[w, 1], down_w[...], 1, 1)
        expand = dot(mixed[w], mix_w[...], 0, 0)
        product[at, :] = (expand * act).astype(low)
        gate_grad[at, :] = (from_out * expand * slope).astype(low)
        grad = (from_out * act).astype(low)
        expand_grad[at, :] = grad
        mg[j, k] = dot(mix_w[...], grad, 1, 1).astype(low)
        return unused

    lax.fori_loop(0, outer_wt, tokens, 0)
    near = wires.send(mg.at[1], mg_in, sibling)
    lax.fori_loop(outer_wt, n_wt, tokens, 0)
    piece = min(256, f_part)
    every = n_wt * row_count

    def down_part(r, unused):
        at = pl.ds(pl.multiple_of(r * piece, piece), piece)
        cot = pair[:, 1].reshape(every, model_width)
        down_flat[at, :] = dot(product[:, at], cot, 0, 0)
        return unused

    lax.fori_loop(0, f_part // piece, down_part, 0)
    def bands(size):
        for s in range(n_seq):
            j = (s % inner_seq + inner_seq - si) % inner_seq
            yield j, s // inner_seq, slice(s * size, (s + 1) * size)

    for j, z, at in bands(f_rows):
        down_s[j, z] = down_flat[at, :].astype(low)
    down_sum.begin(1, 2, 3)
    near.wait_recv()
    far = []
    for k in range(1, outer_wt):
        mg[0, k] = (mg[0, k].astype(wide) + mg_in[k].astype(wide)).astype(low)
        far.append(wires.send(mg.at[0, k], mg_far.at[k - 1], far_to(k)))

    for j, z, at in bands(d_band):
        normed = pair[:, 0, :, at].reshape(every, d_band)
        gate_s[j, z] = dot(normed, gate_grad[...], 0, 0).astype(low)

    total = mg[0, 0].astype(wide) + mg_in[0].astype(wide)
    for k in range(1, outer_wt):
        far[k - 1].wait_recv()
        total = total + mg_far[k - 1].astype(wide)
    turned[...] = total
    for p in range(n):
        back[p] = turned[p * channels : (p + 1) * channels, :].astype(low)
    into = lambda peer, slot: got.at[slot]
    swap_start(back, into, in_send, in_recv, flat, n, n_wt)
    got[flat] = back[flat]

    for j, z, at in bands(h_band):
        total = dot(mixed[0, at, :], expand_grad[0:row_count, :])
        for w in range(1, n_wt):
            total = total + dot(
                mixed[w, at, :], expand_grad[w * row_count : (w + 1) * row_count, :]
            )
        mix_s[j, z] = total.astype(low)

    def token_part(t, unused):
        j, k = 1 - t // outer_wt, outer_wt - 1 - t % outer_wt
        w = ((o + k) % outer_wt) * 2 + (i + j) % 2
        at = pl.ds(pl.multiple_of(w * row_count, row_count), row_count)
        tok[j, k, 0] = dot(product[at, :], down_w[...]).astype(low)
        tok[j, k, 1] = dot(gate_grad[at, :], gate_w[...], 1, 1).astype(low)
        return unused

    lax.fori_loop(0, outer_wt, token_part, 0)
    tok_near = wires.send(tok.at[1], tok_in, sibling)
    lax.fori_loop(outer_wt, n_wt, token_part, 0)

    mine = lambda ref: own_rows(ref, w_me, n_wt, channels)
    for one, every_one in ((kr_ref, kr_all), (ki_ref, ki_all), (rate_ref, rate_all), (freq_ref, freq_all)):
        one[...] = mine(every_one)
    dt = jnp.exp(own_column(step_ref, w_me * channels, channels))
    dt_ref[...] = jnp.broadcast_to(dt, (channels, states))
    fill_powers(rate_ref[...], freq_ref[...], dt, pw_re, pw_im)
    skip_ref[...] = jnp.broadcast_to(
        own_column(skip_all, w_me * channels, channels), (channels, LANES)
    )
    zero_pad = jnp.zeros((PAD, LANES), wide)
    clear_unused(table, n_wt * seq_count, n_seq * local_blocks, per, channels)
    vf[0:PAD, :] = zero_pad
    gf[0:PAD, :] = zero_pad
    vp[0:PAD, :] = zero_pad
    gp[pl.ds(rows, PAD), :] = zero_pad
    yp[pl.ds(rows, PAD), :] = zero_pad
    tok_near.wait_recv()
    tok_sent = []
    for k in range(1, outer_wt):
        for a in range(2):
            tok[0, k, a] = (tok[0, k, a].astype(wide) + tok_in[k, a].astype(wide)).astype(low)
        tok_sent.append(wires.send(tok.at[0, k], tok_far.at[k - 1], far_to(k)))
    swap_wait(back, into, in_send, in_recv, flat, n, n_wt)
    down_sum.turn(1, 2)
    down_sum.begin(0)
    gate_sum.begin(1, 2)
    rows_to_table(got, table, *shape)

    lane = lax.broadcasted_iota(jnp.int32, (LANES, LANES), 1)
    row = lax.broadcasted_iota(jnp.int32, (LANES, LANES), 0)
    lower = lane >= row
    wraps = lane + row >= LANES
    flip = (lane + row == LANES - 1).astype(jnp.bfloat16)
    lag_place = (
        lax.broadcasted_iota(jnp.int32, (n_lag, LANES), 0) * LANES
        + lax.broadcasted_iota(jnp.int32, (n_lag, LANES), 1)
        + 1
    ).astype(jnp.float32)

    def channel(c, unused):
        own = pl.ds(c, 1)
        val = v_ref[c].astype(jnp.float32)
        grad = table[pl.ds(c, rows, stride=channels), :]
        vf[pl.ds(PAD, rows), :] = val
        gf[pl.ds(PAD, rows), :] = grad
        skip_grad = jnp.sum(jnp.sum(val * grad, axis=0, keepdims=True), axis=1, keepdims=True)
        g_piece = to_pieces(seg_ref, gf, rows, docs)
        gp[0:rows, :] = g_piece
        v_piece = to_pieces(seg_ref, vf, rows, docs).astype(jnp.bfloat16)
        vp[pl.ds(PAD, rows), :] = dot(v_piece, flip)
        g_turned = jnp.transpose(g_piece).astype(jnp.bfloat16)
        sid = sid_ref[pl.ds(PAD, rows), :]
        lags = lag_ref[c]
        before = jnp.zeros((LANES, LANES), jnp.float32)
        total = jnp.zeros((rows, LANES), jnp.float32)
        earlier = None
        sums = []
        for d in range(n_lag + 1):
            ahead = pl.ds(PAD + d, rows)
            x = jnp.where(sid_ref[ahead, :] == sid, gp[pl.ds(d, rows), :], 0.0)
            t, before = toeplitz(lags, d, n_lag, lower, before)
            total = total + dot(x.astype(jnp.bfloat16), t, 1, 1)
            at = pl.ds(PAD - d, rows)
            back = jnp.where(sid_ref[at, :] == sid, vp[at, :], 0.0).astype(jnp.bfloat16)
            pairs = dot(g_turned, back)
            if d:
                skew = jnp.where(wraps, earlier, pairs)
                skew = pltpu.roll(skew, 0, 1, stride=1, stride_axis=0)
                sums.append(jnp.sum(skew, axis=0, keepdims=True))
            earlier = pairs
        yp[0:rows, :] = total
        out = from_pieces(seg_ref, yp, rows, docs) + skip_ref[own, :] * grad
        table[pl.ds(c, rows, stride=channels), :] = out
        lag_grad = jnp.concatenate(sums, axis=0)
        fill_lane_powers(pw_re, pw_im, c, tab_re, tab_im, 1)
        both = jnp.concatenate([lag_grad, lag_grad * lag_place], axis=0).astype(jnp.bfloat16)
        part_re = dot(both, tab_re[...].astype(jnp.bfloat16))
        part_im = dot(both, tab_im[...].astype(jnp.bfloat16))
        dr, di = power_rows(pw_re, pw_im, c, 7, bits, n_lag)
        gr, gi = cmul(dr, di, part_re[0:n_lag], part_im[0:n_lag])
        hr, hi = cmul(dr, di, part_re[n_lag:], part_im[n_lag:])
        gr, gi, hr, hi = (jnp.sum(a, axis=0, keepdims=True) for a in (gr, gi, hr, hi))
        kr, ki, dt = kr_ref[own, :], ki_ref[own, :], dt_ref[own, :]
        rate_grad = -dt * (kr * hr - ki * hi)
        freq_grad = -dt * (kr * hi + ki * hr)
        for at, row_out in enumerate((rate_grad, freq_grad, gr + skip_grad, -gi)):
            grads[at][own, :] = row_out
        step = jnp.sum(
            rate_grad * rate_ref[own, :] + freq_grad * freq_ref[own, :], axis=1, keepdims=True
        )
        for at, one in enumerate((step, skip_grad)):
            thin[at][own, :] = jnp.broadcast_to(one, (1, LANES))
        return unused

    lax.fori_loop(0 * channels // 4, 1 * channels // 4, channel, 0)
    down_sum.turn(3)
    gate_sum.begin(3)
    lax.fori_loop(1 * channels // 4, 2 * channels // 4, channel, 0)
    gate_sum.turn(1)
    gate_sum.begin(0)
    lax.fori_loop(2 * channels // 4, 3 * channels // 4, channel, 0)
    down_sum.turn(0)
    gate_sum.turn(2)
    lax.fori_loop(3 * channels // 4, 4 * channels // 4, channel, 0)
    gate_sum.turn(3)
    table_to_rows(table, back, *shape)
    home = lambda peer, slot: dv_ref.at[slot]
    swap_start(back, home, out_send, out_recv, flat, n, n_wt)
    own = pltpu.make_async_copy(back.at[flat], dv_ref.at[flat], local_sem)
    own.start()
    mix_sum.begin()
    for at in range(4):
        all_out[w_me, :, pl.ds(at * states, states)] = grads[at][...]
    for at in range(2):
        all_out[w_me, :, pl.ds(4 * states + at * LANES, LANES)] = thin[at][...]
    block = all_out.at[w_me]
    far_all = [wires.send(block, block, far_to(k)) for k in range(1, outer_wt)]
    near_all = [wires.send(block, block, sibling)]

    for c in tok_sent:
        c.wait_recv()
    result = x_ref[...].astype(wide) + tok[0, 0, 0].astype(wide) + tok_in[0, 0].astype(wide)
    for k in range(1, outer_wt):
        result = result + tok_far[k - 1, 0].astype(wide)
    out_ref[...] = result.astype(low)
    own.wait()
    swap_wait(back, home, out_send, out_recv, flat, n, n_wt)

    gate_sum.turn(0)
    for p in range(n):
        turned[pl.ds(p * channels, channels), :] = dv_ref[p].astype(wide)
    value_grad = jnp.transpose(turned[...]) * gelu_pair(pre_ref[...])[1]
    value_low = value_grad.astype(low)
    for w in range(n_wt):
        value_cut[w] = value_low[:, w * v_band : (w + 1) * v_band]
    value_all[w_me] = value_cut[w_me]
    moves = []
    for k in range(outer_wt):
        for j in range(2):
            if k or j:
                w = ((o + k) % outer_wt) * 2 + (i + j) % 2
                moves.append(wires.send(value_cut.at[w], value_all.at[w_me], (s_me, w)))

    normed_grad = dot(value_low, value_full[...], 1, 1)
    normed_grad = normed_grad + tok[0, 0, 1].astype(wide) + tok_in[0, 1].astype(wide)
    for k in range(1, outer_wt):
        normed_grad = normed_grad + tok_far[k - 1, 1].astype(wide)
    x32 = x_ref[...].astype(wide)
    centered = x32 - jnp.mean(x32, axis=-1, keepdims=True)
    scale = lax.rsqrt(jnp.mean(centered * centered, axis=-1, keepdims=True) + norm_epsilon)
    xhat = centered * scale
    g = normed_grad * norm_vec[0:1, :]
    inner_grad = g - jnp.mean(g, axis=-1, keepdims=True)
    inner_grad = inner_grad - xhat * jnp.mean(g * xhat, axis=-1, keepdims=True)
    in_grad[...] = pair[w_me, 1].astype(wide) + inner_grad * scale
    vectors = jnp.concatenate(
        [
            jnp.sum(normed_grad * xhat, axis=0, keepdims=True),
            jnp.sum(normed_grad, axis=0, keepdims=True),
            jnp.zeros((14, model_width), wide),
        ],
        axis=0,
    )
    norm_last[...] = vectors

    mix_sum.turn()
    for c in moves:
        c.wait_recv()
    vector_lanes = min(d_band, LANES)
    for j, z, at in bands(d_band):
        normed = pair[:, 0, :, at].reshape(every, d_band)
        value_s[j, z, 0:d_band, :] = dot(
            normed, value_all[...].reshape(every, v_band), 0, 0
        ).astype(low)
        value_s[j, z, pl.ds(d_band, 16), 0:vector_lanes] = norm_last[:, at].astype(low)
    value_sum.begin()
    for one in (down_sum, gate_sum, mix_sum):
        one.begin()
        one.turn()
    down_out[...] = down_sum.end()
    mix_band = mix_sum.end().astype(low)
    gate_band = gate_sum.end().astype(low)
    value_sum.turn()
    for w in range(n_wt):
        gate_cut = gate_band[w * d_rows : (w + 1) * d_rows, :]
        mix_cut = mix_band[w * h_rows : (w + 1) * h_rows, :]
        last_send[w] = jnp.concatenate([gate_cut, mix_cut], axis=0)
    heads = gate_last
    heads[w_me] = last_send[w_me]
    ends = []

    def spread(source, target):
        for k in range(outer_wt):
            for j in range(2):
                if k or j:
                    w = ((o + k) % outer_wt) * 2 + (i + j) % 2
                    ends.append(wires.send(source.at[w], target.at[w_me], (s_me, w)))

    spread(last_send, heads)
    for k in range(1, outer_wt):
        far_all[k - 1].wait_recv()
        block = all_out.at[((o + outer_wt - k) % outer_wt) * 2 + i]
        near_all.append(wires.send(block, block, sibling))
    value_band = value_sum.end()
    tail_send = mix_last
    for w in range(n_wt):
        tail_send[w, 0:d_rows, :] = value_band[w * d_rows : (w + 1) * d_rows, :].astype(low)
        tail_send[w, pl.ds(d_rows, 16), :] = value_band[d_band : d_band + 16, :].astype(low)
    value_last[w_me] = tail_send[w_me]
    spread(tail_send, value_last)
    for c in ends + near_all:
        c.wait_recv()
    wires.sent()
    norm = jnp.zeros((16, v_band), wide)
    for w in range(n_wt):
        norm = norm + value_last[w, pl.ds(d_rows, 16), :].astype(wide)
    norm_out[...] = norm


def back_call(
    pair, gate_w, mix_w, down_w, mixed, v, lags, pre, value_full, norm_vec, x, seg, sid, rate, freq, kr,
    ki, step, skip, seq_count, docs, n_lag, inner_seq,
):
    n_seq, n_wt = lax.axis_size("seq"), lax.axis_size("wt")
    n = n_seq * n_wt
    channels, rows, _ = v.shape
    states = kr.shape[1]
    per = rows // (n_wt * seq_count)
    bits = (n_lag - 1).bit_length()
    local, model_width = x.shape
    width, f_part = mix_w.shape
    d_band, h_band, v_band = model_width // n_seq, width // n_seq, width // n_wt
    d_rows, h_rows = d_band // n_wt, h_band // n_wt
    f_rows = f_part // n_seq
    inner, outer, outer_wt = inner_seq, n_seq // inner_seq, n_wt // 2
    low = jnp.bfloat16
    half = lambda *s: pltpu.VMEM(s, low)
    out = jax.ShapeDtypeStruct
    wires = back_wires(n_seq, n_wt, inner)

    def seq_scratch(*block):
        return [
            half(inner, outer, *block), half(max(inner - 1, 1), outer, *block),
            half(max(outer - 1, 1), *block),
        ]

    every = n_wt * local
    return pl.pallas_call(
        functools.partial(back_kernel, n_lag, docs, bits, seq_count, per, inner_seq),
        out_shape=(
            out((local, model_width), low),
            out((local, model_width), jnp.float32),
            out((n_wt, d_rows + h_rows, f_part), low),
            out((n_wt, d_rows + 16, v_band), low),
            out((n_wt, d_rows + 16, v_band), low),
            out((f_rows, model_width), jnp.float32),
            out((16, v_band), jnp.float32),
            out((n_wt, channels, 4 * states + 2 * LANES), jnp.float32),
        ),
        in_specs=[pl.BlockSpec(memory_space=pltpu.VMEM)] * 19,
        out_specs=(pl.BlockSpec(memory_space=pltpu.VMEM),) * 8,
        scratch_shapes=[vmem(7 + bits, channels, states)] * 2
        + [vmem(channels, states)] * 5
        + [vmem(channels, LANES)]
        + [vmem(PAD + rows, LANES)] * 5
        + [vmem(LANES, states), vmem(LANES, states), vmem(rows * channels, LANES)]
        + [half(n, channels, local)] * 3
        + [half(every, f_part)] * 3
        + [half(2, outer_wt, width, local), half(outer_wt, width, local)]
        + [half(max(outer_wt - 1, 1), width, local)]
        + [half(2, outer_wt, 2, local, model_width), half(outer_wt, 2, local, model_width)]
        + [half(max(outer_wt - 1, 1), 2, local, model_width)]
        + [vmem(f_part, model_width)]
        + seq_scratch(f_rows, model_width)
        + seq_scratch(h_band, f_part)
        + seq_scratch(d_band, f_part)
        + seq_scratch(d_band + 16, v_band)
        + [vmem(width, local), half(n_wt, local, v_band), half(n_wt, local, v_band)]
        + [half(n_wt, d_rows + h_rows, f_part), vmem(16, model_width)]
        + [pltpu.SemaphoreType.DMA((n,))] * 4
        + [pltpu.SemaphoreType.DMA((wires,))] * 2
        + [pltpu.SemaphoreType.DMA]
        + [vmem(channels, states)] * 4
        + [vmem(channels, LANES)] * 2,
        compiler_params=pltpu.CompilerParams(
            vmem_limit_bytes=(39 if n <= 32 else 62) << 20, collective_id=2, has_side_effects=True
        ),
        cost_estimate=pl.CostEstimate(
            flops=60_000_000_000, bytes_accessed=4_000_000, transcendentals=0
        ),
        name="back",
    )(
        pair, gate_w, mix_w, down_w, mixed, v, lags, pre, value_full, norm_vec, x, seg, sid, rate, freq,
        kr, ki, step, skip,
    )


def finish_kernel(
    out_ref, grad_ref, heads, tails, down_ref, norm_ref, all_ref,
    outputs, in_grad, gain, bias, gate, value, mix, down, rate, freq, kr, ki, step, skip,
):
    n_seq, n_wt = lax.axis_size("seq"), lax.axis_size("wt")
    w_me = lax.axis_index("wt")
    wide = jnp.float32
    d_rows, h_rows = gate.shape[0], mix.shape[0]
    f_rows = heads.shape[2] // n_seq
    channels, states = all_ref.shape[1], rate.shape[1]
    outputs[...] = out_ref[...]
    in_grad[...] = grad_ref[...]
    down[...] = down_ref[...]
    for ref, first, rows in ((gate, 0, d_rows), (mix, d_rows, h_rows)):
        parts = [heads[w].astype(wide)[first : first + rows, :] for w in range(n_wt)]
        cut = [
            parts[w][:, s * f_rows : (s + 1) * f_rows] for s in range(n_seq) for w in range(n_wt)
        ]
        ref[...] = jnp.concatenate(cut, axis=1)
    value[...] = jnp.concatenate(
        [tails[w].astype(wide)[0:d_rows, :] for w in range(n_wt)], axis=1
    )
    share = norm_ref.shape[1]
    own = pltpu.roll(norm_ref[...], (share - w_me * d_rows) % share, 1)[:, 0:d_rows]
    gain[...] = own[0:1, :]
    bias[...] = own[1:2, :]
    for at, ref in enumerate((rate, freq, kr, ki)):
        for w in range(n_wt):
            ref[pl.ds(w * channels, channels), :] = all_ref[w, :, pl.ds(at * states, states)]
    total = n_wt * channels
    lane = lax.broadcasted_iota(jnp.int32, (channels, LANES), 1)
    place = lax.broadcasted_iota(jnp.int32, (channels, LANES), 0)
    for at, ref in enumerate((step, skip)):
        row = jnp.zeros((1, LANES), wide)
        for w in range(n_wt):
            thin = all_ref[w, :, pl.ds(4 * states + at * LANES, LANES)]
            hit = jnp.where(lane == place + w * channels, thin, 0.0)
            row = row + jnp.sum(hit, axis=0, keepdims=True)
        ref[...] = row[:, 0:total]


def finish_call(out, grad, heads, tails, down, norm, packed, gate_width, d_rows, h_rows, states):
    n_wt, channels, _ = packed.shape
    total = n_wt * channels
    wide = jnp.float32
    shape = jax.ShapeDtypeStruct
    full = shape((total, states), wide)
    return pl.pallas_call(
        finish_kernel,
        out_shape=(
            shape(out.shape, out.dtype), shape(grad.shape, wide), shape((1, d_rows), wide),
            shape((1, d_rows), wide), shape((d_rows, gate_width), wide),
            shape((d_rows, n_wt * tails.shape[2]), wide), shape((h_rows, gate_width), wide),
            shape(down.shape, wide), full, full, full, full, shape((1, total), wide),
            shape((1, total), wide),
        ),
        in_specs=[pl.BlockSpec(memory_space=pltpu.VMEM)] * 7,
        out_specs=(pl.BlockSpec(memory_space=pltpu.VMEM),) * 14,
        compiler_params=pltpu.CompilerParams(vmem_limit_bytes=12 << 20),
        name="finish",
    )(out, grad, heads, tails, down, norm, packed)


BOTH = ("seq", "wt")
norm_epsilon = 1e-05


def gelu_tanh(pre_act):
    return jax.nn.gelu(pre_act, approximate=True)


def on_device(
    inputs, cotangent, doc_lengths, norm_gain, norm_bias, gate_weight, value_weight, mix_weight,
    down_weight, decay_rate, frequency, kernel_re, kernel_im, log_step, skip_gain,
):
    seq_count, local_len, model_width = inputs.shape
    n_seq, n_wt = lax.axis_size("seq"), lax.axis_size("wt")
    inner_seq = 2 if n_seq <= 8 else 8
    rows = lambda x: x.reshape(seq_count * local_len, model_width)
    line = lambda x: x.reshape(1, -1)
    width, gate_width = mix_weight.shape[0] * n_seq * n_wt, gate_weight.shape[1]
    f_part = gate_width // n_wt
    n_lag = local_len * n_seq // 2 // LANES
    params = (decay_rate, frequency, kernel_re, kernel_im, line(log_step), line(skip_gain))
    pair, gate_own, mix_own, down_own, mixed, value_ch, lags, pre, value_full, norm, seg, sid = front_call(
        rows(inputs), rows(cotangent), value_weight, line(norm_gain), line(norm_bias), gate_weight,
        mix_weight, down_weight, doc_lengths, *params, n_lag, inner_seq,
    )
    raw = back_call(
        pair, gate_own.reshape(model_width, f_part), mix_own.reshape(width, f_part),
        down_own.reshape(f_part, model_width), mixed.reshape(n_wt, width, -1), value_ch, lags, pre,
        value_full, norm, rows(inputs), seg, sid, *params, seq_count, doc_lengths.shape[1], n_lag,
        inner_seq,
    )
    out, grad, heads, tails, unused, down, vectors, packed = raw
    done = finish_call(
        out, grad, heads, tails, down, vectors, packed, gate_width, value_weight.shape[0],
        mix_weight.shape[0], kernel_re.shape[1],
    )
    flat = [done[i].reshape(-1) for i in (2, 3, 12, 13)]
    return (
        done[0].reshape(inputs.shape), done[1].reshape(inputs.shape), flat[0], flat[1], *done[4:8],
        *done[8:12], flat[2], flat[3],
    )


def solution(mesh):
    in_specs = (
        P("wt", "seq", None),
        P("wt", "seq", None),
        P("wt", None),
        P(("seq", "wt")),
        P(("seq", "wt")),
        P(("seq", "wt"), None),
        P(("seq", "wt"), None),
        P(("seq", "wt"), None),
        P(("seq", "wt"), None),
        P("seq", None),
        P("seq", None),
        P("seq", None),
        P("seq", None),
        P("seq"),
        P("seq"),
    )
    out_specs = (
        P("wt", "seq", None),
        P("wt", "seq", None),
        P(("seq", "wt")),
        P(("seq", "wt")),
        P(("seq", "wt"), None),
        P(("seq", "wt"), None),
        P(("seq", "wt"), None),
        P(("seq", "wt"), None),
        P("seq", None),
        P("seq", None),
        P("seq", None),
        P("seq", None),
        P("seq"),
        P("seq"),
    )
    return jax.shard_map(
        on_device, mesh=mesh, in_specs=in_specs, out_specs=out_specs, check_vma=False
    )
```

```python
import functools

import jax
import jax.numpy as jnp
from jax import lax
from jax.experimental import pallas as pl
from jax.experimental.pallas import tpu as pltpu
from jax.sharding import PartitionSpec as P

LANES = 128
PAD = 16


MESH = pl.DeviceIdType.MESH


def place_of(flat, n_wt):
    return (flat // n_wt, flat % n_wt)


def meet(flat, n, n_wt):
    barrier = pltpu.get_barrier_semaphore()

    def tell(r, unused):
        pl.semaphore_signal(
            barrier, inc=1, device_id=place_of((flat + r) % n, n_wt), device_id_type=MESH
        )
        return unused

    lax.fori_loop(1, n, tell, 0)
    pl.semaphore_wait(barrier, n - 1)


def swap_start(send, target_of, send_sem, recv_sem, flat, n, n_wt, part, of):
    rows = pl.ds(part * (send.shape[1] // of), send.shape[1] // of)

    def one(r, unused):
        peer = (flat + r) % n
        pltpu.make_async_remote_copy(
            src_ref=send.at[peer, rows], dst_ref=target_of(peer).at[flat, rows],
            send_sem=send_sem.at[part], recv_sem=recv_sem.at[part],
            device_id=place_of(peer, n_wt), device_id_type=MESH,
        ).start()
        return unused

    lax.fori_loop(1, n, one, 0)


def swap_wait(send, target_of, send_sem, recv_sem, flat, n, n_wt, part, of):
    every, rows = pl.ds(0, n - 1), pl.ds(part * (send.shape[1] // of), send.shape[1] // of)
    pltpu.make_async_remote_copy(
        src_ref=send.at[every, rows], dst_ref=target_of(flat).at[every, rows],
        send_sem=send_sem.at[part], recv_sem=recv_sem.at[part],
        device_id=place_of((flat + 1) % n, n_wt), device_id_type=MESH,
    ).wait()


def halves_of(channels):
    return 2 if channels % 16 == 0 else 1


def rows_to_table(got, table, first, count, n_seq, n_wt, seq_count, local_blocks, per, channels):
    for s in range(n_seq):
        for w in range(n_wt):
            for k in range(seq_count):
                for b in range(local_blocks):
                    row = (w * seq_count + k) * per + s * local_blocks + b
                    lanes = pl.ds((k * local_blocks + b) * LANES, LANES)
                    table[pl.ds(row * channels + first, count), :] = got[
                        s * n_wt + w, pl.ds(first, count), lanes
                    ].astype(jnp.float32)


def table_to_rows(table, send, first, count, n_seq, n_wt, seq_count, local_blocks, per, channels):
    for s in range(n_seq):
        for w in range(n_wt):
            for k in range(seq_count):
                for b in range(local_blocks):
                    row = (w * seq_count + k) * per + s * local_blocks + b
                    lanes = pl.ds((k * local_blocks + b) * LANES, LANES)
                    send[s * n_wt + w, pl.ds(first, count), lanes] = table[
                        pl.ds(row * channels + first, count), :
                    ].astype(jnp.bfloat16)


def clear_unused(table, seqs, blocks, per, channels):
    for s in range(seqs):
        table[pl.ds((s * per + blocks) * channels, (per - blocks) * channels), :] = jnp.zeros(
            ((per - blocks) * channels, LANES), jnp.float32
        )


def share_over_wt(ref, s_me, w_me, n_wt, send_sem, recv_sem):
    inner = 2
    outer = n_wt // inner
    o, i = w_me // inner, w_me % inner
    other = (s_me, o * inner + 1 - i)

    def copy(block, slot, to):
        return pltpu.make_async_remote_copy(
            src_ref=ref.at[block], dst_ref=ref.at[block], send_sem=send_sem.at[slot],
            recv_sem=recv_sem.at[slot], device_id=to, device_id_type=MESH,
        )

    far = [copy(w_me, k, (s_me, ((o + k) % outer) * inner + i)) for k in range(1, outer)]
    near = [copy(w_me, outer, other)]
    for c in far + near:
        c.start()
    for k in range(1, outer):
        block = ((o + outer - k) % outer) * inner + i
        far[k - 1].wait_recv()
        c = copy(block, outer + k, other)
        c.start()
        near.append(c)
    for c in far:
        c.wait_send()
    for c in near:
        c.wait()


def cmul(ar, ai, br, bi):
    return ar * br - ai * bi, ar * bi + ai * br


def power_rows(pw_re, pw_im, c, first, count, rows):
    width = pw_re.shape[2]
    place = lax.broadcasted_iota(jnp.int32, (rows, width), 0)
    re = jnp.ones((rows, width), jnp.float32)
    im = jnp.zeros((rows, width), jnp.float32)
    for bit in range(count):
        on = (place & (1 << bit)) != 0
        fr = jnp.where(on, pw_re[first + bit, pl.ds(c, 1), :], 1.0)
        fi = jnp.where(on, pw_im[first + bit, pl.ds(c, 1), :], 0.0)
        re, im = cmul(re, im, fr, fi)
    return re, im


def fill_lane_powers(pw_re, pw_im, c, tab_re, tab_im, extra):
    re, im = power_rows(pw_re, pw_im, c, 0, 3, 8)
    if extra:
        re, im = cmul(re, im, pw_re[0, pl.ds(c, 1), :], pw_im[0, pl.ds(c, 1), :])
    tab_re[0:8, :] = re
    tab_im[0:8, :] = im
    have, bit = 8, 3
    while have < LANES:
        re, im = cmul(
            tab_re[0:have, :],
            tab_im[0:have, :],
            pw_re[bit, pl.ds(c, 1), :],
            pw_im[bit, pl.ds(c, 1), :],
        )
        tab_re[have : 2 * have, :] = re
        tab_im[have : 2 * have, :] = im
        have, bit = 2 * have, bit + 1


def to_pieces(seg, val, rows, docs):
    total = jnp.zeros((rows, LANES), jnp.float32)
    for j in range(docs):
        at = pl.ds(PAD - j, rows)
        total = total + jnp.where(seg[at, :] == j, val[at, :], 0.0)
    return total


def from_pieces(seg, piece, rows, docs):
    own = seg[pl.ds(PAD, rows), :]
    total = jnp.zeros((rows, LANES), jnp.float32)
    for j in range(docs):
        total = total + jnp.where(own == j, piece[pl.ds(j, rows), :], 0.0)
    return total


def toeplitz(lags, d, last, lower, before):
    if d < last:
        row = jnp.broadcast_to(lags[d : d + 1, :], (LANES, LANES))
        here = pltpu.roll(row, 0, 1, stride=1, stride_axis=0)
    else:
        here = jnp.zeros((LANES, LANES), jnp.float32)
    return jnp.where(lower, here, before).astype(jnp.bfloat16), here


def dot(a, b, ca=1, cb=0):
    return lax.dot_general(a, b, (((ca,), (cb,)), ((), ())), preferred_element_type=jnp.float32)


def vmem(*shape):
    return pltpu.VMEM(shape, jnp.float32)


def own_column(row_ref, first, count):
    size = row_ref.shape[1]
    lane = lax.broadcasted_iota(jnp.int32, (count, size), 1)
    place = lax.broadcasted_iota(jnp.int32, (count, size), 0)
    return jnp.sum(jnp.where(lane == place + first, row_ref[...], 0.0), axis=1, keepdims=True)


def own_rows(ref, w_me, n_wt, count):
    out = ref[0:count, :]
    for w in range(1, n_wt):
        out = jnp.where(w_me == w, ref[w * count : (w + 1) * count, :], out)
    return out


def fill_powers(rate, freq, dt, pw_re, pw_im):
    for p in range(pw_re.shape[0]):
        if p % 4:
            re, im = cmul(re, im, re, im)
        else:
            mag, angle = jnp.exp(-rate * dt * float(1 << p)), freq * dt * float(1 << p)
            re, im = mag * jnp.cos(angle), mag * jnp.sin(angle)
        pw_re[p] = re
        pw_im[p] = im


def fill_segments(lens, seg_ref, sid_ref, docs, blocks, per, seqs):
    rows = seg_ref.shape[0]
    seg_ref[0:PAD, :] = jnp.full((PAD, LANES), -1, jnp.int32)
    sid_ref[0:PAD, :] = jnp.full((PAD, LANES), -2, jnp.int32)
    seg_ref[rows - PAD : rows, :] = jnp.full((PAD, LANES), -1, jnp.int32)
    sid_ref[rows - PAD : rows, :] = jnp.full((PAD, LANES), -2, jnp.int32)
    row = lax.broadcasted_iota(jnp.int32, (per, LANES), 0)
    position = row * LANES + lax.broadcasted_iota(jnp.int32, (per, LANES), 1)
    group = seqs // lens.shape[0]
    for q in range(seqs):
        ends = jnp.zeros((1, 1), jnp.int32)
        seg = jnp.zeros((per, LANES), jnp.int32)
        for j in range(docs):
            ends = ends + lens[q // group, q % group : q % group + 1, j : j + 1]
            seg = seg + (position >= ends).astype(jnp.int32)
        seg = jnp.where(row < blocks, seg, -1)
        at = pl.ds(PAD + q * per, per)
        seg_ref[at, :] = seg
        best = jnp.full((per, LANES), -1, jnp.int32)
        for i in range(blocks):
            one = seg[i : i + 1, :]
            best = jnp.maximum(best, jnp.where(one + i == row, one, -1))
        best = jnp.max(best.astype(jnp.float32), axis=1, keepdims=True).astype(jnp.int32)
        best = jnp.where(best >= 0, best + docs * q, -1)
        sid_ref[at, :] = jnp.broadcast_to(best, (per, LANES))


class Wires:
    def __init__(self, send_sem, recv_sem):
        self.send_sem, self.recv_sem, self.used, self.open = send_sem, recv_sem, 0, []

    def send(self, source, target, to):
        c = pltpu.make_async_remote_copy(
            src_ref=source, dst_ref=target, send_sem=self.send_sem.at[self.used],
            recv_sem=self.recv_sem.at[self.used], device_id=to, device_id_type=MESH,
        )
        self.used += 1
        self.open.append(c)
        c.start()
        return c

    def sent(self):
        for c in self.open:
            c.wait_send()
        self.open = []


class SeqGather:
    def __init__(self, ref, send_sem, recv_sem, so, si, outer, inner, w_me):
        self.ref, self.send_sem, self.recv_sem = ref, send_sem, recv_sem
        self.so, self.si, self.outer, self.inner, self.w_me = so, si, outer, inner, w_me

    def copy(self, z, slot, to_z, j):
        block = self.ref.at[z * self.inner + self.si]
        to = (to_z * self.inner + (self.si + j) % self.inner, self.w_me)
        return pltpu.make_async_remote_copy(
            src_ref=block, dst_ref=block, send_sem=self.send_sem.at[slot],
            recv_sem=self.recv_sem.at[slot], device_id=to, device_id_type=MESH,
        )

    def along(self, up, k, z):
        slot = (0 if up else self.outer) + k
        return self.copy(z, slot, self.so + 1 if up else self.so - 1, 0)

    def across(self, z, j):
        return self.copy(z, 2 * self.outer + z * self.inner + j, self.so, j)

    def ends(self, up):
        return self.so < self.outer - 1 if up else self.so > 0

    def launch(self, z, k, ups):
        for up in ups:
            if k < self.outer:
                pl.when(self.ends(up))(lambda up=up: self.along(up, k, z).start())
        for j in range(1, self.inner):
            self.across(z, j).start()

    def begin(self):
        self.launch(self.so, 1, (True, False))

    def hop(self, k):
        for up in (True, False):
            z = self.so - k if up else self.so + k
            there = z >= 0 if up else z < self.outer

            @pl.when(there)
            def _():
                self.along(up, k, z).wait_recv()
                self.launch(z, k + 1, (up,))

    def end(self):
        for z in range(self.outer):
            for j in range(1, self.inner):
                block = self.copy(z, 2 * self.outer + z * self.inner + j, self.so, j)
                block.wait_recv()
                block.wait_send()
        for k in range(1, self.outer):
            for up in (True, False):
                z = self.so - k + 1 if up else self.so + k - 1
                from_here = (z >= 0 if up else z < self.outer) & self.ends(up)
                pl.when(from_here)(lambda up=up, k=k, z=z: self.along(up, k, z).wait_send())


def rms(x32):
    mean = jnp.mean(x32, axis=-1, keepdims=True)
    centered = x32 - mean
    spread = jnp.mean(centered * centered, axis=-1, keepdims=True)
    return centered * lax.rsqrt(spread + norm_epsilon)


def regroup(x, n_seq, n_wt, width):
    cut = lambda s, w: x[:, (s * n_wt + w) * width : (s * n_wt + w + 1) * width]
    return [jnp.concatenate([cut(s, w) for s in range(n_seq)], axis=1) for w in range(n_wt)]


def front_wires(n_seq, n_wt):
    value = (n_seq - 1) + n_seq * (n_wt // 2 - 1) + n_seq * (n_wt // 2)
    weights = 2 * (n_wt - 1)
    tokens = 2 * (n_wt // 2 - 1) + 2 * (n_wt // 2)
    mixed = 2 * ((n_wt // 2 - 1) + n_wt // 2)
    return value + weights + tokens + mixed


def front_kernel(
    n_lag, docs, bits, seq_count, per, inner_seq, loads,
    x_ref, cot_ref, value_in, gain_in, bias_in, gate_in, mix_in, down_in, lens_in, rate_ref, freq_ref,
    kr_all, ki_all, step_ref, skip_all,
    pair, gate_out, mix_out, down_out, mixed_ref, v_ref, lag_ref, pre_ref, value_full, norm_out,
    seg_ref, sid_ref,
    lens, pw_re, pw_im, kr_ref, ki_ref, skip_ref, vf, vp, yp, tab_re, tab_im, table, got, back, front, xhat, act_send, gate_cut, mix_cut,
    in_send, in_recv, out_send, out_recv, wire_send, wire_recv, local_sem, *hop_sems,
):
    channels, rows, _ = v_ref.shape
    n_seq, n_wt = lax.axis_size("seq"), lax.axis_size("wt")
    n = n_seq * n_wt
    s_me, w_me = lax.axis_index("seq"), lax.axis_index("wt")
    flat = s_me * n_wt + w_me
    row_count, model_width = x_ref.shape
    width = pre_ref.shape[1]
    d_rows, h_rows, f_rows = gate_in.shape[0], mix_in.shape[0], down_in.shape[0]
    local_blocks = row_count // LANES // seq_count
    shape = (n_seq, n_wt, seq_count, local_blocks, per, channels)
    outer_wt = n_wt // 2
    o, i = w_me // 2, w_me % 2
    sibling = o * 2 + 1 - i
    far_to = lambda k: ((o + k) % outer_wt) * 2 + i
    far_from = lambda k: ((o + outer_wt - k) % outer_wt) * 2 + i
    outer_seq = n_seq // inner_seq
    so, si = s_me // inner_seq, s_me % inner_seq
    rings = [
        SeqGather(ref, hop_sems[2 * at], hop_sems[2 * at + 1], so, si, outer_seq, inner_seq, w_me)
        for at, ref in enumerate((down_out, gate_out, mix_out))
    ]
    down_ring, gate_ring, mix_ring = rings
    wires = Wires(wire_send, wire_recv)

    meet(flat, n, n_wt)
    for c in loads:
        c.wait()

    lens[w_me, 0:seq_count, 0:docs] = lens_in[...]
    block = lens.at[w_me]
    far_lens = [wires.send(block, block, (s_me, far_to(k))) for k in range(1, outer_wt)]
    near_lens = [wires.send(block, block, (s_me, sibling))]

    norm_rows = jnp.concatenate(
        [gain_in[...], bias_in[...], jnp.zeros((14, d_rows), jnp.bfloat16)], axis=0
    ).astype(jnp.float32)
    norm_rows = jnp.concatenate([norm_rows, jnp.zeros((16, LANES - d_rows), jnp.float32)], axis=1)
    norm_rows = pltpu.roll(norm_rows, (flat * d_rows) % LANES, 1)
    front[s_me, w_me, 0:16, :] = jnp.zeros((16, width), jnp.bfloat16)
    front[s_me, w_me, 0:16, 0:LANES] = norm_rows.astype(jnp.bfloat16)
    front[s_me, w_me, pl.ds(16, d_rows), :] = value_in[...]
    first = []
    for k in range(1, n_seq):
        to = ((s_me + k) % n_seq, w_me)
        first.append(wires.send(front.at[s_me, w_me], front.at[s_me, w_me], to))

    second, third = [], []

    def spread_value(s):
        block = front.at[s, w_me]
        for k in range(1, outer_wt):
            second.append((s, k, wires.send(block, block, (s_me, far_to(k)))))
        third.append(wires.send(block, block, (s_me, sibling)))

    spread_value(s_me)
    down_out[s_me] = down_in[...]
    down_ring.begin()

    for ref, cut in ((gate_in, gate_cut), (mix_in, mix_cut)):
        whole = ref[...].astype(jnp.float32)
        for w, part in enumerate(regroup(whole, n_seq, n_wt, f_rows)):
            cut[w] = part.astype(jnp.bfloat16)
    gate_out[s_me, w_me] = gate_cut[w_me]
    mix_out[s_me, w_me] = mix_cut[w_me]
    turn = []
    for source, target in ((gate_cut, gate_out), (mix_cut, mix_out)):
        for k in range(outer_wt):
            for j in range(2):
                if k or j:
                    w = ((o + k) % outer_wt) * 2 + (i + j) % 2
                    turn.append(wires.send(source.at[w], target.at[s_me, w_me], (s_me, w)))

    chunk = min(32, row_count)

    def normalise(r, unused):
        at = pl.ds(r * chunk, chunk)
        xhat[at, :] = rms(x_ref[at, :].astype(jnp.float32))
        return unused

    lax.fori_loop(0, row_count // chunk, normalise, 0)
    pair[w_me, 1] = cot_ref[...]
    mine = lambda ref: own_rows(ref, w_me, n_wt, channels)
    fill_powers(
        mine(rate_ref), mine(freq_ref),
        jnp.exp(own_column(step_ref, w_me * channels, channels)), pw_re, pw_im,
    )
    kr_ref[...] = mine(kr_all)
    ki_ref[...] = mine(ki_all)
    skip_ref[...] = jnp.broadcast_to(
        own_column(skip_all, w_me * channels, channels), (channels, LANES)
    )

    for k in range(1, n_seq):
        first[k - 1].wait_recv()
        spread_value((s_me + n_seq - k) % n_seq)

    for c in turn[: n_wt - 1]:
        c.wait_recv()
    gate_ring.begin()
    for c in turn[n_wt - 1 :]:
        c.wait_recv()
    mix_ring.begin()
    if outer_seq > 1:
        down_ring.hop(1)
    for k in range(1, outer_wt):
        far_lens[k - 1].wait_recv()
        block = lens.at[far_from(k)]
        near_lens.append(wires.send(block, block, (s_me, sibling)))
    for s, k, c in second:
        c.wait_recv()
        block = front.at[s, far_from(k)]
        third.append(wires.send(block, block, (s_me, sibling)))
    for c in third + near_lens:
        c.wait_recv()

    for f in range(n):
        value_full[pl.ds(f * d_rows, d_rows), :] = front[f // n_wt, f % n_wt, pl.ds(16, d_rows), :]
    share = LANES // d_rows
    for b in range(model_width // LANES):
        total = jnp.zeros((2, LANES), jnp.float32)
        for f in range(b * share, (b + 1) * share):
            total = total + front[f // n_wt, f % n_wt, 0:16, 0:LANES].astype(jnp.float32)[0:2]
        norm_out[:, pl.ds(b * LANES, LANES)] = total

    def project(r, unused):
        at = pl.ds(pl.multiple_of(r * LANES, LANES), LANES)
        normed = (xhat[at, :] * norm_out[0:1, :] + norm_out[1:2, :]).astype(jnp.bfloat16)
        pair[w_me, 0, at, :] = normed
        pre = dot(normed, value_full[...])
        pre_ref[at, :] = pre
        turned = jnp.transpose(gelu_tanh(pre))
        for p in range(n):
            act_send[p, :, at] = turned[p * channels : (p + 1) * channels, :].astype(jnp.bfloat16)
        return unused

    lax.fori_loop(0, row_count // LANES, project, 0)
    into = lambda peer: got
    of = halves_of(channels)
    each = channels // of
    for part in range(of):
        swap_start(act_send, into, in_send, in_recv, flat, n, n_wt, part, of)
    got[flat] = act_send[flat]
    fill_segments(lens, seg_ref, sid_ref, docs, n_seq * local_blocks, per, n_wt * seq_count)

    if outer_seq > 1:
        gate_ring.hop(1)
        mix_ring.hop(1)
    clear_unused(table, n_wt * seq_count, n_seq * local_blocks, per, channels)
    zero_pad = jnp.zeros((PAD, LANES), jnp.float32)
    vf[0:PAD, :] = zero_pad
    vp[0:PAD, :] = zero_pad
    yp[pl.ds(rows, PAD), :] = zero_pad
    lower = lax.broadcasted_iota(jnp.int32, (LANES, LANES), 1) >= lax.broadcasted_iota(
        jnp.int32, (LANES, LANES), 0
    )
    swap_wait(act_send, into, in_send, in_recv, flat, n, n_wt, 0, of)

    far_pair = []
    for at in range(2):
        block = pair.at[w_me, at]
        for k in range(1, outer_wt):
            far_pair.append((k, at, wires.send(block, block, (s_me, far_to(k)))))
    near_pair = [wires.send(pair.at[w_me, at], pair.at[w_me, at], (s_me, sibling)) for at in range(2)]

    rows_to_table(got, table, 0, each, *shape)

    def channel(c, unused):
        fill_lane_powers(pw_re, pw_im, c, tab_re, tab_im, 0)
        dr, di = power_rows(pw_re, pw_im, c, 7, bits, n_lag)
        ar, ai = cmul(dr, di, kr_ref[pl.ds(c, 1), :], ki_ref[pl.ds(c, 1), :])
        lags = dot(ar.astype(jnp.bfloat16), tab_re[...].astype(jnp.bfloat16), 1, 1) - dot(
            ai.astype(jnp.bfloat16), tab_im[...].astype(jnp.bfloat16), 1, 1
        )
        lag_ref[c] = lags
        val = table[pl.ds(c, rows, stride=channels), :]
        v_ref[c] = val.astype(jnp.bfloat16)
        vf[pl.ds(PAD, rows), :] = val
        vp[pl.ds(PAD, rows), :] = to_pieces(seg_ref, vf, rows, docs)
        sid = sid_ref[pl.ds(PAD, rows), :]
        before = jnp.zeros((LANES, LANES), jnp.float32)
        total = jnp.zeros((rows, LANES), jnp.float32)
        for d in range(n_lag + 1):
            at = pl.ds(PAD - d, rows)
            x = jnp.where(sid_ref[at, :] == sid, vp[at, :], 0.0).astype(jnp.bfloat16)
            t, before = toeplitz(lags, d, n_lag, lower, before)
            total = total + dot(x, t)
        yp[0:rows, :] = total
        out = from_pieces(seg_ref, yp, rows, docs) + skip_ref[pl.ds(c, 1), :] * val
        table[pl.ds(c, rows, stride=channels), :] = out
        return unused

    hops = [(ring, k) for k in range(2, outer_seq) for ring in rings]
    home = lambda peer: mixed_ref.at[peer % n_wt]
    runs = min(4, channels)
    for run in range(runs):
        if of == 2 and run == runs // 2:
            table_to_rows(table, back, 0, each, *shape)
            swap_start(back, home, out_send, out_recv, flat, n, n_wt, 0, of)
            swap_wait(act_send, into, in_send, in_recv, flat, n, n_wt, 1, of)
            rows_to_table(got, table, each, each, *shape)
        lax.fori_loop(run * channels // runs, (run + 1) * channels // runs, channel, 0)
        for ring, k in hops[run * len(hops) // (runs + 1) : (run + 1) * len(hops) // (runs + 1)]:
            ring.hop(k)
    table_to_rows(table, back, channels - each, each, *shape)
    swap_start(back, home, out_send, out_recv, flat, n, n_wt, of - 1, of)
    own = pltpu.make_async_copy(back.at[flat], mixed_ref.at[w_me, flat], local_sem)
    own.start()
    for ring, k in hops[runs * len(hops) // (runs + 1) :]:
        ring.hop(k)
    own.wait()
    for part in range(of):
        swap_wait(back, home, out_send, out_recv, flat, n, n_wt, part, of)

    block = mixed_ref.at[w_me]
    far_mixed = [wires.send(block, block, (s_me, far_to(k))) for k in range(1, outer_wt)]
    ends = [wires.send(block, block, (s_me, sibling))]
    for k, at, c in far_pair:
        c.wait_recv()
        block = pair.at[far_from(k), at]
        near_pair.append(wires.send(block, block, (s_me, sibling)))
    for k in range(1, outer_wt):
        far_mixed[k - 1].wait_recv()
        block = mixed_ref.at[far_from(k)]
        ends.append(wires.send(block, block, (s_me, sibling)))
    for c in near_pair + ends:
        c.wait_recv()
    for ring in rings:
        ring.end()
    wires.sent()


def front_loading(n_lag, docs, bits, seq_count, per, inner_seq, n_in, *refs):
    sources, held, load_sem = refs[:n_in], refs[-n_in - 1 : -1], refs[-1]
    loads = [
        pltpu.make_async_copy(source, target, load_sem.at[at])
        for at, (source, target) in enumerate(zip(sources, held))
    ]
    for c in loads:
        c.start()
    front_kernel(
        n_lag, docs, bits, seq_count, per, inner_seq, loads, *held, *refs[n_in : -n_in - 1]
    )


def front_call(
    x, cot, value, gain, bias, gate, mix, down, lens, rate, freq, kr, ki, step, skip, n_lag, inner_seq,
):
    n_seq, n_wt = lax.axis_size("seq"), lax.axis_size("wt")
    n = n_seq * n_wt
    seq_count, docs = lens.shape
    local, model_width = x.shape
    states = kr.shape[1]
    width = value.shape[1]
    channels = width // n
    blocks = n_seq * local // seq_count // LANES
    per = -(-(blocks + docs) // 8) * 8
    rows = n_wt * seq_count * per
    bits = (n_lag - 1).bit_length()
    f_part = gate.shape[1] // n_wt
    low = jnp.bfloat16
    wires = front_wires(n_seq, n_wt)
    hops = (2 + inner_seq) * (n_seq // inner_seq)
    out = jax.ShapeDtypeStruct
    arrays = (x, cot, value, gain, bias, gate, mix, down, lens, rate, freq, kr, ki, step, skip)
    table = out((rows + 2 * PAD, LANES), jnp.int32)
    return pl.pallas_call(
        functools.partial(
            front_loading, n_lag, docs, bits, seq_count, per, inner_seq, len(arrays)
        ),
        out_shape=(
            out((n_wt, 2, local, model_width), low),
            out((n_seq, n_wt) + (gate.shape[0], f_part), low),
            out((n_seq, n_wt) + (mix.shape[0], f_part), low),
            out((n_seq,) + down.shape, low),
            out((n_wt, n, channels, local), low),
            out((channels, rows, LANES), low),
            out((channels, n_lag, LANES), jnp.float32),
            out((local, width), jnp.float32),
            out((model_width, width), low),
            out((2, model_width), jnp.float32),
            table, table,
        ),
        in_specs=[pl.BlockSpec(memory_space=pltpu.HBM)] * len(arrays),
        out_specs=(pl.BlockSpec(memory_space=pltpu.VMEM),) * 12,
        scratch_shapes=[pltpu.VMEM((n_wt, 8, LANES), jnp.int32)]
        + [vmem(7 + bits, channels, states)] * 2
        + [vmem(channels, states)] * 2
        + [vmem(channels, LANES)]
        + [vmem(PAD + rows, LANES)] * 3
        + [vmem(LANES, states), vmem(LANES, states), vmem(rows * channels, LANES)]
        + [pltpu.VMEM((n, channels, local), low)] * 2
        + [pltpu.VMEM((n_seq, n_wt, 16 + value.shape[0], width), low), vmem(local, model_width)]
        + [pltpu.VMEM((n, channels, local), low)]
        + [pltpu.VMEM((n_wt, gate.shape[0], f_part), low), pltpu.VMEM((n_wt, mix.shape[0], f_part), low)]
        + [pltpu.SemaphoreType.DMA((halves_of(channels),))] * 4
        + [pltpu.SemaphoreType.DMA((wires,))] * 2
        + [pltpu.SemaphoreType.DMA]
        + [pltpu.SemaphoreType.DMA((hops,))] * 6
        + [pltpu.VMEM(a.shape, a.dtype) for a in arrays]
        + [pltpu.SemaphoreType.DMA((len(arrays),))],
        compiler_params=pltpu.CompilerParams(
            vmem_limit_bytes=(38 if n <= 32 else 58) << 20, collective_id=1, has_side_effects=True
        ),
        cost_estimate=pl.CostEstimate(
            flops=60_000_000_000, bytes_accessed=4_000_000, transcendentals=0
        ),
        name="front",
    )(*[pltpu.with_memory_space_constraint(a, pltpu.HBM) for a in arrays])


GELU_A = 0.7978845608028654
GELU_B = 0.044715


def gelu_pair(v):
    square = v * v
    t = jnp.tanh(GELU_A * (v + GELU_B * v * square))
    half = 0.5 * (1.0 + t)
    slope = half + 0.5 * v * (1.0 - t * t) * (GELU_A * (1.0 + 3.0 * GELU_B * square))
    return v * half, slope


def back_wires(n_seq, n_wt, inner):
    outer = n_seq // inner
    over_seq = 4 * ((inner - 1) * outer + (outer - 1))
    over_wt = 2 * (1 + n_wt // 2 - 1)
    return over_seq + over_wt + 3 * (n_wt - 1) + (n_wt // 2 - 1) + n_wt // 2 + n_wt - 1


class SeqSum:
    def __init__(self, wires, send, near_in, far_in, so, si, outer, inner, s_to):
        self.wires, self.send, self.near_in, self.far_in = wires, send, near_in, far_in
        self.so, self.outer, self.inner, self.s_to = so, outer, inner, s_to
        self.near, self.far, self.held = {}, [], None

    def begin(self, *distances):
        for k in distances or range(1, self.outer + 1):
            k = k % self.outer
            if k in self.near:
                continue
            z = (self.so + k) % self.outer
            self.near[k] = [
                self.wires.send(self.send.at[j, z], self.near_in.at[j - 1, k], self.s_to(0, j))
                for j in range(1, self.inner)
            ]

    def turn(self, *distances):
        for k in distances or range(1, self.outer + 1):
            k = k % self.outer
            if k not in self.near or k in self.far:
                continue
            for c in self.near[k]:
                c.wait_recv()
            z = (self.so + k) % self.outer
            total = self.send[0, z].astype(jnp.float32)
            for j in range(1, self.inner):
                total = total + self.near_in[j - 1, k].astype(jnp.float32)
            self.send[0, z] = total.astype(jnp.bfloat16)
            if k:
                self.near[-k] = self.wires.send(
                    self.send.at[0, z], self.far_in.at[k - 1], self.s_to(k, 0)
                )
            self.far.append(k)

    def end(self):
        total = self.send[0, self.so].astype(jnp.float32)
        for k in range(1, self.outer):
            self.near[-k].wait_recv()
            total = total + self.far_in[k - 1].astype(jnp.float32)
        return total


def back_kernel(
    n_lag, docs, bits, seq_count, per, inner_seq,
    pair, gate_w, mix_w, down_w, mixed, v_ref, lag_ref, pre_ref, value_full, norm_vec, x_ref,
    seg_ref, sid_ref, rate_all, freq_all, kr_all, ki_all, step_ref, skip_all,
    out_ref, in_grad, gate_last, value_last, mix_last, down_out, norm_out, all_out,
    pw_re, pw_im, kr_ref, ki_ref, rate_ref, freq_ref, dt_ref, skip_ref, vf, gf, vp, gp, yp, tab_re, tab_im, table, got, back, dv_ref,
    product, expand_grad, gate_grad, mg, mg_in, mg_far, tok, tok_in, tok_far,
    down_flat, down_s, down_n, down_f, mix_s, mix_n, mix_f, gate_s, gate_n, gate_f,
    value_s, value_n, value_f, turned, value_cut, value_all, last_send, norm_last,
    in_send, in_recv, out_send, out_recv, wire_send, wire_recv, local_sem, *held,
):
    grads, thin = held[:4], held[4:]
    low, wide = jnp.bfloat16, jnp.float32
    channels, rows, _ = v_ref.shape
    states = kr_all.shape[1]
    n_seq, n_wt = lax.axis_size("seq"), lax.axis_size("wt")
    n = n_seq * n_wt
    s_me, w_me = lax.axis_index("seq"), lax.axis_index("wt")
    flat = s_me * n_wt + w_me
    row_count, model_width = x_ref.shape
    width = mix_w.shape[0]
    f_part = gate_w.shape[1]
    f_rows = f_part // n_seq
    d_band, h_band, v_band = model_width // n_seq, width // n_seq, width // n_wt
    d_rows, h_rows = d_band // n_wt, h_band // n_wt
    local_blocks = row_count // LANES // seq_count
    shape = (n_seq, n_wt, seq_count, local_blocks, per, channels)
    outer_wt = n_wt // 2
    o, i = w_me // 2, w_me % 2
    sibling = (s_me, o * 2 + 1 - i)
    far_to = lambda k: (s_me, ((o + k) % outer_wt) * 2 + i)
    outer_seq = n_seq // inner_seq
    so, si = s_me // inner_seq, s_me % inner_seq
    s_to = lambda k, j: (((so + k) % outer_seq) * inner_seq + (si + j) % inner_seq, w_me)
    wires = Wires(wire_send, wire_recv)
    sums = lambda send, near_in, far_in: SeqSum(
        wires, send, near_in, far_in, so, si, outer_seq, inner_seq, s_to
    )
    down_sum, mix_sum = sums(down_s, down_n, down_f), sums(mix_s, mix_n, mix_f)
    gate_sum, value_sum = sums(gate_s, gate_n, gate_f), sums(value_s, value_n, value_f)

    meet(flat, n, n_wt)

    def tokens(t, unused):
        j, k = 1 - t // outer_wt, outer_wt - 1 - t % outer_wt
        w = ((o + k) % outer_wt) * 2 + (i + j) % 2
        at = pl.ds(pl.multiple_of(w * row_count, row_count), row_count)
        act, slope = gelu_pair(dot(pair[w, 0], gate_w[...]))
        from_out = dot(pair[w, 1], down_w[...], 1, 1)
        expand = dot(mixed[w], mix_w[...], 0, 0)
        product[at, :] = (expand * act).astype(low)
        gate_grad[at, :] = (from_out * expand * slope).astype(low)
        grad = (from_out * act).astype(low)
        expand_grad[at, :] = grad
        mg[j, k] = dot(mix_w[...], grad, 1, 1).astype(low)
        return unused

    lax.fori_loop(0, outer_wt, tokens, 0)
    near = wires.send(mg.at[1], mg_in, sibling)
    lax.fori_loop(outer_wt, n_wt, tokens, 0)
    piece = min(256, f_part)
    every = n_wt * row_count

    def down_part(r, unused):
        at = pl.ds(pl.multiple_of(r * piece, piece), piece)
        cot = pair[:, 1].reshape(every, model_width)
        down_flat[at, :] = dot(product[:, at], cot, 0, 0)
        return unused

    lax.fori_loop(0, f_part // piece, down_part, 0)
    def bands(size):
        for s in range(n_seq):
            j = (s % inner_seq + inner_seq - si) % inner_seq
            yield j, s // inner_seq, slice(s * size, (s + 1) * size)

    for j, z, at in bands(f_rows):
        down_s[j, z] = down_flat[at, :].astype(low)
    down_sum.begin(1, 2, 3)
    near.wait_recv()
    far = []
    for k in range(1, outer_wt):
        mg[0, k] = (mg[0, k].astype(wide) + mg_in[k].astype(wide)).astype(low)
        far.append(wires.send(mg.at[0, k], mg_far.at[k - 1], far_to(k)))

    for j, z, at in bands(d_band):
        normed = pair[:, 0, :, at].reshape(every, d_band)
        gate_s[j, z] = dot(normed, gate_grad[...], 0, 0).astype(low)

    total = mg[0, 0].astype(wide) + mg_in[0].astype(wide)
    for k in range(1, outer_wt):
        far[k - 1].wait_recv()
        total = total + mg_far[k - 1].astype(wide)
    turned[...] = total
    for p in range(n):
        back[p] = turned[p * channels : (p + 1) * channels, :].astype(low)
    into = lambda peer: got
    of = halves_of(channels)
    each = channels // of
    for part in range(of):
        swap_start(back, into, in_send, in_recv, flat, n, n_wt, part, of)
    got[flat] = back[flat]

    for j, z, at in bands(h_band):
        total = dot(mixed[0, at, :], expand_grad[0:row_count, :])
        for w in range(1, n_wt):
            total = total + dot(
                mixed[w, at, :], expand_grad[w * row_count : (w + 1) * row_count, :]
            )
        mix_s[j, z] = total.astype(low)

    def token_part(t, unused):
        j, k = 1 - t // outer_wt, outer_wt - 1 - t % outer_wt
        w = ((o + k) % outer_wt) * 2 + (i + j) % 2
        at = pl.ds(pl.multiple_of(w * row_count, row_count), row_count)
        tok[j, k, 0] = dot(product[at, :], down_w[...]).astype(low)
        tok[j, k, 1] = dot(gate_grad[at, :], gate_w[...], 1, 1).astype(low)
        return unused

    lax.fori_loop(0, outer_wt, token_part, 0)
    tok_near = wires.send(tok.at[1], tok_in, sibling)
    lax.fori_loop(outer_wt, n_wt, token_part, 0)

    mine = lambda ref: own_rows(ref, w_me, n_wt, channels)
    for one, every_one in ((kr_ref, kr_all), (ki_ref, ki_all), (rate_ref, rate_all), (freq_ref, freq_all)):
        one[...] = mine(every_one)
    dt = jnp.exp(own_column(step_ref, w_me * channels, channels))
    dt_ref[...] = jnp.broadcast_to(dt, (channels, states))
    fill_powers(rate_ref[...], freq_ref[...], dt, pw_re, pw_im)
    skip_ref[...] = jnp.broadcast_to(
        own_column(skip_all, w_me * channels, channels), (channels, LANES)
    )
    zero_pad = jnp.zeros((PAD, LANES), wide)
    clear_unused(table, n_wt * seq_count, n_seq * local_blocks, per, channels)
    vf[0:PAD, :] = zero_pad
    gf[0:PAD, :] = zero_pad
    vp[0:PAD, :] = zero_pad
    gp[pl.ds(rows, PAD), :] = zero_pad
    yp[pl.ds(rows, PAD), :] = zero_pad
    tok_near.wait_recv()
    tok_sent = []
    for k in range(1, outer_wt):
        for a in range(2):
            tok[0, k, a] = (tok[0, k, a].astype(wide) + tok_in[k, a].astype(wide)).astype(low)
        tok_sent.append(wires.send(tok.at[0, k], tok_far.at[k - 1], far_to(k)))
    swap_wait(back, into, in_send, in_recv, flat, n, n_wt, 0, of)
    down_sum.turn(1, 2)
    down_sum.begin(0)
    gate_sum.begin(1, 2)
    rows_to_table(got, table, 0, each, *shape)

    lane = lax.broadcasted_iota(jnp.int32, (LANES, LANES), 1)
    row = lax.broadcasted_iota(jnp.int32, (LANES, LANES), 0)
    lower = lane >= row
    wraps = lane + row >= LANES
    flip = (lane + row == LANES - 1).astype(jnp.bfloat16)
    lag_place = (
        lax.broadcasted_iota(jnp.int32, (n_lag, LANES), 0) * LANES
        + lax.broadcasted_iota(jnp.int32, (n_lag, LANES), 1)
        + 1
    ).astype(jnp.float32)

    def channel(c, unused):
        own = pl.ds(c, 1)
        val = v_ref[c].astype(jnp.float32)
        grad = table[pl.ds(c, rows, stride=channels), :]
        vf[pl.ds(PAD, rows), :] = val
        gf[pl.ds(PAD, rows), :] = grad
        skip_grad = jnp.sum(jnp.sum(val * grad, axis=0, keepdims=True), axis=1, keepdims=True)
        g_piece = to_pieces(seg_ref, gf, rows, docs)
        gp[0:rows, :] = g_piece
        v_piece = to_pieces(seg_ref, vf, rows, docs).astype(jnp.bfloat16)
        vp[pl.ds(PAD, rows), :] = dot(v_piece, flip)
        g_turned = jnp.transpose(g_piece).astype(jnp.bfloat16)
        sid = sid_ref[pl.ds(PAD, rows), :]
        lags = lag_ref[c]
        before = jnp.zeros((LANES, LANES), jnp.float32)
        total = jnp.zeros((rows, LANES), jnp.float32)
        earlier = None
        sums = []
        for d in range(n_lag + 1):
            ahead = pl.ds(PAD + d, rows)
            x = jnp.where(sid_ref[ahead, :] == sid, gp[pl.ds(d, rows), :], 0.0)
            t, before = toeplitz(lags, d, n_lag, lower, before)
            total = total + dot(x.astype(jnp.bfloat16), t, 1, 1)
            at = pl.ds(PAD - d, rows)
            back = jnp.where(sid_ref[at, :] == sid, vp[at, :], 0.0).astype(jnp.bfloat16)
            pairs = dot(g_turned, back)
            if d:
                skew = jnp.where(wraps, earlier, pairs)
                skew = pltpu.roll(skew, 0, 1, stride=1, stride_axis=0)
                sums.append(jnp.sum(skew, axis=0, keepdims=True))
            earlier = pairs
        yp[0:rows, :] = total
        out = from_pieces(seg_ref, yp, rows, docs) + skip_ref[own, :] * grad
        table[pl.ds(c, rows, stride=channels), :] = out
        lag_grad = jnp.concatenate(sums, axis=0)
        fill_lane_powers(pw_re, pw_im, c, tab_re, tab_im, 1)
        both = jnp.concatenate([lag_grad, lag_grad * lag_place], axis=0).astype(jnp.bfloat16)
        part_re = dot(both, tab_re[...].astype(jnp.bfloat16))
        part_im = dot(both, tab_im[...].astype(jnp.bfloat16))
        dr, di = power_rows(pw_re, pw_im, c, 7, bits, n_lag)
        gr, gi = cmul(dr, di, part_re[0:n_lag], part_im[0:n_lag])
        hr, hi = cmul(dr, di, part_re[n_lag:], part_im[n_lag:])
        gr, gi, hr, hi = (jnp.sum(a, axis=0, keepdims=True) for a in (gr, gi, hr, hi))
        kr, ki, dt = kr_ref[own, :], ki_ref[own, :], dt_ref[own, :]
        rate_grad = -dt * (kr * hr - ki * hi)
        freq_grad = -dt * (kr * hi + ki * hr)
        for at, row_out in enumerate((rate_grad, freq_grad, gr + skip_grad, -gi)):
            grads[at][own, :] = row_out
        step = jnp.sum(
            rate_grad * rate_ref[own, :] + freq_grad * freq_ref[own, :], axis=1, keepdims=True
        )
        for at, one in enumerate((step, skip_grad)):
            thin[at][own, :] = jnp.broadcast_to(one, (1, LANES))
        return unused

    lax.fori_loop(0 * channels // 4, 1 * channels // 4, channel, 0)
    down_sum.turn(3)
    gate_sum.begin(3)
    lax.fori_loop(1 * channels // 4, 2 * channels // 4, channel, 0)
    gate_sum.turn(1)
    gate_sum.begin(0)
    home = lambda peer: dv_ref
    if of == 2:
        table_to_rows(table, back, 0, each, *shape)
        swap_start(back, home, out_send, out_recv, flat, n, n_wt, 0, of)
        swap_wait(back, into, in_send, in_recv, flat, n, n_wt, 1, of)
        rows_to_table(got, table, each, each, *shape)
    lax.fori_loop(2 * channels // 4, 3 * channels // 4, channel, 0)
    down_sum.turn(0)
    gate_sum.turn(2)
    lax.fori_loop(3 * channels // 4, 4 * channels // 4, channel, 0)
    gate_sum.turn(3)
    table_to_rows(table, back, channels - each, each, *shape)
    swap_start(back, home, out_send, out_recv, flat, n, n_wt, of - 1, of)
    own = pltpu.make_async_copy(back.at[flat], dv_ref.at[flat], local_sem)
    own.start()
    mix_sum.begin()
    for at in range(4):
        all_out[w_me, :, pl.ds(at * states, states)] = grads[at][...]
    for at in range(2):
        all_out[w_me, :, pl.ds(4 * states + at * LANES, LANES)] = thin[at][...]
    block = all_out.at[w_me]
    far_all = [wires.send(block, block, far_to(k)) for k in range(1, outer_wt)]
    near_all = [wires.send(block, block, sibling)]

    for c in tok_sent:
        c.wait_recv()
    result = x_ref[...].astype(wide) + tok[0, 0, 0].astype(wide) + tok_in[0, 0].astype(wide)
    for k in range(1, outer_wt):
        result = result + tok_far[k - 1, 0].astype(wide)
    out_ref[...] = result.astype(low)
    own.wait()
    for part in range(of):
        swap_wait(back, home, out_send, out_recv, flat, n, n_wt, part, of)

    gate_sum.turn(0)
    for p in range(n):
        turned[pl.ds(p * channels, channels), :] = dv_ref[p].astype(wide)
    value_grad = jnp.transpose(turned[...]) * gelu_pair(pre_ref[...])[1]
    value_low = value_grad.astype(low)
    for w in range(n_wt):
        value_cut[w] = value_low[:, w * v_band : (w + 1) * v_band]
    value_all[w_me] = value_cut[w_me]
    moves = []
    for k in range(outer_wt):
        for j in range(2):
            if k or j:
                w = ((o + k) % outer_wt) * 2 + (i + j) % 2
                moves.append(wires.send(value_cut.at[w], value_all.at[w_me], (s_me, w)))

    normed_grad = dot(value_low, value_full[...], 1, 1)
    normed_grad = normed_grad + tok[0, 0, 1].astype(wide) + tok_in[0, 1].astype(wide)
    for k in range(1, outer_wt):
        normed_grad = normed_grad + tok_far[k - 1, 1].astype(wide)
    x32 = x_ref[...].astype(wide)
    centered = x32 - jnp.mean(x32, axis=-1, keepdims=True)
    scale = lax.rsqrt(jnp.mean(centered * centered, axis=-1, keepdims=True) + norm_epsilon)
    xhat = centered * scale
    g = normed_grad * norm_vec[0:1, :]
    inner_grad = g - jnp.mean(g, axis=-1, keepdims=True)
    inner_grad = inner_grad - xhat * jnp.mean(g * xhat, axis=-1, keepdims=True)
    in_grad[...] = pair[w_me, 1].astype(wide) + inner_grad * scale
    vectors = jnp.concatenate(
        [
            jnp.sum(normed_grad * xhat, axis=0, keepdims=True),
            jnp.sum(normed_grad, axis=0, keepdims=True),
            jnp.zeros((14, model_width), wide),
        ],
        axis=0,
    )
    norm_last[...] = vectors

    mix_sum.turn()
    for c in moves:
        c.wait_recv()
    vector_lanes = min(d_band, LANES)
    for j, z, at in bands(d_band):
        normed = pair[:, 0, :, at].reshape(every, d_band)
        value_s[j, z, 0:d_band, :] = dot(
            normed, value_all[...].reshape(every, v_band), 0, 0
        ).astype(low)
        value_s[j, z, pl.ds(d_band, 16), 0:vector_lanes] = norm_last[:, at].astype(low)
    value_sum.begin()
    for one in (down_sum, gate_sum, mix_sum):
        one.begin()
        one.turn()
    down_out[...] = down_sum.end()
    mix_band = mix_sum.end().astype(low)
    gate_band = gate_sum.end().astype(low)
    value_sum.turn()
    for w in range(n_wt):
        gate_cut = gate_band[w * d_rows : (w + 1) * d_rows, :]
        mix_cut = mix_band[w * h_rows : (w + 1) * h_rows, :]
        last_send[w] = jnp.concatenate([gate_cut, mix_cut], axis=0)
    heads = gate_last
    heads[w_me] = last_send[w_me]
    ends = []

    def spread(source, target):
        for k in range(outer_wt):
            for j in range(2):
                if k or j:
                    w = ((o + k) % outer_wt) * 2 + (i + j) % 2
                    ends.append(wires.send(source.at[w], target.at[w_me], (s_me, w)))

    spread(last_send, heads)
    for k in range(1, outer_wt):
        far_all[k - 1].wait_recv()
        block = all_out.at[((o + outer_wt - k) % outer_wt) * 2 + i]
        near_all.append(wires.send(block, block, sibling))
    value_band = value_sum.end()
    tail_send = mix_last
    for w in range(n_wt):
        tail_send[w, 0:d_rows, :] = value_band[w * d_rows : (w + 1) * d_rows, :].astype(low)
        tail_send[w, pl.ds(d_rows, 16), :] = value_band[d_band : d_band + 16, :].astype(low)
    value_last[w_me] = tail_send[w_me]
    spread(tail_send, value_last)
    for c in ends + near_all:
        c.wait_recv()
    wires.sent()
    norm = jnp.zeros((16, v_band), wide)
    for w in range(n_wt):
        norm = norm + value_last[w, pl.ds(d_rows, 16), :].astype(wide)
    norm_out[...] = norm


def back_call(
    pair, gate_w, mix_w, down_w, mixed, v, lags, pre, value_full, norm_vec, x, seg, sid, rate, freq, kr,
    ki, step, skip, seq_count, docs, n_lag, inner_seq,
):
    n_seq, n_wt = lax.axis_size("seq"), lax.axis_size("wt")
    n = n_seq * n_wt
    channels, rows, _ = v.shape
    states = kr.shape[1]
    per = rows // (n_wt * seq_count)
    bits = (n_lag - 1).bit_length()
    local, model_width = x.shape
    width, f_part = mix_w.shape
    d_band, h_band, v_band = model_width // n_seq, width // n_seq, width // n_wt
    d_rows, h_rows = d_band // n_wt, h_band // n_wt
    f_rows = f_part // n_seq
    inner, outer, outer_wt = inner_seq, n_seq // inner_seq, n_wt // 2
    low = jnp.bfloat16
    half = lambda *s: pltpu.VMEM(s, low)
    out = jax.ShapeDtypeStruct
    wires = back_wires(n_seq, n_wt, inner)

    def seq_scratch(*block):
        return [
            half(inner, outer, *block), half(max(inner - 1, 1), outer, *block),
            half(max(outer - 1, 1), *block),
        ]

    every = n_wt * local
    return pl.pallas_call(
        functools.partial(back_kernel, n_lag, docs, bits, seq_count, per, inner_seq),
        out_shape=(
            out((local, model_width), low),
            out((local, model_width), jnp.float32),
            out((n_wt, d_rows + h_rows, f_part), low),
            out((n_wt, d_rows + 16, v_band), low),
            out((n_wt, d_rows + 16, v_band), low),
            out((f_rows, model_width), jnp.float32),
            out((16, v_band), jnp.float32),
            out((n_wt, channels, 4 * states + 2 * LANES), jnp.float32),
        ),
        in_specs=[pl.BlockSpec(memory_space=pltpu.VMEM)] * 19,
        out_specs=(pl.BlockSpec(memory_space=pltpu.VMEM),) * 8,
        scratch_shapes=[vmem(7 + bits, channels, states)] * 2
        + [vmem(channels, states)] * 5
        + [vmem(channels, LANES)]
        + [vmem(PAD + rows, LANES)] * 5
        + [vmem(LANES, states), vmem(LANES, states), vmem(rows * channels, LANES)]
        + [half(n, channels, local)] * 3
        + [half(every, f_part)] * 3
        + [half(2, outer_wt, width, local), half(outer_wt, width, local)]
        + [half(max(outer_wt - 1, 1), width, local)]
        + [half(2, outer_wt, 2, local, model_width), half(outer_wt, 2, local, model_width)]
        + [half(max(outer_wt - 1, 1), 2, local, model_width)]
        + [vmem(f_part, model_width)]
        + seq_scratch(f_rows, model_width)
        + seq_scratch(h_band, f_part)
        + seq_scratch(d_band, f_part)
        + seq_scratch(d_band + 16, v_band)
        + [vmem(width, local), half(n_wt, local, v_band), half(n_wt, local, v_band)]
        + [half(n_wt, d_rows + h_rows, f_part), vmem(16, model_width)]
        + [pltpu.SemaphoreType.DMA((halves_of(channels),))] * 4
        + [pltpu.SemaphoreType.DMA((wires,))] * 2
        + [pltpu.SemaphoreType.DMA]
        + [vmem(channels, states)] * 4
        + [vmem(channels, LANES)] * 2,
        compiler_params=pltpu.CompilerParams(
            vmem_limit_bytes=(39 if n <= 32 else 62) << 20, collective_id=2, has_side_effects=True
        ),
        cost_estimate=pl.CostEstimate(
            flops=60_000_000_000, bytes_accessed=4_000_000, transcendentals=0
        ),
        name="back",
    )(
        pair, gate_w, mix_w, down_w, mixed, v, lags, pre, value_full, norm_vec, x, seg, sid, rate, freq,
        kr, ki, step, skip,
    )


def finish_kernel(
    out_ref, grad_ref, heads, tails, down_ref, norm_ref, all_ref,
    outputs, in_grad, gain, bias, gate, value, mix, down, rate, freq, kr, ki, step, skip,
):
    n_seq, n_wt = lax.axis_size("seq"), lax.axis_size("wt")
    w_me = lax.axis_index("wt")
    wide = jnp.float32
    d_rows, h_rows = gate.shape[0], mix.shape[0]
    f_rows = heads.shape[2] // n_seq
    channels, states = all_ref.shape[1], rate.shape[1]
    outputs[...] = out_ref[...]
    in_grad[...] = grad_ref[...]
    down[...] = down_ref[...]
    for ref, first, rows in ((gate, 0, d_rows), (mix, d_rows, h_rows)):
        parts = [heads[w].astype(wide)[first : first + rows, :] for w in range(n_wt)]
        cut = [
            parts[w][:, s * f_rows : (s + 1) * f_rows] for s in range(n_seq) for w in range(n_wt)
        ]
        ref[...] = jnp.concatenate(cut, axis=1)
    value[...] = jnp.concatenate(
        [tails[w].astype(wide)[0:d_rows, :] for w in range(n_wt)], axis=1
    )
    share = norm_ref.shape[1]
    own = pltpu.roll(norm_ref[...], (share - w_me * d_rows) % share, 1)[:, 0:d_rows]
    gain[...] = own[0:1, :]
    bias[...] = own[1:2, :]
    for at, ref in enumerate((rate, freq, kr, ki)):
        for w in range(n_wt):
            ref[pl.ds(w * channels, channels), :] = all_ref[w, :, pl.ds(at * states, states)]
    total = n_wt * channels
    lane = lax.broadcasted_iota(jnp.int32, (channels, LANES), 1)
    place = lax.broadcasted_iota(jnp.int32, (channels, LANES), 0)
    for at, ref in enumerate((step, skip)):
        row = jnp.zeros((1, LANES), wide)
        for w in range(n_wt):
            thin = all_ref[w, :, pl.ds(4 * states + at * LANES, LANES)]
            hit = jnp.where(lane == place + w * channels, thin, 0.0)
            row = row + jnp.sum(hit, axis=0, keepdims=True)
        ref[...] = row[:, 0:total]


def finish_call(out, grad, heads, tails, down, norm, packed, gate_width, d_rows, h_rows, states):
    n_wt, channels, _ = packed.shape
    total = n_wt * channels
    wide = jnp.float32
    shape = jax.ShapeDtypeStruct
    full = shape((total, states), wide)
    return pl.pallas_call(
        finish_kernel,
        out_shape=(
            shape(out.shape, out.dtype), shape(grad.shape, wide), shape((1, d_rows), wide),
            shape((1, d_rows), wide), shape((d_rows, gate_width), wide),
            shape((d_rows, n_wt * tails.shape[2]), wide), shape((h_rows, gate_width), wide),
            shape(down.shape, wide), full, full, full, full, shape((1, total), wide),
            shape((1, total), wide),
        ),
        in_specs=[pl.BlockSpec(memory_space=pltpu.VMEM)] * 7,
        out_specs=(pl.BlockSpec(memory_space=pltpu.VMEM),) * 14,
        compiler_params=pltpu.CompilerParams(vmem_limit_bytes=12 << 20),
        name="finish",
    )(out, grad, heads, tails, down, norm, packed)


BOTH = ("seq", "wt")
norm_epsilon = 1e-05


def gelu_tanh(pre_act):
    return jax.nn.gelu(pre_act, approximate=True)


def on_device(
    inputs, cotangent, doc_lengths, norm_gain, norm_bias, gate_weight, value_weight, mix_weight,
    down_weight, decay_rate, frequency, kernel_re, kernel_im, log_step, skip_gain,
):
    seq_count, local_len, model_width = inputs.shape
    n_seq, n_wt = lax.axis_size("seq"), lax.axis_size("wt")
    inner_seq = 2 if n_seq <= 8 else 8
    rows = lambda x: x.reshape(seq_count * local_len, model_width)
    line = lambda x: x.reshape(1, -1)
    width, gate_width = mix_weight.shape[0] * n_seq * n_wt, gate_weight.shape[1]
    f_part = gate_width // n_wt
    n_lag = local_len * n_seq // 2 // LANES
    params = (decay_rate, frequency, kernel_re, kernel_im, line(log_step), line(skip_gain))
    pair, gate_own, mix_own, down_own, mixed, value_ch, lags, pre, value_full, norm, seg, sid = front_call(
        rows(inputs), rows(cotangent), value_weight, line(norm_gain), line(norm_bias), gate_weight,
        mix_weight, down_weight, doc_lengths, *params, n_lag, inner_seq,
    )
    raw = back_call(
        pair, gate_own.reshape(model_width, f_part), mix_own.reshape(width, f_part),
        down_own.reshape(f_part, model_width), mixed.reshape(n_wt, width, -1), value_ch, lags, pre,
        value_full, norm, rows(inputs), seg, sid, *params, seq_count, doc_lengths.shape[1], n_lag,
        inner_seq,
    )
    out, grad, heads, tails, unused, down, vectors, packed = raw
    done = finish_call(
        out, grad, heads, tails, down, vectors, packed, gate_width, value_weight.shape[0],
        mix_weight.shape[0], kernel_re.shape[1],
    )
    flat = [done[i].reshape(-1) for i in (2, 3, 12, 13)]
    return (
        done[0].reshape(inputs.shape), done[1].reshape(inputs.shape), flat[0], flat[1], *done[4:8],
        *done[8:12], flat[2], flat[3],
    )


def solution(mesh):
    in_specs = (
        P("wt", "seq", None),
        P("wt", "seq", None),
        P("wt", None),
        P(("seq", "wt")),
        P(("seq", "wt")),
        P(("seq", "wt"), None),
        P(("seq", "wt"), None),
        P(("seq", "wt"), None),
        P(("seq", "wt"), None),
        P("seq", None),
        P("seq", None),
        P("seq", None),
        P("seq", None),
        P("seq"),
        P("seq"),
    )
    out_specs = (
        P("wt", "seq", None),
        P("wt", "seq", None),
        P(("seq", "wt")),
        P(("seq", "wt")),
        P(("seq", "wt"), None),
        P(("seq", "wt"), None),
        P(("seq", "wt"), None),
        P(("seq", "wt"), None),
        P("seq", None),
        P("seq", None),
        P("seq", None),
        P("seq", None),
        P("seq"),
        P("seq"),
    )
    return jax.shard_map(
        on_device, mesh=mesh, in_specs=in_specs, out_specs=out_specs, check_vma=False
    )
```

```python
import functools

import jax
import jax.numpy as jnp
from jax import lax
from jax.experimental import pallas as pl
from jax.experimental.pallas import tpu as pltpu
from jax.sharding import PartitionSpec as P

LANES = 128
PAD = 16


MESH = pl.DeviceIdType.MESH


def place_of(flat, n_wt):
    return (flat // n_wt, flat % n_wt)


def meet(flat, n, n_wt):
    barrier = pltpu.get_barrier_semaphore()

    def tell(r, unused):
        pl.semaphore_signal(
            barrier, inc=1, device_id=place_of((flat + r) % n, n_wt), device_id_type=MESH
        )
        return unused

    lax.fori_loop(1, n, tell, 0)
    pl.semaphore_wait(barrier, n - 1)


def swap_start(send, target_of, send_sem, recv_sem, flat, n, n_wt, part, of):
    rows = pl.ds(part * (send.shape[1] // of), send.shape[1] // of)

    def one(r, unused):
        peer = (flat + r) % n
        pltpu.make_async_remote_copy(
            src_ref=send.at[peer, rows], dst_ref=target_of(peer).at[flat, rows],
            send_sem=send_sem.at[part], recv_sem=recv_sem.at[part],
            device_id=place_of(peer, n_wt), device_id_type=MESH,
        ).start()
        return unused

    lax.fori_loop(1, n, one, 0)


def swap_wait(send, target_of, send_sem, recv_sem, flat, n, n_wt, part, of):
    every, rows = pl.ds(0, n - 1), pl.ds(part * (send.shape[1] // of), send.shape[1] // of)
    pltpu.make_async_remote_copy(
        src_ref=send.at[every, rows], dst_ref=target_of(flat).at[every, rows],
        send_sem=send_sem.at[part], recv_sem=recv_sem.at[part],
        device_id=place_of((flat + 1) % n, n_wt), device_id_type=MESH,
    ).wait()


def halves_of(channels):
    return 2 if channels % 16 == 0 else 1


def rows_to_table(got, table, first, count, n_seq, n_wt, seq_count, local_blocks, per, channels):
    for s in range(n_seq):
        for w in range(n_wt):
            for k in range(seq_count):
                for b in range(local_blocks):
                    row = (w * seq_count + k) * per + s * local_blocks + b
                    lanes = pl.ds((k * local_blocks + b) * LANES, LANES)
                    table[pl.ds(row * channels + first, count), :] = got[
                        s * n_wt + w, pl.ds(first, count), lanes
                    ].astype(jnp.float32)


def table_to_rows(table, send, first, count, n_seq, n_wt, seq_count, local_blocks, per, channels):
    for s in range(n_seq):
        for w in range(n_wt):
            for k in range(seq_count):
                for b in range(local_blocks):
                    row = (w * seq_count + k) * per + s * local_blocks + b
                    lanes = pl.ds((k * local_blocks + b) * LANES, LANES)
                    send[s * n_wt + w, pl.ds(first, count), lanes] = table[
                        pl.ds(row * channels + first, count), :
                    ].astype(jnp.bfloat16)


def clear_unused(table, seqs, blocks, per, channels):
    for s in range(seqs):
        table[pl.ds((s * per + blocks) * channels, (per - blocks) * channels), :] = jnp.zeros(
            ((per - blocks) * channels, LANES), jnp.float32
        )


def share_over_wt(ref, s_me, w_me, n_wt, send_sem, recv_sem):
    inner = 2
    outer = n_wt // inner
    o, i = w_me // inner, w_me % inner
    other = (s_me, o * inner + 1 - i)

    def copy(block, slot, to):
        return pltpu.make_async_remote_copy(
            src_ref=ref.at[block], dst_ref=ref.at[block], send_sem=send_sem.at[slot],
            recv_sem=recv_sem.at[slot], device_id=to, device_id_type=MESH,
        )

    far = [copy(w_me, k, (s_me, ((o + k) % outer) * inner + i)) for k in range(1, outer)]
    near = [copy(w_me, outer, other)]
    for c in far + near:
        c.start()
    for k in range(1, outer):
        block = ((o + outer - k) % outer) * inner + i
        far[k - 1].wait_recv()
        c = copy(block, outer + k, other)
        c.start()
        near.append(c)
    for c in far:
        c.wait_send()
    for c in near:
        c.wait()


def cmul(ar, ai, br, bi):
    return ar * br - ai * bi, ar * bi + ai * br


def power_rows(pw_re, pw_im, c, first, count, rows):
    width = pw_re.shape[2]
    place = lax.broadcasted_iota(jnp.int32, (rows, width), 0)
    re = jnp.ones((rows, width), jnp.float32)
    im = jnp.zeros((rows, width), jnp.float32)
    for bit in range(count):
        on = (place & (1 << bit)) != 0
        fr = jnp.where(on, pw_re[first + bit, pl.ds(c, 1), :], 1.0)
        fi = jnp.where(on, pw_im[first + bit, pl.ds(c, 1), :], 0.0)
        re, im = cmul(re, im, fr, fi)
    return re, im


def fill_lane_powers(pw_re, pw_im, c, tab_re, tab_im, extra):
    re, im = power_rows(pw_re, pw_im, c, 0, 3, 8)
    if extra:
        re, im = cmul(re, im, pw_re[0, pl.ds(c, 1), :], pw_im[0, pl.ds(c, 1), :])
    tab_re[0:8, :] = re
    tab_im[0:8, :] = im
    have, bit = 8, 3
    while have < LANES:
        re, im = cmul(
            tab_re[0:have, :],
            tab_im[0:have, :],
            pw_re[bit, pl.ds(c, 1), :],
            pw_im[bit, pl.ds(c, 1), :],
        )
        tab_re[have : 2 * have, :] = re
        tab_im[have : 2 * have, :] = im
        have, bit = 2 * have, bit + 1


def to_pieces(seg, val, rows, docs):
    total = jnp.zeros((rows, LANES), jnp.float32)
    for j in range(docs):
        at = pl.ds(PAD - j, rows)
        total = total + jnp.where(seg[at, :] == j, val[at, :], 0.0)
    return total


def from_pieces(seg, piece, rows, docs):
    own = seg[pl.ds(PAD, rows), :]
    total = jnp.zeros((rows, LANES), jnp.float32)
    for j in range(docs):
        total = total + jnp.where(own == j, piece[pl.ds(j, rows), :], 0.0)
    return total


def toeplitz(lags, d, last, lower, before):
    if d < last:
        row = jnp.broadcast_to(lags[d : d + 1, :], (LANES, LANES))
        here = pltpu.roll(row, 0, 1, stride=1, stride_axis=0)
    else:
        here = jnp.zeros((LANES, LANES), jnp.float32)
    return jnp.where(lower, here, before).astype(jnp.bfloat16), here


def dot(a, b, ca=1, cb=0):
    return lax.dot_general(a, b, (((ca,), (cb,)), ((), ())), preferred_element_type=jnp.float32)


def vmem(*shape):
    return pltpu.VMEM(shape, jnp.float32)


def own_column(row_ref, first, count):
    size = row_ref.shape[1]
    lane = lax.broadcasted_iota(jnp.int32, (count, size), 1)
    place = lax.broadcasted_iota(jnp.int32, (count, size), 0)
    return jnp.sum(jnp.where(lane == place + first, row_ref[...], 0.0), axis=1, keepdims=True)


def own_rows(ref, w_me, n_wt, count):
    out = ref[0:count, :]
    for w in range(1, n_wt):
        out = jnp.where(w_me == w, ref[w * count : (w + 1) * count, :], out)
    return out


def fill_powers(rate, freq, dt, pw_re, pw_im):
    for p in range(pw_re.shape[0]):
        if p % 4:
            re, im = cmul(re, im, re, im)
        else:
            mag, angle = jnp.exp(-rate * dt * float(1 << p)), freq * dt * float(1 << p)
            re, im = mag * jnp.cos(angle), mag * jnp.sin(angle)
        pw_re[p] = re
        pw_im[p] = im


def fill_segments(lens, seg_ref, sid_ref, docs, blocks, per, seqs):
    rows = seg_ref.shape[0]
    seg_ref[0:PAD, :] = jnp.full((PAD, LANES), -1, jnp.int32)
    sid_ref[0:PAD, :] = jnp.full((PAD, LANES), -2, jnp.int32)
    seg_ref[rows - PAD : rows, :] = jnp.full((PAD, LANES), -1, jnp.int32)
    sid_ref[rows - PAD : rows, :] = jnp.full((PAD, LANES), -2, jnp.int32)
    row = lax.broadcasted_iota(jnp.int32, (per, LANES), 0)
    position = row * LANES + lax.broadcasted_iota(jnp.int32, (per, LANES), 1)
    group = seqs // lens.shape[0]
    for q in range(seqs):
        ends = jnp.zeros((1, 1), jnp.int32)
        seg = jnp.zeros((per, LANES), jnp.int32)
        for j in range(docs):
            ends = ends + lens[q // group, q % group : q % group + 1, j : j + 1]
            seg = seg + (position >= ends).astype(jnp.int32)
        seg = jnp.where(row < blocks, seg, -1)
        at = pl.ds(PAD + q * per, per)
        seg_ref[at, :] = seg
        best = jnp.full((per, LANES), -1, jnp.int32)
        for i in range(blocks):
            one = seg[i : i + 1, :]
            best = jnp.maximum(best, jnp.where(one + i == row, one, -1))
        best = jnp.max(best.astype(jnp.float32), axis=1, keepdims=True).astype(jnp.int32)
        best = jnp.where(best >= 0, best + docs * q, -1)
        sid_ref[at, :] = jnp.broadcast_to(best, (per, LANES))


class Wires:
    def __init__(self, send_sem, recv_sem):
        self.send_sem, self.recv_sem, self.used, self.open = send_sem, recv_sem, 0, []

    def send(self, source, target, to):
        c = pltpu.make_async_remote_copy(
            src_ref=source, dst_ref=target, send_sem=self.send_sem.at[self.used],
            recv_sem=self.recv_sem.at[self.used], device_id=to, device_id_type=MESH,
        )
        self.used += 1
        self.open.append(c)
        c.start()
        return c

    def sent(self):
        for c in self.open:
            c.wait_send()
        self.open = []


class SeqGather:
    def __init__(self, ref, send_sem, recv_sem, so, si, outer, inner, w_me):
        self.ref, self.send_sem, self.recv_sem = ref, send_sem, recv_sem
        self.so, self.si, self.outer, self.inner, self.w_me = so, si, outer, inner, w_me

    def copy(self, z, slot, to_z, j):
        block = self.ref.at[z * self.inner + self.si]
        to = (to_z * self.inner + (self.si + j) % self.inner, self.w_me)
        return pltpu.make_async_remote_copy(
            src_ref=block, dst_ref=block, send_sem=self.send_sem.at[slot],
            recv_sem=self.recv_sem.at[slot], device_id=to, device_id_type=MESH,
        )

    def along(self, up, k, z):
        slot = (0 if up else self.outer) + k
        return self.copy(z, slot, self.so + 1 if up else self.so - 1, 0)

    def across(self, z, j):
        return self.copy(z, 2 * self.outer + z * self.inner + j, self.so, j)

    def ends(self, up):
        return self.so < self.outer - 1 if up else self.so > 0

    def launch(self, z, k, ups):
        for up in ups:
            if k < self.outer:
                pl.when(self.ends(up))(lambda up=up: self.along(up, k, z).start())
        for j in range(1, self.inner):
            self.across(z, j).start()

    def begin(self):
        self.launch(self.so, 1, (True, False))

    def hop(self, k):
        for up in (True, False):
            z = self.so - k if up else self.so + k
            there = z >= 0 if up else z < self.outer

            @pl.when(there)
            def _():
                self.along(up, k, z).wait_recv()
                self.launch(z, k + 1, (up,))

    def end(self):
        for z in range(self.outer):
            for j in range(1, self.inner):
                block = self.copy(z, 2 * self.outer + z * self.inner + j, self.so, j)
                block.wait_recv()
                block.wait_send()
        for k in range(1, self.outer):
            for up in (True, False):
                z = self.so - k + 1 if up else self.so + k - 1
                from_here = (z >= 0 if up else z < self.outer) & self.ends(up)
                pl.when(from_here)(lambda up=up, k=k, z=z: self.along(up, k, z).wait_send())


def rms(x32):
    mean = jnp.mean(x32, axis=-1, keepdims=True)
    centered = x32 - mean
    spread = jnp.mean(centered * centered, axis=-1, keepdims=True)
    return centered * lax.rsqrt(spread + norm_epsilon)


def regroup(x, n_seq, n_wt, width):
    cut = lambda s, w: x[:, (s * n_wt + w) * width : (s * n_wt + w + 1) * width]
    return [jnp.concatenate([cut(s, w) for s in range(n_seq)], axis=1) for w in range(n_wt)]


def front_wires(n_seq, n_wt):
    value = (n_seq - 1) + n_seq * (n_wt // 2 - 1) + n_seq * (n_wt // 2)
    weights = 2 * (n_wt - 1)
    tokens = 2 * (n_wt // 2 - 1) + 2 * (n_wt // 2)
    mixed = 2 * ((n_wt // 2 - 1) + n_wt // 2)
    return value + weights + tokens + mixed


def front_kernel(
    n_lag, docs, bits, seq_count, per, inner_seq, loads,
    x_ref, cot_ref, value_in, gain_in, bias_in, gate_in, mix_in, down_in, lens_in, rate_ref, freq_ref,
    kr_all, ki_all, step_ref, skip_all,
    pair, gate_out, mix_out, down_out, mixed_ref, v_ref, lag_ref, pre_ref, value_full, norm_out,
    seg_ref, sid_ref,
    lens, pw_re, pw_im, kr_ref, ki_ref, skip_ref, vf, vp, yp, tab_re, tab_im, table, got, back, front, xhat, act_send, gate_cut, mix_cut,
    in_send, in_recv, out_send, out_recv, wire_send, wire_recv, local_sem, *hop_sems,
):
    channels, rows, _ = v_ref.shape
    n_seq, n_wt = lax.axis_size("seq"), lax.axis_size("wt")
    n = n_seq * n_wt
    s_me, w_me = lax.axis_index("seq"), lax.axis_index("wt")
    flat = s_me * n_wt + w_me
    row_count, model_width = x_ref.shape
    width = pre_ref.shape[1]
    d_rows, h_rows, f_rows = gate_in.shape[0], mix_in.shape[0], down_in.shape[0]
    local_blocks = row_count // LANES // seq_count
    shape = (n_seq, n_wt, seq_count, local_blocks, per, channels)
    outer_wt = n_wt // 2
    o, i = w_me // 2, w_me % 2
    sibling = o * 2 + 1 - i
    far_to = lambda k: ((o + k) % outer_wt) * 2 + i
    far_from = lambda k: ((o + outer_wt - k) % outer_wt) * 2 + i
    outer_seq = n_seq // inner_seq
    so, si = s_me // inner_seq, s_me % inner_seq
    rings = [
        SeqGather(ref, hop_sems[2 * at], hop_sems[2 * at + 1], so, si, outer_seq, inner_seq, w_me)
        for at, ref in enumerate((down_out, gate_out, mix_out))
    ]
    down_ring, gate_ring, mix_ring = rings
    wires = Wires(wire_send, wire_recv)

    meet(flat, n, n_wt)
    for c in loads:
        c.wait()

    lens[w_me, 0:seq_count, 0:docs] = lens_in[...]
    block = lens.at[w_me]
    far_lens = [wires.send(block, block, (s_me, far_to(k))) for k in range(1, outer_wt)]
    near_lens = [wires.send(block, block, (s_me, sibling))]

    norm_rows = jnp.concatenate(
        [gain_in[...], bias_in[...], jnp.zeros((14, d_rows), jnp.bfloat16)], axis=0
    ).astype(jnp.float32)
    norm_rows = jnp.concatenate([norm_rows, jnp.zeros((16, LANES - d_rows), jnp.float32)], axis=1)
    norm_rows = pltpu.roll(norm_rows, (flat * d_rows) % LANES, 1)
    front[s_me, w_me, 0:16, :] = jnp.zeros((16, width), jnp.bfloat16)
    front[s_me, w_me, 0:16, 0:LANES] = norm_rows.astype(jnp.bfloat16)
    front[s_me, w_me, pl.ds(16, d_rows), :] = value_in[...]
    first = []
    for k in range(1, n_seq):
        to = ((s_me + k) % n_seq, w_me)
        first.append(wires.send(front.at[s_me, w_me], front.at[s_me, w_me], to))

    second, third = [], []

    def spread_value(s):
        block = front.at[s, w_me]
        for k in range(1, outer_wt):
            second.append((s, k, wires.send(block, block, (s_me, far_to(k)))))
        third.append(wires.send(block, block, (s_me, sibling)))

    spread_value(s_me)
    down_out[s_me] = down_in[...]
    down_ring.begin()

    for ref, cut in ((gate_in, gate_cut), (mix_in, mix_cut)):
        whole = ref[...].astype(jnp.float32)
        for w, part in enumerate(regroup(whole, n_seq, n_wt, f_rows)):
            cut[w] = part.astype(jnp.bfloat16)
    gate_out[s_me, w_me] = gate_cut[w_me]
    mix_out[s_me, w_me] = mix_cut[w_me]
    turn = []
    for source, target in ((gate_cut, gate_out), (mix_cut, mix_out)):
        for k in range(outer_wt):
            for j in range(2):
                if k or j:
                    w = ((o + k) % outer_wt) * 2 + (i + j) % 2
                    turn.append(wires.send(source.at[w], target.at[s_me, w_me], (s_me, w)))

    chunk = min(32, row_count)

    def normalise(r, unused):
        at = pl.ds(r * chunk, chunk)
        xhat[at, :] = rms(x_ref[at, :].astype(jnp.float32))
        return unused

    lax.fori_loop(0, row_count // chunk, normalise, 0)
    pair[w_me, 1] = cot_ref[...]
    mine = lambda ref: own_rows(ref, w_me, n_wt, channels)
    fill_powers(
        mine(rate_ref), mine(freq_ref),
        jnp.exp(own_column(step_ref, w_me * channels, channels)), pw_re, pw_im,
    )
    kr_ref[...] = mine(kr_all)
    ki_ref[...] = mine(ki_all)
    skip_ref[...] = jnp.broadcast_to(
        own_column(skip_all, w_me * channels, channels), (channels, LANES)
    )

    for k in range(1, n_seq):
        first[k - 1].wait_recv()
        spread_value((s_me + n_seq - k) % n_seq)

    for c in turn[: n_wt - 1]:
        c.wait_recv()
    gate_ring.begin()
    for c in turn[n_wt - 1 :]:
        c.wait_recv()
    mix_ring.begin()
    if outer_seq > 1:
        down_ring.hop(1)
    for k in range(1, outer_wt):
        far_lens[k - 1].wait_recv()
        block = lens.at[far_from(k)]
        near_lens.append(wires.send(block, block, (s_me, sibling)))
    for s, k, c in second:
        c.wait_recv()
        block = front.at[s, far_from(k)]
        third.append(wires.send(block, block, (s_me, sibling)))
    for c in third + near_lens:
        c.wait_recv()

    for f in range(n):
        value_full[pl.ds(f * d_rows, d_rows), :] = front[f // n_wt, f % n_wt, pl.ds(16, d_rows), :]
    share = LANES // d_rows
    for b in range(model_width // LANES):
        total = jnp.zeros((2, LANES), jnp.float32)
        for f in range(b * share, (b + 1) * share):
            total = total + front[f // n_wt, f % n_wt, 0:16, 0:LANES].astype(jnp.float32)[0:2]
        norm_out[:, pl.ds(b * LANES, LANES)] = total

    def project(r, unused):
        at = pl.ds(pl.multiple_of(r * LANES, LANES), LANES)
        normed = (xhat[at, :] * norm_out[0:1, :] + norm_out[1:2, :]).astype(jnp.bfloat16)
        pair[w_me, 0, at, :] = normed
        pre = dot(normed, value_full[...])
        pre_ref[at, :] = pre
        turned = jnp.transpose(gelu_tanh(pre))
        for p in range(n):
            act_send[p, :, at] = turned[p * channels : (p + 1) * channels, :].astype(jnp.bfloat16)
        return unused

    lax.fori_loop(0, row_count // LANES, project, 0)
    into = lambda peer: got
    of = halves_of(channels)
    each = channels // of
    for part in range(of):
        swap_start(act_send, into, in_send, in_recv, flat, n, n_wt, part, of)
    got[flat] = act_send[flat]
    fill_segments(lens, seg_ref, sid_ref, docs, n_seq * local_blocks, per, n_wt * seq_count)

    if outer_seq > 1:
        gate_ring.hop(1)
        mix_ring.hop(1)
    clear_unused(table, n_wt * seq_count, n_seq * local_blocks, per, channels)
    zero_pad = jnp.zeros((PAD, LANES), jnp.float32)
    vf[0:PAD, :] = zero_pad
    vp[0:PAD, :] = zero_pad
    yp[pl.ds(rows, PAD), :] = zero_pad
    lower = lax.broadcasted_iota(jnp.int32, (LANES, LANES), 1) >= lax.broadcasted_iota(
        jnp.int32, (LANES, LANES), 0
    )
    swap_wait(act_send, into, in_send, in_recv, flat, n, n_wt, 0, of)

    far_pair = []
    for at in range(2):
        block = pair.at[w_me, at]
        for k in range(1, outer_wt):
            far_pair.append((k, at, wires.send(block, block, (s_me, far_to(k)))))
    near_pair = [wires.send(pair.at[w_me, at], pair.at[w_me, at], (s_me, sibling)) for at in range(2)]

    rows_to_table(got, table, 0, each, *shape)

    def channel(c, unused):
        fill_lane_powers(pw_re, pw_im, c, tab_re, tab_im, 0)
        dr, di = power_rows(pw_re, pw_im, c, 7, bits, n_lag)
        ar, ai = cmul(dr, di, kr_ref[pl.ds(c, 1), :], ki_ref[pl.ds(c, 1), :])
        lags = dot(ar.astype(jnp.bfloat16), tab_re[...].astype(jnp.bfloat16), 1, 1) - dot(
            ai.astype(jnp.bfloat16), tab_im[...].astype(jnp.bfloat16), 1, 1
        )
        lag_ref[c] = lags
        val = table[pl.ds(c, rows, stride=channels), :]
        v_ref[c] = val.astype(jnp.bfloat16)
        vf[pl.ds(PAD, rows), :] = val
        vp[pl.ds(PAD, rows), :] = to_pieces(seg_ref, vf, rows, docs)
        sid = sid_ref[pl.ds(PAD, rows), :]
        before = jnp.zeros((LANES, LANES), jnp.float32)
        total = jnp.zeros((rows, LANES), jnp.float32)
        for d in range(n_lag + 1):
            at = pl.ds(PAD - d, rows)
            x = jnp.where(sid_ref[at, :] == sid, vp[at, :], 0.0).astype(jnp.bfloat16)
            t, before = toeplitz(lags, d, n_lag, lower, before)
            total = total + dot(x, t)
        yp[0:rows, :] = total
        out = from_pieces(seg_ref, yp, rows, docs) + skip_ref[pl.ds(c, 1), :] * val
        table[pl.ds(c, rows, stride=channels), :] = out
        return unused

    hops = [(ring, k) for k in range(2, outer_seq) for ring in rings]
    home = lambda peer: mixed_ref.at[peer % n_wt]
    runs = min(4, channels)
    for run in range(runs):
        if of == 2 and run == runs // 2:
            table_to_rows(table, back, 0, each, *shape)
            swap_start(back, home, out_send, out_recv, flat, n, n_wt, 0, of)
            swap_wait(act_send, into, in_send, in_recv, flat, n, n_wt, 1, of)
            rows_to_table(got, table, each, each, *shape)
        lax.fori_loop(run * channels // runs, (run + 1) * channels // runs, channel, 0)
        for ring, k in hops[run * len(hops) // (runs + 1) : (run + 1) * len(hops) // (runs + 1)]:
            ring.hop(k)
    table_to_rows(table, back, channels - each, each, *shape)
    swap_start(back, home, out_send, out_recv, flat, n, n_wt, of - 1, of)
    own = pltpu.make_async_copy(back.at[flat], mixed_ref.at[w_me, flat], local_sem)
    own.start()
    for ring, k in hops[runs * len(hops) // (runs + 1) :]:
        ring.hop(k)
    own.wait()
    for part in range(of):
        swap_wait(back, home, out_send, out_recv, flat, n, n_wt, part, of)

    block = mixed_ref.at[w_me]
    far_mixed = [wires.send(block, block, (s_me, far_to(k))) for k in range(1, outer_wt)]
    ends = [wires.send(block, block, (s_me, sibling))]
    for k, at, c in far_pair:
        c.wait_recv()
        block = pair.at[far_from(k), at]
        near_pair.append(wires.send(block, block, (s_me, sibling)))
    for k in range(1, outer_wt):
        far_mixed[k - 1].wait_recv()
        block = mixed_ref.at[far_from(k)]
        ends.append(wires.send(block, block, (s_me, sibling)))
    for c in near_pair + ends:
        c.wait_recv()
    for ring in rings:
        ring.end()
    wires.sent()


def front_loading(n_lag, docs, bits, seq_count, per, inner_seq, n_in, *refs):
    sources, held, load_sem = refs[:n_in], refs[-n_in - 1 : -1], refs[-1]
    loads = [
        pltpu.make_async_copy(source, target, load_sem.at[at])
        for at, (source, target) in enumerate(zip(sources, held))
    ]
    for c in loads:
        c.start()
    front_kernel(
        n_lag, docs, bits, seq_count, per, inner_seq, loads, *held, *refs[n_in : -n_in - 1]
    )


def front_call(
    x, cot, value, gain, bias, gate, mix, down, lens, rate, freq, kr, ki, step, skip, n_lag, inner_seq,
):
    n_seq, n_wt = lax.axis_size("seq"), lax.axis_size("wt")
    n = n_seq * n_wt
    seq_count, docs = lens.shape
    local, model_width = x.shape
    states = kr.shape[1]
    width = value.shape[1]
    channels = width // n
    blocks = n_seq * local // seq_count // LANES
    per = -(-(blocks + docs) // 8) * 8
    rows = n_wt * seq_count * per
    bits = (n_lag - 1).bit_length()
    f_part = gate.shape[1] // n_wt
    low = jnp.bfloat16
    wires = front_wires(n_seq, n_wt)
    hops = (2 + inner_seq) * (n_seq // inner_seq)
    out = jax.ShapeDtypeStruct
    arrays = (x, cot, value, gain, bias, gate, mix, down, lens, rate, freq, kr, ki, step, skip)
    table = out((rows + 2 * PAD, LANES), jnp.int32)
    return pl.pallas_call(
        functools.partial(
            front_loading, n_lag, docs, bits, seq_count, per, inner_seq, len(arrays)
        ),
        out_shape=(
            out((n_wt, 2, local, model_width), low),
            out((n_seq, n_wt) + (gate.shape[0], f_part), low),
            out((n_seq, n_wt) + (mix.shape[0], f_part), low),
            out((n_seq,) + down.shape, low),
            out((n_wt, n, channels, local), low),
            out((channels, rows, LANES), low),
            out((channels, n_lag, LANES), jnp.float32),
            out((local, width), jnp.float32),
            out((model_width, width), low),
            out((2, model_width), jnp.float32),
            table, table,
        ),
        in_specs=[pl.BlockSpec(memory_space=pltpu.HBM)] * len(arrays),
        out_specs=(pl.BlockSpec(memory_space=pltpu.VMEM),) * 12,
        scratch_shapes=[pltpu.VMEM((n_wt, 8, LANES), jnp.int32)]
        + [vmem(7 + bits, channels, states)] * 2
        + [vmem(channels, states)] * 2
        + [vmem(channels, LANES)]
        + [vmem(PAD + rows, LANES)] * 3
        + [vmem(LANES, states), vmem(LANES, states), vmem(rows * channels, LANES)]
        + [pltpu.VMEM((n, channels, local), low)] * 2
        + [pltpu.VMEM((n_seq, n_wt, 16 + value.shape[0], width), low), vmem(local, model_width)]
        + [pltpu.VMEM((n, channels, local), low)]
        + [pltpu.VMEM((n_wt, gate.shape[0], f_part), low), pltpu.VMEM((n_wt, mix.shape[0], f_part), low)]
        + [pltpu.SemaphoreType.DMA((halves_of(channels),))] * 4
        + [pltpu.SemaphoreType.DMA((wires,))] * 2
        + [pltpu.SemaphoreType.DMA]
        + [pltpu.SemaphoreType.DMA((hops,))] * 6
        + [pltpu.VMEM(a.shape, a.dtype) for a in arrays]
        + [pltpu.SemaphoreType.DMA((len(arrays),))],
        compiler_params=pltpu.CompilerParams(
            vmem_limit_bytes=(38 if n <= 32 else 58) << 20, collective_id=1, has_side_effects=True
        ),
        cost_estimate=pl.CostEstimate(
            flops=60_000_000_000, bytes_accessed=4_000_000, transcendentals=0
        ),
        name="front",
    )(*[pltpu.with_memory_space_constraint(a, pltpu.HBM) for a in arrays])


GELU_A = 0.7978845608028654
GELU_B = 0.044715


def gelu_pair(v):
    square = v * v
    t = jnp.tanh(GELU_A * (v + GELU_B * v * square))
    half = 0.5 * (1.0 + t)
    slope = half + 0.5 * v * (1.0 - t * t) * (GELU_A * (1.0 + 3.0 * GELU_B * square))
    return v * half, slope


def back_wires(n_seq, n_wt, inner):
    outer = n_seq // inner
    over_seq = 4 * ((inner - 1) * outer + (outer - 1))
    over_wt = 2 * (1 + n_wt // 2 - 1)
    return over_seq + over_wt + 3 * (n_wt - 1) + (n_wt // 2 - 1) + n_wt // 2 + n_wt - 1


class SeqSum:
    def __init__(self, wires, send, near_in, far_in, so, si, outer, inner, s_to):
        self.wires, self.send, self.near_in, self.far_in = wires, send, near_in, far_in
        self.so, self.outer, self.inner, self.s_to = so, outer, inner, s_to
        self.near, self.far, self.held = {}, [], None

    def begin(self, *distances):
        for k in distances or range(1, self.outer + 1):
            k = k % self.outer
            if k in self.near:
                continue
            z = (self.so + k) % self.outer
            self.near[k] = [
                self.wires.send(self.send.at[j, z], self.near_in.at[j - 1, k], self.s_to(0, j))
                for j in range(1, self.inner)
            ]

    def turn(self, *distances):
        for k in distances or range(1, self.outer + 1):
            k = k % self.outer
            if k not in self.near or k in self.far:
                continue
            for c in self.near[k]:
                c.wait_recv()
            z = (self.so + k) % self.outer
            total = self.send[0, z].astype(jnp.float32)
            for j in range(1, self.inner):
                total = total + self.near_in[j - 1, k].astype(jnp.float32)
            self.send[0, z] = total.astype(jnp.bfloat16)
            if k:
                self.near[-k] = self.wires.send(
                    self.send.at[0, z], self.far_in.at[k - 1], self.s_to(k, 0)
                )
            self.far.append(k)

    def end(self):
        total = self.send[0, self.so].astype(jnp.float32)
        for k in range(1, self.outer):
            self.near[-k].wait_recv()
            total = total + self.far_in[k - 1].astype(jnp.float32)
        return total


def back_kernel(
    n_lag, docs, bits, seq_count, per, inner_seq,
    pair, gate_w, mix_w, down_w, mixed, v_ref, lag_ref, pre_ref, value_full, norm_vec, x_ref,
    seg_ref, sid_ref, rate_all, freq_all, kr_all, ki_all, step_ref, skip_all,
    out_ref, in_grad, gate_last, value_last, mix_last, down_out, norm_out, all_out,
    pw_re, pw_im, kr_ref, ki_ref, rate_ref, freq_ref, dt_ref, skip_ref, vf, gf, vp, gp, yp, tab_re, tab_im, table, got, back, dv_ref,
    product, expand_grad, gate_grad, mg, mg_in, mg_far, tok, tok_in, tok_far,
    down_flat, down_s, down_n, down_f, mix_s, mix_n, mix_f, gate_s, gate_n, gate_f,
    value_s, value_n, value_f, turned, value_cut, value_all, last_send, norm_last,
    in_send, in_recv, out_send, out_recv, wire_send, wire_recv, local_sem, *held,
):
    grads, thin = held[:4], held[4:]
    low, wide = jnp.bfloat16, jnp.float32
    channels, rows, _ = v_ref.shape
    states = kr_all.shape[1]
    n_seq, n_wt = lax.axis_size("seq"), lax.axis_size("wt")
    n = n_seq * n_wt
    s_me, w_me = lax.axis_index("seq"), lax.axis_index("wt")
    flat = s_me * n_wt + w_me
    row_count, model_width = x_ref.shape
    width = mix_w.shape[0]
    f_part = gate_w.shape[1]
    f_rows = f_part // n_seq
    d_band, h_band, v_band = model_width // n_seq, width // n_seq, width // n_wt
    d_rows, h_rows = d_band // n_wt, h_band // n_wt
    local_blocks = row_count // LANES // seq_count
    shape = (n_seq, n_wt, seq_count, local_blocks, per, channels)
    outer_wt = n_wt // 2
    o, i = w_me // 2, w_me % 2
    sibling = (s_me, o * 2 + 1 - i)
    far_to = lambda k: (s_me, ((o + k) % outer_wt) * 2 + i)
    outer_seq = n_seq // inner_seq
    so, si = s_me // inner_seq, s_me % inner_seq
    s_to = lambda k, j: (((so + k) % outer_seq) * inner_seq + (si + j) % inner_seq, w_me)
    wires = Wires(wire_send, wire_recv)
    sums = lambda send, near_in, far_in: SeqSum(
        wires, send, near_in, far_in, so, si, outer_seq, inner_seq, s_to
    )
    down_sum, mix_sum = sums(down_s, down_n, down_f), sums(mix_s, mix_n, mix_f)
    gate_sum, value_sum = sums(gate_s, gate_n, gate_f), sums(value_s, value_n, value_f)

    meet(flat, n, n_wt)

    def tokens(t, unused):
        j, k = 1 - t // outer_wt, outer_wt - 1 - t % outer_wt
        w = ((o + k) % outer_wt) * 2 + (i + j) % 2
        at = pl.ds(pl.multiple_of(w * row_count, row_count), row_count)
        act, slope = gelu_pair(dot(pair[w, 0], gate_w[...]))
        from_out = dot(pair[w, 1], down_w[...], 1, 1)
        expand = dot(mixed[w], mix_w[...], 0, 0)
        product[at, :] = (expand * act).astype(low)
        gate_grad[at, :] = (from_out * expand * slope).astype(low)
        grad = (from_out * act).astype(low)
        expand_grad[at, :] = grad
        mg[j, k] = dot(mix_w[...], grad, 1, 1).astype(low)
        return unused

    lax.fori_loop(0, outer_wt, tokens, 0)
    near = wires.send(mg.at[1], mg_in, sibling)
    lax.fori_loop(outer_wt, n_wt, tokens, 0)
    piece = min(256, f_part)
    every = n_wt * row_count

    def down_part(r, unused):
        at = pl.ds(pl.multiple_of(r * piece, piece), piece)
        cot = pair[:, 1].reshape(every, model_width)
        down_flat[at, :] = dot(product[:, at], cot, 0, 0)
        return unused

    lax.fori_loop(0, f_part // piece, down_part, 0)
    def bands(size):
        for s in range(n_seq):
            j = (s % inner_seq + inner_seq - si) % inner_seq
            yield j, s // inner_seq, slice(s * size, (s + 1) * size)

    for j, z, at in bands(f_rows):
        down_s[j, z] = down_flat[at, :].astype(low)
    down_sum.begin(1, 2, 3)
    near.wait_recv()
    far = []
    for k in range(1, outer_wt):
        mg[0, k] = (mg[0, k].astype(wide) + mg_in[k].astype(wide)).astype(low)
        far.append(wires.send(mg.at[0, k], mg_far.at[k - 1], far_to(k)))

    for j, z, at in bands(d_band):
        normed = pair[:, 0, :, at].reshape(every, d_band)
        gate_s[j, z] = dot(normed, gate_grad[...], 0, 0).astype(low)

    total = mg[0, 0].astype(wide) + mg_in[0].astype(wide)
    for k in range(1, outer_wt):
        far[k - 1].wait_recv()
        total = total + mg_far[k - 1].astype(wide)
    turned[...] = total
    for p in range(n):
        back[p] = turned[p * channels : (p + 1) * channels, :].astype(low)
    into = lambda peer: got
    of = halves_of(channels)
    each = channels // of
    for part in range(of):
        swap_start(back, into, in_send, in_recv, flat, n, n_wt, part, of)
    got[flat] = back[flat]

    for j, z, at in bands(h_band):
        total = dot(mixed[0, at, :], expand_grad[0:row_count, :])
        for w in range(1, n_wt):
            total = total + dot(
                mixed[w, at, :], expand_grad[w * row_count : (w + 1) * row_count, :]
            )
        mix_s[j, z] = total.astype(low)

    def token_part(t, unused):
        j, k = 1 - t // outer_wt, outer_wt - 1 - t % outer_wt
        w = ((o + k) % outer_wt) * 2 + (i + j) % 2
        at = pl.ds(pl.multiple_of(w * row_count, row_count), row_count)
        tok[j, k, 0] = dot(product[at, :], down_w[...]).astype(low)
        tok[j, k, 1] = dot(gate_grad[at, :], gate_w[...], 1, 1).astype(low)
        return unused

    lax.fori_loop(0, outer_wt, token_part, 0)
    tok_near = wires.send(tok.at[1], tok_in, sibling)
    lax.fori_loop(outer_wt, n_wt, token_part, 0)

    mine = lambda ref: own_rows(ref, w_me, n_wt, channels)
    for one, every_one in ((kr_ref, kr_all), (ki_ref, ki_all), (rate_ref, rate_all), (freq_ref, freq_all)):
        one[...] = mine(every_one)
    dt = jnp.exp(own_column(step_ref, w_me * channels, channels))
    dt_ref[...] = jnp.broadcast_to(dt, (channels, states))
    fill_powers(rate_ref[...], freq_ref[...], dt, pw_re, pw_im)
    skip_ref[...] = jnp.broadcast_to(
        own_column(skip_all, w_me * channels, channels), (channels, LANES)
    )
    zero_pad = jnp.zeros((PAD, LANES), wide)
    clear_unused(table, n_wt * seq_count, n_seq * local_blocks, per, channels)
    vf[0:PAD, :] = zero_pad
    gf[0:PAD, :] = zero_pad
    vp[0:PAD, :] = zero_pad
    gp[pl.ds(rows, PAD), :] = zero_pad
    yp[pl.ds(rows, PAD), :] = zero_pad
    tok_near.wait_recv()
    tok_sent = []
    for k in range(1, outer_wt):
        for a in range(2):
            tok[0, k, a] = (tok[0, k, a].astype(wide) + tok_in[k, a].astype(wide)).astype(low)
        tok_sent.append(wires.send(tok.at[0, k], tok_far.at[k - 1], far_to(k)))
    swap_wait(back, into, in_send, in_recv, flat, n, n_wt, 0, of)
    down_sum.turn(1, 2)
    down_sum.begin(0)
    gate_sum.begin(1, 2)
    rows_to_table(got, table, 0, each, *shape)

    lane = lax.broadcasted_iota(jnp.int32, (LANES, LANES), 1)
    row = lax.broadcasted_iota(jnp.int32, (LANES, LANES), 0)
    lower = lane >= row
    wraps = lane + row >= LANES
    flip = (lane + row == LANES - 1).astype(jnp.bfloat16)
    lag_place = (
        lax.broadcasted_iota(jnp.int32, (n_lag, LANES), 0) * LANES
        + lax.broadcasted_iota(jnp.int32, (n_lag, LANES), 1)
        + 1
    ).astype(jnp.float32)

    def channel(c, unused):
        own = pl.ds(c, 1)
        val = v_ref[c].astype(jnp.float32)
        grad = table[pl.ds(c, rows, stride=channels), :]
        vf[pl.ds(PAD, rows), :] = val
        gf[pl.ds(PAD, rows), :] = grad
        skip_grad = jnp.sum(jnp.sum(val * grad, axis=0, keepdims=True), axis=1, keepdims=True)
        g_piece = to_pieces(seg_ref, gf, rows, docs)
        gp[0:rows, :] = g_piece
        v_piece = to_pieces(seg_ref, vf, rows, docs).astype(jnp.bfloat16)
        vp[pl.ds(PAD, rows), :] = dot(v_piece, flip)
        g_turned = jnp.transpose(g_piece).astype(jnp.bfloat16)
        sid = sid_ref[pl.ds(PAD, rows), :]
        lags = lag_ref[c]
        before = jnp.zeros((LANES, LANES), jnp.float32)
        total = jnp.zeros((rows, LANES), jnp.float32)
        earlier = None
        sums = []
        for d in range(n_lag + 1):
            ahead = pl.ds(PAD + d, rows)
            x = jnp.where(sid_ref[ahead, :] == sid, gp[pl.ds(d, rows), :], 0.0)
            t, before = toeplitz(lags, d, n_lag, lower, before)
            total = total + dot(x.astype(jnp.bfloat16), t, 1, 1)
            at = pl.ds(PAD - d, rows)
            back = jnp.where(sid_ref[at, :] == sid, vp[at, :], 0.0).astype(jnp.bfloat16)
            pairs = dot(g_turned, back)
            if d:
                skew = jnp.where(wraps, earlier, pairs)
                skew = pltpu.roll(skew, 0, 1, stride=1, stride_axis=0)
                sums.append(jnp.sum(skew, axis=0, keepdims=True))
            earlier = pairs
        yp[0:rows, :] = total
        out = from_pieces(seg_ref, yp, rows, docs) + skip_ref[own, :] * grad
        table[pl.ds(c, rows, stride=channels), :] = out
        lag_grad = jnp.concatenate(sums, axis=0)
        fill_lane_powers(pw_re, pw_im, c, tab_re, tab_im, 1)
        both = jnp.concatenate([lag_grad, lag_grad * lag_place], axis=0).astype(jnp.bfloat16)
        part_re = dot(both, tab_re[...].astype(jnp.bfloat16))
        part_im = dot(both, tab_im[...].astype(jnp.bfloat16))
        dr, di = power_rows(pw_re, pw_im, c, 7, bits, n_lag)
        gr, gi = cmul(dr, di, part_re[0:n_lag], part_im[0:n_lag])
        hr, hi = cmul(dr, di, part_re[n_lag:], part_im[n_lag:])
        gr, gi, hr, hi = (jnp.sum(a, axis=0, keepdims=True) for a in (gr, gi, hr, hi))
        kr, ki, dt = kr_ref[own, :], ki_ref[own, :], dt_ref[own, :]
        rate_grad = -dt * (kr * hr - ki * hi)
        freq_grad = -dt * (kr * hi + ki * hr)
        for at, row_out in enumerate((rate_grad, freq_grad, gr + skip_grad, -gi)):
            grads[at][own, :] = row_out
        step = jnp.sum(
            rate_grad * rate_ref[own, :] + freq_grad * freq_ref[own, :], axis=1, keepdims=True
        )
        for at, one in enumerate((step, skip_grad)):
            thin[at][own, :] = jnp.broadcast_to(one, (1, LANES))
        return unused

    lax.fori_loop(0 * channels // 4, 1 * channels // 4, channel, 0)
    down_sum.turn(3)
    gate_sum.begin(3)
    lax.fori_loop(1 * channels // 4, 2 * channels // 4, channel, 0)
    gate_sum.turn(1)
    gate_sum.begin(0)
    home = lambda peer: dv_ref
    if of == 2:
        table_to_rows(table, back, 0, each, *shape)
        swap_start(back, home, out_send, out_recv, flat, n, n_wt, 0, of)
        swap_wait(back, into, in_send, in_recv, flat, n, n_wt, 1, of)
        rows_to_table(got, table, each, each, *shape)
    lax.fori_loop(2 * channels // 4, 3 * channels // 4, channel, 0)
    down_sum.turn(0)
    gate_sum.turn(2)
    mix_sum.begin(1, 2)
    lax.fori_loop(3 * channels // 4, 4 * channels // 4, channel, 0)
    gate_sum.turn(3)
    table_to_rows(table, back, channels - each, each, *shape)
    swap_start(back, home, out_send, out_recv, flat, n, n_wt, of - 1, of)
    own = pltpu.make_async_copy(back.at[flat], dv_ref.at[flat], local_sem)
    own.start()
    mix_sum.begin(3, 0)
    for at in range(4):
        all_out[w_me, :, pl.ds(at * states, states)] = grads[at][...]
    for at in range(2):
        all_out[w_me, :, pl.ds(4 * states + at * LANES, LANES)] = thin[at][...]
    block = all_out.at[w_me]
    far_all = [wires.send(block, block, far_to(k)) for k in range(1, outer_wt)]
    near_all = [wires.send(block, block, sibling)]

    for c in tok_sent:
        c.wait_recv()
    result = x_ref[...].astype(wide) + tok[0, 0, 0].astype(wide) + tok_in[0, 0].astype(wide)
    for k in range(1, outer_wt):
        result = result + tok_far[k - 1, 0].astype(wide)
    out_ref[...] = result.astype(low)
    own.wait()
    for part in range(of):
        swap_wait(back, home, out_send, out_recv, flat, n, n_wt, part, of)

    gate_sum.turn(0)
    mix_sum.turn(1, 2)

    for p in range(n):
        turned[pl.ds(p * channels, channels), :] = dv_ref[p].astype(wide)
    value_grad = jnp.transpose(turned[...]) * gelu_pair(pre_ref[...])[1]
    value_low = value_grad.astype(low)
    for w in range(n_wt):
        value_cut[w] = value_low[:, w * v_band : (w + 1) * v_band]
    value_all[w_me] = value_cut[w_me]
    moves = []
    for k in range(outer_wt):
        for j in range(2):
            if k or j:
                w = ((o + k) % outer_wt) * 2 + (i + j) % 2
                moves.append(wires.send(value_cut.at[w], value_all.at[w_me], (s_me, w)))

    normed_grad = dot(value_low, value_full[...], 1, 1)
    normed_grad = normed_grad + tok[0, 0, 1].astype(wide) + tok_in[0, 1].astype(wide)
    for k in range(1, outer_wt):
        normed_grad = normed_grad + tok_far[k - 1, 1].astype(wide)
    x32 = x_ref[...].astype(wide)
    centered = x32 - jnp.mean(x32, axis=-1, keepdims=True)
    scale = lax.rsqrt(jnp.mean(centered * centered, axis=-1, keepdims=True) + norm_epsilon)
    xhat = centered * scale
    g = normed_grad * norm_vec[0:1, :]
    inner_grad = g - jnp.mean(g, axis=-1, keepdims=True)
    inner_grad = inner_grad - xhat * jnp.mean(g * xhat, axis=-1, keepdims=True)
    in_grad[...] = pair[w_me, 1].astype(wide) + inner_grad * scale
    vectors = jnp.concatenate(
        [
            jnp.sum(normed_grad * xhat, axis=0, keepdims=True),
            jnp.sum(normed_grad, axis=0, keepdims=True),
            jnp.zeros((14, model_width), wide),
        ],
        axis=0,
    )
    norm_last[...] = vectors

    mix_sum.turn(3, 0)
    for c in moves:
        c.wait_recv()
    vector_lanes = min(d_band, LANES)
    for j, z, at in bands(d_band):
        normed = pair[:, 0, :, at].reshape(every, d_band)
        value_s[j, z, 0:d_band, :] = dot(
            normed, value_all[...].reshape(every, v_band), 0, 0
        ).astype(low)
        value_s[j, z, pl.ds(d_band, 16), 0:vector_lanes] = norm_last[:, at].astype(low)
    value_sum.begin()
    for one in (down_sum, gate_sum, mix_sum):
        one.begin()
        one.turn()
    down_out[...] = down_sum.end()
    mix_band = mix_sum.end().astype(low)
    gate_band = gate_sum.end().astype(low)
    value_sum.turn()
    for w in range(n_wt):
        gate_cut = gate_band[w * d_rows : (w + 1) * d_rows, :]
        mix_cut = mix_band[w * h_rows : (w + 1) * h_rows, :]
        last_send[w] = jnp.concatenate([gate_cut, mix_cut], axis=0)
    heads = gate_last
    heads[w_me] = last_send[w_me]
    ends = []

    def spread(source, target):
        for k in range(outer_wt):
            for j in range(2):
                if k or j:
                    w = ((o + k) % outer_wt) * 2 + (i + j) % 2
                    ends.append(wires.send(source.at[w], target.at[w_me], (s_me, w)))

    spread(last_send, heads)
    for k in range(1, outer_wt):
        far_all[k - 1].wait_recv()
        block = all_out.at[((o + outer_wt - k) % outer_wt) * 2 + i]
        near_all.append(wires.send(block, block, sibling))
    value_band = value_sum.end()
    tail_send = mix_last
    for w in range(n_wt):
        tail_send[w, 0:d_rows, :] = value_band[w * d_rows : (w + 1) * d_rows, :].astype(low)
        tail_send[w, pl.ds(d_rows, 16), :] = value_band[d_band : d_band + 16, :].astype(low)
    value_last[w_me] = tail_send[w_me]
    spread(tail_send, value_last)
    for c in ends + near_all:
        c.wait_recv()
    wires.sent()
    norm = jnp.zeros((16, v_band), wide)
    for w in range(n_wt):
        norm = norm + value_last[w, pl.ds(d_rows, 16), :].astype(wide)
    norm_out[...] = norm


def back_call(
    pair, gate_w, mix_w, down_w, mixed, v, lags, pre, value_full, norm_vec, x, seg, sid, rate, freq, kr,
    ki, step, skip, seq_count, docs, n_lag, inner_seq,
):
    n_seq, n_wt = lax.axis_size("seq"), lax.axis_size("wt")
    n = n_seq * n_wt
    channels, rows, _ = v.shape
    states = kr.shape[1]
    per = rows // (n_wt * seq_count)
    bits = (n_lag - 1).bit_length()
    local, model_width = x.shape
    width, f_part = mix_w.shape
    d_band, h_band, v_band = model_width // n_seq, width // n_seq, width // n_wt
    d_rows, h_rows = d_band // n_wt, h_band // n_wt
    f_rows = f_part // n_seq
    inner, outer, outer_wt = inner_seq, n_seq // inner_seq, n_wt // 2
    low = jnp.bfloat16
    half = lambda *s: pltpu.VMEM(s, low)
    out = jax.ShapeDtypeStruct
    wires = back_wires(n_seq, n_wt, inner)

    def seq_scratch(*block):
        return [
            half(inner, outer, *block), half(max(inner - 1, 1), outer, *block),
            half(max(outer - 1, 1), *block),
        ]

    every = n_wt * local
    return pl.pallas_call(
        functools.partial(back_kernel, n_lag, docs, bits, seq_count, per, inner_seq),
        out_shape=(
            out((local, model_width), low),
            out((local, model_width), jnp.float32),
            out((n_wt, d_rows + h_rows, f_part), low),
            out((n_wt, d_rows + 16, v_band), low),
            out((n_wt, d_rows + 16, v_band), low),
            out((f_rows, model_width), jnp.float32),
            out((16, v_band), jnp.float32),
            out((n_wt, channels, 4 * states + 2 * LANES), jnp.float32),
        ),
        in_specs=[pl.BlockSpec(memory_space=pltpu.VMEM)] * 19,
        out_specs=(pl.BlockSpec(memory_space=pltpu.VMEM),) * 8,
        scratch_shapes=[vmem(7 + bits, channels, states)] * 2
        + [vmem(channels, states)] * 5
        + [vmem(channels, LANES)]
        + [vmem(PAD + rows, LANES)] * 5
        + [vmem(LANES, states), vmem(LANES, states), vmem(rows * channels, LANES)]
        + [half(n, channels, local)] * 3
        + [half(every, f_part)] * 3
        + [half(2, outer_wt, width, local), half(outer_wt, width, local)]
        + [half(max(outer_wt - 1, 1), width, local)]
        + [half(2, outer_wt, 2, local, model_width), half(outer_wt, 2, local, model_width)]
        + [half(max(outer_wt - 1, 1), 2, local, model_width)]
        + [vmem(f_part, model_width)]
        + seq_scratch(f_rows, model_width)
        + seq_scratch(h_band, f_part)
        + seq_scratch(d_band, f_part)
        + seq_scratch(d_band + 16, v_band)
        + [vmem(width, local), half(n_wt, local, v_band), half(n_wt, local, v_band)]
        + [half(n_wt, d_rows + h_rows, f_part), vmem(16, model_width)]
        + [pltpu.SemaphoreType.DMA((halves_of(channels),))] * 4
        + [pltpu.SemaphoreType.DMA((wires,))] * 2
        + [pltpu.SemaphoreType.DMA]
        + [vmem(channels, states)] * 4
        + [vmem(channels, LANES)] * 2,
        compiler_params=pltpu.CompilerParams(
            vmem_limit_bytes=(39 if n <= 32 else 62) << 20, collective_id=2, has_side_effects=True
        ),
        cost_estimate=pl.CostEstimate(
            flops=60_000_000_000, bytes_accessed=4_000_000, transcendentals=0
        ),
        name="back",
    )(
        pair, gate_w, mix_w, down_w, mixed, v, lags, pre, value_full, norm_vec, x, seg, sid, rate, freq,
        kr, ki, step, skip,
    )


def finish_kernel(
    out_ref, grad_ref, heads, tails, down_ref, norm_ref, all_ref,
    outputs, in_grad, gain, bias, gate, value, mix, down, rate, freq, kr, ki, step, skip,
):
    n_seq, n_wt = lax.axis_size("seq"), lax.axis_size("wt")
    w_me = lax.axis_index("wt")
    wide = jnp.float32
    d_rows, h_rows = gate.shape[0], mix.shape[0]
    f_rows = heads.shape[2] // n_seq
    channels, states = all_ref.shape[1], rate.shape[1]
    outputs[...] = out_ref[...]
    in_grad[...] = grad_ref[...]
    down[...] = down_ref[...]
    for ref, first, rows in ((gate, 0, d_rows), (mix, d_rows, h_rows)):
        parts = [heads[w].astype(wide)[first : first + rows, :] for w in range(n_wt)]
        cut = [
            parts[w][:, s * f_rows : (s + 1) * f_rows] for s in range(n_seq) for w in range(n_wt)
        ]
        ref[...] = jnp.concatenate(cut, axis=1)
    value[...] = jnp.concatenate(
        [tails[w].astype(wide)[0:d_rows, :] for w in range(n_wt)], axis=1
    )
    share = norm_ref.shape[1]
    own = pltpu.roll(norm_ref[...], (share - w_me * d_rows) % share, 1)[:, 0:d_rows]
    gain[...] = own[0:1, :]
    bias[...] = own[1:2, :]
    for at, ref in enumerate((rate, freq, kr, ki)):
        for w in range(n_wt):
            ref[pl.ds(w * channels, channels), :] = all_ref[w, :, pl.ds(at * states, states)]
    total = n_wt * channels
    lane = lax.broadcasted_iota(jnp.int32, (channels, LANES), 1)
    place = lax.broadcasted_iota(jnp.int32, (channels, LANES), 0)
    for at, ref in enumerate((step, skip)):
        row = jnp.zeros((1, LANES), wide)
        for w in range(n_wt):
            thin = all_ref[w, :, pl.ds(4 * states + at * LANES, LANES)]
            hit = jnp.where(lane == place + w * channels, thin, 0.0)
            row = row + jnp.sum(hit, axis=0, keepdims=True)
        ref[...] = row[:, 0:total]


def finish_call(out, grad, heads, tails, down, norm, packed, gate_width, d_rows, h_rows, states):
    n_wt, channels, _ = packed.shape
    total = n_wt * channels
    wide = jnp.float32
    shape = jax.ShapeDtypeStruct
    full = shape((total, states), wide)
    return pl.pallas_call(
        finish_kernel,
        out_shape=(
            shape(out.shape, out.dtype), shape(grad.shape, wide), shape((1, d_rows), wide),
            shape((1, d_rows), wide), shape((d_rows, gate_width), wide),
            shape((d_rows, n_wt * tails.shape[2]), wide), shape((h_rows, gate_width), wide),
            shape(down.shape, wide), full, full, full, full, shape((1, total), wide),
            shape((1, total), wide),
        ),
        in_specs=[pl.BlockSpec(memory_space=pltpu.VMEM)] * 7,
        out_specs=(pl.BlockSpec(memory_space=pltpu.VMEM),) * 14,
        compiler_params=pltpu.CompilerParams(vmem_limit_bytes=12 << 20),
        name="finish",
    )(out, grad, heads, tails, down, norm, packed)


BOTH = ("seq", "wt")
norm_epsilon = 1e-05


def gelu_tanh(pre_act):
    return jax.nn.gelu(pre_act, approximate=True)


def on_device(
    inputs, cotangent, doc_lengths, norm_gain, norm_bias, gate_weight, value_weight, mix_weight,
    down_weight, decay_rate, frequency, kernel_re, kernel_im, log_step, skip_gain,
):
    seq_count, local_len, model_width = inputs.shape
    n_seq, n_wt = lax.axis_size("seq"), lax.axis_size("wt")
    inner_seq = 2 if n_seq <= 8 else 8
    rows = lambda x: x.reshape(seq_count * local_len, model_width)
    line = lambda x: x.reshape(1, -1)
    width, gate_width = mix_weight.shape[0] * n_seq * n_wt, gate_weight.shape[1]
    f_part = gate_width // n_wt
    n_lag = local_len * n_seq // 2 // LANES
    params = (decay_rate, frequency, kernel_re, kernel_im, line(log_step), line(skip_gain))
    pair, gate_own, mix_own, down_own, mixed, value_ch, lags, pre, value_full, norm, seg, sid = front_call(
        rows(inputs), rows(cotangent), value_weight, line(norm_gain), line(norm_bias), gate_weight,
        mix_weight, down_weight, doc_lengths, *params, n_lag, inner_seq,
    )
    raw = back_call(
        pair, gate_own.reshape(model_width, f_part), mix_own.reshape(width, f_part),
        down_own.reshape(f_part, model_width), mixed.reshape(n_wt, width, -1), value_ch, lags, pre,
        value_full, norm, rows(inputs), seg, sid, *params, seq_count, doc_lengths.shape[1], n_lag,
        inner_seq,
    )
    out, grad, heads, tails, unused, down, vectors, packed = raw
    done = finish_call(
        out, grad, heads, tails, down, vectors, packed, gate_width, value_weight.shape[0],
        mix_weight.shape[0], kernel_re.shape[1],
    )
    flat = [done[i].reshape(-1) for i in (2, 3, 12, 13)]
    return (
        done[0].reshape(inputs.shape), done[1].reshape(inputs.shape), flat[0], flat[1], *done[4:8],
        *done[8:12], flat[2], flat[3],
    )


def solution(mesh):
    in_specs = (
        P("wt", "seq", None),
        P("wt", "seq", None),
        P("wt", None),
        P(("seq", "wt")),
        P(("seq", "wt")),
        P(("seq", "wt"), None),
        P(("seq", "wt"), None),
        P(("seq", "wt"), None),
        P(("seq", "wt"), None),
        P("seq", None),
        P("seq", None),
        P("seq", None),
        P("seq", None),
        P("seq"),
        P("seq"),
    )
    out_specs = (
        P("wt", "seq", None),
        P("wt", "seq", None),
        P(("seq", "wt")),
        P(("seq", "wt")),
        P(("seq", "wt"), None),
        P(("seq", "wt"), None),
        P(("seq", "wt"), None),
        P(("seq", "wt"), None),
        P("seq", None),
        P("seq", None),
        P("seq", None),
        P("seq", None),
        P("seq"),
        P("seq"),
    )
    return jax.shard_map(
        on_device, mesh=mesh, in_specs=in_specs, out_specs=out_specs, check_vma=False
    )
```
